32 devices in a mesh: dp: 16 (over z, x, core), seq: 2 (over y).
Axes of the slice: x: 2, y: 2, z: 4, core: 2. Of those that a mesh axis runs over, the one named last changes fastest.
Arguments:
- hidden_in: bfloat16 [32, 1024, 1024], P('dp', 'seq'), may hold values from -6 to 6
- family: int32 [16], P('dp'), may hold values from 0 to 63
- orient: int32 [32], P('dp'), may hold values from 0 to 1, as said below
- norm_gain: bfloat16 [1024], replicated, may hold values from 0.099609375 to 1.8984375
- norm_bias: bfloat16 [1024], replicated, may hold values from -4 to 4
- qkv_weight: bfloat16 [1024, 3072], replicated, may hold values from -0.1875 to 0.1875
- out_weight: bfloat16 [1024, 1024], replicated, may hold values from -0.5 to 0.5
- up_weight: bfloat16 [1024, 4096], replicated, may hold values from -0.1875 to 0.1875
- up_bias: bfloat16 [4096], replicated, may hold values from -6 to 6
- down_weight: bfloat16 [4096, 1024], replicated, may hold values from -0.09375 to 0.09375
- down_bias: bfloat16 [1024], replicated, may hold values from -4 to 4
- family_table: bfloat16 [64, 1024], replicated, may hold values from -6 to 6
- orient_table: bfloat16 [2, 1024], replicated, may hold values from -6 to 6
- cotangent: bfloat16 [32, 1024, 1024], P('dp', 'seq'), may hold values from -6 to 6
Outputs:
- layer_out: bfloat16 [32, 1024, 1024], P('dp', 'seq')
- input_grad: float32 [32, 1024, 1024], P('dp', 'seq')
- norm_gain_grad: float32 [1024], replicated
- norm_bias_grad: float32 [1024], replicated
- qkv_weight_grad: float32 [1024, 3072], P(('dp', 'seq'))
- out_weight_grad: float32 [1024, 1024], P(('dp', 'seq'))
- up_weight_grad: float32 [1024, 4096], P(('dp', 'seq'))
- up_bias_grad: float32 [4096], replicated
- down_weight_grad: float32 [4096, 1024], P(('dp', 'seq'))
- down_bias_grad: float32 [1024], replicated
- family_table_grad: float32 [64, 1024], replicated
- orient_table_grad: float32 [2, 1024], replicated
The draws below stay inside these ranges and needn't reach their ends.
Inputs may be any that keep to these rules, and one draw needn't show every extreme that they name: `orient`: in each pair of rows 2p and 2p + 1 one row has flag 0 and the other flag 1.
All inputs are finite; a program needn't handle non-finite values.
Results may differ from the reference program's by a relative error of at most 0.006.
Values may be sent and summed in bfloat16 or wider, within the bound.
A program may use at most 256 MiB of HBM per device.

```python
import math
import jax
import jax.numpy as jnp
from jax import lax

D = 1024
H = 16
FF = 4096
HD = 64
ROT = 32
FAMILIES = 64
LEN = 1024
ROWS = 32
PAIRS = 16


def draw_orient(key, part):
    flipped = jax.random.randint(key, (ROWS // 2,), 0, 2)
    return jnp.stack([flipped, 1 - flipped], axis=1).reshape(ROWS).astype(jnp.int32)


def with_ends(entries, key, low, high):
    index_at = [jax.random.randint(jax.random.fold_in(key, axis), (), 0, length) for axis, length in enumerate(entries.shape)]
    main_axis = entries.shape.index(max(entries.shape))
    beside = index_at[:main_axis] + [(index_at[main_axis] + 1) % entries.shape[main_axis]] + index_at[main_axis + 1:]
    return entries.at[tuple(index_at)].set(low).at[tuple(beside)].set(high)


def levels(rng, shape, cuts, low, largest):
    def one(dim, shards_of):
        draws = jax.random.uniform(jax.random.fold_in(jax.random.fold_in(rng, 6), dim), (shards_of,), jnp.float32, low / len(cuts), largest / len(cuts))
        return jnp.repeat(jnp.exp(draws), shape[dim] // shards_of).reshape((-1,) + (1,) * (len(shape) - dim - 1))

    factor_of = one(*cuts[0])
    for cut in cuts[1:]:
        factor_of = factor_of * one(*cut)
    return factor_of


def normal_values(stream_key, dims, width, reach, cuts=(), held_as=jnp.bfloat16):
    array = jax.random.normal(stream_key, dims, jnp.float32) * width
    if len(cuts) > 0:
        array = levels(stream_key, dims, cuts, -0.22, 0.18) * array
    return jnp.clip(array, min=-reach, max=reach).astype(held_as)


def setup_inputs(seed: int = 0) -> dict:
    key_of = jax.random.split(jax.random.key(seed), 15)
    return {
        "hidden_in": normal_values(key_of[0], (ROWS, LEN, D), 1.0, 6.0, ((0, 16), (1, 2))),
        "family": with_ends(jax.random.randint(key_of[1], (PAIRS,), 0, FAMILIES), jax.random.fold_in(key_of[1], 1), 0, FAMILIES - 1).astype(jnp.int32),
        "orient": draw_orient(jax.random.fold_in(key_of[14], 71), 0),
        "norm_gain": jnp.clip(1.0 + 0.18 * jax.random.normal(key_of[3], (D,), jnp.float32), 0.099609375, 1.8984375).astype(jnp.bfloat16),
        "norm_bias": normal_values(key_of[4], (D,), 0.3, 4.0),
        "qkv_weight": normal_values(key_of[5], (D, 3 * D), D ** -0.5, 0.1875),
        "out_weight": normal_values(key_of[6], (D, D), (D // 8) ** -0.5, 0.5),
        "up_weight": normal_values(key_of[7], (D, FF), D ** -0.5, 0.1875),
        "up_bias": normal_values(key_of[8], (FF,), 0.5, 6.0),
        "down_weight": normal_values(key_of[9], (FF, D), FF ** -0.5, 0.09375),
        "down_bias": normal_values(key_of[10], (D,), 0.3, 4.0),
        "family_table": normal_values(key_of[11], (FAMILIES, D), 0.5, 6.0),
        "orient_table": normal_values(key_of[12], (2, D), 0.5, 6.0),
        "cotangent": normal_values(key_of[13], (ROWS, LEN, D), 1.0, 6.0, ((0, 16), (1, 2))),
    }


@jax.custom_vjp
def low(v):
    return lax.optimization_barrier(v.astype(jnp.bfloat16)).astype(jnp.float32)

@jax.custom_vjp
def low_back(v):
    return v

def low_keep(v):
    return (low(v), None)

def low_pass(kept, grad):
    return (grad,)

def back_keep(v):
    return (v, None)

def back_low(kept, grad):
    return (low(grad),)
low.defvjp(low_keep, low_pass)
low_back.defvjp(back_keep, back_low)

def matmul(left, right):
    return jnp.einsum('...d,de->...e', left, right, precision=lax.Precision.HIGHEST)

def rope_tables(positions):
    column = jnp.arange(D, dtype=jnp.int32)
    within = column % HD
    frequency = jnp.exp(-(2.0 * (within // 2).astype(jnp.float32) / ROT) * math.log(10000.0))
    angles = positions[:, None] * frequency[None, :]
    rotary = within < ROT
    cosine = jnp.where(rotary[None, :], jnp.cos(angles), 1.0)
    sign_term = jnp.where(within % 2 == 0, -1.0, 1.0)
    sine_term = jnp.where(rotary[None, :], sign_term[None, :] * jnp.sin(angles), 0.0)
    return (cosine, sine_term)

def pair_swap(values):
    even_cols = jnp.arange(values.shape[-1]) % 2 == 0
    return jnp.where(even_cols, jnp.roll(values, -1, axis=-1), jnp.roll(values, 1, axis=-1))

def rotate(values, cosine, sine_term):
    return values * cosine + pair_swap(values) * sine_term

def layer_group(group_rows, family_rows, orient_rows, params):
    norm_gain, norm_bias, qkv_weight, out_weight, up_weight, up_bias, down_weight, down_bias, family_table, orient_table = params
    group_size = group_rows.shape[0]
    family_hot = (family_rows[:, None] == jnp.arange(FAMILIES)[None, :]).astype(jnp.float32)
    orient_hot = (orient_rows[:, None] == jnp.arange(2)[None, :]).astype(jnp.float32)
    embedded = group_rows + (matmul(family_hot, family_table) + matmul(orient_hot, orient_table))[:, None, :]
    row_mean = lax.optimization_barrier(jnp.mean(embedded, -1, keepdims=True))
    centred = embedded - row_mean
    row_var = lax.optimization_barrier(jnp.mean(centred * centred, -1, keepdims=True))
    normed_low = low(centred * lax.rsqrt(row_var + 1e-05) * norm_gain + norm_bias)
    projected = low_back(matmul(normed_low, qkv_weight))
    positions = jnp.arange(LEN).astype(jnp.float32)
    cosine, sine_term = rope_tables(positions)
    queries = low(low_back(rotate(projected[..., :D], cosine, sine_term)))
    keys_rot = low(low_back(rotate(projected[..., D:2 * D], cosine, sine_term)))
    values = low(low_back(projected[..., 2 * D:]))
    query_heads = queries.reshape(group_size, LEN, H, HD)
    key_heads = keys_rot.reshape(group_size, LEN, H, HD)
    value_heads = values.reshape(group_size, LEN, H, HD)
    scores = low_back(jnp.einsum('bqhd,bkhd->bhqk', query_heads, key_heads, precision=lax.Precision.HIGHEST) * HD ** (-0.5))
    causal = jnp.arange(LEN)[:, None] >= jnp.arange(LEN)[None, :]
    scores = jnp.where(causal, scores, -1e+30)
    softmaxed = low(jax.nn.softmax(scores, axis=-1))
    attended = jnp.einsum('bhqk,bkhd->bqhd', softmaxed, value_heads, precision=lax.Precision.HIGHEST)
    attended = low(low_back(attended.reshape(group_size, LEN, D)))
    branch_attn = matmul(attended, out_weight)
    up_pre = low_back(matmul(normed_low, up_weight) + up_bias)
    up_act = low(jax.nn.gelu(up_pre, approximate=True))
    return embedded + branch_attn + matmul(up_act, down_weight) + down_bias

def reference(hidden_in, family, orient, norm_gain, norm_bias, qkv_weight, out_weight, up_weight, up_bias, down_weight, down_bias, family_table, orient_table, cotangent):
    params = tuple((argument.astype(jnp.float32) for argument in (norm_gain, norm_bias, qkv_weight, out_weight, up_weight, up_bias, down_weight, down_bias, family_table, orient_table)))
    pair_count = ROWS // 2
    grouped = hidden_in.astype(jnp.float32).reshape(pair_count, 2, LEN, D)
    family_rows = jnp.repeat(family, 2).reshape(pair_count, 2)
    orient_rows = orient.reshape(pair_count, 2)
    cot_grouped = cotangent.astype(jnp.float32).reshape(pair_count, 2, LEN, D)

    def forward(inputs, weights):

        def one_group(group_args):
            return layer_group(group_args[0], group_args[1], group_args[2], weights)
        return lax.map(jax.checkpoint(one_group), (inputs, family_rows, orient_rows))
    outputs, pullback = jax.vjp(forward, grouped, params)
    input_grad, weight_grads = pullback(cot_grouped)
    return (outputs.reshape(ROWS, LEN, D).astype(jnp.bfloat16), input_grad.reshape(ROWS, LEN, D), weight_grads[0], weight_grads[1], weight_grads[2], weight_grads[3], weight_grads[4], weight_grads[5], weight_grads[6], weight_grads[7], weight_grads[8], weight_grads[9])
```

```python
import functools
import math

import jax
import jax.numpy as jnp
from jax import lax
from jax.experimental import pallas as pl
from jax.experimental.pallas import tpu as pltpu
from jax.sharding import PartitionSpec as P

H = 16
HD = 64
ROT = 32
MESH = pl.DeviceIdType.MESH
VMEM_LIMIT = 60 * 1024 * 1024
F32 = jnp.float32
BF16 = jnp.bfloat16


def for_sending(shard):

    def short(part):
        return part.astype(jnp.bfloat16) if part.dtype == jnp.float32 else part

    return jax.tree.map(short, shard)


def rope_tables(positions, features):
    column = jnp.arange(features, dtype=jnp.int32)
    within = column % HD
    frequency = jnp.exp(-(2.0 * (within // 2).astype(jnp.float32) / ROT) * math.log(10000.0))
    angles = positions[:, None] * frequency[None, :]
    rotary = within < ROT
    cosine = jnp.where(rotary[None, :], jnp.cos(angles), 1.0)
    sign_term = jnp.where(within % 2 == 0, -1.0, 1.0)
    sine_term = jnp.where(rotary[None, :], sign_term[None, :] * jnp.sin(angles), 0.0)
    return (cosine, sine_term)


def pair_swap(values):
    even_cols = jnp.arange(values.shape[-1]) % 2 == 0
    return jnp.where(even_cols, jnp.roll(values, -1, axis=-1), jnp.roll(values, 1, axis=-1))


def rotate(values, cosine, sine_term):
    return values * cosine + pair_swap(values) * sine_term


def rotate_back(values, cosine, sine_term):
    return values * cosine + pair_swap(values * sine_term)


def gelu_tanh(pre_values):
    return jax.nn.gelu(pre_values, approximate=True)


def body_by_heads(
    hidden_in,
    family,
    orient,
    norm_gain,
    norm_bias,
    qkv_weight,
    out_weight,
    up_weight,
    up_bias,
    down_weight,
    down_bias,
    family_table,
    orient_table,
    cotangent,
):
    seq_count = lax.axis_size("seq")
    row_count, seg_length, features = hidden_in.shape
    full_length = seg_length * seq_count
    local_heads = H // seq_count
    head_size = features // H
    slab_width = features // seq_count
    block_rows = min(512, full_length)
    block_count = full_length // block_rows
    score_scale = head_size ** (-0.5)
    token_count = row_count * seg_length
    family_rows = jnp.repeat(family, 2)
    family_hot = (family_rows[:, None] == jnp.arange(family_table.shape[0])[None, :]).astype(
        jnp.bfloat16
    )
    orient_hot = (orient[:, None] == jnp.arange(2)[None, :]).astype(jnp.bfloat16)
    embedding = jnp.dot(family_hot, family_table, preferred_element_type=jnp.float32) + jnp.dot(
        orient_hot, orient_table, preferred_element_type=jnp.float32
    )
    embedded = (hidden_in.astype(jnp.float32) + embedding[:, None, :]).reshape(
        token_count, features
    )
    row_mean = jnp.mean(embedded, -1, keepdims=True)
    centred = embedded - row_mean
    row_var = jnp.mean(centred * centred, -1, keepdims=True)
    inv_std = lax.rsqrt(row_var + 1e-05)
    normed_hat = centred * inv_std
    gain_f32 = norm_gain.astype(jnp.float32)
    normed_low = (normed_hat * gain_f32 + norm_bias.astype(jnp.float32)).astype(jnp.bfloat16)
    projected = jnp.dot(normed_low, qkv_weight, preferred_element_type=jnp.float32).reshape(
        row_count, seg_length, 3 * features
    )
    positions = (lax.axis_index("seq") * seg_length + jnp.arange(seg_length)).astype(jnp.float32)
    cosine, sine_term = rope_tables(positions, features)
    queries = rotate(projected[..., :features], cosine, sine_term).astype(jnp.bfloat16)
    keys_rot = rotate(projected[..., features : 2 * features], cosine, sine_term).astype(
        jnp.bfloat16
    )
    values = projected[..., 2 * features :].astype(jnp.bfloat16)
    query_heads, key_heads, value_heads = (
        lax.all_to_all(queries, "seq", split_axis=2, concat_axis=1, tiled=True),
        lax.all_to_all(keys_rot, "seq", split_axis=2, concat_axis=1, tiled=True),
        lax.all_to_all(values, "seq", split_axis=2, concat_axis=1, tiled=True),
    )

    def scores_for(query_block, key_rows, block_start):
        logits = (
            jnp.einsum("qhd,khd->hqk", query_block, key_rows, preferred_element_type=jnp.float32)
            * score_scale
        )
        causal = (block_start + jnp.arange(block_rows))[:, None] >= jnp.arange(full_length)[None, :]
        return jnp.where(causal[None], logits, -1e30)

    def attend(row_args):
        query_row, key_row, value_row = row_args
        key_rows = key_row.reshape(full_length, local_heads, head_size)
        value_rows = value_row.reshape(full_length, local_heads, head_size)
        pieces = []
        log_parts = []
        for block_index in range(block_count):
            block_start = block_index * block_rows
            query_block = query_row[block_start : block_start + block_rows].reshape(
                block_rows, local_heads, head_size
            )
            logits = scores_for(query_block, key_rows, block_start)
            row_peak = jnp.max(logits, -1, keepdims=True)
            weights = jnp.exp(logits - row_peak)
            row_total = jnp.sum(weights, -1, keepdims=True)
            prob_low = (weights / row_total).astype(jnp.bfloat16)
            output_block = jnp.einsum(
                "hqk,khd->qhd", prob_low, value_rows, preferred_element_type=jnp.float32
            )
            pieces.append(output_block.reshape(block_rows, slab_width).astype(jnp.bfloat16))
            log_parts.append((row_peak + jnp.log(row_total))[..., 0])
        return (jnp.concatenate(pieces, 0), jnp.concatenate(log_parts, 1))

    attended_heads, log_sums = lax.map(attend, (query_heads, key_heads, value_heads))
    attended = jax.tree.map(
        lambda part, own: part.astype(own.dtype),
        lax.all_to_all(for_sending(attended_heads), "seq", split_axis=1, concat_axis=2, tiled=True),
        attended_heads,
    )
    attended_flat = attended.reshape(token_count, features)
    branch_attn = jnp.dot(attended_flat, out_weight, preferred_element_type=jnp.float32)
    up_pre = jnp.dot(normed_low, up_weight, preferred_element_type=jnp.float32) + up_bias.astype(
        jnp.float32
    )
    up_act = gelu_tanh(up_pre).astype(jnp.bfloat16)
    branch_feed = jnp.dot(
        up_act, down_weight, preferred_element_type=jnp.float32
    ) + down_bias.astype(jnp.float32)
    layer_out = (
        (embedded + branch_attn + branch_feed)
        .astype(jnp.bfloat16)
        .reshape(row_count, seg_length, features)
    )
    grad_low = cotangent.reshape(token_count, features)
    grad_f32 = grad_low.astype(jnp.float32)
    down_grad = jnp.einsum("nf,nd->fd", up_act, grad_low, preferred_element_type=jnp.float32)
    down_bias_grad = jnp.sum(grad_f32, 0)
    act_grad = jnp.einsum("nd,fd->nf", grad_low, down_weight, preferred_element_type=jnp.float32)
    gelu_out, gelu_pull = jax.vjp(gelu_tanh, up_pre)
    pre_grad = gelu_pull(act_grad)[0].astype(jnp.bfloat16)
    up_bias_grad = jnp.sum(pre_grad.astype(jnp.float32), 0)
    up_grad = jnp.einsum("nd,nf->df", normed_low, pre_grad, preferred_element_type=jnp.float32)
    normed_grad = jnp.einsum("nf,df->nd", pre_grad, up_weight, preferred_element_type=jnp.float32)
    out_grad = jnp.einsum("nd,ne->de", attended_flat, grad_low, preferred_element_type=jnp.float32)
    attended_grad = jnp.einsum(
        "ne,de->nd", grad_low, out_weight, preferred_element_type=jnp.float32
    )
    attended_grad = attended_grad.astype(jnp.bfloat16).reshape(row_count, seg_length, features)
    grad_heads = lax.all_to_all(attended_grad, "seq", split_axis=2, concat_axis=1, tiled=True)

    def attend_back(row_args):
        query_row, key_row, value_row, grad_row, log_row = row_args
        key_rows = key_row.reshape(full_length, local_heads, head_size)
        value_rows = value_row.reshape(full_length, local_heads, head_size)
        keys_total = jnp.zeros((full_length, local_heads, head_size), jnp.float32)
        values_total = jnp.zeros((full_length, local_heads, head_size), jnp.float32)
        query_parts = []
        for block_index in range(block_count):
            block_start = block_index * block_rows
            query_block = query_row[block_start : block_start + block_rows].reshape(
                block_rows, local_heads, head_size
            )
            grad_block = grad_row[block_start : block_start + block_rows].reshape(
                block_rows, local_heads, head_size
            )
            logits = scores_for(query_block, key_rows, block_start)
            probs_full = jnp.exp(logits - log_row[:, block_start : block_start + block_rows, None])
            prob_low = probs_full.astype(jnp.bfloat16)
            probs_grad = jnp.einsum(
                "qhd,khd->hqk", grad_block, value_rows, preferred_element_type=jnp.float32
            )
            inner_sum = jnp.sum(probs_full * probs_grad, -1, keepdims=True)
            scores_grad = (probs_full * (probs_grad - inner_sum)).astype(jnp.bfloat16)
            values_total = values_total + jnp.einsum(
                "hqk,qhd->khd", prob_low, grad_block, preferred_element_type=jnp.float32
            )
            query_grad = (
                jnp.einsum(
                    "hqk,khd->qhd", scores_grad, key_rows, preferred_element_type=jnp.float32
                )
                * score_scale
            )
            query_parts.append(query_grad.reshape(block_rows, slab_width).astype(jnp.bfloat16))
            keys_total = (
                keys_total
                + jnp.einsum(
                    "hqk,qhd->khd", scores_grad, query_block, preferred_element_type=jnp.float32
                )
                * score_scale
            )
        return (
            jnp.concatenate(query_parts, 0),
            keys_total.reshape(full_length, slab_width).astype(jnp.bfloat16),
            values_total.reshape(full_length, slab_width).astype(jnp.bfloat16),
        )

    query_grad_heads, key_grad_heads, value_grad_heads = lax.map(
        attend_back, (query_heads, key_heads, value_heads, grad_heads, log_sums)
    )
    query_grad_pos, key_grad_pos, value_grad_pos = (
        lax.all_to_all(
            for_sending(query_grad_heads), "seq", split_axis=1, concat_axis=2, tiled=True
        ).astype(query_grad_heads.dtype),
        lax.all_to_all(
            for_sending(key_grad_heads), "seq", split_axis=1, concat_axis=2, tiled=True
        ).astype(key_grad_heads.dtype),
        lax.all_to_all(
            for_sending(value_grad_heads), "seq", split_axis=1, concat_axis=2, tiled=True
        ).astype(value_grad_heads.dtype),
    )
    projected_grad = jnp.concatenate(
        [
            rotate_back(query_grad_pos.astype(jnp.float32), cosine, sine_term),
            rotate_back(key_grad_pos.astype(jnp.float32), cosine, sine_term),
            value_grad_pos.astype(jnp.float32),
        ],
        -1,
    )
    projected_grad = projected_grad.astype(jnp.bfloat16).reshape(token_count, 3 * features)
    qkv_grad = jnp.einsum(
        "nd,ne->de", normed_low, projected_grad, preferred_element_type=jnp.float32
    )
    normed_grad = normed_grad + jnp.einsum(
        "ne,de->nd", projected_grad, qkv_weight, preferred_element_type=jnp.float32
    )
    gain_grad = jnp.sum(normed_grad * normed_hat, 0)
    bias_grad = jnp.sum(normed_grad, 0)
    scaled_grad = normed_grad * gain_f32
    hat_grad = (
        scaled_grad
        - jnp.mean(scaled_grad, -1, keepdims=True)
        - normed_hat * jnp.mean(scaled_grad * normed_hat, -1, keepdims=True)
    )
    input_grad = (grad_f32 + inv_std * hat_grad).reshape(row_count, seg_length, features)
    row_sums = jnp.sum(input_grad, 1)
    family_grad = jnp.einsum(
        "rf,rd->fd", family_hot.astype(jnp.float32), row_sums, precision=lax.Precision.HIGHEST
    )
    orient_grad = jnp.einsum(
        "rf,rd->fd", orient_hot.astype(jnp.float32), row_sums, precision=lax.Precision.HIGHEST
    )
    gain_sum, bias_sum, up_bias_sum, down_bias_sum, family_sum, orient_sum = lax.psum(
        (gain_grad, bias_grad, up_bias_grad, down_bias_grad, family_grad, orient_grad),
        ("dp", "seq"),
    )
    qkv_sum, out_sum, up_sum, down_sum = (
        lax.psum_scatter(qkv_grad, ("dp", "seq"), scatter_dimension=0, tiled=True),
        lax.psum_scatter(out_grad, ("dp", "seq"), scatter_dimension=0, tiled=True),
        lax.psum_scatter(up_grad, ("dp", "seq"), scatter_dimension=0, tiled=True),
        lax.psum_scatter(down_grad, ("dp", "seq"), scatter_dimension=0, tiled=True),
    )
    return (
        layer_out,
        input_grad,
        gain_sum,
        bias_sum,
        qkv_sum,
        out_sum,
        up_sum,
        up_bias_sum,
        down_sum,
        down_bias_sum,
        family_sum,
        orient_sum,
    )


def dot_nn(a, b):
    return lax.dot_general(a, b, (((1,), (0,)), ((), ())), preferred_element_type=F32)


def dot_nt(a, b):
    return lax.dot_general(a, b, (((1,), (1,)), ((), ())), preferred_element_type=F32)


def dot_tn(a, b):
    return lax.dot_general(a, b, (((0,), (0,)), ((), ())), preferred_element_type=F32)


def params(**more):
    return pltpu.CompilerParams(vmem_limit_bytes=VMEM_LIMIT, **more)


def cost(flops, moved, exps=0):
    return pl.CostEstimate(flops=flops, bytes_accessed=moved, transcendentals=exps)


def whole(shape):
    return pl.BlockSpec(shape, lambda *_: (0,) * len(shape), pipeline_mode=pl.Buffered(1))


def table_row(table, wanted):
    rows = lax.broadcasted_iota(jnp.int32, table.shape, 0)
    return jnp.sum(jnp.where(rows == wanted, table[...].astype(F32), 0.0), 0, keepdims=True)


def normalise(entries):
    centred = entries - jnp.mean(entries, -1, keepdims=True)
    inv_std = lax.rsqrt(jnp.mean(centred * centred, -1, keepdims=True) + 1e-05)
    return centred * inv_std, inv_std


GELU_C = math.sqrt(2.0 / math.pi)


def gelu_both(z):
    square = z * z
    t = jnp.tanh(GELU_C * z * (1.0 + 0.044715 * square))
    half = 0.5 * (1.0 + t)
    slope = half + (0.5 * GELU_C) * z * (1.0 - t * t) * (1.0 + (3 * 0.044715) * square)
    return z * half, slope


def ffn_kernel(rows, ids, hid, cot, fam, ori, gain, bias, wup, bup, wdn, norm, act, pre, bupg, bdng):
    tokens = hid.shape[0]
    seg = tokens // rows
    step = 256

    @pl.when(pl.program_id(0) == 0)
    def _():
        total = jnp.zeros((1, cot.shape[1]), F32)
        for row in range(rows):
            emb = table_row(fam, ids[0]) + table_row(ori, ids[1 + row])
            for start in range(row * seg, (row + 1) * seg, step):
                part = pl.ds(start, step)
                hat, _ = normalise(hid[part, :].astype(F32) + emb)
                norm[part, :] = (hat * gain[...].astype(F32) + bias[...].astype(F32)).astype(BF16)
                total = total + jnp.sum(cot[part, :].astype(F32), 0, keepdims=True)
        bdng[...] = total

    total = jnp.zeros((1, wup.shape[1]), F32)
    for start in range(0, tokens, step):
        part = pl.ds(start, step)
        z = dot_nn(norm[part, :], wup[...]) + bup[...].astype(F32)
        into = dot_nt(cot[part, :], wdn[...])
        value, slope = gelu_both(z)
        act[part, :] = value.astype(BF16)
        low = (into * slope).astype(BF16)
        pre[part, :] = low
        total = total + jnp.sum(low.astype(F32), 0, keepdims=True)
    bupg[...] = total


def ffn_forward(ids, hid, cot, fam, ori, gain, bias, wup, bup, wdn, rows):
    tokens, d = hid.shape
    ff = wup.shape[1]
    tile = 512
    return pl.pallas_call(
        functools.partial(ffn_kernel, rows),
        grid_spec=pltpu.PrefetchScalarGridSpec(
            num_scalar_prefetch=1,
            grid=(ff // tile,),
            in_specs=[
                whole((tokens, d)),
                whole((tokens, d)),
                whole(fam.shape),
                whole(ori.shape),
                whole((1, d)),
                whole((1, d)),
                pl.BlockSpec((d, tile), lambda i, s: (0, i)),
                pl.BlockSpec((1, tile), lambda i, s: (0, i)),
                pl.BlockSpec((tile, d), lambda i, s: (i, 0)),
            ],
            out_specs=[
                whole((tokens, d)),
                pl.BlockSpec((tokens, tile), lambda i, s: (0, i)),
                pl.BlockSpec((tokens, tile), lambda i, s: (0, i)),
                pl.BlockSpec((1, tile), lambda i, s: (0, i)),
                whole((1, d)),
            ],
        ),
        out_shape=[
            jax.ShapeDtypeStruct((tokens, d), BF16),
            jax.ShapeDtypeStruct((tokens, ff), BF16),
            jax.ShapeDtypeStruct((tokens, ff), BF16),
            jax.ShapeDtypeStruct((1, ff), F32),
            jax.ShapeDtypeStruct((1, d), F32),
        ],
        compiler_params=params(),
        cost_estimate=cost(4 * tokens * d * ff, 4 * tokens * ff + 4 * d * ff, tokens * ff),
        name="ffn_forward",
    )(ids, hid, cot, fam, ori, gain, bias, wup, bup, wdn)


def turn(entries, cosine, sine):
    even = lax.broadcasted_iota(jnp.int32, entries.shape, 1) % 2 == 0
    other = jnp.where(even, pltpu.roll(entries, 127, 1), pltpu.roll(entries, 1, 1))
    return entries * cosine + other * sine


def turn_back(entries, cosine, sine):
    even = lax.broadcasted_iota(jnp.int32, entries.shape, 1) % 2 == 0
    side = entries * sine
    other = jnp.where(even, pltpu.roll(side, 127, 1), pltpu.roll(side, 1, 1))
    return entries * cosine + other


def qkv_kernel(tiles, ids, own, far, cown, cfar, fam, ori, gain, bias, wqkv, wout, cos, sin, norm, cot, qkv, datt):
    seg = own.shape[0]
    step = 256
    i = pl.program_id(0)
    me = ids[1]

    @pl.when(i == 0)
    def _():
        emb = table_row(fam, ids[0]) + table_row(ori, ids[2])
        for source, csource, where in ((own, cown, me), (far, cfar, 1 - me)):
            for start in range(0, seg, step):
                part = pl.ds(start, step)
                there = pl.ds(pl.multiple_of(where * seg + start, step), step)
                hat, _ = normalise(source[part, :].astype(F32) + emb)
                norm[there, :] = (hat * gain[...].astype(F32) + bias[...].astype(F32)).astype(BF16)
                cot[there, :] = csource[part, :]

    @pl.when(i < 2 * tiles)
    def _():
        for start in range(0, 2 * seg, step):
            part = pl.ds(start, step)
            lin = dot_nn(norm[part, :], wqkv[...])
            for lane in range(0, lin.shape[1], 128):
                piece = turn(lin[:, lane : lane + 128], cos[part, :], sin[part, :])
                qkv[part, lane : lane + 128] = piece.astype(BF16)

    @pl.when((i >= 2 * tiles) & (i < 3 * tiles))
    def _():
        for start in range(0, 2 * seg, step):
            part = pl.ds(start, step)
            qkv[part, :] = dot_nn(norm[part, :], wqkv[...]).astype(BF16)

    @pl.when(i >= 3 * tiles)
    def _():
        for start in range(0, 2 * seg, step):
            part = pl.ds(start, step)
            datt[part, :] = dot_nt(cot[part, :], wout[...]).astype(BF16)


def qkv_forward(ids, own, far, cown, cfar, fam, ori, gain, bias, wqkv, wout, cos, sin):
    seg, d = own.shape
    full = 2 * seg
    tile = 512
    tiles = d // tile
    return pl.pallas_call(
        functools.partial(qkv_kernel, tiles),
        grid_spec=pltpu.PrefetchScalarGridSpec(
            num_scalar_prefetch=1,
            grid=(4 * tiles,),
            in_specs=[
                whole((seg, d)),
                whole((seg, d)),
                whole((seg, d)),
                whole((seg, d)),
                whole(fam.shape),
                whole(ori.shape),
                whole((1, d)),
                whole((1, d)),
                pl.BlockSpec((d, tile), lambda i, s: (0, jnp.minimum(i, 3 * tiles - 1))),
                pl.BlockSpec((tile, d), lambda i, s: (jnp.maximum(i - 3 * tiles, 0), 0)),
                whole((full, 128)),
                whole((full, 128)),
            ],
            out_specs=[
                whole((full, d)),
                whole((full, d)),
                pl.BlockSpec((full, tile), lambda i, s: (0, jnp.minimum(i, 3 * tiles - 1))),
                pl.BlockSpec((full, tile), lambda i, s: (0, jnp.maximum(i - 3 * tiles, 0))),
            ],
        ),
        out_shape=[
            jax.ShapeDtypeStruct((full, d), BF16),
            jax.ShapeDtypeStruct((full, d), BF16),
            jax.ShapeDtypeStruct((full, 3 * d), BF16),
            jax.ShapeDtypeStruct((full, d), BF16),
        ],
        compiler_params=params(),
        cost_estimate=cost(8 * full * d * d, 8 * d * d + 18 * full * d),
        name="qkv_forward",
    )(ids, own, far, cown, cfar, fam, ori, gain, bias, wqkv, wout, cos, sin)


def attention_kernel(head_size, q_ref, k_ref, v_ref, g_ref, cos, sin, o_ref, dq_ref, dk_ref, dv_ref, dkt, dvt):
    full = q_ref.shape[0]
    block = 256
    scale = head_size ** (-0.5)
    lane = lax.broadcasted_iota(jnp.int32, (block, 128), 1)
    below = lax.broadcasted_iota(jnp.int32, (block, block), 0) >= lax.broadcasted_iota(
        jnp.int32, (block, block), 1
    )
    dkt[...] = jnp.zeros_like(dkt)
    dvt[...] = jnp.zeros_like(dvt)
    for start in range(0, full, block):
        part = pl.ds(start, block)
        end = start + block
        query = q_ref[part, :]
        grad = g_ref[part, :]
        out = None
        dq = None
        for head in range(128 // head_size):
            mine = (lane >= head * head_size) & (lane < (head + 1) * head_size)
            qm = jnp.where(mine, query.astype(F32) * scale, 0.0).astype(BF16)
            gm = jnp.where(mine, grad.astype(F32), 0.0).astype(BF16)
            scores = dot_nt(qm, k_ref[0:end, :])
            last = jnp.where(below, scores[:, start:end], -1e30)
            scores = last if start == 0 else jnp.concatenate([scores[:, :start], last], 1)
            weights = jnp.exp(scores - jnp.max(scores, -1, keepdims=True))
            probs = weights * (1.0 / jnp.sum(weights, -1, keepdims=True))
            low = probs.astype(BF16)
            piece = dot_nn(low, v_ref[0:end, :])
            out = piece if out is None else jnp.where(mine, piece, out)
            pg = dot_nt(gm, v_ref[0:end, :])
            inner = jnp.sum(probs * pg, -1, keepdims=True)
            sg = (probs * (pg - inner)).astype(BF16)
            piece = dot_nn(sg, k_ref[0:end, :])
            dq = piece if dq is None else jnp.where(mine, piece, dq)
            dkt[:, 0:end] += dot_tn(qm, sg)
            dvt[:, 0:end] += dot_tn(gm, low)
        o_ref[part, :] = out.astype(BF16)
        dq_ref[part, :] = turn_back(dq * scale, cos[part, :], sin[part, :]).astype(BF16)
    for start in range(0, full, block):
        part = pl.ds(start, block)
        dk = dkt[:, start : start + block].T
        dk_ref[part, :] = turn_back(dk, cos[part, :], sin[part, :]).astype(BF16)
        dv_ref[part, :] = dvt[:, start : start + block].T.astype(BF16)


def attention(qkv, datt, cos, sin, head_size):
    full, d = datt.shape
    pairs = d // 128
    shape = jax.ShapeDtypeStruct((full, d), BF16)
    spec = pl.BlockSpec((full, 128), lambda i: (0, i))
    return pl.pallas_call(
        functools.partial(attention_kernel, head_size),
        grid=(pairs,),
        in_specs=[
            spec,
            pl.BlockSpec((full, 128), lambda i: (0, pairs + i)),
            pl.BlockSpec((full, 128), lambda i: (0, 2 * pairs + i)),
            spec,
            whole((full, 128)),
            whole((full, 128)),
        ],
        out_specs=[spec] * 4,
        out_shape=[shape] * 4,
        scratch_shapes=[pltpu.VMEM((128, full), F32), pltpu.VMEM((128, full), F32)],
        compiler_params=params(),
        cost_estimate=cost(12 * full * full * d * 2, 16 * full * d, full * full * H),
        name="attention",
    )(qkv, qkv, qkv, datt, cos, sin)


def store_blocks(meta, value, keep, send, upper, seqs):
    size = keep.shape[-2]
    core = meta[0]
    for up in range(upper):
        for seq in range(seqs):
            first = (up * 2 * seqs + seq) * size
            second = first + seqs * size
            a = value[first : first + size, :].astype(BF16)
            b = value[second : second + size, :].astype(BF16)
            at = meta[2 + up] if upper > 1 else 0
            there = lax.rem(meta[1] + seq, 2)
            keep[at, there] = jnp.where(core == 0, a, b)
            send[at, there] = jnp.where(core == 0, b, a)


def up_grad_kernel(meta, left, right, keep, send, turned):
    @pl.when(pl.program_id(0) == 0)
    def _():
        turned[...] = left[...].T

    store_blocks(meta, dot_nn(turned[...], right[...]), keep, send, keep.shape[0], 2)


def up_grad(meta, left, right, upper):
    tokens, d = left.shape
    n = right.shape[1]
    tile = 512
    size = d // (upper * 4)
    shape = jax.ShapeDtypeStruct((upper, 2, size, n), BF16)
    spec = pl.BlockSpec((upper, 2, size, tile), lambda j, s: (0, 0, 0, j))
    return pl.pallas_call(
        up_grad_kernel,
        grid_spec=pltpu.PrefetchScalarGridSpec(
            num_scalar_prefetch=1,
            grid=(n // tile,),
            in_specs=[whole((tokens, d)), pl.BlockSpec((tokens, tile), lambda j, s: (0, j))],
            out_specs=[spec, spec],
            scratch_shapes=[pltpu.VMEM((d, tokens), BF16)],
        ),
        out_shape=[shape, shape],
        compiler_params=params(),
        cost_estimate=cost(2 * tokens * d * n, 2 * (tokens * n + d * n + tokens * d)),
        name="up_grad",
    )(meta, left, right)


def down_grad_kernel(meta, left, right, keep, send):
    store_blocks(meta, dot_nn(left[...].T, right[...]), keep, send, 1, 2)


def down_grad(meta, left, right, upper):
    tokens, m = left.shape
    d = right.shape[1]
    tile = m // upper
    size = tile // 4
    shape = jax.ShapeDtypeStruct((upper, 2, size, d), BF16)
    spec = pl.BlockSpec((1, 2, size, d), lambda i, s: (s[2 + i], 0, 0, 0))
    return pl.pallas_call(
        down_grad_kernel,
        grid_spec=pltpu.PrefetchScalarGridSpec(
            num_scalar_prefetch=1,
            grid=(upper,),
            in_specs=[pl.BlockSpec((tokens, tile), lambda i, s: (0, i)), whole((tokens, d))],
            out_specs=[spec, spec],
        ),
        out_shape=[shape, shape],
        compiler_params=params(),
        cost_estimate=cost(2 * tokens * d * m, 2 * (tokens * m + d * m + tokens * d)),
        name="down_grad",
    )(meta, left, right)


def late_grad_kernel(tiles, meta, att, cot, norm, dq, dk, dv, keep, send, turned):
    j = pl.program_id(0)

    @pl.when(j == 0)
    def _():
        turned[...] = att[...].T

    @pl.when(j == tiles)
    def _():
        turned[...] = norm[...].T

    for index, right in enumerate((cot, dq, dk, dv)):

        @pl.when((j >= index * tiles) & (j < (index + 1) * tiles))
        def _():
            store_blocks(meta, dot_nn(turned[...], right[...]), keep, send, keep.shape[0], 2)


def late_grad(meta, att, cot, norm, dq, dk, dv, upper):
    tokens, d = att.shape
    tile = 512
    tiles = d // tile
    size = d // (upper * 4)
    shape = jax.ShapeDtypeStruct((upper, 2, size, 4 * d), BF16)
    spec = pl.BlockSpec((upper, 2, size, tile), lambda j, s: (0, 0, 0, j))

    def part(index):
        return pl.BlockSpec(
            (tokens, tile), lambda j, s: (0, jnp.clip(j - index * tiles, 0, tiles - 1))
        )

    return pl.pallas_call(
        functools.partial(late_grad_kernel, tiles),
        grid_spec=pltpu.PrefetchScalarGridSpec(
            num_scalar_prefetch=1,
            grid=(4 * tiles,),
            in_specs=[whole((tokens, d)), part(0), whole((tokens, d)), part(1), part(2), part(3)],
            out_specs=[spec, spec],
            scratch_shapes=[pltpu.VMEM((d, tokens), BF16)],
        ),
        out_shape=[shape, shape],
        compiler_params=params(),
        cost_estimate=cost(8 * tokens * d * d, 20 * tokens * d),
        name="late_grad",
    )(meta, att, cot, norm, dq, dk, dv)


def reduce_blocks(keep, send):
    bits = int(math.log2(lax.axis_size("dp")))

    def swap(bit):
        return [(i, i ^ (1 << bit)) for i in range(1 << bits)]

    keep = keep.reshape((-1,) + keep.shape[2:])
    got = lax.ppermute(send, "dp", swap(0)).reshape(keep.shape)
    for bit in range(1, bits):
        half = keep.shape[0] // 2
        send = (keep[half:].astype(F32) + got[half:].astype(F32)).astype(BF16)
        keep = (keep[:half].astype(F32) + got[:half].astype(F32)).astype(BF16)
        got = lax.ppermute(send, "dp", swap(bit))
    send = (keep[1].astype(F32) + got[1].astype(F32)).astype(BF16)
    keep = keep[0].astype(F32) + got[0].astype(F32)
    return keep + lax.ppermute(send, "seq", [(0, 1), (1, 0)]).astype(F32)


def back_kernel(dq, dk, dv, w, out):
    d = dq.shape[1]
    total = dot_nt(dq[...], w[:, 0:d])
    total = total + dot_nt(dk[...], w[:, d : 2 * d])
    total = total + dot_nt(dv[...], w[:, 2 * d : 3 * d])
    out[...] = total.astype(BF16)


def project_back(dq, dk, dv, w):
    tokens, d = dq.shape
    step = 256
    spec = pl.BlockSpec((step, d), lambda i: (i, 0))
    return pl.pallas_call(
        back_kernel,
        grid=(tokens // step,),
        in_specs=[spec, spec, spec, whole(w.shape)],
        out_specs=spec,
        out_shape=jax.ShapeDtypeStruct((tokens, d), BF16),
        compiler_params=params(),
        cost_estimate=cost(6 * tokens * d * d, 6 * d * d + 8 * tokens * d),
        name="project_back",
    )(dq, dk, dv, w)


def out_kernel(per_row, ids, hid, fam, ori, act, wdn, own, far, wout, bdn, out):
    row = pl.program_id(0) // per_row
    emb = table_row(fam, ids[0]) + table_row(ori, ids[2 + row])
    att = jnp.where(row == ids[1], own[...], far[...])
    total = hid[...].astype(F32) + emb + dot_nn(att, wout[...])
    total = total + (dot_nn(act[...], wdn[...]) + bdn[...].astype(F32))
    out[...] = total.astype(BF16)


def input_kernel(per_row, ids, hid, fam, ori, pre, wup, own, far, gain, cot, out, gg, bg, rg):
    i = pl.program_id(0)
    row = i // per_row
    emb = table_row(fam, ids[0]) + table_row(ori, ids[2 + row])
    hat, inv_std = normalise(hid[...].astype(F32) + emb)
    grad = dot_nt(pre[...], wup[...]) + jnp.where(row == ids[1], own[...], far[...]).astype(F32)

    @pl.when(i == 0)
    def _():
        gg[...] = jnp.zeros_like(gg)
        bg[...] = jnp.zeros_like(bg)
        rg[...] = jnp.zeros_like(rg)

    gg[...] += jnp.sum(grad * hat, 0, keepdims=True)
    bg[...] += jnp.sum(grad, 0, keepdims=True)
    scaled = grad * gain[...].astype(F32)
    inner = (
        scaled
        - jnp.mean(scaled, -1, keepdims=True)
        - hat * jnp.mean(scaled * hat, -1, keepdims=True)
    )
    result = cot[...].astype(F32) + inv_std * inner
    out[...] = result
    sums = jnp.sum(result, 0, keepdims=True)
    rows = lax.broadcasted_iota(jnp.int32, rg.shape, 0)
    rg[...] += jnp.where(rows == row, sums, 0.0)


def home_specs(tokens, d, rows, step):
    per_row = tokens // rows // step
    local = pl.BlockSpec((step, d), lambda i, s: (i, 0))
    own = pl.BlockSpec((step, d), lambda i, s: (s[1] * per_row + i % per_row, 0))
    far = pl.BlockSpec((step, d), lambda i, s: (i % per_row, 0))
    return per_row, local, own, far


def layer_output(ids, hid, fam, ori, act, wdn, own, far, wout, bdn, rows):
    tokens, d = hid.shape
    ff = act.shape[1]
    step = 256
    per_row, local, own_spec, far_spec = home_specs(tokens, d, rows, step)
    return pl.pallas_call(
        functools.partial(out_kernel, per_row),
        grid_spec=pltpu.PrefetchScalarGridSpec(
            num_scalar_prefetch=1,
            grid=(tokens // step,),
            in_specs=[
                local,
                whole(fam.shape),
                whole(ori.shape),
                pl.BlockSpec((step, ff), lambda i, s: (i, 0)),
                whole(wdn.shape),
                own_spec,
                far_spec,
                whole(wout.shape),
                whole((1, d)),
            ],
            out_specs=local,
        ),
        out_shape=jax.ShapeDtypeStruct((tokens, d), BF16),
        compiler_params=params(),
        cost_estimate=cost(2 * tokens * d * (ff + d), 2 * (d * (ff + d) + tokens * ff + 4 * tokens * d)),
        name="layer_output",
    )(ids, hid, fam, ori, act, wdn, own, far, wout, bdn)


def input_gradient(ids, hid, fam, ori, pre, wup, own, far, gain, cot, rows):
    tokens, d = hid.shape
    ff = pre.shape[1]
    step = 256
    per_row, local, own_spec, far_spec = home_specs(tokens, d, rows, step)
    return pl.pallas_call(
        functools.partial(input_kernel, per_row),
        grid_spec=pltpu.PrefetchScalarGridSpec(
            num_scalar_prefetch=1,
            grid=(tokens // step,),
            in_specs=[
                local,
                whole(fam.shape),
                whole(ori.shape),
                pl.BlockSpec((step, ff), lambda i, s: (i, 0)),
                whole(wup.shape),
                own_spec,
                far_spec,
                whole((1, d)),
                local,
            ],
            out_specs=[local, whole((1, d)), whole((1, d)), whole((rows, d))],
        ),
        out_shape=[
            jax.ShapeDtypeStruct((tokens, d), F32),
            jax.ShapeDtypeStruct((1, d), F32),
            jax.ShapeDtypeStruct((1, d), F32),
            jax.ShapeDtypeStruct((rows, d), F32),
        ],
        compiler_params=params(),
        cost_estimate=cost(2 * tokens * d * ff, 2 * (d * ff + tokens * ff + 6 * tokens * d)),
        name="input_gradient",
    )(ids, hid, fam, ori, pre, wup, own, far, gain, cot)


def sums_kernel(bits, sums_ref, vec_ref, sums_out, all_out, held, got, vgot, send_sem, recv_sem, gsend, grecv):
    dp = lax.axis_index("dp")
    seq = lax.axis_index("seq")
    partners = [(dp, 1 - seq)]
    for bit in range(bits):
        size = 1 << bit
        partners.append((dp + (1 - 2 * lax.rem(dp // size, 2)) * size, seq))
    barrier = pltpu.get_barrier_semaphore()
    for partner in partners:
        pl.semaphore_signal(barrier, inc=1, device_id=partner, device_id_type=MESH)
    pl.semaphore_wait(barrier, len(partners))

    def remote(src, dst, send, recv, partner):
        copy = pltpu.make_async_remote_copy(
            src_ref=src, dst_ref=dst, send_sem=send, recv_sem=recv, device_id=partner, device_id_type=MESH
        )
        copy.start()
        return copy

    for index, partner in enumerate(partners):
        source = sums_ref if index == 0 else held.at[index]
        main = remote(source, got.at[index], send_sem.at[index], recv_sem.at[index], partner)
        if index == 0:
            side = remote(vec_ref, vgot, gsend.at[0], grecv.at[0], partner)
        else:
            size = 1 << (index - 1)
            held_now = pl.ds(dp - lax.rem(dp, size), size)
            side = remote(
                all_out.at[held_now], all_out.at[held_now], gsend.at[index], grecv.at[index], partner
            )
        main.wait()
        total = source[...] + got[index]
        if index + 1 < len(partners):
            held[index + 1] = total
        else:
            sums_out[...] = total
        side.wait()
        if index == 0:
            all_out[dp] = vec_ref[...] + vgot[...]


def sum_small(sums, vec):
    count = lax.axis_size("dp")
    bits = int(math.log2(count))
    rounds = bits + 1
    return pl.pallas_call(
        functools.partial(sums_kernel, bits),
        in_specs=[pl.BlockSpec(memory_space=pltpu.VMEM)] * 2,
        out_specs=[pl.BlockSpec(memory_space=pltpu.VMEM)] * 2,
        out_shape=[
            jax.ShapeDtypeStruct(sums.shape, F32),
            jax.ShapeDtypeStruct((count,) + vec.shape, F32),
        ],
        scratch_shapes=[
            pltpu.VMEM((rounds,) + sums.shape, F32),
            pltpu.VMEM((rounds,) + sums.shape, F32),
            pltpu.VMEM(vec.shape, F32),
            pltpu.SemaphoreType.DMA((rounds,)),
            pltpu.SemaphoreType.DMA((rounds,)),
            pltpu.SemaphoreType.DMA((rounds,)),
            pltpu.SemaphoreType.DMA((rounds,)),
        ],
        compiler_params=pltpu.CompilerParams(collective_id=0, has_side_effects=True),
        name="sum_small",
    )(sums, vec)


def body_by_rows(
    hidden_in,
    family,
    orient,
    norm_gain,
    norm_bias,
    qkv_weight,
    out_weight,
    up_weight,
    up_bias,
    down_weight,
    down_bias,
    family_table,
    orient_table,
    cotangent,
):
    rows, seg, d = hidden_in.shape
    ff = up_weight.shape[1]
    tokens = rows * seg
    full = 2 * seg
    dp_count = lax.axis_size("dp")
    bits = int(math.log2(dp_count))
    upper = dp_count // 2
    dp = lax.axis_index("dp")
    seq = lax.axis_index("seq")
    ring = [(0, 1), (1, 0)]

    def mine(pair):
        return lax.dynamic_index_in_dim(pair, seq, 0, keepdims=False)

    def theirs(pair):
        return lax.dynamic_index_in_dim(pair, 1 - seq, 0, keepdims=False)

    far_hidden = lax.ppermute(theirs(hidden_in), "seq", ring)
    far_cot = lax.ppermute(theirs(cotangent), "seq", ring)

    gain = norm_gain.reshape(1, d)
    bias = norm_bias.reshape(1, d)
    hid = hidden_in.reshape(tokens, d)
    cot = cotangent.reshape(tokens, d)
    ids = jnp.concatenate([family, orient])
    tail_ids = jnp.concatenate([family, seq[None].astype(jnp.int32), orient])
    row_ids = jnp.stack([family[0], seq.astype(jnp.int32), mine(orient)])

    group = jnp.arange(upper, dtype=jnp.int32) ^ (dp // 2)
    place = jnp.zeros_like(group)
    for bit in range(bits - 1):
        place = place + (((group >> bit) & 1) << (bits - 2 - bit))
    meta = jnp.concatenate([jnp.stack([dp % 2, seq]).astype(jnp.int32), place])

    normed, act, pre, up_bias_part, down_bias_part = ffn_forward(
        ids, hid, cot, family_table, orient_table, gain, bias, up_weight, up_bias.reshape(1, ff), down_weight, rows
    )
    up_keep, up_send = up_grad(meta, normed, pre, upper)
    down_keep, down_send = down_grad(meta, act, cot, upper)
    up_total = reduce_blocks(up_keep, up_send)
    down_total = reduce_blocks(down_keep, down_send)

    cosine, sine = rope_tables(jnp.arange(full).astype(F32), 128)
    row_normed, row_cot, qkv, datt = qkv_forward(
        row_ids,
        mine(hidden_in),
        far_hidden,
        mine(cotangent),
        far_cot,
        family_table,
        orient_table,
        gain,
        bias,
        qkv_weight,
        out_weight,
        cosine,
        sine,
    )
    att, dq, dk, dv = attention(qkv, datt, cosine, sine, d // H)
    keep, send = late_grad(meta, att, row_cot, row_normed, dq, dk, dv, upper)
    late_total = reduce_blocks(keep, send)
    far_att = lax.ppermute(theirs(att.reshape(2, seg, d)), "seq", ring)
    back = project_back(dq, dk, dv, qkv_weight)
    far_back = lax.ppermute(theirs(back.reshape(2, seg, d)), "seq", ring)

    layer_out = layer_output(
        tail_ids,
        hid,
        family_table,
        orient_table,
        act,
        down_weight,
        att,
        far_att,
        out_weight,
        down_bias.reshape(1, d),
        rows,
    )
    input_grad, gain_part, bias_part, row_part = input_gradient(
        tail_ids, hid, family_table, orient_table, pre, up_weight, back, far_back, gain, cot, rows
    )

    flag = orient[0]
    by_flag = jnp.where(flag == 0, row_part, row_part[::-1])
    packed = jnp.concatenate(
        [
            part.reshape(-1, 128)
            for part in (up_bias_part, down_bias_part, gain_part, bias_part, by_flag)
        ],
        0,
    )
    vec = jnp.concatenate(
        [
            (row_part[0] + row_part[1]).reshape(-1, 128),
            jnp.full((8, 128), 0.5, F32) * family.astype(F32)[0],
        ],
        0,
    )
    sums, gathered = sum_small(packed, vec)
    flat = sums.reshape(-1)
    up_bias_sum = flat[:ff]
    down_bias_sum, gain_sum, bias_sum = flat[ff : ff + 3 * d].reshape(3, d)
    orient_sum = flat[ff + 3 * d :].reshape(2, d)
    families = family_table.shape[0]
    hot = gathered[:, -1, 0].astype(jnp.int32)[None, :] == jnp.arange(families)[:, None]
    family_sum = jnp.dot(
        hot.astype(F32), gathered[:, :-8].reshape(dp_count, d), precision=lax.Precision.HIGHEST
    )
    return (
        layer_out.reshape(rows, seg, d),
        input_grad.reshape(rows, seg, d),
        gain_sum,
        bias_sum,
        late_total[:, d:],
        late_total[:, :d],
        up_total,
        up_bias_sum,
        down_total,
        down_bias_sum,
        family_sum,
        orient_sum,
    )


def body(*args):
    hidden_in = args[0]
    dp_count = lax.axis_size("dp")
    two_rows = lax.axis_size("seq") == 2 and hidden_in.shape[0] == 2
    if two_rows and dp_count >= 4 and dp_count & (dp_count - 1) == 0:
        return body_by_rows(*args)
    return body_by_heads(*args)


def solution(mesh):
    return jax.shard_map(
        body,
        mesh=mesh,
        in_specs=(
            P("dp", "seq", None),
            P("dp"),
            P("dp"),
            P(),
            P(),
            P(),
            P(),
            P(),
            P(),
            P(),
            P(),
            P(),
            P(),
            P("dp", "seq", None),
        ),
        out_specs=(
            P("dp", "seq", None),
            P("dp", "seq", None),
            P(),
            P(),
            P(("dp", "seq"), None),
            P(("dp", "seq"), None),
            P(("dp", "seq"), None),
            P(),
            P(("dp", "seq"), None),
            P(),
            P(),
            P(),
        ),
        check_vma=False,
    )
```

```python
import functools
import math

import jax
import jax.numpy as jnp
from jax import lax
from jax.experimental import pallas as pl
from jax.experimental.pallas import tpu as pltpu
from jax.sharding import PartitionSpec as P

H = 16
HD = 64
ROT = 32
MESH = pl.DeviceIdType.MESH
VMEM_LIMIT = 60 * 1024 * 1024
F32 = jnp.float32
BF16 = jnp.bfloat16


def for_sending(shard):

    def short(part):
        return part.astype(jnp.bfloat16) if part.dtype == jnp.float32 else part

    return jax.tree.map(short, shard)


def rope_tables(positions, features):
    column = jnp.arange(features, dtype=jnp.int32)
    within = column % HD
    frequency = jnp.exp(-(2.0 * (within // 2).astype(jnp.float32) / ROT) * math.log(10000.0))
    angles = positions[:, None] * frequency[None, :]
    rotary = within < ROT
    cosine = jnp.where(rotary[None, :], jnp.cos(angles), 1.0)
    sign_term = jnp.where(within % 2 == 0, -1.0, 1.0)
    sine_term = jnp.where(rotary[None, :], sign_term[None, :] * jnp.sin(angles), 0.0)
    return (cosine, sine_term)


def pair_swap(values):
    even_cols = jnp.arange(values.shape[-1]) % 2 == 0
    return jnp.where(even_cols, jnp.roll(values, -1, axis=-1), jnp.roll(values, 1, axis=-1))


def rotate(values, cosine, sine_term):
    return values * cosine + pair_swap(values) * sine_term


def rotate_back(values, cosine, sine_term):
    return values * cosine + pair_swap(values * sine_term)


def gelu_tanh(pre_values):
    return jax.nn.gelu(pre_values, approximate=True)


def body_by_heads(
    hidden_in,
    family,
    orient,
    norm_gain,
    norm_bias,
    qkv_weight,
    out_weight,
    up_weight,
    up_bias,
    down_weight,
    down_bias,
    family_table,
    orient_table,
    cotangent,
):
    seq_count = lax.axis_size("seq")
    row_count, seg_length, features = hidden_in.shape
    full_length = seg_length * seq_count
    local_heads = H // seq_count
    head_size = features // H
    slab_width = features // seq_count
    block_rows = min(512, full_length)
    block_count = full_length // block_rows
    score_scale = head_size ** (-0.5)
    token_count = row_count * seg_length
    family_rows = jnp.repeat(family, 2)
    family_hot = (family_rows[:, None] == jnp.arange(family_table.shape[0])[None, :]).astype(
        jnp.bfloat16
    )
    orient_hot = (orient[:, None] == jnp.arange(2)[None, :]).astype(jnp.bfloat16)
    embedding = jnp.dot(family_hot, family_table, preferred_element_type=jnp.float32) + jnp.dot(
        orient_hot, orient_table, preferred_element_type=jnp.float32
    )
    embedded = (hidden_in.astype(jnp.float32) + embedding[:, None, :]).reshape(
        token_count, features
    )
    row_mean = jnp.mean(embedded, -1, keepdims=True)
    centred = embedded - row_mean
    row_var = jnp.mean(centred * centred, -1, keepdims=True)
    inv_std = lax.rsqrt(row_var + 1e-05)
    normed_hat = centred * inv_std
    gain_f32 = norm_gain.astype(jnp.float32)
    normed_low = (normed_hat * gain_f32 + norm_bias.astype(jnp.float32)).astype(jnp.bfloat16)
    projected = jnp.dot(normed_low, qkv_weight, preferred_element_type=jnp.float32).reshape(
        row_count, seg_length, 3 * features
    )
    positions = (lax.axis_index("seq") * seg_length + jnp.arange(seg_length)).astype(jnp.float32)
    cosine, sine_term = rope_tables(positions, features)
    queries = rotate(projected[..., :features], cosine, sine_term).astype(jnp.bfloat16)
    keys_rot = rotate(projected[..., features : 2 * features], cosine, sine_term).astype(
        jnp.bfloat16
    )
    values = projected[..., 2 * features :].astype(jnp.bfloat16)
    query_heads, key_heads, value_heads = (
        lax.all_to_all(queries, "seq", split_axis=2, concat_axis=1, tiled=True),
        lax.all_to_all(keys_rot, "seq", split_axis=2, concat_axis=1, tiled=True),
        lax.all_to_all(values, "seq", split_axis=2, concat_axis=1, tiled=True),
    )

    def scores_for(query_block, key_rows, block_start):
        logits = (
            jnp.einsum("qhd,khd->hqk", query_block, key_rows, preferred_element_type=jnp.float32)
            * score_scale
        )
        causal = (block_start + jnp.arange(block_rows))[:, None] >= jnp.arange(full_length)[None, :]
        return jnp.where(causal[None], logits, -1e30)

    def attend(row_args):
        query_row, key_row, value_row = row_args
        key_rows = key_row.reshape(full_length, local_heads, head_size)
        value_rows = value_row.reshape(full_length, local_heads, head_size)
        pieces = []
        log_parts = []
        for block_index in range(block_count):
            block_start = block_index * block_rows
            query_block = query_row[block_start : block_start + block_rows].reshape(
                block_rows, local_heads, head_size
            )
            logits = scores_for(query_block, key_rows, block_start)
            row_peak = jnp.max(logits, -1, keepdims=True)
            weights = jnp.exp(logits - row_peak)
            row_total = jnp.sum(weights, -1, keepdims=True)
            prob_low = (weights / row_total).astype(jnp.bfloat16)
            output_block = jnp.einsum(
                "hqk,khd->qhd", prob_low, value_rows, preferred_element_type=jnp.float32
            )
            pieces.append(output_block.reshape(block_rows, slab_width).astype(jnp.bfloat16))
            log_parts.append((row_peak + jnp.log(row_total))[..., 0])
        return (jnp.concatenate(pieces, 0), jnp.concatenate(log_parts, 1))

    attended_heads, log_sums = lax.map(attend, (query_heads, key_heads, value_heads))
    attended = jax.tree.map(
        lambda part, own: part.astype(own.dtype),
        lax.all_to_all(for_sending(attended_heads), "seq", split_axis=1, concat_axis=2, tiled=True),
        attended_heads,
    )
    attended_flat = attended.reshape(token_count, features)
    branch_attn = jnp.dot(attended_flat, out_weight, preferred_element_type=jnp.float32)
    up_pre = jnp.dot(normed_low, up_weight, preferred_element_type=jnp.float32) + up_bias.astype(
        jnp.float32
    )
    up_act = gelu_tanh(up_pre).astype(jnp.bfloat16)
    branch_feed = jnp.dot(
        up_act, down_weight, preferred_element_type=jnp.float32
    ) + down_bias.astype(jnp.float32)
    layer_out = (
        (embedded + branch_attn + branch_feed)
        .astype(jnp.bfloat16)
        .reshape(row_count, seg_length, features)
    )
    grad_low = cotangent.reshape(token_count, features)
    grad_f32 = grad_low.astype(jnp.float32)
    down_grad = jnp.einsum("nf,nd->fd", up_act, grad_low, preferred_element_type=jnp.float32)
    down_bias_grad = jnp.sum(grad_f32, 0)
    act_grad = jnp.einsum("nd,fd->nf", grad_low, down_weight, preferred_element_type=jnp.float32)
    gelu_out, gelu_pull = jax.vjp(gelu_tanh, up_pre)
    pre_grad = gelu_pull(act_grad)[0].astype(jnp.bfloat16)
    up_bias_grad = jnp.sum(pre_grad.astype(jnp.float32), 0)
    up_grad = jnp.einsum("nd,nf->df", normed_low, pre_grad, preferred_element_type=jnp.float32)
    normed_grad = jnp.einsum("nf,df->nd", pre_grad, up_weight, preferred_element_type=jnp.float32)
    out_grad = jnp.einsum("nd,ne->de", attended_flat, grad_low, preferred_element_type=jnp.float32)
    attended_grad = jnp.einsum(
        "ne,de->nd", grad_low, out_weight, preferred_element_type=jnp.float32
    )
    attended_grad = attended_grad.astype(jnp.bfloat16).reshape(row_count, seg_length, features)
    grad_heads = lax.all_to_all(attended_grad, "seq", split_axis=2, concat_axis=1, tiled=True)

    def attend_back(row_args):
        query_row, key_row, value_row, grad_row, log_row = row_args
        key_rows = key_row.reshape(full_length, local_heads, head_size)
        value_rows = value_row.reshape(full_length, local_heads, head_size)
        keys_total = jnp.zeros((full_length, local_heads, head_size), jnp.float32)
        values_total = jnp.zeros((full_length, local_heads, head_size), jnp.float32)
        query_parts = []
        for block_index in range(block_count):
            block_start = block_index * block_rows
            query_block = query_row[block_start : block_start + block_rows].reshape(
                block_rows, local_heads, head_size
            )
            grad_block = grad_row[block_start : block_start + block_rows].reshape(
                block_rows, local_heads, head_size
            )
            logits = scores_for(query_block, key_rows, block_start)
            probs_full = jnp.exp(logits - log_row[:, block_start : block_start + block_rows, None])
            prob_low = probs_full.astype(jnp.bfloat16)
            probs_grad = jnp.einsum(
                "qhd,khd->hqk", grad_block, value_rows, preferred_element_type=jnp.float32
            )
            inner_sum = jnp.sum(probs_full * probs_grad, -1, keepdims=True)
            scores_grad = (probs_full * (probs_grad - inner_sum)).astype(jnp.bfloat16)
            values_total = values_total + jnp.einsum(
                "hqk,qhd->khd", prob_low, grad_block, preferred_element_type=jnp.float32
            )
            query_grad = (
                jnp.einsum(
                    "hqk,khd->qhd", scores_grad, key_rows, preferred_element_type=jnp.float32
                )
                * score_scale
            )
            query_parts.append(query_grad.reshape(block_rows, slab_width).astype(jnp.bfloat16))
            keys_total = (
                keys_total
                + jnp.einsum(
                    "hqk,qhd->khd", scores_grad, query_block, preferred_element_type=jnp.float32
                )
                * score_scale
            )
        return (
            jnp.concatenate(query_parts, 0),
            keys_total.reshape(full_length, slab_width).astype(jnp.bfloat16),
            values_total.reshape(full_length, slab_width).astype(jnp.bfloat16),
        )

    query_grad_heads, key_grad_heads, value_grad_heads = lax.map(
        attend_back, (query_heads, key_heads, value_heads, grad_heads, log_sums)
    )
    query_grad_pos, key_grad_pos, value_grad_pos = (
        lax.all_to_all(
            for_sending(query_grad_heads), "seq", split_axis=1, concat_axis=2, tiled=True
        ).astype(query_grad_heads.dtype),
        lax.all_to_all(
            for_sending(key_grad_heads), "seq", split_axis=1, concat_axis=2, tiled=True
        ).astype(key_grad_heads.dtype),
        lax.all_to_all(
            for_sending(value_grad_heads), "seq", split_axis=1, concat_axis=2, tiled=True
        ).astype(value_grad_heads.dtype),
    )
    projected_grad = jnp.concatenate(
        [
            rotate_back(query_grad_pos.astype(jnp.float32), cosine, sine_term),
            rotate_back(key_grad_pos.astype(jnp.float32), cosine, sine_term),
            value_grad_pos.astype(jnp.float32),
        ],
        -1,
    )
    projected_grad = projected_grad.astype(jnp.bfloat16).reshape(token_count, 3 * features)
    qkv_grad = jnp.einsum(
        "nd,ne->de", normed_low, projected_grad, preferred_element_type=jnp.float32
    )
    normed_grad = normed_grad + jnp.einsum(
        "ne,de->nd", projected_grad, qkv_weight, preferred_element_type=jnp.float32
    )
    gain_grad = jnp.sum(normed_grad * normed_hat, 0)
    bias_grad = jnp.sum(normed_grad, 0)
    scaled_grad = normed_grad * gain_f32
    hat_grad = (
        scaled_grad
        - jnp.mean(scaled_grad, -1, keepdims=True)
        - normed_hat * jnp.mean(scaled_grad * normed_hat, -1, keepdims=True)
    )
    input_grad = (grad_f32 + inv_std * hat_grad).reshape(row_count, seg_length, features)
    row_sums = jnp.sum(input_grad, 1)
    family_grad = jnp.einsum(
        "rf,rd->fd", family_hot.astype(jnp.float32), row_sums, precision=lax.Precision.HIGHEST
    )
    orient_grad = jnp.einsum(
        "rf,rd->fd", orient_hot.astype(jnp.float32), row_sums, precision=lax.Precision.HIGHEST
    )
    gain_sum, bias_sum, up_bias_sum, down_bias_sum, family_sum, orient_sum = lax.psum(
        (gain_grad, bias_grad, up_bias_grad, down_bias_grad, family_grad, orient_grad),
        ("dp", "seq"),
    )
    qkv_sum, out_sum, up_sum, down_sum = (
        lax.psum_scatter(qkv_grad, ("dp", "seq"), scatter_dimension=0, tiled=True),
        lax.psum_scatter(out_grad, ("dp", "seq"), scatter_dimension=0, tiled=True),
        lax.psum_scatter(up_grad, ("dp", "seq"), scatter_dimension=0, tiled=True),
        lax.psum_scatter(down_grad, ("dp", "seq"), scatter_dimension=0, tiled=True),
    )
    return (
        layer_out,
        input_grad,
        gain_sum,
        bias_sum,
        qkv_sum,
        out_sum,
        up_sum,
        up_bias_sum,
        down_sum,
        down_bias_sum,
        family_sum,
        orient_sum,
    )


def dot_nn(a, b):
    return lax.dot_general(a, b, (((1,), (0,)), ((), ())), preferred_element_type=F32)


def dot_nt(a, b):
    return lax.dot_general(a, b, (((1,), (1,)), ((), ())), preferred_element_type=F32)


def dot_tn(a, b):
    return lax.dot_general(a, b, (((0,), (0,)), ((), ())), preferred_element_type=F32)


def params(**more):
    return pltpu.CompilerParams(vmem_limit_bytes=VMEM_LIMIT, **more)


def cost(flops, moved, exps=0):
    return pl.CostEstimate(flops=flops, bytes_accessed=moved, transcendentals=exps)


def whole(shape):
    return pl.BlockSpec(shape, lambda *_: (0,) * len(shape), pipeline_mode=pl.Buffered(1))


def table_row(table, wanted):
    rows = lax.broadcasted_iota(jnp.int32, table.shape, 0)
    return jnp.sum(jnp.where(rows == wanted, table[...].astype(F32), 0.0), 0, keepdims=True)


def normalise(entries):
    centred = entries - jnp.mean(entries, -1, keepdims=True)
    inv_std = lax.rsqrt(jnp.mean(centred * centred, -1, keepdims=True) + 1e-05)
    return centred * inv_std, inv_std


GELU_C = math.sqrt(2.0 / math.pi)


def gelu_both(z):
    square = z * z
    t = jnp.tanh(GELU_C * z * (1.0 + 0.044715 * square))
    half = 0.5 * (1.0 + t)
    slope = half + (0.5 * GELU_C) * z * (1.0 - t * t) * (1.0 + (3 * 0.044715) * square)
    return z * half, slope


def ffn_kernel(rows, ids, hid, cot, fam, ori, gain, bias, wup, bup, wdn, norm, act, pre, bupg, bdng):
    tokens = hid.shape[0]
    seg = tokens // rows
    step = 256

    @pl.when(pl.program_id(0) == 0)
    def _():
        total = jnp.zeros((1, cot.shape[1]), F32)
        for row in range(rows):
            emb = table_row(fam, ids[0]) + table_row(ori, ids[1 + row])
            for start in range(row * seg, (row + 1) * seg, step):
                part = pl.ds(start, step)
                hat, _ = normalise(hid[part, :].astype(F32) + emb)
                norm[part, :] = (hat * gain[...].astype(F32) + bias[...].astype(F32)).astype(BF16)
                total = total + jnp.sum(cot[part, :].astype(F32), 0, keepdims=True)
        bdng[...] = total

    total = jnp.zeros((1, wup.shape[1]), F32)
    for start in range(0, tokens, step):
        part = pl.ds(start, step)
        z = dot_nn(norm[part, :], wup[...]) + bup[...].astype(F32)
        into = dot_nt(cot[part, :], wdn[...])
        value, slope = gelu_both(z)
        act[part, :] = value.astype(BF16)
        low = (into * slope).astype(BF16)
        pre[part, :] = low
        total = total + jnp.sum(low.astype(F32), 0, keepdims=True)
    bupg[...] = total


def ffn_forward(ids, hid, cot, fam, ori, gain, bias, wup, bup, wdn, rows):
    tokens, d = hid.shape
    ff = wup.shape[1]
    tile = 512
    return pl.pallas_call(
        functools.partial(ffn_kernel, rows),
        grid_spec=pltpu.PrefetchScalarGridSpec(
            num_scalar_prefetch=1,
            grid=(ff // tile,),
            in_specs=[
                whole((tokens, d)),
                whole((tokens, d)),
                whole(fam.shape),
                whole(ori.shape),
                whole((1, d)),
                whole((1, d)),
                pl.BlockSpec((d, tile), lambda i, s: (0, i)),
                pl.BlockSpec((1, tile), lambda i, s: (0, i)),
                pl.BlockSpec((tile, d), lambda i, s: (i, 0)),
            ],
            out_specs=[
                whole((tokens, d)),
                pl.BlockSpec((tokens, tile), lambda i, s: (0, i)),
                pl.BlockSpec((tokens, tile), lambda i, s: (0, i)),
                pl.BlockSpec((1, tile), lambda i, s: (0, i)),
                whole((1, d)),
            ],
        ),
        out_shape=[
            jax.ShapeDtypeStruct((tokens, d), BF16),
            jax.ShapeDtypeStruct((tokens, ff), BF16),
            jax.ShapeDtypeStruct((tokens, ff), BF16),
            jax.ShapeDtypeStruct((1, ff), F32),
            jax.ShapeDtypeStruct((1, d), F32),
        ],
        compiler_params=params(),
        cost_estimate=cost(4 * tokens * d * ff, 4 * tokens * ff + 4 * d * ff, tokens * ff),
        name="ffn_forward",
    )(ids, hid, cot, fam, ori, gain, bias, wup, bup, wdn)


def turn(entries, cosine, sine):
    even = lax.broadcasted_iota(jnp.int32, entries.shape, 1) % 2 == 0
    other = jnp.where(even, pltpu.roll(entries, 127, 1), pltpu.roll(entries, 1, 1))
    return entries * cosine + other * sine


def turn_back(entries, cosine, sine):
    even = lax.broadcasted_iota(jnp.int32, entries.shape, 1) % 2 == 0
    side = entries * sine
    other = jnp.where(even, pltpu.roll(side, 127, 1), pltpu.roll(side, 1, 1))
    return entries * cosine + other


def qkv_kernel(tiles, ids, own, far, cown, cfar, fam, ori, gain, bias, wqkv, wout, cos, sin, norm, cot, qkv, datt):
    seg = own.shape[0]
    step = 256
    i = pl.program_id(0)
    me = ids[1]

    @pl.when(i == 0)
    def _():
        emb = table_row(fam, ids[0]) + table_row(ori, ids[2])
        for source, csource, where in ((own, cown, me), (far, cfar, 1 - me)):
            for start in range(0, seg, step):
                part = pl.ds(start, step)
                there = pl.ds(pl.multiple_of(where * seg + start, step), step)
                hat, _ = normalise(source[part, :].astype(F32) + emb)
                norm[there, :] = (hat * gain[...].astype(F32) + bias[...].astype(F32)).astype(BF16)
                cot[there, :] = csource[part, :]

    @pl.when(i < 2 * tiles)
    def _():
        for start in range(0, 2 * seg, step):
            part = pl.ds(start, step)
            lin = dot_nn(norm[part, :], wqkv[...])
            for lane in range(0, lin.shape[1], 128):
                piece = turn(lin[:, lane : lane + 128], cos[part, :], sin[part, :])
                qkv[part, lane : lane + 128] = piece.astype(BF16)

    @pl.when((i >= 2 * tiles) & (i < 3 * tiles))
    def _():
        for start in range(0, 2 * seg, step):
            part = pl.ds(start, step)
            qkv[part, :] = dot_nn(norm[part, :], wqkv[...]).astype(BF16)

    @pl.when(i >= 3 * tiles)
    def _():
        for start in range(0, 2 * seg, step):
            part = pl.ds(start, step)
            datt[part, :] = dot_nt(cot[part, :], wout[...]).astype(BF16)


def qkv_forward(ids, own, far, cown, cfar, fam, ori, gain, bias, wqkv, wout, cos, sin):
    seg, d = own.shape
    full = 2 * seg
    tile = 512
    tiles = d // tile
    return pl.pallas_call(
        functools.partial(qkv_kernel, tiles),
        grid_spec=pltpu.PrefetchScalarGridSpec(
            num_scalar_prefetch=1,
            grid=(4 * tiles,),
            in_specs=[
                whole((seg, d)),
                whole((seg, d)),
                whole((seg, d)),
                whole((seg, d)),
                whole(fam.shape),
                whole(ori.shape),
                whole((1, d)),
                whole((1, d)),
                pl.BlockSpec((d, tile), lambda i, s: (0, jnp.minimum(i, 3 * tiles - 1))),
                pl.BlockSpec((tile, d), lambda i, s: (jnp.maximum(i - 3 * tiles, 0), 0)),
                whole((full, 128)),
                whole((full, 128)),
            ],
            out_specs=[
                whole((full, d)),
                whole((full, d)),
                pl.BlockSpec((full, tile), lambda i, s: (0, jnp.minimum(i, 3 * tiles - 1))),
                pl.BlockSpec((full, tile), lambda i, s: (0, jnp.maximum(i - 3 * tiles, 0))),
            ],
        ),
        out_shape=[
            jax.ShapeDtypeStruct((full, d), BF16),
            jax.ShapeDtypeStruct((full, d), BF16),
            jax.ShapeDtypeStruct((full, 3 * d), BF16),
            jax.ShapeDtypeStruct((full, d), BF16),
        ],
        compiler_params=params(),
        cost_estimate=cost(8 * full * d * d, 8 * d * d + 18 * full * d),
        name="qkv_forward",
    )(ids, own, far, cown, cfar, fam, ori, gain, bias, wqkv, wout, cos, sin)


def attention_kernel(head_size, skipped, q_ref, k_ref, v_ref, g_ref, cos, sin, *rest):
    o_ref, dq_ref, dk_ref, dv_ref, dkt, dvt = rest[skipped:]
    full = q_ref.shape[0]
    block = 256
    scale = head_size ** (-0.5)
    lane = lax.broadcasted_iota(jnp.int32, (block, 128), 1)
    below = lax.broadcasted_iota(jnp.int32, (block, block), 0) >= lax.broadcasted_iota(
        jnp.int32, (block, block), 1
    )
    dkt[...] = jnp.zeros_like(dkt)
    dvt[...] = jnp.zeros_like(dvt)
    for start in range(0, full, block):
        part = pl.ds(start, block)
        end = start + block
        query = q_ref[part, :]
        grad = g_ref[part, :]
        out = None
        dq = None
        for head in range(128 // head_size):
            mine = (lane >= head * head_size) & (lane < (head + 1) * head_size)
            qm = jnp.where(mine, query.astype(F32) * scale, 0.0).astype(BF16)
            gm = jnp.where(mine, grad.astype(F32), 0.0).astype(BF16)
            scores = dot_nt(qm, k_ref[0:end, :])
            last = jnp.where(below, scores[:, start:end], -1e30)
            scores = last if start == 0 else jnp.concatenate([scores[:, :start], last], 1)
            weights = jnp.exp(scores - jnp.max(scores, -1, keepdims=True))
            probs = weights * (1.0 / jnp.sum(weights, -1, keepdims=True))
            low = probs.astype(BF16)
            piece = dot_nn(low, v_ref[0:end, :])
            out = piece if out is None else jnp.where(mine, piece, out)
            pg = dot_nt(gm, v_ref[0:end, :])
            inner = jnp.sum(probs * pg, -1, keepdims=True)
            sg = (probs * (pg - inner)).astype(BF16)
            piece = dot_nn(sg, k_ref[0:end, :])
            dq = piece if dq is None else jnp.where(mine, piece, dq)
            dkt[:, 0:end] += dot_tn(qm, sg)
            dvt[:, 0:end] += dot_tn(gm, low)
        o_ref[part, :] = out.astype(BF16)
        dq_ref[part, :] = turn_back(dq * scale, cos[part, :], sin[part, :]).astype(BF16)
    for start in range(0, full, block):
        part = pl.ds(start, block)
        dk = dkt[:, start : start + block].T
        dk_ref[part, :] = turn_back(dk, cos[part, :], sin[part, :]).astype(BF16)
        dv_ref[part, :] = dvt[:, start : start + block].T.astype(BF16)


def attention(qkv, datt, cos, sin, head_size, part, parts, before):
    full, d = datt.shape
    pairs = d // 128
    count = pairs // parts
    first = part * count
    shape = jax.ShapeDtypeStruct((full, d), BF16)
    spec = pl.BlockSpec((full, 128), lambda i: (0, first + i))
    anywhere = pl.BlockSpec(memory_space=pl.ANY)
    return pl.pallas_call(
        functools.partial(attention_kernel, head_size, len(before)),
        grid=(count,),
        in_specs=[
            spec,
            pl.BlockSpec((full, 128), lambda i: (0, pairs + first + i)),
            pl.BlockSpec((full, 128), lambda i: (0, 2 * pairs + first + i)),
            spec,
            whole((full, 128)),
            whole((full, 128)),
        ]
        + [anywhere] * len(before),
        out_specs=[spec] * 4,
        out_shape=[shape] * 4,
        scratch_shapes=[pltpu.VMEM((128, full), F32), pltpu.VMEM((128, full), F32)],
        input_output_aliases={6 + index: index for index in range(len(before))},
        compiler_params=params(),
        cost_estimate=cost(12 * full * full * d * 2 // parts, 16 * full * d // parts, full * full * H // parts),
        name="attention",
    )(qkv, qkv, qkv, datt, cos, sin, *before)


def store_blocks(meta, value, keep, send):
    size = keep.shape[-2]
    core = meta[0]
    for up in range(keep.shape[0] // 2):
        for seq in range(2):
            first = (4 * up + seq) * size
            second = first + 2 * size
            a = value[first : first + size, :].astype(BF16)
            b = value[second : second + size, :].astype(BF16)
            there = meta[2 + 2 * up + seq]
            keep[there] = jnp.where(core == 0, a, b)
            send[there] = jnp.where(core == 0, b, a)


def up_grad_kernel(meta, left, right, keep, send, turned):
    @pl.when(pl.program_id(0) == 0)
    def _():
        turned[...] = left[...].T

    store_blocks(meta, dot_nn(turned[...], right[...]), keep, send)


def up_grad(meta, left, right, upper):
    tokens, d = left.shape
    n = right.shape[1]
    tile = 512
    size = d // (upper * 4)
    shape = jax.ShapeDtypeStruct((2 * upper, size, n), BF16)
    spec = pl.BlockSpec((2 * upper, size, tile), lambda j, s: (0, 0, j))
    return pl.pallas_call(
        up_grad_kernel,
        grid_spec=pltpu.PrefetchScalarGridSpec(
            num_scalar_prefetch=1,
            grid=(n // tile,),
            in_specs=[whole((tokens, d)), pl.BlockSpec((tokens, tile), lambda j, s: (0, j))],
            out_specs=[spec, spec],
            scratch_shapes=[pltpu.VMEM((d, tokens), BF16)],
        ),
        out_shape=[shape, shape],
        compiler_params=params(),
        cost_estimate=cost(2 * tokens * d * n, 2 * (tokens * n + d * n + tokens * d)),
        name="up_grad",
    )(meta, left, right)


def down_grad_kernel(seq_first, meta, left, right, keep, send):
    size = keep.shape[-2]
    core = meta[0]
    value = dot_nn(left[...].T, right[...])
    for seq in range(2):
        first = seq * size
        second = first + 2 * size
        a = value[first : first + size, :].astype(BF16)
        b = value[second : second + size, :].astype(BF16)
        apart = lax.rem(seq + meta[1], 2)
        there = (apart, 0) if seq_first else (0, apart)
        keep[there] = jnp.where(core == 0, a, b)
        send[there] = jnp.where(core == 0, b, a)


def down_grad(meta, left, right, upper, seq_first):
    tokens, m = left.shape
    d = right.shape[1]
    tile = m // upper
    size = tile // 4
    if seq_first:
        dims, block = (2, upper, size, d), (2, 1, size, d)
    else:
        dims, block = (upper, 2, size, d), (1, 2, size, d)

    def at(i, s):
        place = s[2 + 2 * i + s[1]]
        return (0, place, 0, 0) if seq_first else (place // 2, 0, 0, 0)

    shape = jax.ShapeDtypeStruct(dims, BF16)
    spec = pl.BlockSpec(block, at)
    keep, send = pl.pallas_call(
        functools.partial(down_grad_kernel, seq_first),
        grid_spec=pltpu.PrefetchScalarGridSpec(
            num_scalar_prefetch=1,
            grid=(upper,),
            in_specs=[pl.BlockSpec((tokens, tile), lambda i, s: (0, i)), whole((tokens, d))],
            out_specs=[spec, spec],
        ),
        out_shape=[shape, shape],
        compiler_params=params(),
        cost_estimate=cost(2 * tokens * d * m, 2 * (tokens * m + d * m + tokens * d)),
        name="down_grad",
    )(meta, left, right)
    return keep.reshape(2 * upper, size, d), send.reshape(2 * upper, size, d)


def pair_grad_kernel(tiles, same, meta, *refs):
    lefts, (first, second, keep, send, turned) = refs[:-5], refs[-5:]
    j = pl.program_id(0)

    @pl.when(j == 0)
    def _():
        turned[...] = lefts[0][...].T

    if not same:

        @pl.when(j == tiles)
        def _():
            turned[...] = lefts[1][...].T

    @pl.when(j < tiles)
    def _():
        store_blocks(meta, dot_nn(turned[...], first[...]), keep, send)

    @pl.when(j >= tiles)
    def _():
        store_blocks(meta, dot_nn(turned[...], second[...]), keep, send)


def pair_grad(meta, lefts, first, second, upper):
    tokens, d = first.shape
    tile = 512
    tiles = d // tile
    size = d // (upper * 4)
    shape = jax.ShapeDtypeStruct((2 * upper, size, 2 * d), BF16)
    spec = pl.BlockSpec((2 * upper, size, tile), lambda j, s: (0, 0, j))
    return pl.pallas_call(
        functools.partial(pair_grad_kernel, tiles, len(lefts) == 1),
        grid_spec=pltpu.PrefetchScalarGridSpec(
            num_scalar_prefetch=1,
            grid=(2 * tiles,),
            in_specs=[whole((tokens, d)) for _ in lefts]
            + [
                pl.BlockSpec((tokens, tile), lambda j, s: (0, jnp.minimum(j, tiles - 1))),
                pl.BlockSpec((tokens, tile), lambda j, s: (0, jnp.maximum(j - tiles, 0))),
            ],
            out_specs=[spec, spec],
            scratch_shapes=[pltpu.VMEM((d, tokens), BF16)],
        ),
        out_shape=[shape, shape],
        compiler_params=params(),
        cost_estimate=cost(4 * tokens * d * d, 10 * tokens * d),
        name="pair_grad",
    )(meta, *lefts, first, second)


class Halving:
    def __init__(self, axes, keep, send):
        self.axes = axes
        self.keep = keep
        self.got = self.swap(send, 0)

    def swap(self, part, axis):
        if axis == "seq":
            return lax.ppermute(part, "seq", [(0, 1), (1, 0)])
        count = lax.axis_size("dp")
        return lax.ppermute(part, "dp", [(i, i ^ (1 << axis)) for i in range(count)])

    def step(self):
        axis, self.axes = self.axes[0], self.axes[1:]
        half = self.keep.shape[0] // 2
        send = self.keep[half:].astype(F32) + self.got[half:].astype(F32)
        keep = self.keep[:half].astype(F32) + self.got[:half].astype(F32)
        send = send.astype(BF16)
        self.keep = keep if half == 1 else keep.astype(BF16)
        self.got = self.swap(send, axis)
        return send

    def total(self):
        return self.keep[0] + self.got[0].astype(F32)


def after(entry, *others):
    return lax.optimization_barrier((entry, *others))[0]


def back_kernel(dq, dk, dv, w, out):
    d = dq.shape[1]
    total = dot_nt(dq[...], w[:, 0:d])
    total = total + dot_nt(dk[...], w[:, d : 2 * d])
    total = total + dot_nt(dv[...], w[:, 2 * d : 3 * d])
    out[...] = total.astype(BF16)


def project_back(dq, dk, dv, w):
    tokens, d = dq.shape
    step = 256
    spec = pl.BlockSpec((step, d), lambda i: (i, 0))
    return pl.pallas_call(
        back_kernel,
        grid=(tokens // step,),
        in_specs=[spec, spec, spec, whole(w.shape)],
        out_specs=spec,
        out_shape=jax.ShapeDtypeStruct((tokens, d), BF16),
        compiler_params=params(),
        cost_estimate=cost(6 * tokens * d * d, 6 * d * d + 8 * tokens * d),
        name="project_back",
    )(dq, dk, dv, w)


def out_kernel(per_row, ids, hid, fam, ori, act, wdn, own, far, wout, bdn, out):
    row = pl.program_id(0) // per_row
    emb = table_row(fam, ids[0]) + table_row(ori, ids[2 + row])
    att = jnp.where(row == ids[1], own[...], far[...])
    total = hid[...].astype(F32) + emb + dot_nn(att, wout[...])
    total = total + (dot_nn(act[...], wdn[...]) + bdn[...].astype(F32))
    out[...] = total.astype(BF16)


def input_kernel(per_row, ids, hid, fam, ori, pre, wup, own, far, gain, cot, out, gg, bg, rg):
    i = pl.program_id(0)
    row = i // per_row
    emb = table_row(fam, ids[0]) + table_row(ori, ids[2 + row])
    hat, inv_std = normalise(hid[...].astype(F32) + emb)
    grad = dot_nt(pre[...], wup[...]) + jnp.where(row == ids[1], own[...], far[...]).astype(F32)

    @pl.when(i == 0)
    def _():
        gg[...] = jnp.zeros_like(gg)
        bg[...] = jnp.zeros_like(bg)
        rg[...] = jnp.zeros_like(rg)

    gg[...] += jnp.sum(grad * hat, 0, keepdims=True)
    bg[...] += jnp.sum(grad, 0, keepdims=True)
    scaled = grad * gain[...].astype(F32)
    inner = (
        scaled
        - jnp.mean(scaled, -1, keepdims=True)
        - hat * jnp.mean(scaled * hat, -1, keepdims=True)
    )
    result = cot[...].astype(F32) + inv_std * inner
    out[...] = result
    sums = jnp.sum(result, 0, keepdims=True)
    rows = lax.broadcasted_iota(jnp.int32, rg.shape, 0)
    rg[...] += jnp.where(rows == row, sums, 0.0)


def home_specs(tokens, d, rows, step):
    per_row = tokens // rows // step
    local = pl.BlockSpec((step, d), lambda i, s: (i, 0))
    own = pl.BlockSpec((step, d), lambda i, s: (s[1] * per_row + i % per_row, 0))
    far = pl.BlockSpec((step, d), lambda i, s: (i % per_row, 0))
    return per_row, local, own, far


def layer_output(ids, hid, fam, ori, act, wdn, own, far, wout, bdn, rows):
    tokens, d = hid.shape
    ff = act.shape[1]
    step = 256
    per_row, local, own_spec, far_spec = home_specs(tokens, d, rows, step)
    return pl.pallas_call(
        functools.partial(out_kernel, per_row),
        grid_spec=pltpu.PrefetchScalarGridSpec(
            num_scalar_prefetch=1,
            grid=(tokens // step,),
            in_specs=[
                local,
                whole(fam.shape),
                whole(ori.shape),
                pl.BlockSpec((step, ff), lambda i, s: (i, 0)),
                whole(wdn.shape),
                own_spec,
                far_spec,
                whole(wout.shape),
                whole((1, d)),
            ],
            out_specs=local,
        ),
        out_shape=jax.ShapeDtypeStruct((tokens, d), BF16),
        compiler_params=params(),
        cost_estimate=cost(2 * tokens * d * (ff + d), 2 * (d * (ff + d) + tokens * ff + 4 * tokens * d)),
        name="layer_output",
    )(ids, hid, fam, ori, act, wdn, own, far, wout, bdn)


def input_gradient(ids, hid, fam, ori, pre, wup, own, far, gain, cot, rows):
    tokens, d = hid.shape
    ff = pre.shape[1]
    step = 256
    per_row, local, own_spec, far_spec = home_specs(tokens, d, rows, step)
    return pl.pallas_call(
        functools.partial(input_kernel, per_row),
        grid_spec=pltpu.PrefetchScalarGridSpec(
            num_scalar_prefetch=1,
            grid=(tokens // step,),
            in_specs=[
                local,
                whole(fam.shape),
                whole(ori.shape),
                pl.BlockSpec((step, ff), lambda i, s: (i, 0)),
                whole(wup.shape),
                own_spec,
                far_spec,
                whole((1, d)),
                local,
            ],
            out_specs=[local, whole((1, d)), whole((1, d)), whole((rows, d))],
        ),
        out_shape=[
            jax.ShapeDtypeStruct((tokens, d), F32),
            jax.ShapeDtypeStruct((1, d), F32),
            jax.ShapeDtypeStruct((1, d), F32),
            jax.ShapeDtypeStruct((rows, d), F32),
        ],
        compiler_params=params(),
        cost_estimate=cost(2 * tokens * d * ff, 2 * (d * ff + tokens * ff + 6 * tokens * d)),
        name="input_gradient",
    )(ids, hid, fam, ori, pre, wup, own, far, gain, cot)


def sums_kernel(bits, sums_ref, vec_ref, sums_out, all_out, held, got, vgot, send_sem, recv_sem, gsend, grecv):
    dp = lax.axis_index("dp")
    seq = lax.axis_index("seq")
    partners = [(dp, 1 - seq)]
    for bit in range(bits):
        size = 1 << bit
        partners.append((dp + (1 - 2 * lax.rem(dp // size, 2)) * size, seq))
    barrier = pltpu.get_barrier_semaphore()
    for partner in partners:
        pl.semaphore_signal(barrier, inc=1, device_id=partner, device_id_type=MESH)
    pl.semaphore_wait(barrier, len(partners))

    def remote(src, dst, send, recv, partner):
        copy = pltpu.make_async_remote_copy(
            src_ref=src, dst_ref=dst, send_sem=send, recv_sem=recv, device_id=partner, device_id_type=MESH
        )
        copy.start()
        return copy

    for index, partner in enumerate(partners):
        source = sums_ref if index == 0 else held.at[index]
        main = remote(source, got.at[index], send_sem.at[index], recv_sem.at[index], partner)
        if index == 0:
            side = remote(vec_ref, vgot, gsend.at[0], grecv.at[0], partner)
        else:
            size = 1 << (index - 1)
            held_now = pl.ds(dp - lax.rem(dp, size), size)
            side = remote(
                all_out.at[held_now], all_out.at[held_now], gsend.at[index], grecv.at[index], partner
            )
        main.wait()
        total = source[...] + got[index]
        if index + 1 < len(partners):
            held[index + 1] = total
        else:
            sums_out[...] = total
        side.wait()
        if index == 0:
            all_out[dp] = vec_ref[...] + vgot[...]


def sum_small(sums, vec):
    count = lax.axis_size("dp")
    bits = int(math.log2(count))
    rounds = bits + 1
    return pl.pallas_call(
        functools.partial(sums_kernel, bits),
        in_specs=[pl.BlockSpec(memory_space=pltpu.VMEM)] * 2,
        out_specs=[pl.BlockSpec(memory_space=pltpu.VMEM)] * 2,
        out_shape=[
            jax.ShapeDtypeStruct(sums.shape, F32),
            jax.ShapeDtypeStruct((count,) + vec.shape, F32),
        ],
        scratch_shapes=[
            pltpu.VMEM((rounds,) + sums.shape, F32),
            pltpu.VMEM((rounds,) + sums.shape, F32),
            pltpu.VMEM(vec.shape, F32),
            pltpu.SemaphoreType.DMA((rounds,)),
            pltpu.SemaphoreType.DMA((rounds,)),
            pltpu.SemaphoreType.DMA((rounds,)),
            pltpu.SemaphoreType.DMA((rounds,)),
        ],
        compiler_params=pltpu.CompilerParams(collective_id=0, has_side_effects=True),
        name="sum_small",
    )(sums, vec)


def body_by_rows(
    hidden_in,
    family,
    orient,
    norm_gain,
    norm_bias,
    qkv_weight,
    out_weight,
    up_weight,
    up_bias,
    down_weight,
    down_bias,
    family_table,
    orient_table,
    cotangent,
):
    rows, seg, d = hidden_in.shape
    ff = up_weight.shape[1]
    tokens = rows * seg
    full = 2 * seg
    dp_count = lax.axis_size("dp")
    bits = int(math.log2(dp_count))
    upper = dp_count // 2
    dp = lax.axis_index("dp")
    seq = lax.axis_index("seq")
    ring = [(0, 1), (1, 0)]

    def mine(pair):
        return lax.dynamic_index_in_dim(pair, seq, 0, keepdims=False)

    def theirs(pair):
        return lax.dynamic_index_in_dim(pair, 1 - seq, 0, keepdims=False)

    far_hidden = lax.ppermute(theirs(hidden_in), "seq", ring)
    far_cot = lax.ppermute(theirs(cotangent), "seq", ring)

    gain = norm_gain.reshape(1, d)
    bias = norm_bias.reshape(1, d)
    hid = hidden_in.reshape(tokens, d)
    cot = cotangent.reshape(tokens, d)
    ids = jnp.concatenate([family, orient])
    tail_ids = jnp.concatenate([family, seq[None].astype(jnp.int32), orient])
    row_ids = jnp.stack([family[0], seq.astype(jnp.int32), mine(orient)])

    def meta_for(axes):
        index = jnp.arange(2 * upper, dtype=jnp.int32)
        apart = {bit: ((index >> bit) & 1) ^ ((dp >> bit) & 1) for bit in range(1, bits)}
        apart["seq"] = (index & 1) ^ seq
        place = jnp.zeros_like(index)
        for axis in axes:
            place = 2 * place + apart[axis]
        return jnp.concatenate([jnp.stack([dp % 2, seq]).astype(jnp.int32), place])

    zs = list(range(2, bits))
    order_a = [1] + zs + ["seq"]
    order_b = ["seq", 1] + zs
    order_c = [2, 1] + zs[1:] + ["seq"]
    meta_a, meta_b, meta_c = meta_for(order_a), meta_for(order_b), meta_for(order_c)

    normed, act, pre, up_bias_part, down_bias_part = ffn_forward(
        ids, hid, cot, family_table, orient_table, gain, bias, up_weight, up_bias.reshape(1, ff), down_weight, rows
    )
    up = Halving(order_a, *up_grad(meta_a, after(normed, far_hidden), pre, upper))
    down = Halving(order_b, *down_grad(meta_b, after(act, far_cot), cot, upper, True))
    up_x = up.step()

    cosine, sine = rope_tables(jnp.arange(full).astype(F32), 128)
    row_normed, row_cot, qkv, datt = qkv_forward(
        row_ids,
        mine(hidden_in),
        after(far_hidden, up_x),
        mine(cotangent),
        far_cot,
        family_table,
        orient_table,
        gain,
        bias,
        qkv_weight,
        out_weight,
        cosine,
        sine,
    )
    parts = 4
    done = ()
    tied = (down.step(),)
    for part in range(parts):
        done = attention(qkv, after(datt, *tied), cosine, sine, d // H, part, parts, done)
        if part == 1:
            tied = (up.step(),)
        if part == 2:
            tied = (down.step(),)
    att, dq, dk, dv = done
    far_att = lax.ppermute(theirs(att.reshape(2, seg, d)), "seq", ring)
    first = Halving(order_a, *pair_grad(meta_a, [row_normed], dq, dk, upper))
    second = Halving(order_c, *pair_grad(meta_c, [row_normed, after(att, first.keep)], dv, row_cot, upper))
    tied = (up.step(), down.step(), first.step())
    back = project_back(after(dq, second.keep, *tied), dk, dv, qkv_weight)
    far_back = lax.ppermute(theirs(back.reshape(2, seg, d)), "seq", ring)
    tied = (second.step(),)
    layer_out = layer_output(
        tail_ids,
        hid,
        family_table,
        orient_table,
        after(act, back, *tied),
        down_weight,
        att,
        far_att,
        out_weight,
        down_bias.reshape(1, d),
        rows,
    )
    tied = (up.step(), down.step(), first.step(), second.step())
    input_grad, gain_part, bias_part, row_part = input_gradient(
        tail_ids, hid, family_table, orient_table, after(pre, layer_out, *tied), up_weight, back, far_back, gain, cot, rows
    )
    for chunk in (first, second, up, down):
        while chunk.axes:
            chunk.step()
    up_total, down_total, first_total, second_total = up.total(), down.total(), first.total(), second.total()

    flag = orient[0]
    by_flag = jnp.where(flag == 0, row_part, row_part[::-1])
    packed = jnp.concatenate(
        [
            part.reshape(-1, 128)
            for part in (up_bias_part, down_bias_part, gain_part, bias_part, by_flag)
        ],
        0,
    )
    vec = jnp.concatenate(
        [
            (row_part[0] + row_part[1]).reshape(-1, 128),
            jnp.full((8, 128), 0.5, F32) * family.astype(F32)[0],
        ],
        0,
    )
    sums, gathered = sum_small(packed, vec)
    flat = sums.reshape(-1)
    up_bias_sum = flat[:ff]
    down_bias_sum, gain_sum, bias_sum = flat[ff : ff + 3 * d].reshape(3, d)
    orient_sum = flat[ff + 3 * d :].reshape(2, d)
    families = family_table.shape[0]
    hot = gathered[:, -1, 0].astype(jnp.int32)[None, :] == jnp.arange(families)[:, None]
    family_sum = jnp.dot(
        hot.astype(F32), gathered[:, :-8].reshape(dp_count, d), precision=lax.Precision.HIGHEST
    )
    return (
        layer_out.reshape(rows, seg, d),
        input_grad.reshape(rows, seg, d),
        gain_sum,
        bias_sum,
        jnp.concatenate([first_total, second_total[:, :d]], 1),
        second_total[:, d:],
        up_total,
        up_bias_sum,
        down_total,
        down_bias_sum,
        family_sum,
        orient_sum,
    )


def body(*args):
    hidden_in = args[0]
    dp_count = lax.axis_size("dp")
    two_rows = lax.axis_size("seq") == 2 and hidden_in.shape[0] == 2
    if two_rows and dp_count >= 4 and dp_count & (dp_count - 1) == 0:
        return body_by_rows(*args)
    return body_by_heads(*args)


def solution(mesh):
    return jax.shard_map(
        body,
        mesh=mesh,
        in_specs=(
            P("dp", "seq", None),
            P("dp"),
            P("dp"),
            P(),
            P(),
            P(),
            P(),
            P(),
            P(),
            P(),
            P(),
            P(),
            P(),
            P("dp", "seq", None),
        ),
        out_specs=(
            P("dp", "seq", None),
            P("dp", "seq", None),
            P(),
            P(),
            P(("dp", "seq"), None),
            P(("dp", "seq"), None),
            P(("dp", "seq"), None),
            P(),
            P(("dp", "seq"), None),
            P(),
            P(),
            P(),
        ),
        check_vma=False,
    )
```

```python
import functools
import math

import jax
import jax.numpy as jnp
from jax import lax
from jax.experimental import pallas as pl
from jax.experimental.pallas import tpu as pltpu
from jax.sharding import PartitionSpec as P

H = 16
HD = 64
ROT = 32
MESH = pl.DeviceIdType.MESH
VMEM_LIMIT = 60 * 1024 * 1024
F32 = jnp.float32
BF16 = jnp.bfloat16


def for_sending(shard):

    def short(part):
        return part.astype(jnp.bfloat16) if part.dtype == jnp.float32 else part

    return jax.tree.map(short, shard)


def rope_tables(positions, features):
    column = jnp.arange(features, dtype=jnp.int32)
    within = column % HD
    frequency = jnp.exp(-(2.0 * (within // 2).astype(jnp.float32) / ROT) * math.log(10000.0))
    angles = positions[:, None] * frequency[None, :]
    rotary = within < ROT
    cosine = jnp.where(rotary[None, :], jnp.cos(angles), 1.0)
    sign_term = jnp.where(within % 2 == 0, -1.0, 1.0)
    sine_term = jnp.where(rotary[None, :], sign_term[None, :] * jnp.sin(angles), 0.0)
    return (cosine, sine_term)


def pair_swap(values):
    even_cols = jnp.arange(values.shape[-1]) % 2 == 0
    return jnp.where(even_cols, jnp.roll(values, -1, axis=-1), jnp.roll(values, 1, axis=-1))


def rotate(values, cosine, sine_term):
    return values * cosine + pair_swap(values) * sine_term


def rotate_back(values, cosine, sine_term):
    return values * cosine + pair_swap(values * sine_term)


def gelu_tanh(pre_values):
    return jax.nn.gelu(pre_values, approximate=True)


def body_by_heads(
    hidden_in,
    family,
    orient,
    norm_gain,
    norm_bias,
    qkv_weight,
    out_weight,
    up_weight,
    up_bias,
    down_weight,
    down_bias,
    family_table,
    orient_table,
    cotangent,
):
    seq_count = lax.axis_size("seq")
    row_count, seg_length, features = hidden_in.shape
    full_length = seg_length * seq_count
    local_heads = H // seq_count
    head_size = features // H
    slab_width = features // seq_count
    block_rows = min(512, full_length)
    block_count = full_length // block_rows
    score_scale = head_size ** (-0.5)
    token_count = row_count * seg_length
    family_rows = jnp.repeat(family, 2)
    family_hot = (family_rows[:, None] == jnp.arange(family_table.shape[0])[None, :]).astype(
        jnp.bfloat16
    )
    orient_hot = (orient[:, None] == jnp.arange(2)[None, :]).astype(jnp.bfloat16)
    embedding = jnp.dot(family_hot, family_table, preferred_element_type=jnp.float32) + jnp.dot(
        orient_hot, orient_table, preferred_element_type=jnp.float32
    )
    embedded = (hidden_in.astype(jnp.float32) + embedding[:, None, :]).reshape(
        token_count, features
    )
    row_mean = jnp.mean(embedded, -1, keepdims=True)
    centred = embedded - row_mean
    row_var = jnp.mean(centred * centred, -1, keepdims=True)
    inv_std = lax.rsqrt(row_var + 1e-05)
    normed_hat = centred * inv_std
    gain_f32 = norm_gain.astype(jnp.float32)
    normed_low = (normed_hat * gain_f32 + norm_bias.astype(jnp.float32)).astype(jnp.bfloat16)
    projected = jnp.dot(normed_low, qkv_weight, preferred_element_type=jnp.float32).reshape(
        row_count, seg_length, 3 * features
    )
    positions = (lax.axis_index("seq") * seg_length + jnp.arange(seg_length)).astype(jnp.float32)
    cosine, sine_term = rope_tables(positions, features)
    queries = rotate(projected[..., :features], cosine, sine_term).astype(jnp.bfloat16)
    keys_rot = rotate(projected[..., features : 2 * features], cosine, sine_term).astype(
        jnp.bfloat16
    )
    values = projected[..., 2 * features :].astype(jnp.bfloat16)
    query_heads, key_heads, value_heads = (
        lax.all_to_all(queries, "seq", split_axis=2, concat_axis=1, tiled=True),
        lax.all_to_all(keys_rot, "seq", split_axis=2, concat_axis=1, tiled=True),
        lax.all_to_all(values, "seq", split_axis=2, concat_axis=1, tiled=True),
    )

    def scores_for(query_block, key_rows, block_start):
        logits = (
            jnp.einsum("qhd,khd->hqk", query_block, key_rows, preferred_element_type=jnp.float32)
            * score_scale
        )
        causal = (block_start + jnp.arange(block_rows))[:, None] >= jnp.arange(full_length)[None, :]
        return jnp.where(causal[None], logits, -1e30)

    def attend(row_args):
        query_row, key_row, value_row = row_args
        key_rows = key_row.reshape(full_length, local_heads, head_size)
        value_rows = value_row.reshape(full_length, local_heads, head_size)
        pieces = []
        log_parts = []
        for block_index in range(block_count):
            block_start = block_index * block_rows
            query_block = query_row[block_start : block_start + block_rows].reshape(
                block_rows, local_heads, head_size
            )
            logits = scores_for(query_block, key_rows, block_start)
            row_peak = jnp.max(logits, -1, keepdims=True)
            weights = jnp.exp(logits - row_peak)
            row_total = jnp.sum(weights, -1, keepdims=True)
            prob_low = (weights / row_total).astype(jnp.bfloat16)
            output_block = jnp.einsum(
                "hqk,khd->qhd", prob_low, value_rows, preferred_element_type=jnp.float32
            )
            pieces.append(output_block.reshape(block_rows, slab_width).astype(jnp.bfloat16))
            log_parts.append((row_peak + jnp.log(row_total))[..., 0])
        return (jnp.concatenate(pieces, 0), jnp.concatenate(log_parts, 1))

    attended_heads, log_sums = lax.map(attend, (query_heads, key_heads, value_heads))
    attended = jax.tree.map(
        lambda part, own: part.astype(own.dtype),
        lax.all_to_all(for_sending(attended_heads), "seq", split_axis=1, concat_axis=2, tiled=True),
        attended_heads,
    )
    attended_flat = attended.reshape(token_count, features)
    branch_attn = jnp.dot(attended_flat, out_weight, preferred_element_type=jnp.float32)
    up_pre = jnp.dot(normed_low, up_weight, preferred_element_type=jnp.float32) + up_bias.astype(
        jnp.float32
    )
    up_act = gelu_tanh(up_pre).astype(jnp.bfloat16)
    branch_feed = jnp.dot(
        up_act, down_weight, preferred_element_type=jnp.float32
    ) + down_bias.astype(jnp.float32)
    layer_out = (
        (embedded + branch_attn + branch_feed)
        .astype(jnp.bfloat16)
        .reshape(row_count, seg_length, features)
    )
    grad_low = cotangent.reshape(token_count, features)
    grad_f32 = grad_low.astype(jnp.float32)
    down_grad = jnp.einsum("nf,nd->fd", up_act, grad_low, preferred_element_type=jnp.float32)
    down_bias_grad = jnp.sum(grad_f32, 0)
    act_grad = jnp.einsum("nd,fd->nf", grad_low, down_weight, preferred_element_type=jnp.float32)
    gelu_out, gelu_pull = jax.vjp(gelu_tanh, up_pre)
    pre_grad = gelu_pull(act_grad)[0].astype(jnp.bfloat16)
    up_bias_grad = jnp.sum(pre_grad.astype(jnp.float32), 0)
    up_grad = jnp.einsum("nd,nf->df", normed_low, pre_grad, preferred_element_type=jnp.float32)
    normed_grad = jnp.einsum("nf,df->nd", pre_grad, up_weight, preferred_element_type=jnp.float32)
    out_grad = jnp.einsum("nd,ne->de", attended_flat, grad_low, preferred_element_type=jnp.float32)
    attended_grad = jnp.einsum(
        "ne,de->nd", grad_low, out_weight, preferred_element_type=jnp.float32
    )
    attended_grad = attended_grad.astype(jnp.bfloat16).reshape(row_count, seg_length, features)
    grad_heads = lax.all_to_all(attended_grad, "seq", split_axis=2, concat_axis=1, tiled=True)

    def attend_back(row_args):
        query_row, key_row, value_row, grad_row, log_row = row_args
        key_rows = key_row.reshape(full_length, local_heads, head_size)
        value_rows = value_row.reshape(full_length, local_heads, head_size)
        keys_total = jnp.zeros((full_length, local_heads, head_size), jnp.float32)
        values_total = jnp.zeros((full_length, local_heads, head_size), jnp.float32)
        query_parts = []
        for block_index in range(block_count):
            block_start = block_index * block_rows
            query_block = query_row[block_start : block_start + block_rows].reshape(
                block_rows, local_heads, head_size
            )
            grad_block = grad_row[block_start : block_start + block_rows].reshape(
                block_rows, local_heads, head_size
            )
            logits = scores_for(query_block, key_rows, block_start)
            probs_full = jnp.exp(logits - log_row[:, block_start : block_start + block_rows, None])
            prob_low = probs_full.astype(jnp.bfloat16)
            probs_grad = jnp.einsum(
                "qhd,khd->hqk", grad_block, value_rows, preferred_element_type=jnp.float32
            )
            inner_sum = jnp.sum(probs_full * probs_grad, -1, keepdims=True)
            scores_grad = (probs_full * (probs_grad - inner_sum)).astype(jnp.bfloat16)
            values_total = values_total + jnp.einsum(
                "hqk,qhd->khd", prob_low, grad_block, preferred_element_type=jnp.float32
            )
            query_grad = (
                jnp.einsum(
                    "hqk,khd->qhd", scores_grad, key_rows, preferred_element_type=jnp.float32
                )
                * score_scale
            )
            query_parts.append(query_grad.reshape(block_rows, slab_width).astype(jnp.bfloat16))
            keys_total = (
                keys_total
                + jnp.einsum(
                    "hqk,qhd->khd", scores_grad, query_block, preferred_element_type=jnp.float32
                )
                * score_scale
            )
        return (
            jnp.concatenate(query_parts, 0),
            keys_total.reshape(full_length, slab_width).astype(jnp.bfloat16),
            values_total.reshape(full_length, slab_width).astype(jnp.bfloat16),
        )

    query_grad_heads, key_grad_heads, value_grad_heads = lax.map(
        attend_back, (query_heads, key_heads, value_heads, grad_heads, log_sums)
    )
    query_grad_pos, key_grad_pos, value_grad_pos = (
        lax.all_to_all(
            for_sending(query_grad_heads), "seq", split_axis=1, concat_axis=2, tiled=True
        ).astype(query_grad_heads.dtype),
        lax.all_to_all(
            for_sending(key_grad_heads), "seq", split_axis=1, concat_axis=2, tiled=True
        ).astype(key_grad_heads.dtype),
        lax.all_to_all(
            for_sending(value_grad_heads), "seq", split_axis=1, concat_axis=2, tiled=True
        ).astype(value_grad_heads.dtype),
    )
    projected_grad = jnp.concatenate(
        [
            rotate_back(query_grad_pos.astype(jnp.float32), cosine, sine_term),
            rotate_back(key_grad_pos.astype(jnp.float32), cosine, sine_term),
            value_grad_pos.astype(jnp.float32),
        ],
        -1,
    )
    projected_grad = projected_grad.astype(jnp.bfloat16).reshape(token_count, 3 * features)
    qkv_grad = jnp.einsum(
        "nd,ne->de", normed_low, projected_grad, preferred_element_type=jnp.float32
    )
    normed_grad = normed_grad + jnp.einsum(
        "ne,de->nd", projected_grad, qkv_weight, preferred_element_type=jnp.float32
    )
    gain_grad = jnp.sum(normed_grad * normed_hat, 0)
    bias_grad = jnp.sum(normed_grad, 0)
    scaled_grad = normed_grad * gain_f32
    hat_grad = (
        scaled_grad
        - jnp.mean(scaled_grad, -1, keepdims=True)
        - normed_hat * jnp.mean(scaled_grad * normed_hat, -1, keepdims=True)
    )
    input_grad = (grad_f32 + inv_std * hat_grad).reshape(row_count, seg_length, features)
    row_sums = jnp.sum(input_grad, 1)
    family_grad = jnp.einsum(
        "rf,rd->fd", family_hot.astype(jnp.float32), row_sums, precision=lax.Precision.HIGHEST
    )
    orient_grad = jnp.einsum(
        "rf,rd->fd", orient_hot.astype(jnp.float32), row_sums, precision=lax.Precision.HIGHEST
    )
    gain_sum, bias_sum, up_bias_sum, down_bias_sum, family_sum, orient_sum = lax.psum(
        (gain_grad, bias_grad, up_bias_grad, down_bias_grad, family_grad, orient_grad),
        ("dp", "seq"),
    )
    qkv_sum, out_sum, up_sum, down_sum = (
        lax.psum_scatter(qkv_grad, ("dp", "seq"), scatter_dimension=0, tiled=True),
        lax.psum_scatter(out_grad, ("dp", "seq"), scatter_dimension=0, tiled=True),
        lax.psum_scatter(up_grad, ("dp", "seq"), scatter_dimension=0, tiled=True),
        lax.psum_scatter(down_grad, ("dp", "seq"), scatter_dimension=0, tiled=True),
    )
    return (
        layer_out,
        input_grad,
        gain_sum,
        bias_sum,
        qkv_sum,
        out_sum,
        up_sum,
        up_bias_sum,
        down_sum,
        down_bias_sum,
        family_sum,
        orient_sum,
    )


def dot_nn(a, b):
    return lax.dot_general(a, b, (((1,), (0,)), ((), ())), preferred_element_type=F32)


def dot_nt(a, b):
    return lax.dot_general(a, b, (((1,), (1,)), ((), ())), preferred_element_type=F32)


def dot_tn(a, b):
    return lax.dot_general(a, b, (((0,), (0,)), ((), ())), preferred_element_type=F32)


def params(**more):
    return pltpu.CompilerParams(vmem_limit_bytes=VMEM_LIMIT, **more)


def cost(flops, moved, exps=0):
    return pl.CostEstimate(flops=flops, bytes_accessed=moved, transcendentals=exps)


def whole(shape):
    return pl.BlockSpec(shape, lambda *_: (0,) * len(shape), pipeline_mode=pl.Buffered(1))


def table_row(table, wanted):
    rows = lax.broadcasted_iota(jnp.int32, table.shape, 0)
    return jnp.sum(jnp.where(rows == wanted, table[...].astype(F32), 0.0), 0, keepdims=True)


def normalise(entries):
    centred = entries - jnp.mean(entries, -1, keepdims=True)
    inv_std = lax.rsqrt(jnp.mean(centred * centred, -1, keepdims=True) + 1e-05)
    return centred * inv_std, inv_std


GELU_C = math.sqrt(2.0 / math.pi)


def gelu_both(z):
    square = z * z
    t = jnp.tanh(GELU_C * z * (1.0 + 0.044715 * square))
    half = 0.5 * (1.0 + t)
    slope = half + (0.5 * GELU_C) * z * (1.0 - t * t) * (1.0 + (3 * 0.044715) * square)
    return z * half, slope


def ffn_kernel(rows, ids, hid, cot, fam, ori, gain, bias, wup, bup, wdn, norm, act, pre, bupg, bdng):
    tokens = hid.shape[0]
    seg = tokens // rows
    step = 256

    @pl.when(pl.program_id(0) == 0)
    def _():
        total = jnp.zeros((1, cot.shape[1]), F32)
        for row in range(rows):
            emb = table_row(fam, ids[0]) + table_row(ori, ids[1 + row])
            for start in range(row * seg, (row + 1) * seg, step):
                part = pl.ds(start, step)
                hat, _ = normalise(hid[part, :].astype(F32) + emb)
                norm[part, :] = (hat * gain[...].astype(F32) + bias[...].astype(F32)).astype(BF16)
                total = total + jnp.sum(cot[part, :].astype(F32), 0, keepdims=True)
        bdng[...] = total

    total = jnp.zeros((1, wup.shape[1]), F32)
    for start in range(0, tokens, step):
        part = pl.ds(start, step)
        z = dot_nn(norm[part, :], wup[...]) + bup[...].astype(F32)
        into = dot_nt(cot[part, :], wdn[...])
        value, slope = gelu_both(z)
        act[part, :] = value.astype(BF16)
        low = (into * slope).astype(BF16)
        pre[part, :] = low
        total = total + jnp.sum(low.astype(F32), 0, keepdims=True)
    bupg[...] = total


def ffn_forward(ids, hid, cot, fam, ori, gain, bias, wup, bup, wdn, rows):
    tokens, d = hid.shape
    ff = wup.shape[1]
    tile = 512
    return pl.pallas_call(
        functools.partial(ffn_kernel, rows),
        grid_spec=pltpu.PrefetchScalarGridSpec(
            num_scalar_prefetch=1,
            grid=(ff // tile,),
            in_specs=[
                whole((tokens, d)),
                whole((tokens, d)),
                whole(fam.shape),
                whole(ori.shape),
                whole((1, d)),
                whole((1, d)),
                pl.BlockSpec((d, tile), lambda i, s: (0, i)),
                pl.BlockSpec((1, tile), lambda i, s: (0, i)),
                pl.BlockSpec((tile, d), lambda i, s: (i, 0)),
            ],
            out_specs=[
                whole((tokens, d)),
                pl.BlockSpec((tokens, tile), lambda i, s: (0, i)),
                pl.BlockSpec((tokens, tile), lambda i, s: (0, i)),
                pl.BlockSpec((1, tile), lambda i, s: (0, i)),
                whole((1, d)),
            ],
        ),
        out_shape=[
            jax.ShapeDtypeStruct((tokens, d), BF16),
            jax.ShapeDtypeStruct((tokens, ff), BF16),
            jax.ShapeDtypeStruct((tokens, ff), BF16),
            jax.ShapeDtypeStruct((1, ff), F32),
            jax.ShapeDtypeStruct((1, d), F32),
        ],
        compiler_params=params(),
        cost_estimate=cost(4 * tokens * d * ff, 4 * tokens * ff + 4 * d * ff, tokens * ff),
        name="ffn_forward",
    )(ids, hid, cot, fam, ori, gain, bias, wup, bup, wdn)


def turn(entries, cosine, sine):
    even = lax.broadcasted_iota(jnp.int32, entries.shape, 1) % 2 == 0
    other = jnp.where(even, pltpu.roll(entries, 127, 1), pltpu.roll(entries, 1, 1))
    return entries * cosine + other * sine


def turn_back(entries, cosine, sine):
    even = lax.broadcasted_iota(jnp.int32, entries.shape, 1) % 2 == 0
    side = entries * sine
    other = jnp.where(even, pltpu.roll(side, 127, 1), pltpu.roll(side, 1, 1))
    return entries * cosine + other


def qkv_kernel(tiles, ids, own, far, cown, cfar, fam, ori, gain, bias, wqkv, wout, cos, sin, norm, cot, qkv, datt):
    seg = own.shape[0]
    step = 256
    i = pl.program_id(0)
    me = ids[1]

    @pl.when(i == 0)
    def _():
        emb = table_row(fam, ids[0]) + table_row(ori, ids[2])
        for source, csource, where in ((own, cown, me), (far, cfar, 1 - me)):
            for start in range(0, seg, step):
                part = pl.ds(start, step)
                there = pl.ds(pl.multiple_of(where * seg + start, step), step)
                hat, _ = normalise(source[part, :].astype(F32) + emb)
                norm[there, :] = (hat * gain[...].astype(F32) + bias[...].astype(F32)).astype(BF16)
                cot[there, :] = csource[part, :]

    @pl.when(i < 2 * tiles)
    def _():
        for start in range(0, 2 * seg, step):
            part = pl.ds(start, step)
            lin = dot_nn(norm[part, :], wqkv[...])
            for lane in range(0, lin.shape[1], 128):
                piece = turn(lin[:, lane : lane + 128], cos[part, :], sin[part, :])
                qkv[part, lane : lane + 128] = piece.astype(BF16)

    @pl.when((i >= 2 * tiles) & (i < 3 * tiles))
    def _():
        for start in range(0, 2 * seg, step):
            part = pl.ds(start, step)
            qkv[part, :] = dot_nn(norm[part, :], wqkv[...]).astype(BF16)

    @pl.when(i >= 3 * tiles)
    def _():
        for start in range(0, 2 * seg, step):
            part = pl.ds(start, step)
            datt[part, :] = dot_nt(cot[part, :], wout[...]).astype(BF16)


def qkv_forward(ids, own, far, cown, cfar, fam, ori, gain, bias, wqkv, wout, cos, sin):
    seg, d = own.shape
    full = 2 * seg
    tile = 512
    tiles = d // tile
    return pl.pallas_call(
        functools.partial(qkv_kernel, tiles),
        grid_spec=pltpu.PrefetchScalarGridSpec(
            num_scalar_prefetch=1,
            grid=(4 * tiles,),
            in_specs=[
                whole((seg, d)),
                whole((seg, d)),
                whole((seg, d)),
                whole((seg, d)),
                whole(fam.shape),
                whole(ori.shape),
                whole((1, d)),
                whole((1, d)),
                pl.BlockSpec((d, tile), lambda i, s: (0, jnp.minimum(i, 3 * tiles - 1))),
                pl.BlockSpec((tile, d), lambda i, s: (jnp.maximum(i - 3 * tiles, 0), 0)),
                whole((full, 128)),
                whole((full, 128)),
            ],
            out_specs=[
                whole((full, d)),
                whole((full, d)),
                pl.BlockSpec((full, tile), lambda i, s: (0, jnp.minimum(i, 3 * tiles - 1))),
                pl.BlockSpec((full, tile), lambda i, s: (0, jnp.maximum(i - 3 * tiles, 0))),
            ],
        ),
        out_shape=[
            jax.ShapeDtypeStruct((full, d), BF16),
            jax.ShapeDtypeStruct((full, d), BF16),
            jax.ShapeDtypeStruct((full, 3 * d), BF16),
            jax.ShapeDtypeStruct((full, d), BF16),
        ],
        compiler_params=params(),
        cost_estimate=cost(8 * full * d * d, 8 * d * d + 18 * full * d),
        name="qkv_forward",
    )(ids, own, far, cown, cfar, fam, ori, gain, bias, wqkv, wout, cos, sin)


def attention_kernel(head_size, skipped, q_ref, k_ref, v_ref, g_ref, cos, sin, *rest):
    o_ref, dq_ref, dk_ref, dv_ref, dkt, dvt = rest[skipped:]
    full = q_ref.shape[0]
    block = 256
    scale = head_size ** (-0.5)
    lane = lax.broadcasted_iota(jnp.int32, (block, 128), 1)
    below = lax.broadcasted_iota(jnp.int32, (block, block), 0) >= lax.broadcasted_iota(
        jnp.int32, (block, block), 1
    )
    dkt[...] = jnp.zeros_like(dkt)
    dvt[...] = jnp.zeros_like(dvt)
    for start in range(0, full, block):
        part = pl.ds(start, block)
        end = start + block
        query = q_ref[part, :]
        grad = g_ref[part, :]
        out = None
        dq = None
        for head in range(128 // head_size):
            mine = (lane >= head * head_size) & (lane < (head + 1) * head_size)
            qm = jnp.where(mine, query.astype(F32) * scale, 0.0).astype(BF16)
            gm = jnp.where(mine, grad.astype(F32), 0.0).astype(BF16)
            scores = dot_nt(qm, k_ref[0:end, :])
            last = jnp.where(below, scores[:, start:end], -1e30)
            scores = last if start == 0 else jnp.concatenate([scores[:, :start], last], 1)
            weights = jnp.exp(scores - jnp.max(scores, -1, keepdims=True))
            probs = weights * (1.0 / jnp.sum(weights, -1, keepdims=True))
            low = probs.astype(BF16)
            piece = dot_nn(low, v_ref[0:end, :])
            out = piece if out is None else jnp.where(mine, piece, out)
            pg = dot_nt(gm, v_ref[0:end, :])
            inner = jnp.sum(probs * pg, -1, keepdims=True)
            sg = (probs * (pg - inner)).astype(BF16)
            piece = dot_nn(sg, k_ref[0:end, :])
            dq = piece if dq is None else jnp.where(mine, piece, dq)
            dkt[:, 0:end] += dot_tn(qm, sg)
            dvt[:, 0:end] += dot_tn(gm, low)
        o_ref[part, :] = out.astype(BF16)
        dq_ref[part, :] = turn_back(dq * scale, cos[part, :], sin[part, :]).astype(BF16)
    for start in range(0, full, block):
        part = pl.ds(start, block)
        dk = dkt[:, start : start + block].T
        dk_ref[part, :] = turn_back(dk, cos[part, :], sin[part, :]).astype(BF16)
        dv_ref[part, :] = dvt[:, start : start + block].T.astype(BF16)


def attention(qkv, datt, cos, sin, head_size, part, parts, before):
    full, d = datt.shape
    pairs = d // 128
    count = pairs // parts
    first = part * count
    shape = jax.ShapeDtypeStruct((full, d), BF16)
    spec = pl.BlockSpec((full, 128), lambda i: (0, first + i))
    anywhere = pl.BlockSpec(memory_space=pl.ANY)
    return pl.pallas_call(
        functools.partial(attention_kernel, head_size, len(before)),
        grid=(count,),
        in_specs=[
            spec,
            pl.BlockSpec((full, 128), lambda i: (0, pairs + first + i)),
            pl.BlockSpec((full, 128), lambda i: (0, 2 * pairs + first + i)),
            spec,
            whole((full, 128)),
            whole((full, 128)),
        ]
        + [anywhere] * len(before),
        out_specs=[spec] * 4,
        out_shape=[shape] * 4,
        scratch_shapes=[pltpu.VMEM((128, full), F32), pltpu.VMEM((128, full), F32)],
        input_output_aliases={6 + index: index for index in range(len(before))},
        compiler_params=params(),
        cost_estimate=cost(12 * full * full * d * 2 // parts, 16 * full * d // parts, full * full * H // parts),
        name="attention",
    )(qkv, qkv, qkv, datt, cos, sin, *before)


def device_bits(bits):
    dp = lax.axis_index("dp")
    found = {bit: lax.rem(dp // (1 << bit), 2) for bit in range(bits)}
    found["seq"] = lax.axis_index("seq")
    return found


def block_place(axes, mine, upper, seq):
    place = 0
    for axis in axes:
        bit = seq if axis == "seq" else (upper >> (axis - 1)) & 1
        place = 2 * place + (1 - mine[axis] if bit else mine[axis])
    return place


def other_core():
    dp = lax.axis_index("dp")
    return (dp + 1 - 2 * lax.rem(dp, 2), lax.axis_index("seq"))


def meet(partners):
    barrier = pltpu.get_barrier_semaphore()
    for partner in partners:
        pl.semaphore_signal(barrier, inc=1, device_id=partner, device_id_type=MESH)
    pl.semaphore_wait(barrier, len(partners))


def remote(src, dst, send_sem, recv_sem, partner):
    return pltpu.make_async_remote_copy(
        src_ref=src,
        dst_ref=dst,
        send_sem=send_sem,
        recv_sem=recv_sem,
        device_id=partner,
        device_id_type=MESH,
    )


def split_blocks(value, keep, send, size, core, places):
    for index, there in enumerate(places):
        up, seq = index // 2, index % 2
        first = (4 * up + seq) * size
        second = first + 2 * size
        a = value[first : first + size, :].astype(BF16)
        b = value[second : second + size, :].astype(BF16)
        keep[there] = jnp.where(core == 0, a, b)
        send[there] = jnp.where(core == 0, b, a)


def add_into(keep, got):
    for index in range(keep.shape[0]):
        keep[index] = (keep[index].astype(F32) + got[index].astype(F32)).astype(BF16)


def wide_grad_kernel(bits, axes, counts, firsts, *refs):
    lefts, rights = refs[: len(counts)], refs[len(counts) : 2 * len(counts)]
    near_out, far_out, turned, keep, send, got, send_sem, recv_sem, out_sem = refs[2 * len(counts) :]
    steps = sum(counts)
    i = pl.program_id(0)
    mine = device_bits(bits)
    partner = other_core()
    blocks = keep.shape[1]
    size = keep.shape[2]
    tile = keep.shape[3]
    places = [block_place(axes, mine, up, seq) for up in range(blocks // 2) for seq in range(2)]

    def crossing(step):
        return remote(send.at[step], got.at[step], send_sem.at[step], recv_sem.at[step], partner)

    def stores(step):
        columns = pl.ds(pl.multiple_of(step * tile, tile), tile)
        half = blocks // 2
        return (
            pltpu.make_async_copy(
                keep.at[step, pl.ds(0, half)], near_out.at[:, :, columns], out_sem.at[0, step]
            ),
            pltpu.make_async_copy(
                keep.at[step, pl.ds(half, half)], far_out.at[:, :, columns], out_sem.at[1, step]
            ),
        )

    @pl.when(i == 0)
    def _():
        meet([partner])

    start = 0
    for left, right, count, first in zip(lefts, rights, counts, firsts):
        if first:

            @pl.when(i == start)
            def _():
                turned[...] = left[...].T

        @pl.when((i >= start) & (i < start + count))
        def _():
            value = dot_nn(turned[...], right[...])
            split_blocks(value, keep.at[i], send.at[i], size, mine[0], places)
            crossing(i).start()

        start += count

    def finish(step):
        crossing(step).wait()
        add_into(keep.at[step], got.at[step])
        for copy in stores(step):
            copy.start()

    @pl.when(i > 0)
    def _():
        finish(i - 1)

    @pl.when(i == steps - 1)
    def _():
        finish(i)
        for step in range(steps):
            for copy in stores(step):
                copy.wait()


def wide_grad(axes, pairs, tile, collective):
    tokens, d = pairs[0][0].shape
    bits = len(axes)
    blocks = 1 << bits
    size = d // (2 * blocks)
    counts = [right.shape[1] // tile for _, right in pairs]
    firsts = [index == 0 or pairs[index][0] is not pairs[index - 1][0] for index in range(len(pairs))]
    steps = sum(counts)
    specs = []
    start = 0
    for count in counts:
        specs.append(
            pl.BlockSpec(
                (tokens, tile),
                functools.partial(lambda first, last, i: (0, jnp.clip(i - first, 0, last)), start, count - 1),
            )
        )
        start += count
    shape = jax.ShapeDtypeStruct((blocks // 2, size, steps * tile), BF16)
    anywhere = pl.BlockSpec(memory_space=pl.ANY)
    buffers = pltpu.VMEM((steps, blocks, size, tile), BF16)
    return pl.pallas_call(
        functools.partial(wide_grad_kernel, bits, axes, counts, firsts),
        grid=(steps,),
        in_specs=[whole((tokens, d)) for _ in pairs] + specs,
        out_specs=[anywhere, anywhere],
        out_shape=[shape, shape],
        scratch_shapes=[
            pltpu.VMEM((d, tokens), BF16),
            buffers,
            buffers,
            buffers,
            pltpu.SemaphoreType.DMA((steps,)),
            pltpu.SemaphoreType.DMA((steps,)),
            pltpu.SemaphoreType.DMA((2, steps)),
        ],
        compiler_params=params(collective_id=collective, has_side_effects=True),
        cost_estimate=cost(2 * tokens * d * steps * tile, 4 * tokens * (d + steps * tile)),
        name="wide_grad",
    )(*[left for left, _ in pairs], *[right for _, right in pairs])


def tall_grad_kernel(bits, axes, left, right, near_out, far_out, keep, send, got, send_sem, recv_sem, out_sem):
    i = pl.program_id(0)
    steps = keep.shape[0]
    size = keep.shape[2]
    mine = device_bits(bits)
    partner = other_core()
    half = steps

    def crossing(step):
        return remote(send.at[step], got.at[step], send_sem.at[step], recv_sem.at[step], partner)

    def store(step, seq, act):
        place = 0
        for axis in axes:
            if axis == "seq":
                apart = lax.rem(mine["seq"] + seq, 2)
            else:
                apart = lax.rem(step // (1 << (axis - 1)) + mine[axis], 2)
            place = 2 * place + apart
        source = keep.at[step, seq]

        @pl.when(place < half)
        def _():
            act(pltpu.make_async_copy(source, near_out.at[lax.rem(place, half)], out_sem.at[step, seq]))

        @pl.when(place >= half)
        def _():
            act(pltpu.make_async_copy(source, far_out.at[lax.rem(place, half)], out_sem.at[step, seq]))

    @pl.when(i == 0)
    def _():
        meet([partner])

    value = dot_nn(left[...].T, right[...])
    split_blocks(value, keep.at[i], send.at[i], size, mine[0], [0, 1])
    crossing(i).start()

    def finish(step):
        crossing(step).wait()
        add_into(keep.at[step], got.at[step])
        for seq in range(2):
            store(step, seq, lambda copy: copy.start())

    @pl.when(i > 0)
    def _():
        finish(i - 1)

    @pl.when(i == steps - 1)
    def _():
        finish(i)
        for step in range(steps):
            for seq in range(2):
                store(step, seq, lambda copy: copy.wait())


def tall_grad(axes, left, right, collective):
    tokens, m = left.shape
    d = right.shape[1]
    bits = len(axes)
    steps = 1 << (bits - 1)
    tile = m // steps
    size = tile // 4
    shape = jax.ShapeDtypeStruct((steps, size, d), BF16)
    anywhere = pl.BlockSpec(memory_space=pl.ANY)
    buffers = pltpu.VMEM((steps, 2, size, d), BF16)
    return pl.pallas_call(
        functools.partial(tall_grad_kernel, bits, axes),
        grid=(steps,),
        in_specs=[pl.BlockSpec((tokens, tile), lambda i: (0, i)), whole((tokens, d))],
        out_specs=[anywhere, anywhere],
        out_shape=[shape, shape],
        scratch_shapes=[
            buffers,
            buffers,
            buffers,
            pltpu.SemaphoreType.DMA((steps,)),
            pltpu.SemaphoreType.DMA((steps,)),
            pltpu.SemaphoreType.DMA((steps, 2)),
        ],
        compiler_params=params(collective_id=collective, has_side_effects=True),
        cost_estimate=cost(2 * tokens * d * m, 2 * (tokens * m + d * m + tokens * d)),
        name="tall_grad",
    )(left, right)


class Halving:
    def __init__(self, axes, keep, send):
        self.axes = axes[1:]
        self.keep = keep
        self.got = self.swap(send, axes[0])

    def swap(self, part, axis):
        if axis == "seq":
            return lax.ppermute(part, "seq", [(0, 1), (1, 0)])
        count = lax.axis_size("dp")
        return lax.ppermute(part, "dp", [(i, i ^ (1 << axis)) for i in range(count)])

    def step(self):
        axis, self.axes = self.axes[0], self.axes[1:]
        half = self.keep.shape[0] // 2
        send = self.keep[half:].astype(F32) + self.got[half:].astype(F32)
        keep = self.keep[:half].astype(F32) + self.got[:half].astype(F32)
        send = send.astype(BF16)
        self.keep = keep if half == 1 else keep.astype(BF16)
        self.got = self.swap(send, axis)
        return send

    def total(self):
        return self.keep[0] + self.got[0].astype(F32)


def after(entry, *others):
    return lax.optimization_barrier((entry, *others))[0]


def back_kernel(dq, dk, dv, w, out):
    d = dq.shape[1]
    total = dot_nt(dq[...], w[:, 0:d])
    total = total + dot_nt(dk[...], w[:, d : 2 * d])
    total = total + dot_nt(dv[...], w[:, 2 * d : 3 * d])
    out[...] = total.astype(BF16)


def project_back(dq, dk, dv, w):
    tokens, d = dq.shape
    step = 256
    spec = pl.BlockSpec((step, d), lambda i: (i, 0))
    return pl.pallas_call(
        back_kernel,
        grid=(tokens // step,),
        in_specs=[spec, spec, spec, whole(w.shape)],
        out_specs=spec,
        out_shape=jax.ShapeDtypeStruct((tokens, d), BF16),
        compiler_params=params(),
        cost_estimate=cost(6 * tokens * d * d, 6 * d * d + 8 * tokens * d),
        name="project_back",
    )(dq, dk, dv, w)


def out_kernel(per_row, ids, hid, fam, ori, act, wdn, own, far, wout, bdn, out):
    row = pl.program_id(0) // per_row
    emb = table_row(fam, ids[0]) + table_row(ori, ids[2 + row])
    att = jnp.where(row == ids[1], own[...], far[...])
    total = hid[...].astype(F32) + emb + dot_nn(att, wout[...])
    total = total + (dot_nn(act[...], wdn[...]) + bdn[...].astype(F32))
    out[...] = total.astype(BF16)


def input_kernel(per_row, ids, hid, fam, ori, pre, wup, own, far, gain, cot, out, gg, bg, rg):
    i = pl.program_id(0)
    row = i // per_row
    emb = table_row(fam, ids[0]) + table_row(ori, ids[2 + row])
    hat, inv_std = normalise(hid[...].astype(F32) + emb)
    grad = dot_nt(pre[...], wup[...]) + jnp.where(row == ids[1], own[...], far[...]).astype(F32)

    @pl.when(i == 0)
    def _():
        gg[...] = jnp.zeros_like(gg)
        bg[...] = jnp.zeros_like(bg)
        rg[...] = jnp.zeros_like(rg)

    gg[...] += jnp.sum(grad * hat, 0, keepdims=True)
    bg[...] += jnp.sum(grad, 0, keepdims=True)
    scaled = grad * gain[...].astype(F32)
    inner = (
        scaled
        - jnp.mean(scaled, -1, keepdims=True)
        - hat * jnp.mean(scaled * hat, -1, keepdims=True)
    )
    result = cot[...].astype(F32) + inv_std * inner
    out[...] = result
    sums = jnp.sum(result, 0, keepdims=True)
    rows = lax.broadcasted_iota(jnp.int32, rg.shape, 0)
    rg[...] += jnp.where(rows == row, sums, 0.0)


def home_specs(tokens, d, rows, step):
    per_row = tokens // rows // step
    local = pl.BlockSpec((step, d), lambda i, s: (i, 0))
    own = pl.BlockSpec((step, d), lambda i, s: (s[1] * per_row + i % per_row, 0))
    far = pl.BlockSpec((step, d), lambda i, s: (i % per_row, 0))
    return per_row, local, own, far


def layer_output(ids, hid, fam, ori, act, wdn, own, far, wout, bdn, rows):
    tokens, d = hid.shape
    ff = act.shape[1]
    step = 256
    per_row, local, own_spec, far_spec = home_specs(tokens, d, rows, step)
    return pl.pallas_call(
        functools.partial(out_kernel, per_row),
        grid_spec=pltpu.PrefetchScalarGridSpec(
            num_scalar_prefetch=1,
            grid=(tokens // step,),
            in_specs=[
                local,
                whole(fam.shape),
                whole(ori.shape),
                pl.BlockSpec((step, ff), lambda i, s: (i, 0)),
                whole(wdn.shape),
                own_spec,
                far_spec,
                whole(wout.shape),
                whole((1, d)),
            ],
            out_specs=local,
        ),
        out_shape=jax.ShapeDtypeStruct((tokens, d), BF16),
        compiler_params=params(),
        cost_estimate=cost(2 * tokens * d * (ff + d), 2 * (d * (ff + d) + tokens * ff + 4 * tokens * d)),
        name="layer_output",
    )(ids, hid, fam, ori, act, wdn, own, far, wout, bdn)


def input_gradient(ids, hid, fam, ori, pre, wup, own, far, gain, cot, rows):
    tokens, d = hid.shape
    ff = pre.shape[1]
    step = 256
    per_row, local, own_spec, far_spec = home_specs(tokens, d, rows, step)
    return pl.pallas_call(
        functools.partial(input_kernel, per_row),
        grid_spec=pltpu.PrefetchScalarGridSpec(
            num_scalar_prefetch=1,
            grid=(tokens // step,),
            in_specs=[
                local,
                whole(fam.shape),
                whole(ori.shape),
                pl.BlockSpec((step, ff), lambda i, s: (i, 0)),
                whole(wup.shape),
                own_spec,
                far_spec,
                whole((1, d)),
                local,
            ],
            out_specs=[local, whole((1, d)), whole((1, d)), whole((rows, d))],
        ),
        out_shape=[
            jax.ShapeDtypeStruct((tokens, d), F32),
            jax.ShapeDtypeStruct((1, d), F32),
            jax.ShapeDtypeStruct((1, d), F32),
            jax.ShapeDtypeStruct((rows, d), F32),
        ],
        compiler_params=params(),
        cost_estimate=cost(2 * tokens * d * ff, 2 * (d * ff + tokens * ff + 6 * tokens * d)),
        name="input_gradient",
    )(ids, hid, fam, ori, pre, wup, own, far, gain, cot)


def sums_kernel(bits, sums_ref, vec_ref, sums_out, all_out, held, got, vgot, send_sem, recv_sem, gsend, grecv):
    dp = lax.axis_index("dp")
    seq = lax.axis_index("seq")
    partners = [(dp, 1 - seq)]
    for bit in range(bits):
        size = 1 << bit
        partners.append((dp + (1 - 2 * lax.rem(dp // size, 2)) * size, seq))
    barrier = pltpu.get_barrier_semaphore()
    for partner in partners:
        pl.semaphore_signal(barrier, inc=1, device_id=partner, device_id_type=MESH)
    pl.semaphore_wait(barrier, len(partners))

    def remote(src, dst, send, recv, partner):
        copy = pltpu.make_async_remote_copy(
            src_ref=src, dst_ref=dst, send_sem=send, recv_sem=recv, device_id=partner, device_id_type=MESH
        )
        copy.start()
        return copy

    for index, partner in enumerate(partners):
        source = sums_ref if index == 0 else held.at[index]
        main = remote(source, got.at[index], send_sem.at[index], recv_sem.at[index], partner)
        if index == 0:
            side = remote(vec_ref, vgot, gsend.at[0], grecv.at[0], partner)
        else:
            size = 1 << (index - 1)
            held_now = pl.ds(dp - lax.rem(dp, size), size)
            side = remote(
                all_out.at[held_now], all_out.at[held_now], gsend.at[index], grecv.at[index], partner
            )
        main.wait()
        total = source[...] + got[index]
        if index + 1 < len(partners):
            held[index + 1] = total
        else:
            sums_out[...] = total
        side.wait()
        if index == 0:
            all_out[dp] = vec_ref[...] + vgot[...]


def sum_small(sums, vec):
    count = lax.axis_size("dp")
    bits = int(math.log2(count))
    rounds = bits + 1
    return pl.pallas_call(
        functools.partial(sums_kernel, bits),
        in_specs=[pl.BlockSpec(memory_space=pltpu.VMEM)] * 2,
        out_specs=[pl.BlockSpec(memory_space=pltpu.VMEM)] * 2,
        out_shape=[
            jax.ShapeDtypeStruct(sums.shape, F32),
            jax.ShapeDtypeStruct((count,) + vec.shape, F32),
        ],
        scratch_shapes=[
            pltpu.VMEM((rounds,) + sums.shape, F32),
            pltpu.VMEM((rounds,) + sums.shape, F32),
            pltpu.VMEM(vec.shape, F32),
            pltpu.SemaphoreType.DMA((rounds,)),
            pltpu.SemaphoreType.DMA((rounds,)),
            pltpu.SemaphoreType.DMA((rounds,)),
            pltpu.SemaphoreType.DMA((rounds,)),
        ],
        compiler_params=pltpu.CompilerParams(collective_id=0, has_side_effects=True),
        name="sum_small",
    )(sums, vec)


def body_by_rows(
    hidden_in,
    family,
    orient,
    norm_gain,
    norm_bias,
    qkv_weight,
    out_weight,
    up_weight,
    up_bias,
    down_weight,
    down_bias,
    family_table,
    orient_table,
    cotangent,
):
    rows, seg, d = hidden_in.shape
    ff = up_weight.shape[1]
    tokens = rows * seg
    full = 2 * seg
    dp_count = lax.axis_size("dp")
    bits = int(math.log2(dp_count))
    upper = dp_count // 2
    dp = lax.axis_index("dp")
    seq = lax.axis_index("seq")
    ring = [(0, 1), (1, 0)]

    def mine(pair):
        return lax.dynamic_index_in_dim(pair, seq, 0, keepdims=False)

    def theirs(pair):
        return lax.dynamic_index_in_dim(pair, 1 - seq, 0, keepdims=False)

    far_hidden = lax.ppermute(theirs(hidden_in), "seq", ring)
    far_cot = lax.ppermute(theirs(cotangent), "seq", ring)

    gain = norm_gain.reshape(1, d)
    bias = norm_bias.reshape(1, d)
    hid = hidden_in.reshape(tokens, d)
    cot = cotangent.reshape(tokens, d)
    ids = jnp.concatenate([family, orient])
    tail_ids = jnp.concatenate([family, seq[None].astype(jnp.int32), orient])
    row_ids = jnp.stack([family[0], seq.astype(jnp.int32), mine(orient)])

    zs = list(range(2, bits))
    order_a = [1] + zs + ["seq"]
    order_b = ["seq", 1] + zs
    order_c = [2, 1] + zs[1:] + ["seq"]

    normed, act, pre, up_bias_part, down_bias_part = ffn_forward(
        ids, hid, cot, family_table, orient_table, gain, bias, up_weight, up_bias.reshape(1, ff), down_weight, rows
    )
    up = Halving(order_a, *wide_grad(order_a, [(after(normed, far_hidden), pre)], 1024, 1))
    down = Halving(order_b, *tall_grad(order_b, after(act, up.keep, far_cot), cot, 2))

    cosine, sine = rope_tables(jnp.arange(full).astype(F32), 128)
    row_normed, row_cot, qkv, datt = qkv_forward(
        row_ids,
        mine(hidden_in),
        after(far_hidden, down.keep),
        mine(cotangent),
        far_cot,
        family_table,
        orient_table,
        gain,
        bias,
        qkv_weight,
        out_weight,
        cosine,
        sine,
    )
    parts = 4
    done = ()
    tied = (up.keep,)
    for part in range(parts):
        done = attention(qkv, after(datt, *tied), cosine, sine, d // H, part, parts, done)
        if part == 1:
            tied = (up.step(),)
        if part == 2:
            tied = (down.step(),)
    att, dq, dk, dv = done
    far_att = lax.ppermute(theirs(att.reshape(2, seg, d)), "seq", ring)
    first = Halving(order_a, *wide_grad(order_a, [(row_normed, dq), (row_normed, dk)], 1024, 3))
    tied = (up.step(), down.step(), first.keep)
    second = Halving(order_c, *wide_grad(order_c, [(row_normed, after(dv, *tied)), (att, row_cot)], 1024, 4))
    tied = (second.keep,)
    back = project_back(after(dq, *tied), dk, dv, qkv_weight)
    far_back = lax.ppermute(theirs(back.reshape(2, seg, d)), "seq", ring)
    tied = ()
    layer_out = layer_output(
        tail_ids,
        hid,
        family_table,
        orient_table,
        after(act, back, *tied),
        down_weight,
        att,
        far_att,
        out_weight,
        down_bias.reshape(1, d),
        rows,
    )
    tied = (up.step(), down.step(), first.step(), second.step())
    input_grad, gain_part, bias_part, row_part = input_gradient(
        tail_ids, hid, family_table, orient_table, after(pre, layer_out, *tied), up_weight, back, far_back, gain, cot, rows
    )
    for chunk in (first, second, up, down):
        while chunk.axes:
            chunk.step()
    up_total, down_total, first_total, second_total = up.total(), down.total(), first.total(), second.total()

    flag = orient[0]
    by_flag = jnp.where(flag == 0, row_part, row_part[::-1])
    packed = jnp.concatenate(
        [
            part.reshape(-1, 128)
            for part in (up_bias_part, down_bias_part, gain_part, bias_part, by_flag)
        ],
        0,
    )
    vec = jnp.concatenate(
        [
            (row_part[0] + row_part[1]).reshape(-1, 128),
            jnp.full((8, 128), 0.5, F32) * family.astype(F32)[0],
        ],
        0,
    )
    sums, gathered = sum_small(packed, vec)
    flat = sums.reshape(-1)
    up_bias_sum = flat[:ff]
    down_bias_sum, gain_sum, bias_sum = flat[ff : ff + 3 * d].reshape(3, d)
    orient_sum = flat[ff + 3 * d :].reshape(2, d)
    families = family_table.shape[0]
    hot = gathered[:, -1, 0].astype(jnp.int32)[None, :] == jnp.arange(families)[:, None]
    family_sum = jnp.dot(
        hot.astype(F32), gathered[:, :-8].reshape(dp_count, d), precision=lax.Precision.HIGHEST
    )
    return (
        layer_out.reshape(rows, seg, d),
        input_grad.reshape(rows, seg, d),
        gain_sum,
        bias_sum,
        jnp.concatenate([first_total, second_total[:, :d]], 1),
        second_total[:, d:],
        up_total,
        up_bias_sum,
        down_total,
        down_bias_sum,
        family_sum,
        orient_sum,
    )


def body(*args):
    hidden_in = args[0]
    dp_count = lax.axis_size("dp")
    two_rows = lax.axis_size("seq") == 2 and hidden_in.shape[0] == 2
    if two_rows and dp_count >= 4 and dp_count & (dp_count - 1) == 0:
        return body_by_rows(*args)
    return body_by_heads(*args)


def solution(mesh):
    return jax.shard_map(
        body,
        mesh=mesh,
        in_specs=(
            P("dp", "seq", None),
            P("dp"),
            P("dp"),
            P(),
            P(),
            P(),
            P(),
            P(),
            P(),
            P(),
            P(),
            P(),
            P(),
            P("dp", "seq", None),
        ),
        out_specs=(
            P("dp", "seq", None),
            P("dp", "seq", None),
            P(),
            P(),
            P(("dp", "seq"), None),
            P(("dp", "seq"), None),
            P(("dp", "seq"), None),
            P(),
            P(("dp", "seq"), None),
            P(),
            P(),
            P(),
        ),
        check_vma=False,
    )
```

```python
import functools
import math

import jax
import jax.numpy as jnp
from jax import lax
from jax.experimental import pallas as pl
from jax.experimental.pallas import tpu as pltpu
from jax.sharding import PartitionSpec as P

H = 16
HD = 64
ROT = 32
MESH = pl.DeviceIdType.MESH
VMEM_LIMIT = 60 * 1024 * 1024
F32 = jnp.float32
BF16 = jnp.bfloat16


def for_sending(shard):

    def short(part):
        return part.astype(jnp.bfloat16) if part.dtype == jnp.float32 else part

    return jax.tree.map(short, shard)


def rope_tables(positions, features):
    column = jnp.arange(features, dtype=jnp.int32)
    within = column % HD
    frequency = jnp.exp(-(2.0 * (within // 2).astype(jnp.float32) / ROT) * math.log(10000.0))
    angles = positions[:, None] * frequency[None, :]
    rotary = within < ROT
    cosine = jnp.where(rotary[None, :], jnp.cos(angles), 1.0)
    sign_term = jnp.where(within % 2 == 0, -1.0, 1.0)
    sine_term = jnp.where(rotary[None, :], sign_term[None, :] * jnp.sin(angles), 0.0)
    return (cosine, sine_term)


def pair_swap(values):
    even_cols = jnp.arange(values.shape[-1]) % 2 == 0
    return jnp.where(even_cols, jnp.roll(values, -1, axis=-1), jnp.roll(values, 1, axis=-1))


def rotate(values, cosine, sine_term):
    return values * cosine + pair_swap(values) * sine_term


def rotate_back(values, cosine, sine_term):
    return values * cosine + pair_swap(values * sine_term)


def gelu_tanh(pre_values):
    return jax.nn.gelu(pre_values, approximate=True)


def body_by_heads(
    hidden_in,
    family,
    orient,
    norm_gain,
    norm_bias,
    qkv_weight,
    out_weight,
    up_weight,
    up_bias,
    down_weight,
    down_bias,
    family_table,
    orient_table,
    cotangent,
):
    seq_count = lax.axis_size("seq")
    row_count, seg_length, features = hidden_in.shape
    full_length = seg_length * seq_count
    local_heads = H // seq_count
    head_size = features // H
    slab_width = features // seq_count
    block_rows = min(512, full_length)
    block_count = full_length // block_rows
    score_scale = head_size ** (-0.5)
    token_count = row_count * seg_length
    family_rows = jnp.repeat(family, 2)
    family_hot = (family_rows[:, None] == jnp.arange(family_table.shape[0])[None, :]).astype(
        jnp.bfloat16
    )
    orient_hot = (orient[:, None] == jnp.arange(2)[None, :]).astype(jnp.bfloat16)
    embedding = jnp.dot(family_hot, family_table, preferred_element_type=jnp.float32) + jnp.dot(
        orient_hot, orient_table, preferred_element_type=jnp.float32
    )
    embedded = (hidden_in.astype(jnp.float32) + embedding[:, None, :]).reshape(
        token_count, features
    )
    row_mean = jnp.mean(embedded, -1, keepdims=True)
    centred = embedded - row_mean
    row_var = jnp.mean(centred * centred, -1, keepdims=True)
    inv_std = lax.rsqrt(row_var + 1e-05)
    normed_hat = centred * inv_std
    gain_f32 = norm_gain.astype(jnp.float32)
    normed_low = (normed_hat * gain_f32 + norm_bias.astype(jnp.float32)).astype(jnp.bfloat16)
    projected = jnp.dot(normed_low, qkv_weight, preferred_element_type=jnp.float32).reshape(
        row_count, seg_length, 3 * features
    )
    positions = (lax.axis_index("seq") * seg_length + jnp.arange(seg_length)).astype(jnp.float32)
    cosine, sine_term = rope_tables(positions, features)
    queries = rotate(projected[..., :features], cosine, sine_term).astype(jnp.bfloat16)
    keys_rot = rotate(projected[..., features : 2 * features], cosine, sine_term).astype(
        jnp.bfloat16
    )
    values = projected[..., 2 * features :].astype(jnp.bfloat16)
    query_heads, key_heads, value_heads = (
        lax.all_to_all(queries, "seq", split_axis=2, concat_axis=1, tiled=True),
        lax.all_to_all(keys_rot, "seq", split_axis=2, concat_axis=1, tiled=True),
        lax.all_to_all(values, "seq", split_axis=2, concat_axis=1, tiled=True),
    )

    def scores_for(query_block, key_rows, block_start):
        logits = (
            jnp.einsum("qhd,khd->hqk", query_block, key_rows, preferred_element_type=jnp.float32)
            * score_scale
        )
        causal = (block_start + jnp.arange(block_rows))[:, None] >= jnp.arange(full_length)[None, :]
        return jnp.where(causal[None], logits, -1e30)

    def attend(row_args):
        query_row, key_row, value_row = row_args
        key_rows = key_row.reshape(full_length, local_heads, head_size)
        value_rows = value_row.reshape(full_length, local_heads, head_size)
        pieces = []
        log_parts = []
        for block_index in range(block_count):
            block_start = block_index * block_rows
            query_block = query_row[block_start : block_start + block_rows].reshape(
                block_rows, local_heads, head_size
            )
            logits = scores_for(query_block, key_rows, block_start)
            row_peak = jnp.max(logits, -1, keepdims=True)
            weights = jnp.exp(logits - row_peak)
            row_total = jnp.sum(weights, -1, keepdims=True)
            prob_low = (weights / row_total).astype(jnp.bfloat16)
            output_block = jnp.einsum(
                "hqk,khd->qhd", prob_low, value_rows, preferred_element_type=jnp.float32
            )
            pieces.append(output_block.reshape(block_rows, slab_width).astype(jnp.bfloat16))
            log_parts.append((row_peak + jnp.log(row_total))[..., 0])
        return (jnp.concatenate(pieces, 0), jnp.concatenate(log_parts, 1))

    attended_heads, log_sums = lax.map(attend, (query_heads, key_heads, value_heads))
    attended = jax.tree.map(
        lambda part, own: part.astype(own.dtype),
        lax.all_to_all(for_sending(attended_heads), "seq", split_axis=1, concat_axis=2, tiled=True),
        attended_heads,
    )
    attended_flat = attended.reshape(token_count, features)
    branch_attn = jnp.dot(attended_flat, out_weight, preferred_element_type=jnp.float32)
    up_pre = jnp.dot(normed_low, up_weight, preferred_element_type=jnp.float32) + up_bias.astype(
        jnp.float32
    )
    up_act = gelu_tanh(up_pre).astype(jnp.bfloat16)
    branch_feed = jnp.dot(
        up_act, down_weight, preferred_element_type=jnp.float32
    ) + down_bias.astype(jnp.float32)
    layer_out = (
        (embedded + branch_attn + branch_feed)
        .astype(jnp.bfloat16)
        .reshape(row_count, seg_length, features)
    )
    grad_low = cotangent.reshape(token_count, features)
    grad_f32 = grad_low.astype(jnp.float32)
    down_grad = jnp.einsum("nf,nd->fd", up_act, grad_low, preferred_element_type=jnp.float32)
    down_bias_grad = jnp.sum(grad_f32, 0)
    act_grad = jnp.einsum("nd,fd->nf", grad_low, down_weight, preferred_element_type=jnp.float32)
    gelu_out, gelu_pull = jax.vjp(gelu_tanh, up_pre)
    pre_grad = gelu_pull(act_grad)[0].astype(jnp.bfloat16)
    up_bias_grad = jnp.sum(pre_grad.astype(jnp.float32), 0)
    up_grad = jnp.einsum("nd,nf->df", normed_low, pre_grad, preferred_element_type=jnp.float32)
    normed_grad = jnp.einsum("nf,df->nd", pre_grad, up_weight, preferred_element_type=jnp.float32)
    out_grad = jnp.einsum("nd,ne->de", attended_flat, grad_low, preferred_element_type=jnp.float32)
    attended_grad = jnp.einsum(
        "ne,de->nd", grad_low, out_weight, preferred_element_type=jnp.float32
    )
    attended_grad = attended_grad.astype(jnp.bfloat16).reshape(row_count, seg_length, features)
    grad_heads = lax.all_to_all(attended_grad, "seq", split_axis=2, concat_axis=1, tiled=True)

    def attend_back(row_args):
        query_row, key_row, value_row, grad_row, log_row = row_args
        key_rows = key_row.reshape(full_length, local_heads, head_size)
        value_rows = value_row.reshape(full_length, local_heads, head_size)
        keys_total = jnp.zeros((full_length, local_heads, head_size), jnp.float32)
        values_total = jnp.zeros((full_length, local_heads, head_size), jnp.float32)
        query_parts = []
        for block_index in range(block_count):
            block_start = block_index * block_rows
            query_block = query_row[block_start : block_start + block_rows].reshape(
                block_rows, local_heads, head_size
            )
            grad_block = grad_row[block_start : block_start + block_rows].reshape(
                block_rows, local_heads, head_size
            )
            logits = scores_for(query_block, key_rows, block_start)
            probs_full = jnp.exp(logits - log_row[:, block_start : block_start + block_rows, None])
            prob_low = probs_full.astype(jnp.bfloat16)
            probs_grad = jnp.einsum(
                "qhd,khd->hqk", grad_block, value_rows, preferred_element_type=jnp.float32
            )
            inner_sum = jnp.sum(probs_full * probs_grad, -1, keepdims=True)
            scores_grad = (probs_full * (probs_grad - inner_sum)).astype(jnp.bfloat16)
            values_total = values_total + jnp.einsum(
                "hqk,qhd->khd", prob_low, grad_block, preferred_element_type=jnp.float32
            )
            query_grad = (
                jnp.einsum(
                    "hqk,khd->qhd", scores_grad, key_rows, preferred_element_type=jnp.float32
                )
                * score_scale
            )
            query_parts.append(query_grad.reshape(block_rows, slab_width).astype(jnp.bfloat16))
            keys_total = (
                keys_total
                + jnp.einsum(
                    "hqk,qhd->khd", scores_grad, query_block, preferred_element_type=jnp.float32
                )
                * score_scale
            )
        return (
            jnp.concatenate(query_parts, 0),
            keys_total.reshape(full_length, slab_width).astype(jnp.bfloat16),
            values_total.reshape(full_length, slab_width).astype(jnp.bfloat16),
        )

    query_grad_heads, key_grad_heads, value_grad_heads = lax.map(
        attend_back, (query_heads, key_heads, value_heads, grad_heads, log_sums)
    )
    query_grad_pos, key_grad_pos, value_grad_pos = (
        lax.all_to_all(
            for_sending(query_grad_heads), "seq", split_axis=1, concat_axis=2, tiled=True
        ).astype(query_grad_heads.dtype),
        lax.all_to_all(
            for_sending(key_grad_heads), "seq", split_axis=1, concat_axis=2, tiled=True
        ).astype(key_grad_heads.dtype),
        lax.all_to_all(
            for_sending(value_grad_heads), "seq", split_axis=1, concat_axis=2, tiled=True
        ).astype(value_grad_heads.dtype),
    )
    projected_grad = jnp.concatenate(
        [
            rotate_back(query_grad_pos.astype(jnp.float32), cosine, sine_term),
            rotate_back(key_grad_pos.astype(jnp.float32), cosine, sine_term),
            value_grad_pos.astype(jnp.float32),
        ],
        -1,
    )
    projected_grad = projected_grad.astype(jnp.bfloat16).reshape(token_count, 3 * features)
    qkv_grad = jnp.einsum(
        "nd,ne->de", normed_low, projected_grad, preferred_element_type=jnp.float32
    )
    normed_grad = normed_grad + jnp.einsum(
        "ne,de->nd", projected_grad, qkv_weight, preferred_element_type=jnp.float32
    )
    gain_grad = jnp.sum(normed_grad * normed_hat, 0)
    bias_grad = jnp.sum(normed_grad, 0)
    scaled_grad = normed_grad * gain_f32
    hat_grad = (
        scaled_grad
        - jnp.mean(scaled_grad, -1, keepdims=True)
        - normed_hat * jnp.mean(scaled_grad * normed_hat, -1, keepdims=True)
    )
    input_grad = (grad_f32 + inv_std * hat_grad).reshape(row_count, seg_length, features)
    row_sums = jnp.sum(input_grad, 1)
    family_grad = jnp.einsum(
        "rf,rd->fd", family_hot.astype(jnp.float32), row_sums, precision=lax.Precision.HIGHEST
    )
    orient_grad = jnp.einsum(
        "rf,rd->fd", orient_hot.astype(jnp.float32), row_sums, precision=lax.Precision.HIGHEST
    )
    gain_sum, bias_sum, up_bias_sum, down_bias_sum, family_sum, orient_sum = lax.psum(
        (gain_grad, bias_grad, up_bias_grad, down_bias_grad, family_grad, orient_grad),
        ("dp", "seq"),
    )
    qkv_sum, out_sum, up_sum, down_sum = (
        lax.psum_scatter(qkv_grad, ("dp", "seq"), scatter_dimension=0, tiled=True),
        lax.psum_scatter(out_grad, ("dp", "seq"), scatter_dimension=0, tiled=True),
        lax.psum_scatter(up_grad, ("dp", "seq"), scatter_dimension=0, tiled=True),
        lax.psum_scatter(down_grad, ("dp", "seq"), scatter_dimension=0, tiled=True),
    )
    return (
        layer_out,
        input_grad,
        gain_sum,
        bias_sum,
        qkv_sum,
        out_sum,
        up_sum,
        up_bias_sum,
        down_sum,
        down_bias_sum,
        family_sum,
        orient_sum,
    )


def dot_nn(a, b):
    return lax.dot_general(a, b, (((1,), (0,)), ((), ())), preferred_element_type=F32)


def dot_nt(a, b):
    return lax.dot_general(a, b, (((1,), (1,)), ((), ())), preferred_element_type=F32)


def dot_tn(a, b):
    return lax.dot_general(a, b, (((0,), (0,)), ((), ())), preferred_element_type=F32)


def params(**more):
    return pltpu.CompilerParams(vmem_limit_bytes=VMEM_LIMIT, **more)


def cost(flops, moved, exps=0):
    return pl.CostEstimate(flops=flops, bytes_accessed=moved, transcendentals=exps)


def whole(shape):
    return pl.BlockSpec(shape, lambda *_: (0,) * len(shape), pipeline_mode=pl.Buffered(1))


def table_row(table, wanted):
    rows = lax.broadcasted_iota(jnp.int32, table.shape, 0)
    return jnp.sum(jnp.where(rows == wanted, table[...].astype(F32), 0.0), 0, keepdims=True)


def normalise(entries):
    centred = entries - jnp.mean(entries, -1, keepdims=True)
    inv_std = lax.rsqrt(jnp.mean(centred * centred, -1, keepdims=True) + 1e-05)
    return centred * inv_std, inv_std


GELU_C = math.sqrt(2.0 / math.pi)


def gelu_both(z):
    square = z * z
    t = jnp.tanh(GELU_C * z * (1.0 + 0.044715 * square))
    half = 0.5 * (1.0 + t)
    slope = half + (0.5 * GELU_C) * z * (1.0 - t * t) * (1.0 + (3 * 0.044715) * square)
    return z * half, slope


def ffn_kernel(rows, ids, hid, cot, fam, ori, gain, bias, wup, bup, wdn, norm, act, pre, bupg, bdng):
    tokens = hid.shape[0]
    seg = tokens // rows
    step = 256

    @pl.when(pl.program_id(0) == 0)
    def _():
        total = jnp.zeros((1, cot.shape[1]), F32)
        for row in range(rows):
            emb = table_row(fam, ids[0]) + table_row(ori, ids[1 + row])
            for start in range(row * seg, (row + 1) * seg, step):
                part = pl.ds(start, step)
                hat, _ = normalise(hid[part, :].astype(F32) + emb)
                norm[part, :] = (hat * gain[...].astype(F32) + bias[...].astype(F32)).astype(BF16)
                total = total + jnp.sum(cot[part, :].astype(F32), 0, keepdims=True)
        bdng[...] = total

    total = jnp.zeros((1, wup.shape[1]), F32)
    for start in range(0, tokens, step):
        part = pl.ds(start, step)
        z = dot_nn(norm[part, :], wup[...]) + bup[...].astype(F32)
        into = dot_nt(cot[part, :], wdn[...])
        value, slope = gelu_both(z)
        act[part, :] = value.astype(BF16)
        low = (into * slope).astype(BF16)
        pre[part, :] = low
        total = total + jnp.sum(low.astype(F32), 0, keepdims=True)
    bupg[...] = total


def ffn_forward(ids, hid, cot, fam, ori, gain, bias, wup, bup, wdn, rows):
    tokens, d = hid.shape
    ff = wup.shape[1]
    tile = 512
    return pl.pallas_call(
        functools.partial(ffn_kernel, rows),
        grid_spec=pltpu.PrefetchScalarGridSpec(
            num_scalar_prefetch=1,
            grid=(ff // tile,),
            in_specs=[
                whole((tokens, d)),
                whole((tokens, d)),
                whole(fam.shape),
                whole(ori.shape),
                whole((1, d)),
                whole((1, d)),
                pl.BlockSpec((d, tile), lambda i, s: (0, i)),
                pl.BlockSpec((1, tile), lambda i, s: (0, i)),
                pl.BlockSpec((tile, d), lambda i, s: (i, 0)),
            ],
            out_specs=[
                whole((tokens, d)),
                pl.BlockSpec((tokens, tile), lambda i, s: (0, i)),
                pl.BlockSpec((tokens, tile), lambda i, s: (0, i)),
                pl.BlockSpec((1, tile), lambda i, s: (0, i)),
                whole((1, d)),
            ],
        ),
        out_shape=[
            jax.ShapeDtypeStruct((tokens, d), BF16),
            jax.ShapeDtypeStruct((tokens, ff), BF16),
            jax.ShapeDtypeStruct((tokens, ff), BF16),
            jax.ShapeDtypeStruct((1, ff), F32),
            jax.ShapeDtypeStruct((1, d), F32),
        ],
        compiler_params=params(),
        cost_estimate=cost(4 * tokens * d * ff, 4 * tokens * ff + 4 * d * ff, tokens * ff),
        name="ffn_forward",
    )(ids, hid, cot, fam, ori, gain, bias, wup, bup, wdn)


def turn(entries, cosine, sine):
    even = lax.broadcasted_iota(jnp.int32, entries.shape, 1) % 2 == 0
    other = jnp.where(even, pltpu.roll(entries, 127, 1), pltpu.roll(entries, 1, 1))
    return entries * cosine + other * sine


def turn_back(entries, cosine, sine):
    even = lax.broadcasted_iota(jnp.int32, entries.shape, 1) % 2 == 0
    side = entries * sine
    other = jnp.where(even, pltpu.roll(side, 127, 1), pltpu.roll(side, 1, 1))
    return entries * cosine + other


def attend(head_size, query_ref, k_ref, v_ref, g_ref, cos, sin, o_ref, dq_ref, dk_ref, dv_ref, dkt, dvt):
    full = query_ref.shape[0]
    block = 256
    scale = head_size ** (-0.5)
    lane = lax.broadcasted_iota(jnp.int32, (block, 128), 1)
    below = lax.broadcasted_iota(jnp.int32, (block, block), 0) >= lax.broadcasted_iota(
        jnp.int32, (block, block), 1
    )
    dkt[...] = jnp.zeros_like(dkt)
    dvt[...] = jnp.zeros_like(dvt)
    for start in range(0, full, block):
        part = pl.ds(start, block)
        end = start + block
        query = query_ref[part, :]
        grad = g_ref[part, :]
        out = None
        dq = None
        for head in range(128 // head_size):
            mine = (lane >= head * head_size) & (lane < (head + 1) * head_size)
            qm = jnp.where(mine, query.astype(F32) * scale, 0.0).astype(BF16)
            gm = jnp.where(mine, grad.astype(F32), 0.0).astype(BF16)
            scores = dot_nt(qm, k_ref[0:end, :])
            last = jnp.where(below, scores[:, start:end], -1e30)
            scores = last if start == 0 else jnp.concatenate([scores[:, :start], last], 1)
            weights = jnp.exp(scores - jnp.max(scores, -1, keepdims=True))
            probs = weights * (1.0 / jnp.sum(weights, -1, keepdims=True))
            low = probs.astype(BF16)
            piece = dot_nn(low, v_ref[0:end, :])
            out = piece if out is None else jnp.where(mine, piece, out)
            pg = dot_nt(gm, v_ref[0:end, :])
            inner = jnp.sum(probs * pg, -1, keepdims=True)
            sg = (probs * (pg - inner)).astype(BF16)
            piece = dot_nn(sg, k_ref[0:end, :])
            dq = piece if dq is None else jnp.where(mine, piece, dq)
            dkt[:, 0:end] += dot_tn(qm, sg)
            dvt[:, 0:end] += dot_tn(gm, low)
        o_ref[part, :] = out.astype(BF16)
        dq_ref[part, :] = turn_back(dq * scale, cos[part, :], sin[part, :]).astype(BF16)
    for start in range(0, full, block):
        part = pl.ds(start, block)
        dk = dkt[:, start : start + block].T
        dk_ref[part, :] = turn_back(dk, cos[part, :], sin[part, :]).astype(BF16)
        dv_ref[part, :] = dvt[:, start : start + block].T.astype(BF16)


def events_for(tiles, pairs):
    first = 4 * tiles
    return {
        0: [(0, 0), (2, 0), (3, 0)],
        first + 1: [(0, 1), (1, 0), (2, 1), (3, 1)],
        first + 3: [(0, 2), (3, 2)],
        first + 5: [(1, 1), (2, 2), (0, 3), (3, 3)],
        first + 6: [(1, 2), (2, 3), (0, 4), (3, 4)],
        first + 7: [(1, 3), (2, 4)],
        first + 8: [(1, 4)],
    }


def middle_kernel(tiles, pairs, head_size, bits, orders, *refs):
    ids, own, far, cown, cfar, fam, ori, gain, bias, wqkv, wout, cos, sin = refs[:13]
    near_up, far_up, near_down, far_down = refs[13:17]
    norm, cot, o_ref, dq_ref, dk_ref, dv_ref, up_out, down_out = refs[17:25]
    heads, dkt, dvt = refs[25:28]
    seg = own.shape[0]
    step = 256
    i = pl.program_id(0)
    me = lax.axis_index("seq")
    mine = device_bits(bits + 1)
    up_half = up_out.shape[1] // 2
    down_half = down_out.shape[1] // 2
    chunks = chunks_from(
        refs[28:],
        bits,
        mine,
        [
            (orders[0], near_up, far_up, pl.ds(0, up_half), up_out),
            (orders[1], near_up, far_up, pl.ds(up_half, up_half), up_out),
            (orders[2], near_down, far_down, pl.ds(0, down_half), down_out),
            (orders[3], near_down, far_down, pl.ds(down_half, down_half), down_out),
        ],
    )

    def happen(events):
        for chunk, stage in events:
            if stage == 0:
                chunks[chunk].begin()
            elif stage == bits:
                chunks[chunk].finish()
            else:
                chunks[chunk].advance(stage)

    @pl.when(i == 0)
    def _():
        meet([partner_along(axis, mine) for axis in orders[0]])

    events = events_for(tiles, pairs)
    last = 4 * tiles + pairs
    for when, what in events.items():
        if when < last:

            @pl.when(i == when)
            def _():
                happen(what)

    @pl.when(i == 0)
    def _():
        emb = table_row(fam, ids[0]) + table_row(ori, ids[1])
        for source, csource, where in ((own, cown, me), (far, cfar, 1 - me)):
            for start in range(0, seg, step):
                part = pl.ds(start, step)
                there = pl.ds(pl.multiple_of(where * seg + start, step), step)
                hat, _ = normalise(source[part, :].astype(F32) + emb)
                norm[there, :] = (hat * gain[...].astype(F32) + bias[...].astype(F32)).astype(BF16)
                cot[there, :] = csource[part, :]

    lanes = wqkv.shape[1] // 128

    @pl.when(i < 2 * tiles)
    def _():
        for start in range(0, 2 * seg, step):
            part = pl.ds(start, step)
            lin = dot_nn(norm[part, :], wqkv[...])
            for lane in range(lanes):
                piece = turn(lin[:, lane * 128 : (lane + 1) * 128], cos[part, :], sin[part, :])
                heads[i * lanes + lane, part, :] = piece.astype(BF16)

    @pl.when((i >= 2 * tiles) & (i < 3 * tiles))
    def _():
        for start in range(0, 2 * seg, step):
            part = pl.ds(start, step)
            lin = dot_nn(norm[part, :], wqkv[...]).astype(BF16)
            for lane in range(lanes):
                heads[i * lanes + lane, part, :] = lin[:, lane * 128 : (lane + 1) * 128]

    @pl.when((i >= 3 * tiles) & (i < 4 * tiles))
    def _():
        for start in range(0, 2 * seg, step):
            part = pl.ds(start, step)
            lin = dot_nt(cot[part, :], wout[...]).astype(BF16)
            for lane in range(lanes):
                heads[i * lanes + lane, part, :] = lin[:, lane * 128 : (lane + 1) * 128]

    @pl.when(i >= 4 * tiles)
    def _():
        pair = i - 4 * tiles
        attend(
            head_size,
            heads.at[pair],
            heads.at[pairs + pair],
            heads.at[2 * pairs + pair],
            heads.at[3 * pairs + pair],
            cos,
            sin,
            o_ref,
            dq_ref,
            dk_ref,
            dv_ref,
            dkt,
            dvt,
        )

    @pl.when(i == last - 1)
    def _():
        happen(events[last])


def middle(ids, own, far, cown, cfar, fam, ori, gain, bias, wqkv, wout, cos, sin, up, down, orders, head_size, collective):
    seg, d = own.shape
    full = 2 * seg
    tile = 512
    tiles = d // tile
    pairs = d // 128
    bits = len(orders[0])
    near_up, far_up = up
    near_down, far_down = down
    up_size, ff = near_up.shape[1:]
    down_size = near_down.shape[1]
    smem = pl.BlockSpec(memory_space=pltpu.SMEM)
    anywhere = pl.BlockSpec(memory_space=pl.ANY)
    head_out = pl.BlockSpec((full, 128), lambda i: (0, jnp.maximum(i - 4 * tiles, 0)))
    rows = jax.ShapeDtypeStruct((full, d), BF16)
    return pl.pallas_call(
        functools.partial(middle_kernel, tiles, pairs, head_size, bits, orders),
        grid=(4 * tiles + pairs,),
        in_specs=[
            smem,
            whole((seg, d)),
            whole((seg, d)),
            whole((seg, d)),
            whole((seg, d)),
            whole(fam.shape),
            whole(ori.shape),
            whole((1, d)),
            whole((1, d)),
            pl.BlockSpec((d, tile), lambda i: (0, jnp.minimum(i, 3 * tiles - 1))),
            pl.BlockSpec((tile, d), lambda i: (jnp.clip(i - 3 * tiles, 0, tiles - 1), 0)),
            whole((full, 128)),
            whole((full, 128)),
        ]
        + [anywhere] * 4,
        out_specs=[
            whole((full, d)),
            whole((full, d)),
            head_out,
            head_out,
            head_out,
            head_out,
            whole((up_size, ff)),
            whole((down_size, d)),
        ],
        out_shape=[
            rows,
            rows,
            rows,
            rows,
            rows,
            rows,
            jax.ShapeDtypeStruct((up_size, ff), F32),
            jax.ShapeDtypeStruct((down_size, d), F32),
        ],
        scratch_shapes=[
            pltpu.VMEM((4 * pairs, full, 128), BF16),
            pltpu.VMEM((128, full), F32),
            pltpu.VMEM((128, full), F32),
        ]
        + chunk_scratch(orders[0], up_size, ff // 2)
        + chunk_scratch(orders[1], up_size, ff // 2)
        + chunk_scratch(orders[2], down_size, d // 2)
        + chunk_scratch(orders[3], down_size, d // 2),
        compiler_params=params(collective_id=collective, has_side_effects=True),
        cost_estimate=cost(8 * full * d * d + 12 * full * full * d, 8 * d * d + 18 * full * d, full * full * H),
        name="middle",
    )(ids, own, far, cown, cfar, fam, ori, gain, bias, wqkv, wout, cos, sin, near_up, far_up, near_down, far_down)


def device_bits(bits):
    dp = lax.axis_index("dp")
    found = {bit: lax.rem(dp // (1 << bit), 2) for bit in range(bits)}
    found["seq"] = lax.axis_index("seq")
    return found


def block_place(axes, mine, upper, seq):
    place = 0
    for axis in axes:
        bit = seq if axis == "seq" else (upper >> (axis - 1)) & 1
        place = 2 * place + (1 - mine[axis] if bit else mine[axis])
    return place


def other_core():
    dp = lax.axis_index("dp")
    return (dp + 1 - 2 * lax.rem(dp, 2), lax.axis_index("seq"))


def meet(partners):
    barrier = pltpu.get_barrier_semaphore()
    for partner in partners:
        pl.semaphore_signal(barrier, inc=1, device_id=partner, device_id_type=MESH)
    pl.semaphore_wait(barrier, len(partners))


def remote(src, dst, send_sem, recv_sem, partner):
    return pltpu.make_async_remote_copy(
        src_ref=src,
        dst_ref=dst,
        send_sem=send_sem,
        recv_sem=recv_sem,
        device_id=partner,
        device_id_type=MESH,
    )


def split_blocks(value, keep, send, size, core, places):
    for index, there in enumerate(places):
        up, seq = index // 2, index % 2
        first = (4 * up + seq) * size
        second = first + 2 * size
        a = value[first : first + size, :].astype(BF16)
        b = value[second : second + size, :].astype(BF16)
        keep[there] = jnp.where(core == 0, a, b)
        send[there] = jnp.where(core == 0, b, a)


def add_into(keep, got):
    for index in range(keep.shape[0]):
        keep[index] = (keep[index].astype(F32) + got[index].astype(F32)).astype(BF16)


def wide_grad_kernel(bits, counts, orders, firsts, *refs):
    lefts, rights = refs[: len(counts)], refs[len(counts) : 2 * len(counts)]
    near_out, far_out, turned, keep, send, got, send_sem, recv_sem, out_sem = refs[2 * len(counts) :]
    steps = sum(counts)
    i = pl.program_id(0)
    mine = device_bits(bits)
    partner = other_core()
    blocks = keep.shape[1]
    size = keep.shape[2]
    tile = keep.shape[3]

    def crossing(step):
        return remote(send.at[step], got.at[step], send_sem.at[step], recv_sem.at[step], partner)

    def stores(step):
        columns = pl.ds(pl.multiple_of(step * tile, tile), tile)
        half = blocks // 2
        return (
            pltpu.make_async_copy(
                keep.at[step, pl.ds(0, half)], near_out.at[:, :, columns], out_sem.at[0, step]
            ),
            pltpu.make_async_copy(
                keep.at[step, pl.ds(half, half)], far_out.at[:, :, columns], out_sem.at[1, step]
            ),
        )

    @pl.when(i == 0)
    def _():
        meet([partner])

    start = 0
    for left, right, count, axes, first in zip(lefts, rights, counts, orders, firsts):
        places = [block_place(axes, mine, up, seq) for up in range(blocks // 2) for seq in range(2)]
        if first:

            @pl.when(i == start)
            def _():
                turned[...] = left[...].T

        @pl.when((i >= start) & (i < start + count))
        def _():
            value = dot_nn(turned[...], right[...])
            split_blocks(value, keep.at[i], send.at[i], size, mine[0], places)
            crossing(i).start()

        start += count

    def finish(step):
        crossing(step).wait()
        add_into(keep.at[step], got.at[step])
        for copy in stores(step):
            copy.start()

    @pl.when(i > 0)
    def _():
        finish(i - 1)

    @pl.when(i == steps - 1)
    def _():
        finish(i)
        for step in range(steps):
            for copy in stores(step):
                copy.wait()


def wide_grad(entries, tile, collective):
    tokens, d = entries[0][0].shape
    bits = len(entries[0][4])
    blocks = 1 << bits
    size = d // (2 * blocks)
    counts = [entry[3] for entry in entries]
    orders = [entry[4] for entry in entries]
    firsts = [index == 0 or entries[index][0] is not entries[index - 1][0] for index in range(len(entries))]
    steps = sum(counts)
    specs = []
    start = 0
    for entry in entries:

        def at(i, start=start, offset=entry[2], last=entry[3] - 1):
            return (0, offset + jnp.clip(i - start, 0, last))

        specs.append(pl.BlockSpec((tokens, tile), at))
        start += entry[3]
    shape = jax.ShapeDtypeStruct((blocks // 2, size, steps * tile), BF16)
    anywhere = pl.BlockSpec(memory_space=pl.ANY)
    buffers = pltpu.VMEM((steps, blocks, size, tile), BF16)
    return pl.pallas_call(
        functools.partial(wide_grad_kernel, bits, counts, orders, firsts),
        grid=(steps,),
        in_specs=[whole((tokens, d)) for _ in entries] + specs,
        out_specs=[anywhere, anywhere],
        out_shape=[shape, shape],
        scratch_shapes=[
            pltpu.VMEM((d, tokens), BF16),
            buffers,
            buffers,
            buffers,
            pltpu.SemaphoreType.DMA((steps,)),
            pltpu.SemaphoreType.DMA((steps,)),
            pltpu.SemaphoreType.DMA((2, steps)),
        ],
        compiler_params=params(collective_id=collective, has_side_effects=True),
        cost_estimate=cost(2 * tokens * d * steps * tile, 4 * tokens * (d + steps * tile)),
        name="wide_grad",
    )(*[entry[0] for entry in entries], *[entry[1] for entry in entries])


def tall_grad_kernel(bits, orders, left, right, near_out, far_out, keep, send, got, send_sem, recv_sem, out_sem):
    i = pl.program_id(0)
    steps, _, size, d = keep.shape
    width = d // len(orders)
    mine = device_bits(bits)
    partner = other_core()
    half = steps

    def crossing(step):
        return remote(send.at[step], got.at[step], send_sem.at[step], recv_sem.at[step], partner)

    def store(step, seq, act):
        for part, axes in enumerate(orders):
            place = 0
            for axis in axes:
                if axis == "seq":
                    apart = lax.rem(mine["seq"] + seq, 2)
                else:
                    apart = lax.rem(step // (1 << (axis - 1)) + mine[axis], 2)
                place = 2 * place + apart
            columns = pl.ds(part * width, width)
            source = keep.at[step, seq, :, columns]
            sem = out_sem.at[step, seq, part]
            there = lax.rem(place, half)

            @pl.when(place < half)
            def _():
                act(pltpu.make_async_copy(source, near_out.at[there, :, columns], sem))

            @pl.when(place >= half)
            def _():
                act(pltpu.make_async_copy(source, far_out.at[there, :, columns], sem))

    @pl.when(i == 0)
    def _():
        meet([partner])

    value = dot_nn(left[...].T, right[...])
    split_blocks(value, keep.at[i], send.at[i], size, mine[0], [0, 1])
    crossing(i).start()

    def finish(step):
        crossing(step).wait()
        add_into(keep.at[step], got.at[step])
        for seq in range(2):
            store(step, seq, lambda copy: copy.start())

    @pl.when(i > 0)
    def _():
        finish(i - 1)

    @pl.when(i == steps - 1)
    def _():
        finish(i)
        for step in range(steps):
            for seq in range(2):
                store(step, seq, lambda copy: copy.wait())


def tall_grad(orders, left, right, collective):
    tokens, m = left.shape
    d = right.shape[1]
    bits = len(orders[0])
    steps = 1 << (bits - 1)
    tile = m // steps
    size = tile // 4
    shape = jax.ShapeDtypeStruct((steps, size, d), BF16)
    anywhere = pl.BlockSpec(memory_space=pl.ANY)
    buffers = pltpu.VMEM((steps, 2, size, d), BF16)
    return pl.pallas_call(
        functools.partial(tall_grad_kernel, bits, orders),
        grid=(steps,),
        in_specs=[pl.BlockSpec((tokens, tile), lambda i: (0, i)), whole((tokens, d))],
        out_specs=[anywhere, anywhere],
        out_shape=[shape, shape],
        scratch_shapes=[
            buffers,
            buffers,
            buffers,
            pltpu.SemaphoreType.DMA((steps,)),
            pltpu.SemaphoreType.DMA((steps,)),
            pltpu.SemaphoreType.DMA((steps, 2, len(orders))),
        ],
        compiler_params=params(collective_id=collective, has_side_effects=True),
        cost_estimate=cost(2 * tokens * d * m, 2 * (tokens * m + d * m + tokens * d)),
        name="tall_grad",
    )(left, right)


def partner_along(axis, mine):
    dp = lax.axis_index("dp")
    seq = lax.axis_index("seq")
    if axis == "seq":
        return (dp, 1 - seq)
    return (dp + (1 - 2 * mine[axis]) * (1 << axis), seq)


class Chunk:
    def __init__(self, axes, mine, near, far, columns, out, keep, got, near_sem, send_sem, recv_sem):
        self.axes, self.mine, self.near, self.far = axes, mine, near, far
        self.columns, self.out, self.keep, self.got = columns, out, keep, got
        self.near_sem, self.send_sem, self.recv_sem = near_sem, send_sem, recv_sem

    def load(self):
        return pltpu.make_async_copy(self.near.at[:, :, self.columns], self.keep, self.near_sem)

    def crossing(self, stage):
        count = self.keep.shape[0] >> stage
        source = self.far.at[:, :, self.columns] if stage == 0 else self.keep.at[pl.ds(count, count)]
        return remote(
            source,
            self.got[stage],
            self.send_sem.at[stage],
            self.recv_sem.at[stage],
            partner_along(self.axes[stage], self.mine),
        )

    def begin(self):
        self.load().start()
        self.crossing(0).start()

    def advance(self, stage):
        if stage == 1:
            self.load().wait()
        self.crossing(stage - 1).wait()
        count = self.keep.shape[0] >> (stage - 1)

        def add(index, carry):
            self.keep[index] = (self.keep[index].astype(F32) + self.got[stage - 1][index].astype(F32)).astype(BF16)
            return carry

        lax.fori_loop(0, count, add, 0)
        self.crossing(stage).start()

    def finish(self):
        last = len(self.axes) - 1
        self.crossing(last).wait()
        self.out[:, self.columns] = self.keep[0].astype(F32) + self.got[last][0].astype(F32)


def chunk_scratch(axes, size, width):
    half = 1 << (len(axes) - 1)
    return (
        [pltpu.VMEM((half, size, width), BF16)]
        + [pltpu.VMEM((half >> stage, size, width), BF16) for stage in range(len(axes))]
        + [
            pltpu.SemaphoreType.DMA,
            pltpu.SemaphoreType.DMA((len(axes),)),
            pltpu.SemaphoreType.DMA((len(axes),)),
        ]
    )


def chunks_from(refs, bits, mine, wanted):
    stages = bits
    found = []
    each = 1 + stages + 3
    for index, (axes, near, far, columns, out) in enumerate(wanted):
        part = refs[index * each : (index + 1) * each]
        found.append(
            Chunk(axes, mine, near, far, columns, out, part[0], part[1 : 1 + stages], *part[1 + stages :])
        )
    return found


class Halving:
    def __init__(self, axes, keep, send):
        self.axes = axes[1:]
        self.keep = keep
        self.got = self.swap(send, axes[0])

    def swap(self, part, axis):
        if axis == "seq":
            return lax.ppermute(part, "seq", [(0, 1), (1, 0)])
        count = lax.axis_size("dp")
        return lax.ppermute(part, "dp", [(i, i ^ (1 << axis)) for i in range(count)])

    def step(self):
        axis, self.axes = self.axes[0], self.axes[1:]
        half = self.keep.shape[0] // 2
        send = self.keep[half:].astype(F32) + self.got[half:].astype(F32)
        keep = self.keep[:half].astype(F32) + self.got[:half].astype(F32)
        send = send.astype(BF16)
        self.keep = keep if half == 1 else keep.astype(BF16)
        self.got = self.swap(send, axis)
        return send

    def total(self):
        return self.keep[0] + self.got[0].astype(F32)


def after(entry, *others):
    return lax.optimization_barrier((entry, *others))[0]


def back_kernel(dq, dk, dv, w, out):
    d = dq.shape[1]
    total = dot_nt(dq[...], w[:, 0:d])
    total = total + dot_nt(dk[...], w[:, d : 2 * d])
    total = total + dot_nt(dv[...], w[:, 2 * d : 3 * d])
    out[...] = total.astype(BF16)


def project_back(dq, dk, dv, w):
    tokens, d = dq.shape
    step = 256
    spec = pl.BlockSpec((step, d), lambda i: (i, 0))
    return pl.pallas_call(
        back_kernel,
        grid=(tokens // step,),
        in_specs=[spec, spec, spec, whole(w.shape)],
        out_specs=spec,
        out_shape=jax.ShapeDtypeStruct((tokens, d), BF16),
        compiler_params=params(),
        cost_estimate=cost(6 * tokens * d * d, 6 * d * d + 8 * tokens * d),
        name="project_back",
    )(dq, dk, dv, w)


def out_kernel(per_row, ids, hid, fam, ori, act, wdn, own, far, wout, bdn, out):
    row = pl.program_id(0) // per_row
    emb = table_row(fam, ids[0]) + table_row(ori, ids[2 + row])
    att = jnp.where(row == ids[1], own[...], far[...])
    total = hid[...].astype(F32) + emb + dot_nn(att, wout[...])
    total = total + (dot_nn(act[...], wdn[...]) + bdn[...].astype(F32))
    out[...] = total.astype(BF16)


def input_kernel(per_row, ids, hid, fam, ori, pre, wup, own, far, gain, cot, out, gg, bg, rg):
    i = pl.program_id(0)
    row = i // per_row
    emb = table_row(fam, ids[0]) + table_row(ori, ids[2 + row])
    hat, inv_std = normalise(hid[...].astype(F32) + emb)
    grad = dot_nt(pre[...], wup[...]) + jnp.where(row == ids[1], own[...], far[...]).astype(F32)

    @pl.when(i == 0)
    def _():
        gg[...] = jnp.zeros_like(gg)
        bg[...] = jnp.zeros_like(bg)
        rg[...] = jnp.zeros_like(rg)

    gg[...] += jnp.sum(grad * hat, 0, keepdims=True)
    bg[...] += jnp.sum(grad, 0, keepdims=True)
    scaled = grad * gain[...].astype(F32)
    inner = (
        scaled
        - jnp.mean(scaled, -1, keepdims=True)
        - hat * jnp.mean(scaled * hat, -1, keepdims=True)
    )
    result = cot[...].astype(F32) + inv_std * inner
    out[...] = result
    sums = jnp.sum(result, 0, keepdims=True)
    rows = lax.broadcasted_iota(jnp.int32, rg.shape, 0)
    rg[...] += jnp.where(rows == row, sums, 0.0)


def home_specs(tokens, d, rows, step):
    per_row = tokens // rows // step
    local = pl.BlockSpec((step, d), lambda i, s: (i, 0))
    own = pl.BlockSpec((step, d), lambda i, s: (s[1] * per_row + i % per_row, 0))
    far = pl.BlockSpec((step, d), lambda i, s: (i % per_row, 0))
    return per_row, local, own, far


def layer_output(ids, hid, fam, ori, act, wdn, own, far, wout, bdn, rows):
    tokens, d = hid.shape
    ff = act.shape[1]
    step = 256
    per_row, local, own_spec, far_spec = home_specs(tokens, d, rows, step)
    return pl.pallas_call(
        functools.partial(out_kernel, per_row),
        grid_spec=pltpu.PrefetchScalarGridSpec(
            num_scalar_prefetch=1,
            grid=(tokens // step,),
            in_specs=[
                local,
                whole(fam.shape),
                whole(ori.shape),
                pl.BlockSpec((step, ff), lambda i, s: (i, 0)),
                whole(wdn.shape),
                own_spec,
                far_spec,
                whole(wout.shape),
                whole((1, d)),
            ],
            out_specs=local,
        ),
        out_shape=jax.ShapeDtypeStruct((tokens, d), BF16),
        compiler_params=params(),
        cost_estimate=cost(2 * tokens * d * (ff + d), 2 * (d * (ff + d) + tokens * ff + 4 * tokens * d)),
        name="layer_output",
    )(ids, hid, fam, ori, act, wdn, own, far, wout, bdn)


def input_gradient(ids, hid, fam, ori, pre, wup, own, far, gain, cot, rows):
    tokens, d = hid.shape
    ff = pre.shape[1]
    step = 256
    per_row, local, own_spec, far_spec = home_specs(tokens, d, rows, step)
    return pl.pallas_call(
        functools.partial(input_kernel, per_row),
        grid_spec=pltpu.PrefetchScalarGridSpec(
            num_scalar_prefetch=1,
            grid=(tokens // step,),
            in_specs=[
                local,
                whole(fam.shape),
                whole(ori.shape),
                pl.BlockSpec((step, ff), lambda i, s: (i, 0)),
                whole(wup.shape),
                own_spec,
                far_spec,
                whole((1, d)),
                local,
            ],
            out_specs=[local, whole((1, d)), whole((1, d)), whole((rows, d))],
        ),
        out_shape=[
            jax.ShapeDtypeStruct((tokens, d), F32),
            jax.ShapeDtypeStruct((1, d), F32),
            jax.ShapeDtypeStruct((1, d), F32),
            jax.ShapeDtypeStruct((rows, d), F32),
        ],
        compiler_params=params(),
        cost_estimate=cost(2 * tokens * d * ff, 2 * (d * ff + tokens * ff + 6 * tokens * d)),
        name="input_gradient",
    )(ids, hid, fam, ori, pre, wup, own, far, gain, cot)


def sums_kernel(bits, sums_ref, vec_ref, sums_out, all_out, held, got, vgot, send_sem, recv_sem, gsend, grecv):
    dp = lax.axis_index("dp")
    seq = lax.axis_index("seq")
    partners = [(dp, 1 - seq)]
    for bit in range(bits):
        size = 1 << bit
        partners.append((dp + (1 - 2 * lax.rem(dp // size, 2)) * size, seq))
    barrier = pltpu.get_barrier_semaphore()
    for partner in partners:
        pl.semaphore_signal(barrier, inc=1, device_id=partner, device_id_type=MESH)
    pl.semaphore_wait(barrier, len(partners))

    def remote(src, dst, send, recv, partner):
        copy = pltpu.make_async_remote_copy(
            src_ref=src, dst_ref=dst, send_sem=send, recv_sem=recv, device_id=partner, device_id_type=MESH
        )
        copy.start()
        return copy

    for index, partner in enumerate(partners):
        source = sums_ref if index == 0 else held.at[index]
        main = remote(source, got.at[index], send_sem.at[index], recv_sem.at[index], partner)
        if index == 0:
            side = remote(vec_ref, vgot, gsend.at[0], grecv.at[0], partner)
        else:
            size = 1 << (index - 1)
            held_now = pl.ds(dp - lax.rem(dp, size), size)
            side = remote(
                all_out.at[held_now], all_out.at[held_now], gsend.at[index], grecv.at[index], partner
            )
        main.wait()
        total = source[...] + got[index]
        if index + 1 < len(partners):
            held[index + 1] = total
        else:
            sums_out[...] = total
        side.wait()
        if index == 0:
            all_out[dp] = vec_ref[...] + vgot[...]


def sum_small(sums, vec):
    count = lax.axis_size("dp")
    bits = int(math.log2(count))
    rounds = bits + 1
    return pl.pallas_call(
        functools.partial(sums_kernel, bits),
        in_specs=[pl.BlockSpec(memory_space=pltpu.VMEM)] * 2,
        out_specs=[pl.BlockSpec(memory_space=pltpu.VMEM)] * 2,
        out_shape=[
            jax.ShapeDtypeStruct(sums.shape, F32),
            jax.ShapeDtypeStruct((count,) + vec.shape, F32),
        ],
        scratch_shapes=[
            pltpu.VMEM((rounds,) + sums.shape, F32),
            pltpu.VMEM((rounds,) + sums.shape, F32),
            pltpu.VMEM(vec.shape, F32),
            pltpu.SemaphoreType.DMA((rounds,)),
            pltpu.SemaphoreType.DMA((rounds,)),
            pltpu.SemaphoreType.DMA((rounds,)),
            pltpu.SemaphoreType.DMA((rounds,)),
        ],
        compiler_params=pltpu.CompilerParams(collective_id=0, has_side_effects=True),
        name="sum_small",
    )(sums, vec)


def body_by_rows(
    hidden_in,
    family,
    orient,
    norm_gain,
    norm_bias,
    qkv_weight,
    out_weight,
    up_weight,
    up_bias,
    down_weight,
    down_bias,
    family_table,
    orient_table,
    cotangent,
):
    rows, seg, d = hidden_in.shape
    ff = up_weight.shape[1]
    tokens = rows * seg
    full = 2 * seg
    dp_count = lax.axis_size("dp")
    bits = int(math.log2(dp_count))
    upper = dp_count // 2
    dp = lax.axis_index("dp")
    seq = lax.axis_index("seq")
    ring = [(0, 1), (1, 0)]

    def mine(pair):
        return lax.dynamic_index_in_dim(pair, seq, 0, keepdims=False)

    def theirs(pair):
        return lax.dynamic_index_in_dim(pair, 1 - seq, 0, keepdims=False)

    far_hidden = lax.ppermute(theirs(hidden_in), "seq", ring)
    far_cot = lax.ppermute(theirs(cotangent), "seq", ring)

    gain = norm_gain.reshape(1, d)
    bias = norm_bias.reshape(1, d)
    hid = hidden_in.reshape(tokens, d)
    cot = cotangent.reshape(tokens, d)
    ids = jnp.concatenate([family, orient])
    tail_ids = jnp.concatenate([family, seq[None].astype(jnp.int32), orient])
    row_ids = jnp.stack([family[0], mine(orient)])

    zs = list(range(2, bits))
    order_a = [1] + zs + ["seq"]
    order_b = [1, "seq"] + zs
    order_c = ["seq", 1] + zs
    order_d = [2, "seq", 1] + zs[1:]
    order_e = [2, 1] + zs[1:] + ["seq"]
    ffn_orders = [order_a, order_b, order_c, order_d]

    normed, act, pre, up_bias_part, down_bias_part = ffn_forward(
        ids, hid, cot, family_table, orient_table, gain, bias, up_weight, up_bias.reshape(1, ff), down_weight, rows
    )
    half_tiles = ff // 2048
    ready = after(normed, far_hidden)
    up = wide_grad([(ready, pre, 0, half_tiles, order_a), (ready, pre, half_tiles, half_tiles, order_b)], 1024, 1)
    down = tall_grad([order_c, order_d], after(act, up[0], far_cot), cot, 2)

    cosine, sine = rope_tables(jnp.arange(full).astype(F32), 128)
    row_normed, row_cot, att, dq, dk, dv, up_total, down_total = middle(
        row_ids,
        mine(hidden_in),
        far_hidden,
        mine(cotangent),
        far_cot,
        family_table,
        orient_table,
        gain,
        bias,
        qkv_weight,
        out_weight,
        cosine,
        sine,
        up,
        down,
        ffn_orders,
        d // H,
        5,
    )
    far_att = lax.ppermute(theirs(att.reshape(2, seg, d)), "seq", ring)
    first = Halving(order_a, *wide_grad([(row_normed, dq, 0, 1, order_a), (row_normed, dk, 0, 1, order_a)], 1024, 3))
    second = Halving(
        order_e,
        *wide_grad([(row_normed, after(dv, first.keep), 0, 1, order_e), (att, row_cot, 0, 1, order_e)], 1024, 4),
    )
    tied = (second.keep,)
    back = project_back(after(dq, *tied), dk, dv, qkv_weight)
    far_back = lax.ppermute(theirs(back.reshape(2, seg, d)), "seq", ring)
    tied = ()
    layer_out = layer_output(
        tail_ids,
        hid,
        family_table,
        orient_table,
        after(act, back, *tied),
        down_weight,
        att,
        far_att,
        out_weight,
        down_bias.reshape(1, d),
        rows,
    )
    tied = (first.step(), second.step())
    input_grad, gain_part, bias_part, row_part = input_gradient(
        tail_ids, hid, family_table, orient_table, after(pre, layer_out, *tied), up_weight, back, far_back, gain, cot, rows
    )
    for chunk in (first, second):
        while chunk.axes:
            chunk.step()
    first_total, second_total = first.total(), second.total()

    flag = orient[0]
    by_flag = jnp.where(flag == 0, row_part, row_part[::-1])
    packed = jnp.concatenate(
        [
            part.reshape(-1, 128)
            for part in (up_bias_part, down_bias_part, gain_part, bias_part, by_flag)
        ],
        0,
    )
    vec = jnp.concatenate(
        [
            (row_part[0] + row_part[1]).reshape(-1, 128),
            jnp.full((8, 128), 0.5, F32) * family.astype(F32)[0],
        ],
        0,
    )
    sums, gathered = sum_small(packed, vec)
    flat = sums.reshape(-1)
    up_bias_sum = flat[:ff]
    down_bias_sum, gain_sum, bias_sum = flat[ff : ff + 3 * d].reshape(3, d)
    orient_sum = flat[ff + 3 * d :].reshape(2, d)
    families = family_table.shape[0]
    hot = gathered[:, -1, 0].astype(jnp.int32)[None, :] == jnp.arange(families)[:, None]
    family_sum = jnp.dot(
        hot.astype(F32), gathered[:, :-8].reshape(dp_count, d), precision=lax.Precision.HIGHEST
    )
    return (
        layer_out.reshape(rows, seg, d),
        input_grad.reshape(rows, seg, d),
        gain_sum,
        bias_sum,
        jnp.concatenate([first_total, second_total[:, :d]], 1),
        second_total[:, d:],
        up_total,
        up_bias_sum,
        down_total,
        down_bias_sum,
        family_sum,
        orient_sum,
    )


def body(*args):
    hidden_in = args[0]
    dp_count = lax.axis_size("dp")
    two_rows = lax.axis_size("seq") == 2 and hidden_in.shape[0] == 2
    if two_rows and dp_count >= 4 and dp_count & (dp_count - 1) == 0:
        return body_by_rows(*args)
    return body_by_heads(*args)


def solution(mesh):
    return jax.shard_map(
        body,
        mesh=mesh,
        in_specs=(
            P("dp", "seq", None),
            P("dp"),
            P("dp"),
            P(),
            P(),
            P(),
            P(),
            P(),
            P(),
            P(),
            P(),
            P(),
            P(),
            P("dp", "seq", None),
        ),
        out_specs=(
            P("dp", "seq", None),
            P("dp", "seq", None),
            P(),
            P(),
            P(("dp", "seq"), None),
            P(("dp", "seq"), None),
            P(("dp", "seq"), None),
            P(),
            P(("dp", "seq"), None),
            P(),
            P(),
            P(),
        ),
        check_vma=False,
    )
```

```python
import functools
import math

import jax
import jax.numpy as jnp
from jax import lax
from jax.experimental import pallas as pl
from jax.experimental.pallas import tpu as pltpu
from jax.sharding import PartitionSpec as P

H = 16
HD = 64
ROT = 32
MESH = pl.DeviceIdType.MESH
VMEM_LIMIT = 60 * 1024 * 1024
F32 = jnp.float32
BF16 = jnp.bfloat16


def for_sending(shard):

    def short(part):
        return part.astype(jnp.bfloat16) if part.dtype == jnp.float32 else part

    return jax.tree.map(short, shard)


def rope_tables(positions, features):
    column = jnp.arange(features, dtype=jnp.int32)
    within = column % HD
    frequency = jnp.exp(-(2.0 * (within // 2).astype(jnp.float32) / ROT) * math.log(10000.0))
    angles = positions[:, None] * frequency[None, :]
    rotary = within < ROT
    cosine = jnp.where(rotary[None, :], jnp.cos(angles), 1.0)
    sign_term = jnp.where(within % 2 == 0, -1.0, 1.0)
    sine_term = jnp.where(rotary[None, :], sign_term[None, :] * jnp.sin(angles), 0.0)
    return (cosine, sine_term)


def pair_swap(values):
    even_cols = jnp.arange(values.shape[-1]) % 2 == 0
    return jnp.where(even_cols, jnp.roll(values, -1, axis=-1), jnp.roll(values, 1, axis=-1))


def rotate(values, cosine, sine_term):
    return values * cosine + pair_swap(values) * sine_term


def rotate_back(values, cosine, sine_term):
    return values * cosine + pair_swap(values * sine_term)


def gelu_tanh(pre_values):
    return jax.nn.gelu(pre_values, approximate=True)


def body_by_heads(
    hidden_in,
    family,
    orient,
    norm_gain,
    norm_bias,
    qkv_weight,
    out_weight,
    up_weight,
    up_bias,
    down_weight,
    down_bias,
    family_table,
    orient_table,
    cotangent,
):
    seq_count = lax.axis_size("seq")
    row_count, seg_length, features = hidden_in.shape
    full_length = seg_length * seq_count
    local_heads = H // seq_count
    head_size = features // H
    slab_width = features // seq_count
    block_rows = min(512, full_length)
    block_count = full_length // block_rows
    score_scale = head_size ** (-0.5)
    token_count = row_count * seg_length
    family_rows = jnp.repeat(family, 2)
    family_hot = (family_rows[:, None] == jnp.arange(family_table.shape[0])[None, :]).astype(
        jnp.bfloat16
    )
    orient_hot = (orient[:, None] == jnp.arange(2)[None, :]).astype(jnp.bfloat16)
    embedding = jnp.dot(family_hot, family_table, preferred_element_type=jnp.float32) + jnp.dot(
        orient_hot, orient_table, preferred_element_type=jnp.float32
    )
    embedded = (hidden_in.astype(jnp.float32) + embedding[:, None, :]).reshape(
        token_count, features
    )
    row_mean = jnp.mean(embedded, -1, keepdims=True)
    centred = embedded - row_mean
    row_var = jnp.mean(centred * centred, -1, keepdims=True)
    inv_std = lax.rsqrt(row_var + 1e-05)
    normed_hat = centred * inv_std
    gain_f32 = norm_gain.astype(jnp.float32)
    normed_low = (normed_hat * gain_f32 + norm_bias.astype(jnp.float32)).astype(jnp.bfloat16)
    projected = jnp.dot(normed_low, qkv_weight, preferred_element_type=jnp.float32).reshape(
        row_count, seg_length, 3 * features
    )
    positions = (lax.axis_index("seq") * seg_length + jnp.arange(seg_length)).astype(jnp.float32)
    cosine, sine_term = rope_tables(positions, features)
    queries = rotate(projected[..., :features], cosine, sine_term).astype(jnp.bfloat16)
    keys_rot = rotate(projected[..., features : 2 * features], cosine, sine_term).astype(
        jnp.bfloat16
    )
    values = projected[..., 2 * features :].astype(jnp.bfloat16)
    query_heads, key_heads, value_heads = (
        lax.all_to_all(queries, "seq", split_axis=2, concat_axis=1, tiled=True),
        lax.all_to_all(keys_rot, "seq", split_axis=2, concat_axis=1, tiled=True),
        lax.all_to_all(values, "seq", split_axis=2, concat_axis=1, tiled=True),
    )

    def scores_for(query_block, key_rows, block_start):
        logits = (
            jnp.einsum("qhd,khd->hqk", query_block, key_rows, preferred_element_type=jnp.float32)
            * score_scale
        )
        causal = (block_start + jnp.arange(block_rows))[:, None] >= jnp.arange(full_length)[None, :]
        return jnp.where(causal[None], logits, -1e30)

    def attend(row_args):
        query_row, key_row, value_row = row_args
        key_rows = key_row.reshape(full_length, local_heads, head_size)
        value_rows = value_row.reshape(full_length, local_heads, head_size)
        pieces = []
        log_parts = []
        for block_index in range(block_count):
            block_start = block_index * block_rows
            query_block = query_row[block_start : block_start + block_rows].reshape(
                block_rows, local_heads, head_size
            )
            logits = scores_for(query_block, key_rows, block_start)
            row_peak = jnp.max(logits, -1, keepdims=True)
            weights = jnp.exp(logits - row_peak)
            row_total = jnp.sum(weights, -1, keepdims=True)
            prob_low = (weights / row_total).astype(jnp.bfloat16)
            output_block = jnp.einsum(
                "hqk,khd->qhd", prob_low, value_rows, preferred_element_type=jnp.float32
            )
            pieces.append(output_block.reshape(block_rows, slab_width).astype(jnp.bfloat16))
            log_parts.append((row_peak + jnp.log(row_total))[..., 0])
        return (jnp.concatenate(pieces, 0), jnp.concatenate(log_parts, 1))

    attended_heads, log_sums = lax.map(attend, (query_heads, key_heads, value_heads))
    attended = jax.tree.map(
        lambda part, own: part.astype(own.dtype),
        lax.all_to_all(for_sending(attended_heads), "seq", split_axis=1, concat_axis=2, tiled=True),
        attended_heads,
    )
    attended_flat = attended.reshape(token_count, features)
    branch_attn = jnp.dot(attended_flat, out_weight, preferred_element_type=jnp.float32)
    up_pre = jnp.dot(normed_low, up_weight, preferred_element_type=jnp.float32) + up_bias.astype(
        jnp.float32
    )
    up_act = gelu_tanh(up_pre).astype(jnp.bfloat16)
    branch_feed = jnp.dot(
        up_act, down_weight, preferred_element_type=jnp.float32
    ) + down_bias.astype(jnp.float32)
    layer_out = (
        (embedded + branch_attn + branch_feed)
        .astype(jnp.bfloat16)
        .reshape(row_count, seg_length, features)
    )
    grad_low = cotangent.reshape(token_count, features)
    grad_f32 = grad_low.astype(jnp.float32)
    down_grad = jnp.einsum("nf,nd->fd", up_act, grad_low, preferred_element_type=jnp.float32)
    down_bias_grad = jnp.sum(grad_f32, 0)
    act_grad = jnp.einsum("nd,fd->nf", grad_low, down_weight, preferred_element_type=jnp.float32)
    gelu_out, gelu_pull = jax.vjp(gelu_tanh, up_pre)
    pre_grad = gelu_pull(act_grad)[0].astype(jnp.bfloat16)
    up_bias_grad = jnp.sum(pre_grad.astype(jnp.float32), 0)
    up_grad = jnp.einsum("nd,nf->df", normed_low, pre_grad, preferred_element_type=jnp.float32)
    normed_grad = jnp.einsum("nf,df->nd", pre_grad, up_weight, preferred_element_type=jnp.float32)
    out_grad = jnp.einsum("nd,ne->de", attended_flat, grad_low, preferred_element_type=jnp.float32)
    attended_grad = jnp.einsum(
        "ne,de->nd", grad_low, out_weight, preferred_element_type=jnp.float32
    )
    attended_grad = attended_grad.astype(jnp.bfloat16).reshape(row_count, seg_length, features)
    grad_heads = lax.all_to_all(attended_grad, "seq", split_axis=2, concat_axis=1, tiled=True)

    def attend_back(row_args):
        query_row, key_row, value_row, grad_row, log_row = row_args
        key_rows = key_row.reshape(full_length, local_heads, head_size)
        value_rows = value_row.reshape(full_length, local_heads, head_size)
        keys_total = jnp.zeros((full_length, local_heads, head_size), jnp.float32)
        values_total = jnp.zeros((full_length, local_heads, head_size), jnp.float32)
        query_parts = []
        for block_index in range(block_count):
            block_start = block_index * block_rows
            query_block = query_row[block_start : block_start + block_rows].reshape(
                block_rows, local_heads, head_size
            )
            grad_block = grad_row[block_start : block_start + block_rows].reshape(
                block_rows, local_heads, head_size
            )
            logits = scores_for(query_block, key_rows, block_start)
            probs_full = jnp.exp(logits - log_row[:, block_start : block_start + block_rows, None])
            prob_low = probs_full.astype(jnp.bfloat16)
            probs_grad = jnp.einsum(
                "qhd,khd->hqk", grad_block, value_rows, preferred_element_type=jnp.float32
            )
            inner_sum = jnp.sum(probs_full * probs_grad, -1, keepdims=True)
            scores_grad = (probs_full * (probs_grad - inner_sum)).astype(jnp.bfloat16)
            values_total = values_total + jnp.einsum(
                "hqk,qhd->khd", prob_low, grad_block, preferred_element_type=jnp.float32
            )
            query_grad = (
                jnp.einsum(
                    "hqk,khd->qhd", scores_grad, key_rows, preferred_element_type=jnp.float32
                )
                * score_scale
            )
            query_parts.append(query_grad.reshape(block_rows, slab_width).astype(jnp.bfloat16))
            keys_total = (
                keys_total
                + jnp.einsum(
                    "hqk,qhd->khd", scores_grad, query_block, preferred_element_type=jnp.float32
                )
                * score_scale
            )
        return (
            jnp.concatenate(query_parts, 0),
            keys_total.reshape(full_length, slab_width).astype(jnp.bfloat16),
            values_total.reshape(full_length, slab_width).astype(jnp.bfloat16),
        )

    query_grad_heads, key_grad_heads, value_grad_heads = lax.map(
        attend_back, (query_heads, key_heads, value_heads, grad_heads, log_sums)
    )
    query_grad_pos, key_grad_pos, value_grad_pos = (
        lax.all_to_all(
            for_sending(query_grad_heads), "seq", split_axis=1, concat_axis=2, tiled=True
        ).astype(query_grad_heads.dtype),
        lax.all_to_all(
            for_sending(key_grad_heads), "seq", split_axis=1, concat_axis=2, tiled=True
        ).astype(key_grad_heads.dtype),
        lax.all_to_all(
            for_sending(value_grad_heads), "seq", split_axis=1, concat_axis=2, tiled=True
        ).astype(value_grad_heads.dtype),
    )
    projected_grad = jnp.concatenate(
        [
            rotate_back(query_grad_pos.astype(jnp.float32), cosine, sine_term),
            rotate_back(key_grad_pos.astype(jnp.float32), cosine, sine_term),
            value_grad_pos.astype(jnp.float32),
        ],
        -1,
    )
    projected_grad = projected_grad.astype(jnp.bfloat16).reshape(token_count, 3 * features)
    qkv_grad = jnp.einsum(
        "nd,ne->de", normed_low, projected_grad, preferred_element_type=jnp.float32
    )
    normed_grad = normed_grad + jnp.einsum(
        "ne,de->nd", projected_grad, qkv_weight, preferred_element_type=jnp.float32
    )
    gain_grad = jnp.sum(normed_grad * normed_hat, 0)
    bias_grad = jnp.sum(normed_grad, 0)
    scaled_grad = normed_grad * gain_f32
    hat_grad = (
        scaled_grad
        - jnp.mean(scaled_grad, -1, keepdims=True)
        - normed_hat * jnp.mean(scaled_grad * normed_hat, -1, keepdims=True)
    )
    input_grad = (grad_f32 + inv_std * hat_grad).reshape(row_count, seg_length, features)
    row_sums = jnp.sum(input_grad, 1)
    family_grad = jnp.einsum(
        "rf,rd->fd", family_hot.astype(jnp.float32), row_sums, precision=lax.Precision.HIGHEST
    )
    orient_grad = jnp.einsum(
        "rf,rd->fd", orient_hot.astype(jnp.float32), row_sums, precision=lax.Precision.HIGHEST
    )
    gain_sum, bias_sum, up_bias_sum, down_bias_sum, family_sum, orient_sum = lax.psum(
        (gain_grad, bias_grad, up_bias_grad, down_bias_grad, family_grad, orient_grad),
        ("dp", "seq"),
    )
    qkv_sum, out_sum, up_sum, down_sum = (
        lax.psum_scatter(qkv_grad, ("dp", "seq"), scatter_dimension=0, tiled=True),
        lax.psum_scatter(out_grad, ("dp", "seq"), scatter_dimension=0, tiled=True),
        lax.psum_scatter(up_grad, ("dp", "seq"), scatter_dimension=0, tiled=True),
        lax.psum_scatter(down_grad, ("dp", "seq"), scatter_dimension=0, tiled=True),
    )
    return (
        layer_out,
        input_grad,
        gain_sum,
        bias_sum,
        qkv_sum,
        out_sum,
        up_sum,
        up_bias_sum,
        down_sum,
        down_bias_sum,
        family_sum,
        orient_sum,
    )


def dot_nn(a, b):
    return lax.dot_general(a, b, (((1,), (0,)), ((), ())), preferred_element_type=F32)


def dot_nt(a, b):
    return lax.dot_general(a, b, (((1,), (1,)), ((), ())), preferred_element_type=F32)


def dot_tn(a, b):
    return lax.dot_general(a, b, (((0,), (0,)), ((), ())), preferred_element_type=F32)


def params(**more):
    return pltpu.CompilerParams(vmem_limit_bytes=VMEM_LIMIT, **more)


def cost(flops, moved, exps=0):
    return pl.CostEstimate(flops=flops, bytes_accessed=moved, transcendentals=exps)


def whole(shape):
    return pl.BlockSpec(shape, lambda *_: (0,) * len(shape), pipeline_mode=pl.Buffered(1))


def table_row(table, wanted):
    rows = lax.broadcasted_iota(jnp.int32, table.shape, 0)
    return jnp.sum(jnp.where(rows == wanted, table[...].astype(F32), 0.0), 0, keepdims=True)


def normalise(entries):
    centred = entries - jnp.mean(entries, -1, keepdims=True)
    inv_std = lax.rsqrt(jnp.mean(centred * centred, -1, keepdims=True) + 1e-05)
    return centred * inv_std, inv_std


GELU_C = math.sqrt(2.0 / math.pi)


def gelu_both(z):
    square = z * z
    t = jnp.tanh(GELU_C * z * (1.0 + 0.044715 * square))
    half = 0.5 * (1.0 + t)
    slope = half + (0.5 * GELU_C) * z * (1.0 - t * t) * (1.0 + (3 * 0.044715) * square)
    return z * half, slope


def ffn_kernel(rows, ids, hid, cot, fam, ori, gain, bias, wup, bup, wdn, norm, both, bupg, bdng):
    tokens = hid.shape[0]
    seg = tokens // rows
    step = 256

    @pl.when(pl.program_id(0) == 0)
    def _():
        total = jnp.zeros((1, cot.shape[1]), F32)
        for row in range(rows):
            emb = table_row(fam, ids[0]) + table_row(ori, ids[1 + row])
            for start in range(row * seg, (row + 1) * seg, step):
                part = pl.ds(start, step)
                hat, _ = normalise(hid[part, :].astype(F32) + emb)
                norm[part, :] = (hat * gain[...].astype(F32) + bias[...].astype(F32)).astype(BF16)
                total = total + jnp.sum(cot[part, :].astype(F32), 0, keepdims=True)
        bdng[...] = total

    total = jnp.zeros((1, wup.shape[1]), F32)
    for start in range(0, tokens, step):
        part = pl.ds(start, step)
        z = dot_nn(norm[part, :], wup[...]) + bup[...].astype(F32)
        into = dot_nt(cot[part, :], wdn[...])
        value, slope = gelu_both(z)
        both[0, part, :] = value.astype(BF16)
        low = (into * slope).astype(BF16)
        both[1, part, :] = low
        total = total + jnp.sum(low.astype(F32), 0, keepdims=True)
    bupg[...] = total


def ffn_forward(ids, hid, cot, fam, ori, gain, bias, wup, bup, wdn, rows):
    tokens, d = hid.shape
    ff = wup.shape[1]
    tile = 512
    return pl.pallas_call(
        functools.partial(ffn_kernel, rows),
        grid_spec=pltpu.PrefetchScalarGridSpec(
            num_scalar_prefetch=1,
            grid=(ff // tile,),
            in_specs=[
                whole((tokens, d)),
                whole((tokens, d)),
                whole(fam.shape),
                whole(ori.shape),
                whole((1, d)),
                whole((1, d)),
                pl.BlockSpec((d, tile), lambda i, s: (0, i)),
                pl.BlockSpec((1, tile), lambda i, s: (0, i)),
                pl.BlockSpec((tile, d), lambda i, s: (i, 0)),
            ],
            out_specs=[
                whole((tokens, d)),
                pl.BlockSpec((2, tokens, tile), lambda i, s: (0, 0, i)),
                pl.BlockSpec((1, tile), lambda i, s: (0, i)),
                whole((1, d)),
            ],
        ),
        out_shape=[
            jax.ShapeDtypeStruct((tokens, d), BF16),
            jax.ShapeDtypeStruct((2, tokens, ff), BF16),
            jax.ShapeDtypeStruct((1, ff), F32),
            jax.ShapeDtypeStruct((1, d), F32),
        ],
        compiler_params=params(),
        cost_estimate=cost(4 * tokens * d * ff, 4 * tokens * ff + 4 * d * ff, tokens * ff),
        name="ffn_forward",
    )(ids, hid, cot, fam, ori, gain, bias, wup, bup, wdn)


def turn(entries, cosine, sine):
    even = lax.broadcasted_iota(jnp.int32, entries.shape, 1) % 2 == 0
    other = jnp.where(even, pltpu.roll(entries, 127, 1), pltpu.roll(entries, 1, 1))
    return entries * cosine + other * sine


def turn_back(entries, cosine, sine):
    even = lax.broadcasted_iota(jnp.int32, entries.shape, 1) % 2 == 0
    side = entries * sine
    other = jnp.where(even, pltpu.roll(side, 127, 1), pltpu.roll(side, 1, 1))
    return entries * cosine + other


def attend(head_size, query_ref, k_ref, v_ref, g_ref, cos, sin, o_ref, dq_ref, dk_ref, dv_ref, dkt, dvt):
    full = query_ref.shape[0]
    block = 256
    scale = head_size ** (-0.5)
    lane = lax.broadcasted_iota(jnp.int32, (block, 128), 1)
    below = lax.broadcasted_iota(jnp.int32, (block, block), 0) >= lax.broadcasted_iota(
        jnp.int32, (block, block), 1
    )
    dkt[...] = jnp.zeros_like(dkt)
    dvt[...] = jnp.zeros_like(dvt)
    for start in range(0, full, block):
        part = pl.ds(start, block)
        end = start + block
        query = query_ref[part, :]
        grad = g_ref[part, :]
        out = None
        dq = None
        for head in range(128 // head_size):
            mine = (lane >= head * head_size) & (lane < (head + 1) * head_size)
            qm = jnp.where(mine, query.astype(F32) * scale, 0.0).astype(BF16)
            gm = jnp.where(mine, grad.astype(F32), 0.0).astype(BF16)
            scores = dot_nt(qm, k_ref[0:end, :])
            last = jnp.where(below, scores[:, start:end], -1e30)
            scores = last if start == 0 else jnp.concatenate([scores[:, :start], last], 1)
            weights = jnp.exp(scores - jnp.max(scores, -1, keepdims=True))
            probs = weights * (1.0 / jnp.sum(weights, -1, keepdims=True))
            low = probs.astype(BF16)
            piece = dot_nn(low, v_ref[0:end, :])
            out = piece if out is None else jnp.where(mine, piece, out)
            pg = dot_nt(gm, v_ref[0:end, :])
            inner = jnp.sum(probs * pg, -1, keepdims=True)
            sg = (probs * (pg - inner)).astype(BF16)
            piece = dot_nn(sg, k_ref[0:end, :])
            dq = piece if dq is None else jnp.where(mine, piece, dq)
            dkt[:, 0:end] += dot_tn(qm, sg)
            dvt[:, 0:end] += dot_tn(gm, low)
        o_ref[part, :] = out.astype(BF16)
        dq_ref[part, :] = turn_back(dq * scale, cos[part, :], sin[part, :]).astype(BF16)
    for start in range(0, full, block):
        part = pl.ds(start, block)
        dk = dkt[:, start : start + block].T
        dk_ref[part, :] = turn_back(dk, cos[part, :], sin[part, :]).astype(BF16)
        dv_ref[part, :] = dvt[:, start : start + block].T.astype(BF16)


def events_for(tiles, pairs):
    first = 4 * tiles
    return {
        0: [(0, 0), (2, 0), (3, 0)],
        first + 1: [(0, 1), (1, 0), (2, 1), (3, 1)],
        first + 3: [(0, 2), (3, 2)],
        first + 5: [(1, 1), (2, 2), (0, 3), (3, 3)],
        first + 6: [(1, 2), (2, 3), (0, 4), (3, 4)],
        first + 7: [(1, 3), (2, 4)],
        first + 8: [(1, 4)],
    }


def middle_kernel(tiles, pairs, head_size, bits, orders, *refs):
    ids, own, far, cown, cfar, fam, ori, gain, bias, wqkv, wout, cos, sin = refs[:13]
    near_up, far_up, near_down, far_down = refs[13:17]
    norm, cot, o_ref, dq_ref, dk_ref, dv_ref, far_att, up_out, down_out = refs[17:26]
    heads, dkt, dvt, att_send, att_got, att_sems = refs[26:32]
    seg = own.shape[0]
    step = 256
    i = pl.program_id(0)
    me = lax.axis_index("seq")
    mine = device_bits(bits + 1)
    up_half = up_out.shape[1] // 2
    down_half = down_out.shape[1] // 2
    chunks = chunks_from(
        refs[32:],
        bits,
        mine,
        [
            (orders[0], near_up, far_up, pl.ds(0, up_half), up_out),
            (orders[1], near_up, far_up, pl.ds(up_half, up_half), up_out),
            (orders[2], near_down, far_down, pl.ds(0, down_half), down_out),
            (orders[3], near_down, far_down, pl.ds(down_half, down_half), down_out),
        ],
    )

    def happen(events):
        for chunk, stage in events:
            chunks[chunk].happen(stage)

    @pl.when(i == 0)
    def _():
        meet([partner_along(axis, mine) for axis in orders[0]])

    events = events_for(tiles, pairs)
    last = 4 * tiles + pairs
    for when, what in events.items():
        if when < last:

            @pl.when(i == when)
            def _():
                happen(what)

    @pl.when(i == 0)
    def _():
        emb = table_row(fam, ids[0]) + table_row(ori, ids[1])
        for source, csource, where in ((own, cown, me), (far, cfar, 1 - me)):
            for start in range(0, seg, step):
                part = pl.ds(start, step)
                there = pl.ds(pl.multiple_of(where * seg + start, step), step)
                hat, _ = normalise(source[part, :].astype(F32) + emb)
                norm[there, :] = (hat * gain[...].astype(F32) + bias[...].astype(F32)).astype(BF16)
                cot[there, :] = csource[part, :]

    lanes = wqkv.shape[1] // 128

    def att_crossing(pair):
        return remote(
            att_send.at[pair],
            att_got.at[pair],
            att_sems.at[0, pair],
            att_sems.at[1, pair],
            partner_along("seq", mine),
        )

    @pl.when(i < 2 * tiles)
    def _():
        for start in range(0, 2 * seg, step):
            part = pl.ds(start, step)
            lin = dot_nn(norm[part, :], wqkv[...])
            for lane in range(lanes):
                piece = turn(lin[:, lane * 128 : (lane + 1) * 128], cos[part, :], sin[part, :])
                heads[i * lanes + lane, part, :] = piece.astype(BF16)

    @pl.when((i >= 2 * tiles) & (i < 3 * tiles))
    def _():
        for start in range(0, 2 * seg, step):
            part = pl.ds(start, step)
            lin = dot_nn(norm[part, :], wqkv[...]).astype(BF16)
            for lane in range(lanes):
                heads[i * lanes + lane, part, :] = lin[:, lane * 128 : (lane + 1) * 128]

    @pl.when((i >= 3 * tiles) & (i < 4 * tiles))
    def _():
        for start in range(0, 2 * seg, step):
            part = pl.ds(start, step)
            lin = dot_nt(cot[part, :], wout[...]).astype(BF16)
            for lane in range(lanes):
                heads[i * lanes + lane, part, :] = lin[:, lane * 128 : (lane + 1) * 128]

    @pl.when(i >= 4 * tiles)
    def _():
        pair = i - 4 * tiles
        attend(
            head_size,
            heads.at[pair],
            heads.at[pairs + pair],
            heads.at[2 * pairs + pair],
            heads.at[3 * pairs + pair],
            cos,
            sin,
            o_ref,
            dq_ref,
            dk_ref,
            dv_ref,
            dkt,
            dvt,
        )
        att_send[pair] = o_ref[pl.ds(pl.multiple_of((1 - me) * seg, seg), seg), :]
        att_crossing(pair).start()

    @pl.when(i == last - 1)
    def _():
        for pair in range(pairs):
            att_crossing(pair).wait()
            far_att[:, pair * 128 : (pair + 1) * 128] = att_got[pair]
        happen(events[last])


def middle(ids, own, far, cown, cfar, fam, ori, gain, bias, wqkv, wout, cos, sin, up, down, orders, head_size, collective):
    seg, d = own.shape
    full = 2 * seg
    tile = 512
    tiles = d // tile
    pairs = d // 128
    bits = len(orders[0])
    near_up, far_up = up
    near_down, far_down = down
    up_size, ff = near_up.shape[1:]
    down_size = near_down.shape[1]
    smem = pl.BlockSpec(memory_space=pltpu.SMEM)
    anywhere = pl.BlockSpec(memory_space=pl.ANY)
    head_out = pl.BlockSpec((full, 128), lambda i: (0, jnp.maximum(i - 4 * tiles, 0)))
    rows = jax.ShapeDtypeStruct((full, d), BF16)
    return pl.pallas_call(
        functools.partial(middle_kernel, tiles, pairs, head_size, bits, orders),
        grid=(4 * tiles + pairs,),
        in_specs=[
            smem,
            whole((seg, d)),
            whole((seg, d)),
            whole((seg, d)),
            whole((seg, d)),
            whole(fam.shape),
            whole(ori.shape),
            whole((1, d)),
            whole((1, d)),
            pl.BlockSpec((d, tile), lambda i: (0, jnp.minimum(i, 3 * tiles - 1))),
            pl.BlockSpec((tile, d), lambda i: (jnp.clip(i - 3 * tiles, 0, tiles - 1), 0)),
            whole((full, 128)),
            whole((full, 128)),
        ]
        + [anywhere] * 4,
        out_specs=[
            whole((full, d)),
            whole((full, d)),
            head_out,
            head_out,
            head_out,
            head_out,
            whole((seg, d)),
            whole((up_size, ff)),
            whole((down_size, d)),
        ],
        out_shape=[
            rows,
            rows,
            rows,
            rows,
            rows,
            rows,
            jax.ShapeDtypeStruct((seg, d), BF16),
            jax.ShapeDtypeStruct((up_size, ff), F32),
            jax.ShapeDtypeStruct((down_size, d), F32),
        ],
        scratch_shapes=[
            pltpu.VMEM((4 * pairs, full, 128), BF16),
            pltpu.VMEM((128, full), F32),
            pltpu.VMEM((128, full), F32),
            pltpu.VMEM((pairs, seg, 128), BF16),
            pltpu.VMEM((pairs, seg, 128), BF16),
            pltpu.SemaphoreType.DMA((2, pairs)),
        ]
        + chunk_scratch(orders[0], up_size, ff // 2)
        + chunk_scratch(orders[1], up_size, ff // 2)
        + chunk_scratch(orders[2], down_size, d // 2)
        + chunk_scratch(orders[3], down_size, d // 2),
        compiler_params=params(collective_id=collective, has_side_effects=True),
        cost_estimate=cost(8 * full * d * d + 12 * full * full * d, 8 * d * d + 18 * full * d, full * full * H),
        name="middle",
    )(ids, own, far, cown, cfar, fam, ori, gain, bias, wqkv, wout, cos, sin, near_up, far_up, near_down, far_down)


def device_bits(bits):
    dp = lax.axis_index("dp")
    found = {bit: lax.rem(dp // (1 << bit), 2) for bit in range(bits)}
    found["seq"] = lax.axis_index("seq")
    return found


def block_place(axes, mine, upper, seq):
    place = 0
    for axis in axes:
        bit = seq if axis == "seq" else (upper >> (axis - 1)) & 1
        place = 2 * place + (1 - mine[axis] if bit else mine[axis])
    return place


def other_core():
    dp = lax.axis_index("dp")
    return (dp + 1 - 2 * lax.rem(dp, 2), lax.axis_index("seq"))


def meet(partners):
    barrier = pltpu.get_barrier_semaphore()
    for partner in partners:
        pl.semaphore_signal(barrier, inc=1, device_id=partner, device_id_type=MESH)
    pl.semaphore_wait(barrier, len(partners))


def remote(src, dst, send_sem, recv_sem, partner):
    return pltpu.make_async_remote_copy(
        src_ref=src,
        dst_ref=dst,
        send_sem=send_sem,
        recv_sem=recv_sem,
        device_id=partner,
        device_id_type=MESH,
    )


def split_blocks(value, keep, send, size, core, places):
    for index, there in enumerate(places):
        up, seq = index // 2, index % 2
        first = (4 * up + seq) * size
        second = first + 2 * size
        a = value[first : first + size, :].astype(BF16)
        b = value[second : second + size, :].astype(BF16)
        keep[there] = jnp.where(core == 0, a, b)
        send[there] = jnp.where(core == 0, b, a)


def add_into(keep, got):
    for index in range(keep.shape[0]):
        keep[index] = (keep[index].astype(F32) + got[index].astype(F32)).astype(BF16)


def wide_grad_kernel(bits, counts, orders, firsts, *refs):
    lefts, rights = refs[: len(counts)], refs[len(counts) : 2 * len(counts)]
    near_out, far_out, turned, keep, send, got, send_sem, recv_sem, out_sem = refs[2 * len(counts) :]
    steps = sum(counts)
    i = pl.program_id(0)
    mine = device_bits(bits)
    partner = other_core()
    blocks = keep.shape[1]
    size = keep.shape[2]
    tile = keep.shape[3]

    def crossing(step):
        return remote(send.at[step], got.at[step], send_sem.at[step], recv_sem.at[step], partner)

    def stores(step):
        columns = pl.ds(pl.multiple_of(step * tile, tile), tile)
        half = blocks // 2
        return (
            pltpu.make_async_copy(
                keep.at[step, pl.ds(0, half)], near_out.at[:, :, columns], out_sem.at[0, step]
            ),
            pltpu.make_async_copy(
                keep.at[step, pl.ds(half, half)], far_out.at[:, :, columns], out_sem.at[1, step]
            ),
        )

    @pl.when(i == 0)
    def _():
        meet([partner])

    start = 0
    for left, right, count, axes, first in zip(lefts, rights, counts, orders, firsts):
        places = [block_place(axes, mine, up, seq) for up in range(blocks // 2) for seq in range(2)]
        if first:

            @pl.when(i == start)
            def _():
                turned[...] = left[...].T

        @pl.when((i >= start) & (i < start + count))
        def _():
            value = dot_nn(turned[...], right[...])
            split_blocks(value, keep.at[i], send.at[i], size, mine[0], places)
            crossing(i).start()

        start += count

    def finish(step):
        crossing(step).wait()
        add_into(keep.at[step], got.at[step])
        for copy in stores(step):
            copy.start()

    @pl.when(i > 0)
    def _():
        finish(i - 1)

    @pl.when(i == steps - 1)
    def _():
        finish(i)
        for step in range(steps):
            for copy in stores(step):
                copy.wait()


def wide_grad(entries, tile, collective):
    tokens, d = entries[0][0].shape
    bits = len(entries[0][4])
    blocks = 1 << bits
    size = d // (2 * blocks)
    counts = [entry[3] for entry in entries]
    orders = [entry[4] for entry in entries]
    firsts = [index == 0 or entries[index][0] is not entries[index - 1][0] for index in range(len(entries))]
    steps = sum(counts)
    specs = []
    start = 0
    for entry in entries:

        def at(i, start=start, offset=entry[2], last=entry[3] - 1):
            return (1, 0, offset + jnp.clip(i - start, 0, last))

        specs.append(pl.BlockSpec((None, tokens, tile), at))
        start += entry[3]
    shape = jax.ShapeDtypeStruct((blocks // 2, size, steps * tile), BF16)
    anywhere = pl.BlockSpec(memory_space=pl.ANY)
    buffers = pltpu.VMEM((steps, blocks, size, tile), BF16)
    return pl.pallas_call(
        functools.partial(wide_grad_kernel, bits, counts, orders, firsts),
        grid=(steps,),
        in_specs=[whole((tokens, d)) for _ in entries] + specs,
        out_specs=[anywhere, anywhere],
        out_shape=[shape, shape],
        scratch_shapes=[
            pltpu.VMEM((d, tokens), BF16),
            buffers,
            buffers,
            buffers,
            pltpu.SemaphoreType.DMA((steps,)),
            pltpu.SemaphoreType.DMA((steps,)),
            pltpu.SemaphoreType.DMA((2, steps)),
        ],
        compiler_params=params(collective_id=collective, has_side_effects=True),
        cost_estimate=cost(2 * tokens * d * steps * tile, 4 * tokens * (d + steps * tile)),
        name="wide_grad",
    )(*[entry[0] for entry in entries], *[entry[1] for entry in entries])


def tall_grad_kernel(bits, orders, left, right, near_out, far_out, keep, send, got, send_sem, recv_sem, out_sem):
    i = pl.program_id(0)
    steps, _, size, d = keep.shape
    width = d // len(orders)
    mine = device_bits(bits)
    partner = other_core()
    half = steps

    def crossing(step):
        return remote(send.at[step], got.at[step], send_sem.at[step], recv_sem.at[step], partner)

    def store(step, seq, act):
        for part, axes in enumerate(orders):
            place = 0
            for axis in axes:
                if axis == "seq":
                    apart = lax.rem(mine["seq"] + seq, 2)
                else:
                    apart = lax.rem(step // (1 << (axis - 1)) + mine[axis], 2)
                place = 2 * place + apart
            columns = pl.ds(part * width, width)
            source = keep.at[step, seq, :, columns]
            sem = out_sem.at[step, seq, part]
            there = lax.rem(place, half)

            @pl.when(place < half)
            def _():
                act(pltpu.make_async_copy(source, near_out.at[there, :, columns], sem))

            @pl.when(place >= half)
            def _():
                act(pltpu.make_async_copy(source, far_out.at[there, :, columns], sem))

    @pl.when(i == 0)
    def _():
        meet([partner])

    value = dot_nn(left[...].T, right[...])
    split_blocks(value, keep.at[i], send.at[i], size, mine[0], [0, 1])
    crossing(i).start()

    def finish(step):
        crossing(step).wait()
        add_into(keep.at[step], got.at[step])
        for seq in range(2):
            store(step, seq, lambda copy: copy.start())

    @pl.when(i > 0)
    def _():
        finish(i - 1)

    @pl.when(i == steps - 1)
    def _():
        finish(i)
        for step in range(steps):
            for seq in range(2):
                store(step, seq, lambda copy: copy.wait())


def tall_grad(orders, left, right, collective):
    _, tokens, m = left.shape
    d = right.shape[1]
    bits = len(orders[0])
    steps = 1 << (bits - 1)
    tile = m // steps
    size = tile // 4
    shape = jax.ShapeDtypeStruct((steps, size, d), BF16)
    anywhere = pl.BlockSpec(memory_space=pl.ANY)
    buffers = pltpu.VMEM((steps, 2, size, d), BF16)
    return pl.pallas_call(
        functools.partial(tall_grad_kernel, bits, orders),
        grid=(steps,),
        in_specs=[pl.BlockSpec((None, tokens, tile), lambda i: (0, 0, i)), whole((tokens, d))],
        out_specs=[anywhere, anywhere],
        out_shape=[shape, shape],
        scratch_shapes=[
            buffers,
            buffers,
            buffers,
            pltpu.SemaphoreType.DMA((steps,)),
            pltpu.SemaphoreType.DMA((steps,)),
            pltpu.SemaphoreType.DMA((steps, 2, len(orders))),
        ],
        compiler_params=params(collective_id=collective, has_side_effects=True),
        cost_estimate=cost(2 * tokens * d * m, 2 * (tokens * m + d * m + tokens * d)),
        name="tall_grad",
    )(left, right)


def partner_along(axis, mine):
    dp = lax.axis_index("dp")
    seq = lax.axis_index("seq")
    if axis == "seq":
        return (dp, 1 - seq)
    return (dp + (1 - 2 * mine[axis]) * (1 << axis), seq)


class Chunk:
    def __init__(self, axes, mine, near, far, columns, out, keep, got, near_sem, send_sem, recv_sem):
        self.axes, self.mine, self.near, self.far = axes, mine, near, far
        self.columns, self.out, self.keep, self.got = columns, out, keep, got
        self.near_sem, self.send_sem, self.recv_sem = near_sem, send_sem, recv_sem

    def load(self):
        return pltpu.make_async_copy(self.near.at[:, :, self.columns], self.keep, self.near_sem)

    def crossing(self, stage):
        count = (1 << len(self.axes)) >> (stage + 1)
        if stage == 0 and self.far is not None:
            source = self.far.at[:, :, self.columns]
        else:
            source = self.keep.at[pl.ds(count, count)]
        return remote(
            source,
            self.got[stage],
            self.send_sem.at[stage],
            self.recv_sem.at[stage],
            partner_along(self.axes[stage], self.mine),
        )

    def begin(self):
        if self.near is not None:
            self.load().start()
        self.crossing(0).start()

    def advance(self, stage):
        if stage == 1 and self.near is not None:
            self.load().wait()
        self.crossing(stage - 1).wait()
        count = (1 << len(self.axes)) >> stage

        def add(index, carry):
            self.keep[index] = (self.keep[index].astype(F32) + self.got[stage - 1][index].astype(F32)).astype(BF16)
            return carry

        lax.fori_loop(0, count, add, 0)
        self.crossing(stage).start()

    def finish(self):
        last = len(self.axes) - 1
        self.crossing(last).wait()
        self.out[:, self.columns] = self.keep[0].astype(F32) + self.got[last][0].astype(F32)

    def happen(self, stage):
        if stage == 0:
            self.begin()
        elif stage == len(self.axes):
            self.finish()
        else:
            self.advance(stage)


def chunk_scratch(axes, size, width, farther=False):
    half = 1 << (len(axes) - 1)
    return (
        [pltpu.VMEM((2 * half if farther else half, size, width), BF16)]
        + [pltpu.VMEM((half >> stage, size, width), BF16) for stage in range(len(axes))]
        + [
            pltpu.SemaphoreType.DMA,
            pltpu.SemaphoreType.DMA((len(axes),)),
            pltpu.SemaphoreType.DMA((len(axes),)),
        ]
    )


def chunks_from(refs, bits, mine, wanted):
    stages = bits
    found = []
    each = 1 + stages + 3
    for index, (axes, near, far, columns, out) in enumerate(wanted):
        part = refs[index * each : (index + 1) * each]
        found.append(
            Chunk(axes, mine, near, far, columns, out, part[0], part[1 : 1 + stages], *part[1 + stages :])
        )
    return found


def after(entry, *others):
    return lax.optimization_barrier((entry, *others))[0]


TAIL_TILE = 512
TAIL_STEP = 256


def tail_events(sums_at):
    return {
        2: [(0, 1)],
        3: [(1, 1)],
        4: [(2, 1)],
        6: [(3, 1)],
        9: [(0, 2), (1, 2)],
        16: [(0, 3), (1, 3), (2, 2), (3, 2)],
        22: [(0, 4), (1, 4), (2, 3), (3, 3)],
        27: [(2, 4), (3, 4), (0, 5), (1, 5)],
        sums_at + 1: [(2, 5), (3, 5)],
    }


def tail_kernel(bits, orders, rows, marks, *refs):
    ids, norm_hbm, att_hbm, cot_hbm, dq_hbm, dk_hbm, dv_hbm, wqkv_hbm, wout_hbm = refs[:9]
    fam, ori, gain, bdn, bup_part, bdn_part, far_att = refs[9:16]
    both, wdn, wup, hid, cot = refs[16:21]
    layer_out, input_out, qkv_out, out_out, sums_out, all_out = refs[21:27]
    left, right, dq, dk, dv, wqkv, wout, turned, acc, ng_send, ng_own, ng_got = refs[27:39]
    gg, bg, rg, load_sem, ng_sem, held, got, vec, vgot, table, ssem, rsem, gsend, grecv = refs[39:53]
    out_start, out_end, in_start, in_end, sums_at = marks
    i = pl.program_id(0)
    me = lax.axis_index("seq")
    dp = lax.axis_index("dp")
    mine = device_bits(bits)
    d = left.shape[1]
    seg = ng_own.shape[0]
    step = TAIL_STEP
    per_row = seg // step
    chunks = chunks_from(
        refs[53:],
        len(orders[0]),
        mine,
        [
            (orders[0], None, None, pl.ds(0, d), qkv_out),
            (orders[1], None, None, pl.ds(d, d), qkv_out),
            (orders[2], None, None, pl.ds(2 * d, d), qkv_out),
            (orders[3], None, None, pl.ds(0, d), out_out),
        ],
    )
    loads = {
        name: pltpu.make_async_copy(source, there, load_sem.at[index])
        for index, (name, source, there) in enumerate(
            (
                ("norm", norm_hbm, left),
                ("dq", dq_hbm, dq),
                ("dk", dk_hbm, dk),
                ("dv", dv_hbm, dv),
                ("wqkv", wqkv_hbm, wqkv),
                ("cot", cot_hbm, right),
                ("wout", wout_hbm, wout),
                ("att", att_hbm, left),
            )
        )
    }
    partners = [partner_along(axis, mine) for axis in ["seq"] + list(range(bits))]

    def gradient(index, operand):
        chunk = chunks[index]
        size = chunk.keep.shape[1]
        value = dot_nn(turned[...], operand[...])
        for block in range(chunk.keep.shape[0]):
            place = 0
            for axis in orders[index]:
                bit = block & 1 if axis == "seq" else (block >> (axis + 1)) & 1
                place = 2 * place + (1 - mine[axis] if bit else mine[axis])
            chunk.keep[place] = value[block * size : (block + 1) * size, :].astype(BF16)
        chunk.begin()

    def back_into(there, half):
        for start in range(0, seg, step):
            part = pl.ds(pl.multiple_of(half * seg + start, step), step)
            total = dot_nt(dq[part, :], wqkv[:, 0:d])
            total = total + dot_nt(dk[part, :], wqkv[:, d : 2 * d])
            total = total + dot_nt(dv[part, :], wqkv[:, 2 * d : 3 * d])
            there[start : start + step, :] = total.astype(BF16)

    ng_crossing = remote(ng_send, ng_got, ng_sem.at[0], ng_sem.at[1], partners[0])

    @pl.when(i == 0)
    def _():
        for name in ("norm", "dq", "dk", "dv", "wqkv", "cot", "wout"):
            loads[name].start()
        meet(partners)
        loads["norm"].wait()
        turned[...] = left[...].T
        loads["att"].start()
        loads["dq"].wait()
        gradient(0, dq)

    for when, what in tail_events(sums_at).items():
        if when <= sums_at:

            @pl.when(i == when)
            def _():
                for chunk, stage in what:
                    chunks[chunk].happen(stage)

    @pl.when(i == 1)
    def _():
        loads["dk"].wait()
        gradient(1, dk)

    @pl.when(i == 2)
    def _():
        loads["dv"].wait()
        gradient(2, dv)

    @pl.when(i == 3)
    def _():
        loads["wqkv"].wait()
        back_into(ng_send, 1 - me)
        ng_crossing.start()

    @pl.when(i == 4)
    def _():
        loads["att"].wait()
        loads["cot"].wait()
        turned[...] = left[...].T
        gradient(3, right)

    @pl.when(i == 5)
    def _():
        back_into(ng_own, me)

    @pl.when((i >= out_start) & (i < out_end))
    def _():
        value = dot_nn(both[0], wdn[...])

        @pl.when(i == out_start)
        def _():
            acc[...] = value

        @pl.when(i > out_start)
        def _():
            acc[...] += value

    @pl.when((i >= in_start) & (i < in_end))
    def _():
        value = dot_nt(both[0], wup[...])

        @pl.when(i == in_start)
        def _():
            acc[...] = value

        @pl.when(i > in_start)
        def _():
            acc[...] += value

    @pl.when(i == out_end)
    def _():
        loads["wout"].wait()

    def home_block(index, own, far, own_offset):
        row = index // per_row
        within = pl.multiple_of(lax.rem(index, per_row) * step, step)
        there = pl.ds(pl.multiple_of(own_offset + within, step), step)
        return row, jnp.where(row == me, own[there, :], far[pl.ds(within, step), :])

    @pl.when((i >= out_end) & (i < in_start))
    def _():
        index = i - out_end
        row, att = home_block(index, left, far_att, me * seg)
        flag = jnp.where(row == 0, ids[1], ids[2])
        emb = table_row(fam, ids[0]) + table_row(ori, flag)
        part = pl.ds(pl.multiple_of(index * step, step), step)
        total = hid[...].astype(F32) + emb + dot_nn(att, wout[...])
        layer_out[...] = (total + (acc[part, :] + bdn[...].astype(F32))).astype(BF16)

    @pl.when(i == in_end)
    def _():
        ng_crossing.wait()
        gg[...] = jnp.zeros_like(gg)
        bg[...] = jnp.zeros_like(bg)
        rg[...] = jnp.zeros_like(rg)

    @pl.when((i >= in_end) & (i < sums_at))
    def _():
        index = i - in_end
        row, back = home_block(index, ng_own, ng_got, 0)
        flag = jnp.where(row == 0, ids[1], ids[2])
        emb = table_row(fam, ids[0]) + table_row(ori, flag)
        part = pl.ds(pl.multiple_of(index * step, step), step)
        hat, inv_std = normalise(hid[...].astype(F32) + emb)
        grad = acc[part, :] + back.astype(F32)
        gg[...] += jnp.sum(grad * hat, 0, keepdims=True)
        bg[...] += jnp.sum(grad, 0, keepdims=True)
        scaled = grad * gain[...].astype(F32)
        inner = (
            scaled
            - jnp.mean(scaled, -1, keepdims=True)
            - hat * jnp.mean(scaled * hat, -1, keepdims=True)
        )
        result = cot[...].astype(F32) + inv_std * inner
        input_out[...] = result
        sums = jnp.sum(result, 0, keepdims=True)
        which = lax.broadcasted_iota(jnp.int32, rg.shape, 0)
        rg[...] += jnp.where(which == flag, sums, 0.0)

    @pl.when(i == sums_at)
    def _():
        at = 0
        for source in (bup_part[...], bdn_part[...], gg[...], bg[...], rg[0:1, :], rg[1:2, :]):
            for lane in range(0, source.shape[1], 128):
                held[0, at : at + 1, :] = source[:, lane : lane + 128]
                at += 1
        both_rows = rg[0:1, :] + rg[1:2, :]
        for lane in range(0, d, 128):
            vec[lane // 128 : lane // 128 + 1, :] = both_rows[:, lane : lane + 128]
        extra = d // 128
        vec[extra:, :] = jnp.full((vec.shape[0] - extra, 128), 0.5, F32) * ids[0].astype(F32)
        for index, partner in enumerate(partners):
            main = remote(held.at[index], got.at[index], ssem.at[index], rsem.at[index], partner)
            main.start()
            if index == 0:
                side = remote(vec, vgot, gsend.at[0], grecv.at[0], partner)
            else:
                size = 1 << (index - 1)
                now = pl.ds(dp - lax.rem(dp, size), size)
                side = remote(table.at[now], table.at[now], gsend.at[index], grecv.at[index], partner)
            side.start()
            main.wait()
            total = held[index] + got[index]
            if index + 1 < len(partners):
                held[index + 1] = total
            else:
                sums_out[...] = total
            side.wait()
            if index == 0:
                table[dp] = vec[...] + vgot[...]
        all_out[...] = table[...]
        for chunk, stage in tail_events(sums_at)[sums_at + 1]:
            chunks[chunk].happen(stage)


def tail(ids, norm, att, row_cot, dq, dk, dv, wqkv, wout, fam, ori, gain, bdn, bup_part, bdn_part, far_att, both, wdn, wup, hid, cot, orders, rows, collective):
    tokens, d = hid.shape
    ff = wup.shape[1]
    bits = len(orders[0]) - 1
    count = 1 << bits
    seg = far_att.shape[0]
    tile, step = TAIL_TILE, TAIL_STEP
    tiles, blocks = ff // tile, tokens // step
    out_start = 6
    out_end = out_start + tiles
    in_start = out_end + blocks
    in_end = in_start + tiles
    sums_at = in_end + blocks
    marks = (out_start, out_end, in_start, in_end, sums_at)
    size = d // (2 * count)
    rounds = bits + 1
    lines = (ff + 5 * d) // 128
    vec_shape = (d // 128 + 8, 128)
    anywhere = pl.BlockSpec(memory_space=pl.ANY)

    def plane(i):
        late = i >= in_start
        return (late.astype(jnp.int32), 0, jnp.clip(jnp.where(late, i - in_start, i - out_start), 0, tiles - 1))

    def home(i):
        return (jnp.clip(jnp.where(i >= in_start, i - in_end, i - out_end), 0, blocks - 1), 0)

    square = pltpu.VMEM((tokens, d), BF16)
    piece = pltpu.VMEM((seg, d), BF16)
    row = pltpu.VMEM((1, d), F32)
    return pl.pallas_call(
        functools.partial(tail_kernel, bits, orders, rows, marks),
        grid=(sums_at + 1,),
        in_specs=[pl.BlockSpec(memory_space=pltpu.SMEM)]
        + [anywhere] * 8
        + [
            whole(fam.shape),
            whole(ori.shape),
            whole((1, d)),
            whole((1, d)),
            whole((1, ff)),
            whole((1, d)),
            whole((seg, d)),
            pl.BlockSpec((1, tokens, tile), plane),
            pl.BlockSpec((tile, d), lambda i: (jnp.clip(i - out_start, 0, tiles - 1), 0)),
            pl.BlockSpec((d, tile), lambda i: (0, jnp.clip(i - in_start, 0, tiles - 1))),
            pl.BlockSpec((step, d), home),
            pl.BlockSpec((step, d), lambda i: (jnp.clip(i - in_end, 0, blocks - 1), 0)),
        ],
        out_specs=[
            pl.BlockSpec((step, d), lambda i: (jnp.clip(i - out_end, 0, blocks - 1), 0)),
            pl.BlockSpec((step, d), lambda i: (jnp.clip(i - in_end, 0, blocks - 1), 0)),
            whole((size, 3 * d)),
            whole((size, d)),
            whole((lines, 128)),
            whole((count,) + vec_shape),
        ],
        out_shape=[
            jax.ShapeDtypeStruct((tokens, d), BF16),
            jax.ShapeDtypeStruct((tokens, d), F32),
            jax.ShapeDtypeStruct((size, 3 * d), F32),
            jax.ShapeDtypeStruct((size, d), F32),
            jax.ShapeDtypeStruct((lines, 128), F32),
            jax.ShapeDtypeStruct((count,) + vec_shape, F32),
        ],
        scratch_shapes=[
            square,
            square,
            square,
            square,
            square,
            pltpu.VMEM((d, 3 * d), BF16),
            pltpu.VMEM((d, d), BF16),
            pltpu.VMEM((d, tokens), BF16),
            pltpu.VMEM((tokens, d), F32),
            piece,
            piece,
            piece,
            row,
            row,
            pltpu.VMEM((2, d), F32),
            pltpu.SemaphoreType.DMA((8,)),
            pltpu.SemaphoreType.DMA((2,)),
            pltpu.VMEM((rounds, lines, 128), F32),
            pltpu.VMEM((rounds, lines, 128), F32),
            pltpu.VMEM(vec_shape, F32),
            pltpu.VMEM(vec_shape, F32),
            pltpu.VMEM((count,) + vec_shape, F32),
            pltpu.SemaphoreType.DMA((rounds,)),
            pltpu.SemaphoreType.DMA((rounds,)),
            pltpu.SemaphoreType.DMA((rounds,)),
            pltpu.SemaphoreType.DMA((rounds,)),
        ]
        + [entry for axes in orders for entry in chunk_scratch(axes, size, d, True)],
        compiler_params=pltpu.CompilerParams(
            vmem_limit_bytes=67043328, collective_id=collective, has_side_effects=True
        ),
        cost_estimate=cost(16 * tokens * d * d + 4 * tokens * d * ff, 8 * d * ff + 40 * tokens * d),
        name="tail",
    )(ids, norm, att, row_cot, dq, dk, dv, wqkv, wout, fam, ori, gain, bdn, bup_part, bdn_part, far_att, both, wdn, wup, hid, cot)


def body_by_rows(
    hidden_in,
    family,
    orient,
    norm_gain,
    norm_bias,
    qkv_weight,
    out_weight,
    up_weight,
    up_bias,
    down_weight,
    down_bias,
    family_table,
    orient_table,
    cotangent,
):
    rows, seg, d = hidden_in.shape
    ff = up_weight.shape[1]
    tokens = rows * seg
    full = 2 * seg
    dp_count = lax.axis_size("dp")
    bits = int(math.log2(dp_count))
    upper = dp_count // 2
    dp = lax.axis_index("dp")
    seq = lax.axis_index("seq")
    ring = [(0, 1), (1, 0)]

    def mine(pair):
        return lax.dynamic_index_in_dim(pair, seq, 0, keepdims=False)

    def theirs(pair):
        return lax.dynamic_index_in_dim(pair, 1 - seq, 0, keepdims=False)

    far_hidden = lax.ppermute(theirs(hidden_in), "seq", ring)
    far_cot = lax.ppermute(theirs(cotangent), "seq", ring)

    gain = norm_gain.reshape(1, d)
    bias = norm_bias.reshape(1, d)
    hid = hidden_in.reshape(tokens, d)
    cot = cotangent.reshape(tokens, d)
    ids = jnp.concatenate([family, orient])
    row_ids = jnp.stack([family[0], mine(orient)])

    zs = list(range(2, bits))
    order_a = [1] + zs + ["seq"]
    order_b = [1, "seq"] + zs
    order_c = ["seq", 1] + zs
    order_d = [2, "seq", 1] + zs[1:]
    order_e = [2, 1] + zs[1:] + ["seq"]
    late_orders = [[0] + order_a, [0] + order_e, [0] + order_a, [0] + order_e]
    ffn_orders = [order_a, order_b, order_c, order_d]

    normed, both, up_bias_part, down_bias_part = ffn_forward(
        ids, hid, cot, family_table, orient_table, gain, bias, up_weight, up_bias.reshape(1, ff), down_weight, rows
    )
    half_tiles = ff // 2048
    ready = after(normed, far_hidden)
    up = wide_grad([(ready, both, 0, half_tiles, order_a), (ready, both, half_tiles, half_tiles, order_b)], 1024, 1)
    down = tall_grad([order_c, order_d], both, after(cot, up[0], far_cot), 2)

    cosine, sine = rope_tables(jnp.arange(full).astype(F32), 128)
    row_normed, row_cot, att, dq, dk, dv, far_att, up_total, down_total = middle(
        row_ids,
        mine(hidden_in),
        far_hidden,
        mine(cotangent),
        far_cot,
        family_table,
        orient_table,
        gain,
        bias,
        qkv_weight,
        out_weight,
        cosine,
        sine,
        up,
        down,
        ffn_orders,
        d // H,
        3,
    )
    layer_out, input_grad, qkv_total, out_total, sums, gathered = tail(
        ids,
        row_normed,
        att,
        row_cot,
        dq,
        dk,
        dv,
        qkv_weight,
        out_weight,
        family_table,
        orient_table,
        gain,
        down_bias.reshape(1, d),
        up_bias_part,
        down_bias_part,
        far_att,
        both,
        down_weight,
        up_weight,
        hid,
        cot,
        late_orders,
        rows,
        4,
    )
    flat = sums.reshape(-1)
    up_bias_sum = flat[:ff]
    down_bias_sum, gain_sum, bias_sum = flat[ff : ff + 3 * d].reshape(3, d)
    orient_sum = flat[ff + 3 * d :].reshape(2, d)
    families = family_table.shape[0]
    hot = gathered[:, -1, 0].astype(jnp.int32)[None, :] == jnp.arange(families)[:, None]
    family_sum = jnp.dot(
        hot.astype(F32), gathered[:, :-8].reshape(dp_count, d), precision=lax.Precision.HIGHEST
    )
    return (
        layer_out.reshape(rows, seg, d),
        input_grad.reshape(rows, seg, d),
        gain_sum,
        bias_sum,
        qkv_total,
        out_total,
        up_total,
        up_bias_sum,
        down_total,
        down_bias_sum,
        family_sum,
        orient_sum,
    )


def body(*args):
    hidden_in = args[0]
    dp_count = lax.axis_size("dp")
    two_rows = lax.axis_size("seq") == 2 and hidden_in.shape[0] == 2
    if two_rows and dp_count >= 4 and dp_count & (dp_count - 1) == 0:
        return body_by_rows(*args)
    return body_by_heads(*args)


def solution(mesh):
    return jax.shard_map(
        body,
        mesh=mesh,
        in_specs=(
            P("dp", "seq", None),
            P("dp"),
            P("dp"),
            P(),
            P(),
            P(),
            P(),
            P(),
            P(),
            P(),
            P(),
            P(),
            P(),
            P("dp", "seq", None),
        ),
        out_specs=(
            P("dp", "seq", None),
            P("dp", "seq", None),
            P(),
            P(),
            P(("dp", "seq"), None),
            P(("dp", "seq"), None),
            P(("dp", "seq"), None),
            P(),
            P(("dp", "seq"), None),
            P(),
            P(),
            P(),
        ),
        check_vma=False,
    )
```

```python
import functools
import math

import jax
import jax.numpy as jnp
from jax import lax
from jax.experimental import pallas as pl
from jax.experimental.pallas import tpu as pltpu
from jax.sharding import PartitionSpec as P

H = 16
HD = 64
ROT = 32
MESH = pl.DeviceIdType.MESH
VMEM_LIMIT = 60 * 1024 * 1024
F32 = jnp.float32
BF16 = jnp.bfloat16


def for_sending(shard):

    def short(part):
        return part.astype(jnp.bfloat16) if part.dtype == jnp.float32 else part

    return jax.tree.map(short, shard)


def rope_tables(positions, features):
    column = jnp.arange(features, dtype=jnp.int32)
    within = column % HD
    frequency = jnp.exp(-(2.0 * (within // 2).astype(jnp.float32) / ROT) * math.log(10000.0))
    angles = positions[:, None] * frequency[None, :]
    rotary = within < ROT
    cosine = jnp.where(rotary[None, :], jnp.cos(angles), 1.0)
    sign_term = jnp.where(within % 2 == 0, -1.0, 1.0)
    sine_term = jnp.where(rotary[None, :], sign_term[None, :] * jnp.sin(angles), 0.0)
    return (cosine, sine_term)


def pair_swap(values):
    even_cols = jnp.arange(values.shape[-1]) % 2 == 0
    return jnp.where(even_cols, jnp.roll(values, -1, axis=-1), jnp.roll(values, 1, axis=-1))


def rotate(values, cosine, sine_term):
    return values * cosine + pair_swap(values) * sine_term


def rotate_back(values, cosine, sine_term):
    return values * cosine + pair_swap(values * sine_term)


def gelu_tanh(pre_values):
    return jax.nn.gelu(pre_values, approximate=True)


def body_by_heads(
    hidden_in,
    family,
    orient,
    norm_gain,
    norm_bias,
    qkv_weight,
    out_weight,
    up_weight,
    up_bias,
    down_weight,
    down_bias,
    family_table,
    orient_table,
    cotangent,
):
    seq_count = lax.axis_size("seq")
    row_count, seg_length, features = hidden_in.shape
    full_length = seg_length * seq_count
    local_heads = H // seq_count
    head_size = features // H
    slab_width = features // seq_count
    block_rows = min(512, full_length)
    block_count = full_length // block_rows
    score_scale = head_size ** (-0.5)
    token_count = row_count * seg_length
    family_rows = jnp.repeat(family, 2)
    family_hot = (family_rows[:, None] == jnp.arange(family_table.shape[0])[None, :]).astype(
        jnp.bfloat16
    )
    orient_hot = (orient[:, None] == jnp.arange(2)[None, :]).astype(jnp.bfloat16)
    embedding = jnp.dot(family_hot, family_table, preferred_element_type=jnp.float32) + jnp.dot(
        orient_hot, orient_table, preferred_element_type=jnp.float32
    )
    embedded = (hidden_in.astype(jnp.float32) + embedding[:, None, :]).reshape(
        token_count, features
    )
    row_mean = jnp.mean(embedded, -1, keepdims=True)
    centred = embedded - row_mean
    row_var = jnp.mean(centred * centred, -1, keepdims=True)
    inv_std = lax.rsqrt(row_var + 1e-05)
    normed_hat = centred * inv_std
    gain_f32 = norm_gain.astype(jnp.float32)
    normed_low = (normed_hat * gain_f32 + norm_bias.astype(jnp.float32)).astype(jnp.bfloat16)
    projected = jnp.dot(normed_low, qkv_weight, preferred_element_type=jnp.float32).reshape(
        row_count, seg_length, 3 * features
    )
    positions = (lax.axis_index("seq") * seg_length + jnp.arange(seg_length)).astype(jnp.float32)
    cosine, sine_term = rope_tables(positions, features)
    queries = rotate(projected[..., :features], cosine, sine_term).astype(jnp.bfloat16)
    keys_rot = rotate(projected[..., features : 2 * features], cosine, sine_term).astype(
        jnp.bfloat16
    )
    values = projected[..., 2 * features :].astype(jnp.bfloat16)
    query_heads, key_heads, value_heads = (
        lax.all_to_all(queries, "seq", split_axis=2, concat_axis=1, tiled=True),
        lax.all_to_all(keys_rot, "seq", split_axis=2, concat_axis=1, tiled=True),
        lax.all_to_all(values, "seq", split_axis=2, concat_axis=1, tiled=True),
    )

    def scores_for(query_block, key_rows, block_start):
        logits = (
            jnp.einsum("qhd,khd->hqk", query_block, key_rows, preferred_element_type=jnp.float32)
            * score_scale
        )
        causal = (block_start + jnp.arange(block_rows))[:, None] >= jnp.arange(full_length)[None, :]
        return jnp.where(causal[None], logits, -1e30)

    def attend(row_args):
        query_row, key_row, value_row = row_args
        key_rows = key_row.reshape(full_length, local_heads, head_size)
        value_rows = value_row.reshape(full_length, local_heads, head_size)
        pieces = []
        log_parts = []
        for block_index in range(block_count):
            block_start = block_index * block_rows
            query_block = query_row[block_start : block_start + block_rows].reshape(
                block_rows, local_heads, head_size
            )
            logits = scores_for(query_block, key_rows, block_start)
            row_peak = jnp.max(logits, -1, keepdims=True)
            weights = jnp.exp(logits - row_peak)
            row_total = jnp.sum(weights, -1, keepdims=True)
            prob_low = (weights / row_total).astype(jnp.bfloat16)
            output_block = jnp.einsum(
                "hqk,khd->qhd", prob_low, value_rows, preferred_element_type=jnp.float32
            )
            pieces.append(output_block.reshape(block_rows, slab_width).astype(jnp.bfloat16))
            log_parts.append((row_peak + jnp.log(row_total))[..., 0])
        return (jnp.concatenate(pieces, 0), jnp.concatenate(log_parts, 1))

    attended_heads, log_sums = lax.map(attend, (query_heads, key_heads, value_heads))
    attended = jax.tree.map(
        lambda part, own: part.astype(own.dtype),
        lax.all_to_all(for_sending(attended_heads), "seq", split_axis=1, concat_axis=2, tiled=True),
        attended_heads,
    )
    attended_flat = attended.reshape(token_count, features)
    branch_attn = jnp.dot(attended_flat, out_weight, preferred_element_type=jnp.float32)
    up_pre = jnp.dot(normed_low, up_weight, preferred_element_type=jnp.float32) + up_bias.astype(
        jnp.float32
    )
    up_act = gelu_tanh(up_pre).astype(jnp.bfloat16)
    branch_feed = jnp.dot(
        up_act, down_weight, preferred_element_type=jnp.float32
    ) + down_bias.astype(jnp.float32)
    layer_out = (
        (embedded + branch_attn + branch_feed)
        .astype(jnp.bfloat16)
        .reshape(row_count, seg_length, features)
    )
    grad_low = cotangent.reshape(token_count, features)
    grad_f32 = grad_low.astype(jnp.float32)
    down_grad = jnp.einsum("nf,nd->fd", up_act, grad_low, preferred_element_type=jnp.float32)
    down_bias_grad = jnp.sum(grad_f32, 0)
    act_grad = jnp.einsum("nd,fd->nf", grad_low, down_weight, preferred_element_type=jnp.float32)
    gelu_out, gelu_pull = jax.vjp(gelu_tanh, up_pre)
    pre_grad = gelu_pull(act_grad)[0].astype(jnp.bfloat16)
    up_bias_grad = jnp.sum(pre_grad.astype(jnp.float32), 0)
    up_grad = jnp.einsum("nd,nf->df", normed_low, pre_grad, preferred_element_type=jnp.float32)
    normed_grad = jnp.einsum("nf,df->nd", pre_grad, up_weight, preferred_element_type=jnp.float32)
    out_grad = jnp.einsum("nd,ne->de", attended_flat, grad_low, preferred_element_type=jnp.float32)
    attended_grad = jnp.einsum(
        "ne,de->nd", grad_low, out_weight, preferred_element_type=jnp.float32
    )
    attended_grad = attended_grad.astype(jnp.bfloat16).reshape(row_count, seg_length, features)
    grad_heads = lax.all_to_all(attended_grad, "seq", split_axis=2, concat_axis=1, tiled=True)

    def attend_back(row_args):
        query_row, key_row, value_row, grad_row, log_row = row_args
        key_rows = key_row.reshape(full_length, local_heads, head_size)
        value_rows = value_row.reshape(full_length, local_heads, head_size)
        keys_total = jnp.zeros((full_length, local_heads, head_size), jnp.float32)
        values_total = jnp.zeros((full_length, local_heads, head_size), jnp.float32)
        query_parts = []
        for block_index in range(block_count):
            block_start = block_index * block_rows
            query_block = query_row[block_start : block_start + block_rows].reshape(
                block_rows, local_heads, head_size
            )
            grad_block = grad_row[block_start : block_start + block_rows].reshape(
                block_rows, local_heads, head_size
            )
            logits = scores_for(query_block, key_rows, block_start)
            probs_full = jnp.exp(logits - log_row[:, block_start : block_start + block_rows, None])
            prob_low = probs_full.astype(jnp.bfloat16)
            probs_grad = jnp.einsum(
                "qhd,khd->hqk", grad_block, value_rows, preferred_element_type=jnp.float32
            )
            inner_sum = jnp.sum(probs_full * probs_grad, -1, keepdims=True)
            scores_grad = (probs_full * (probs_grad - inner_sum)).astype(jnp.bfloat16)
            values_total = values_total + jnp.einsum(
                "hqk,qhd->khd", prob_low, grad_block, preferred_element_type=jnp.float32
            )
            query_grad = (
                jnp.einsum(
                    "hqk,khd->qhd", scores_grad, key_rows, preferred_element_type=jnp.float32
                )
                * score_scale
            )
            query_parts.append(query_grad.reshape(block_rows, slab_width).astype(jnp.bfloat16))
            keys_total = (
                keys_total
                + jnp.einsum(
                    "hqk,qhd->khd", scores_grad, query_block, preferred_element_type=jnp.float32
                )
                * score_scale
            )
        return (
            jnp.concatenate(query_parts, 0),
            keys_total.reshape(full_length, slab_width).astype(jnp.bfloat16),
            values_total.reshape(full_length, slab_width).astype(jnp.bfloat16),
        )

    query_grad_heads, key_grad_heads, value_grad_heads = lax.map(
        attend_back, (query_heads, key_heads, value_heads, grad_heads, log_sums)
    )
    query_grad_pos, key_grad_pos, value_grad_pos = (
        lax.all_to_all(
            for_sending(query_grad_heads), "seq", split_axis=1, concat_axis=2, tiled=True
        ).astype(query_grad_heads.dtype),
        lax.all_to_all(
            for_sending(key_grad_heads), "seq", split_axis=1, concat_axis=2, tiled=True
        ).astype(key_grad_heads.dtype),
        lax.all_to_all(
            for_sending(value_grad_heads), "seq", split_axis=1, concat_axis=2, tiled=True
        ).astype(value_grad_heads.dtype),
    )
    projected_grad = jnp.concatenate(
        [
            rotate_back(query_grad_pos.astype(jnp.float32), cosine, sine_term),
            rotate_back(key_grad_pos.astype(jnp.float32), cosine, sine_term),
            value_grad_pos.astype(jnp.float32),
        ],
        -1,
    )
    projected_grad = projected_grad.astype(jnp.bfloat16).reshape(token_count, 3 * features)
    qkv_grad = jnp.einsum(
        "nd,ne->de", normed_low, projected_grad, preferred_element_type=jnp.float32
    )
    normed_grad = normed_grad + jnp.einsum(
        "ne,de->nd", projected_grad, qkv_weight, preferred_element_type=jnp.float32
    )
    gain_grad = jnp.sum(normed_grad * normed_hat, 0)
    bias_grad = jnp.sum(normed_grad, 0)
    scaled_grad = normed_grad * gain_f32
    hat_grad = (
        scaled_grad
        - jnp.mean(scaled_grad, -1, keepdims=True)
        - normed_hat * jnp.mean(scaled_grad * normed_hat, -1, keepdims=True)
    )
    input_grad = (grad_f32 + inv_std * hat_grad).reshape(row_count, seg_length, features)
    row_sums = jnp.sum(input_grad, 1)
    family_grad = jnp.einsum(
        "rf,rd->fd", family_hot.astype(jnp.float32), row_sums, precision=lax.Precision.HIGHEST
    )
    orient_grad = jnp.einsum(
        "rf,rd->fd", orient_hot.astype(jnp.float32), row_sums, precision=lax.Precision.HIGHEST
    )
    gain_sum, bias_sum, up_bias_sum, down_bias_sum, family_sum, orient_sum = lax.psum(
        (gain_grad, bias_grad, up_bias_grad, down_bias_grad, family_grad, orient_grad),
        ("dp", "seq"),
    )
    qkv_sum, out_sum, up_sum, down_sum = (
        lax.psum_scatter(qkv_grad, ("dp", "seq"), scatter_dimension=0, tiled=True),
        lax.psum_scatter(out_grad, ("dp", "seq"), scatter_dimension=0, tiled=True),
        lax.psum_scatter(up_grad, ("dp", "seq"), scatter_dimension=0, tiled=True),
        lax.psum_scatter(down_grad, ("dp", "seq"), scatter_dimension=0, tiled=True),
    )
    return (
        layer_out,
        input_grad,
        gain_sum,
        bias_sum,
        qkv_sum,
        out_sum,
        up_sum,
        up_bias_sum,
        down_sum,
        down_bias_sum,
        family_sum,
        orient_sum,
    )


def dot_nn(a, b):
    return lax.dot_general(a, b, (((1,), (0,)), ((), ())), preferred_element_type=F32)


def dot_nt(a, b):
    return lax.dot_general(a, b, (((1,), (1,)), ((), ())), preferred_element_type=F32)


def dot_tn(a, b):
    return lax.dot_general(a, b, (((0,), (0,)), ((), ())), preferred_element_type=F32)


def params(**more):
    return pltpu.CompilerParams(vmem_limit_bytes=VMEM_LIMIT, **more)


def cost(flops, moved, exps=0):
    return pl.CostEstimate(flops=flops, bytes_accessed=moved, transcendentals=exps)


def whole(shape):
    return pl.BlockSpec(shape, lambda *_: (0,) * len(shape), pipeline_mode=pl.Buffered(1))


def table_row(table, wanted):
    rows = lax.broadcasted_iota(jnp.int32, table.shape, 0)
    return jnp.sum(jnp.where(rows == wanted, table[...].astype(F32), 0.0), 0, keepdims=True)


def normalise(entries):
    centred = entries - jnp.mean(entries, -1, keepdims=True)
    inv_std = lax.rsqrt(jnp.mean(centred * centred, -1, keepdims=True) + 1e-05)
    return centred * inv_std, inv_std


GELU_C = math.sqrt(2.0 / math.pi)


def gelu_both(z):
    square = z * z
    half = 0.5 + 0.5 * jnp.tanh(z * (GELU_C + (GELU_C * 0.044715) * square))
    value = z * half
    slope = half + value * (1.0 - half) * (2 * GELU_C + (6 * GELU_C * 0.044715) * square)
    return value, slope


def ffn_kernel(rows, ids, hid, cot, fam, ori, gain, bias, wup, bup, wdn, norm, both, bupg, bdng):
    tokens = hid.shape[0]
    seg = tokens // rows
    step = 256

    @pl.when(pl.program_id(0) == 0)
    def _():
        total = jnp.zeros((1, cot.shape[1]), F32)
        for row in range(rows):
            emb = table_row(fam, ids[0]) + table_row(ori, ids[1 + row])
            for start in range(row * seg, (row + 1) * seg, step):
                part = pl.ds(start, step)
                hat, _ = normalise(hid[part, :].astype(F32) + emb)
                norm[part, :] = (hat * gain[...].astype(F32) + bias[...].astype(F32)).astype(BF16)
                total = total + jnp.sum(cot[part, :].astype(F32), 0, keepdims=True)
        bdng[...] = total

    width = wup.shape[1]
    total = jnp.zeros((8, width), F32)
    lin = dot_nn(norm[...], wup[...])
    into = dot_nt(cot[...], wdn[...])
    step = 64
    for start in range(0, tokens, step):
        part = pl.ds(start, step)
        value, slope = gelu_both(lin[start : start + step] + bup[...].astype(F32))
        low = into[start : start + step] * slope
        both[0, part, :] = value.astype(BF16)
        both[1, part, :] = low.astype(BF16)
        total = total + jnp.sum(low.reshape(step // 8, 8, width), 0)
    bupg[...] = jnp.sum(total, 0, keepdims=True)


def ffn_forward(ids, hid, cot, fam, ori, gain, bias, wup, bup, wdn, rows):
    tokens, d = hid.shape
    ff = wup.shape[1]
    tile = 512
    return pl.pallas_call(
        functools.partial(ffn_kernel, rows),
        grid_spec=pltpu.PrefetchScalarGridSpec(
            num_scalar_prefetch=1,
            grid=(ff // tile,),
            in_specs=[
                whole((tokens, d)),
                whole((tokens, d)),
                whole(fam.shape),
                whole(ori.shape),
                whole((1, d)),
                whole((1, d)),
                pl.BlockSpec((d, tile), lambda i, s: (0, i)),
                pl.BlockSpec((1, tile), lambda i, s: (0, i)),
                pl.BlockSpec((tile, d), lambda i, s: (i, 0)),
            ],
            out_specs=[
                whole((tokens, d)),
                pl.BlockSpec((2, tokens, tile), lambda i, s: (0, 0, i)),
                pl.BlockSpec((1, tile), lambda i, s: (0, i)),
                whole((1, d)),
            ],
        ),
        out_shape=[
            jax.ShapeDtypeStruct((tokens, d), BF16),
            jax.ShapeDtypeStruct((2, tokens, ff), BF16),
            jax.ShapeDtypeStruct((1, ff), F32),
            jax.ShapeDtypeStruct((1, d), F32),
        ],
        compiler_params=params(),
        cost_estimate=cost(4 * tokens * d * ff, 4 * tokens * ff + 4 * d * ff, tokens * ff),
        name="ffn_forward",
    )(ids, hid, cot, fam, ori, gain, bias, wup, bup, wdn)


def turn(entries, cosine, sine):
    even = lax.broadcasted_iota(jnp.int32, entries.shape, 1) % 2 == 0
    other = jnp.where(even, pltpu.roll(entries, 127, 1), pltpu.roll(entries, 1, 1))
    return entries * cosine + other * sine


def turn_back(entries, cosine, sine):
    even = lax.broadcasted_iota(jnp.int32, entries.shape, 1) % 2 == 0
    side = entries * sine
    other = jnp.where(even, pltpu.roll(side, 127, 1), pltpu.roll(side, 1, 1))
    return entries * cosine + other


def attend(head_size, query_ref, k_ref, v_ref, g_ref, cos, sin, o_ref, dq_ref, dk_ref, dv_ref, dkt, dvt):
    full = query_ref.shape[0]
    block = 256
    scale = head_size ** (-0.5)
    first = lax.broadcasted_iota(jnp.int32, (block, 128), 1) < head_size
    below = lax.broadcasted_iota(jnp.int32, (block, block), 0) >= lax.broadcasted_iota(
        jnp.int32, (block, block), 1
    )
    dkt[...] = jnp.zeros_like(dkt)
    dvt[...] = jnp.zeros_like(dvt)

    def by_head(entries):
        none = jnp.zeros_like(entries)
        return jnp.concatenate([jnp.where(first, entries, none), jnp.where(first, none, entries)], 0)

    def front(start):
        part, end = pl.ds(start, block), start + block
        query = by_head((query_ref[part, :].astype(F32) * scale).astype(BF16))
        grad = by_head(g_ref[part, :])
        return query, grad, dot_nt(query, k_ref[0:end, :]), dot_nt(grad, v_ref[0:end, :])

    def back(start, query, grad, scores, into):
        part, end = pl.ds(start, block), start + block
        lows, slopes = [], []
        for head in range(2):
            rows = slice(head * block, (head + 1) * block)
            score = scores[rows]
            last = jnp.where(below, score[:, start:end], -1e30)
            score = last if start == 0 else jnp.concatenate([score[:, :start], last], 1)
            weights = jnp.exp(score - jnp.max(score, -1, keepdims=True))
            probs = weights * (1.0 / jnp.sum(weights, -1, keepdims=True))
            lows.append(probs.astype(BF16))
            inner = jnp.sum(probs * into[rows], -1, keepdims=True)
            slopes.append((probs * (into[rows] - inner)).astype(BF16))
        low = jnp.concatenate(lows, 0)
        slope = jnp.concatenate(slopes, 0)
        out = dot_nn(low, v_ref[0:end, :])
        dq = dot_nn(slope, k_ref[0:end, :])
        o_ref[part, :] = jnp.where(first, out[:block], out[block:]).astype(BF16)
        dq = jnp.where(first, dq[:block], dq[block:]) * scale
        dq_ref[part, :] = turn_back(dq, cos[part, :], sin[part, :]).astype(BF16)
        dkt[:, 0:end] += dot_tn(query, slope)
        dvt[:, 0:end] += dot_tn(grad, low)

    ready = front(0)
    for start in range(0, full, block):
        later = front(start + block) if start + block < full else None
        back(start, *ready)
        ready = later
    for start in range(0, full, block):
        part = pl.ds(start, block)
        dk = dkt[:, start : start + block].T
        dk_ref[part, :] = turn_back(dk, cos[part, :], sin[part, :]).astype(BF16)
        dv_ref[part, :] = dvt[:, start : start + block].T.astype(BF16)


FFN_ORDERS = [
    [2, 3, 1, "seq"],
    [2, 1, 3, "seq"],
    ["seq", 1, 2, 3],
    ["seq", 3, 1, 2],
    [1, "seq", 2, 3],
    ["seq", 2, 1, 3],
    [2, 1, 3, "seq"],
    ["seq", 3, 1, 2],
]
LATE_ORDERS = [
    [0, 1, 2, "seq", 3],
    [0, 2, 1, "seq", 3],
    [0, 1, 2, 3, "seq"],
    [0, 2, 1, "seq", 3],
]
FFN_EVENTS = {
    0: [(0, 0), (1, 0), (2, 0), (3, 0)],
    9: [(4, 0), (5, 0), (6, 0), (7, 0)],
    10: [(0, 1), (1, 1), (2, 1), (3, 1)],
    18: [(1, 2), (2, 2), (4, 1), (0, 2), (5, 1), (7, 1), (3, 2)],
    19: [(6, 1), (0, 3)],
    20: [(1, 3), (2, 3), (3, 3), (4, 2), (0, 4)],
    21: [(1, 4), (5, 2), (6, 2), (7, 2)],
    22: [(2, 4), (3, 4), (4, 3)],
    23: [(5, 3), (6, 3), (7, 3), (4, 4)],
    24: [(6, 4), (5, 4), (7, 4)],
}
LATE_EVENTS = {
    2: [(0, 1)],
    3: [(1, 1)],
    4: [(2, 1)],
    6: [(3, 1)],
    8: [(0, 2), (1, 2)],
    13: [(2, 2)],
    14: [(1, 3)],
    16: [(0, 3)],
    18: [(1, 4), (3, 2)],
    19: [(2, 3)],
    20: [(0, 4)],
    22: [(1, 5)],
    24: [(3, 3)],
    26: [(0, 5), (2, 4)],
    29: [(3, 4)],
    30: [(2, 5), (3, 5)],
}


def middle_kernel(tiles, pairs, head_size, bits, orders, *refs):
    ids, own, far, home_cot, cfar, act, fam, ori, gain, bias, wqkv, wout, cos, sin = refs[:14]
    near_up, far_up = refs[14:16]
    norm, cot, o_ref, dq_ref, dk_ref, dv_ref, far_att, up_out, down_out, near_down, far_down = refs[16:27]
    heads, dkt, dvt, att_send, att_got, att_sems, keep, send, got, send_sem, recv_sem, out_sem = refs[27:39]
    seg = own.shape[0]
    step = 256
    base = 1 << (bits - 1)
    now = pl.program_id(0)
    i = now - base
    me = lax.axis_index("seq")
    mine = device_bits(bits)
    parts = len(orders) // 2
    up_part = up_out.shape[1] // parts
    down_part = down_out.shape[1] // parts
    chunks = chunks_from(
        refs[39:],
        bits,
        mine,
        [
            (orders[part], near_up, far_up, pl.ds(part * up_part, up_part), up_out)
            for part in range(parts)
        ]
        + [
            (orders[parts + part], near_down, far_down, pl.ds(part * down_part, down_part), down_out)
            for part in range(parts)
        ],
    )

    def happen(events):
        for chunk, stage in events:
            chunks[chunk].happen(stage)

    @pl.when(now == 0)
    def _():
        meet([partner_along(axis, mine) for axis in [0] + orders[0]])

    last = base + 4 * tiles + pairs
    for when, what in FFN_EVENTS.items():
        if when < last:

            @pl.when(now == when)
            def _():
                happen(what)

    def crossing(index):
        slot = lax.rem(index, 2)
        return remote(
            send.at[slot], got.at[slot], send_sem.at[slot], recv_sem.at[slot], partner_along(0, mine)
        )

    def store(index, act_on):
        slot = lax.rem(index, 2)
        width = home_cot.shape[1] // parts
        for seq in range(2):
            for part in range(parts):
                place = 0
                for axis in orders[parts + part]:
                    if axis == "seq":
                        apart = lax.rem(mine["seq"] + seq, 2)
                    else:
                        apart = lax.rem(index // (1 << (axis - 1)) + mine[axis], 2)
                    place = 2 * place + apart
                columns = pl.ds(part * width, width)
                source = keep.at[slot, seq, :, columns]
                sem = out_sem.at[slot, seq, part]
                there = lax.rem(place, base)

                @pl.when(place < base)
                def _():
                    act_on(pltpu.make_async_copy(source, near_down.at[there, :, columns], sem))

                @pl.when(place >= base)
                def _():
                    act_on(pltpu.make_async_copy(source, far_down.at[there, :, columns], sem))

    @pl.when((now > 0) & (now <= base))
    def _():
        crossing(now - 1).wait()
        add_into(keep.at[lax.rem(now - 1, 2)], got.at[lax.rem(now - 1, 2)])
        store(now - 1, lambda copy: copy.start())

    @pl.when((now > 1) & (now <= base))
    def _():
        store(now - 2, lambda copy: copy.wait())

    @pl.when(now < base)
    def _():
        value = dot_nn(act[...].T, home_cot[...])
        slot = lax.rem(now, 2)
        split_blocks(value, keep.at[slot], send.at[slot], keep.shape[2], mine[0], [0, 1])
        crossing(now).start()

    @pl.when(now == base)
    def _():
        store(now - 1, lambda copy: copy.wait())

    @pl.when(i == 0)
    def _():
        emb = table_row(fam, ids[0]) + table_row(ori, ids[1])
        for source, where in ((own, me), (far, 1 - me)):
            for start in range(0, seg, step):
                part = pl.ds(start, step)
                there = pl.ds(pl.multiple_of(where * seg + start, step), step)
                hat, _ = normalise(source[part, :].astype(F32) + emb)
                norm[there, :] = (hat * gain[...].astype(F32) + bias[...].astype(F32)).astype(BF16)
        held = pl.ds(pl.multiple_of(me * seg, seg), seg)
        cot[held, :] = home_cot[held, :]
        cot[pl.ds(pl.multiple_of((1 - me) * seg, seg), seg), :] = cfar[...]

    lanes = wqkv.shape[1] // 128

    def att_crossing(pair):
        return remote(
            att_send.at[pair],
            att_got.at[pair],
            att_sems.at[0, pair],
            att_sems.at[1, pair],
            partner_along("seq", mine),
        )

    @pl.when((i >= 0) & (i < 2 * tiles))
    def _():
        lin = dot_nn(norm[...], wqkv[...])
        for start in range(0, 2 * seg, step):
            part = pl.ds(start, step)
            for lane in range(lanes):
                piece = lin[start : start + step, lane * 128 : (lane + 1) * 128]
                heads[i * lanes + lane, part, :] = turn(piece, cos[part, :], sin[part, :]).astype(BF16)

    @pl.when((i >= 2 * tiles) & (i < 3 * tiles))
    def _():
        lin = dot_nn(norm[...], wqkv[...]).astype(BF16)
        for lane in range(lanes):
            heads[i * lanes + lane] = lin[:, lane * 128 : (lane + 1) * 128]

    @pl.when((i >= 3 * tiles) & (i < 4 * tiles))
    def _():
        lin = dot_nt(cot[...], wout[...]).astype(BF16)
        for lane in range(lanes):
            heads[i * lanes + lane] = lin[:, lane * 128 : (lane + 1) * 128]

    @pl.when(i >= 4 * tiles)
    def _():
        pair = i - 4 * tiles
        attend(
            head_size,
            heads.at[pair],
            heads.at[pairs + pair],
            heads.at[2 * pairs + pair],
            heads.at[3 * pairs + pair],
            cos,
            sin,
            o_ref,
            dq_ref,
            dk_ref,
            dv_ref,
            dkt,
            dvt,
        )
        att_send[pair] = o_ref[pl.ds(pl.multiple_of((1 - me) * seg, seg), seg), :]
        att_crossing(pair).start()

    @pl.when(now == last - 1)
    def _():
        for pair in range(pairs):
            att_crossing(pair).wait()
            far_att[:, pair * 128 : (pair + 1) * 128] = att_got[pair]
        happen(FFN_EVENTS[last])


def middle(
    ids, own, far, home_cot, cfar, both, fam, ori, gain, bias, wqkv, wout, cos, sin, up, orders, head_size, collective
):
    seg, d = own.shape
    full = 2 * seg
    tile = 512
    tiles = d // tile
    pairs = d // 128
    bits = len(orders[0])
    base = 1 << (bits - 1)
    parts = len(orders) // 2
    near_up, far_up = up
    up_size, ff = near_up.shape[1:]
    down_tile = ff // base
    down_size = down_tile // 4
    smem = pl.BlockSpec(memory_space=pltpu.SMEM)
    anywhere = pl.BlockSpec(memory_space=pl.ANY)
    attend_at = base + 4 * tiles
    head_out = pl.BlockSpec((full, 128), lambda i: (0, jnp.maximum(i - attend_at, 0)))
    rows = jax.ShapeDtypeStruct((full, d), BF16)
    down = jax.ShapeDtypeStruct((base, down_size, d), BF16)
    slots = pltpu.VMEM((2, 2, down_size, d), BF16)
    return pl.pallas_call(
        functools.partial(middle_kernel, tiles, pairs, head_size, bits, orders),
        grid=(attend_at + pairs,),
        in_specs=[
            smem,
            whole((seg, d)),
            whole((seg, d)),
            whole((full, d)),
            whole((seg, d)),
            pl.BlockSpec((None, full, down_tile), lambda i: (0, 0, jnp.minimum(i, base - 1))),
            whole(fam.shape),
            whole(ori.shape),
            whole((1, d)),
            whole((1, d)),
            pl.BlockSpec((d, tile), lambda i: (0, jnp.clip(i - base, 0, 3 * tiles - 1))),
            pl.BlockSpec((tile, d), lambda i: (jnp.clip(i - base - 3 * tiles, 0, tiles - 1), 0)),
            whole((full, 128)),
            whole((full, 128)),
        ]
        + [anywhere] * 2,
        out_specs=[
            whole((full, d)),
            whole((full, d)),
            head_out,
            head_out,
            head_out,
            head_out,
            whole((seg, d)),
            whole((up_size, ff)),
            whole((down_size, d)),
            anywhere,
            anywhere,
        ],
        out_shape=[
            rows,
            rows,
            rows,
            rows,
            rows,
            rows,
            jax.ShapeDtypeStruct((seg, d), BF16),
            jax.ShapeDtypeStruct((up_size, ff), F32),
            jax.ShapeDtypeStruct((down_size, d), F32),
            down,
            down,
        ],
        scratch_shapes=[
            pltpu.VMEM((4 * pairs, full, 128), BF16),
            pltpu.VMEM((128, full), F32),
            pltpu.VMEM((128, full), F32),
            pltpu.VMEM((pairs, seg, 128), BF16),
            pltpu.VMEM((pairs, seg, 128), BF16),
            pltpu.SemaphoreType.DMA((2, pairs)),
            slots,
            slots,
            slots,
            pltpu.SemaphoreType.DMA((2,)),
            pltpu.SemaphoreType.DMA((2,)),
            pltpu.SemaphoreType.DMA((2, 2, parts)),
        ]
        + [
            entry
            for index, axes in enumerate(orders)
            for entry in chunk_scratch(
                axes, *((up_size, ff // parts) if index < parts else (down_size, d // parts))
            )
        ],
        compiler_params=params(collective_id=collective, has_side_effects=True),
        cost_estimate=cost(16 * full * d * d + 12 * full * full * d, 8 * d * d + 18 * full * d, full * full * H),
        name="middle",
    )(ids, own, far, home_cot, cfar, both, fam, ori, gain, bias, wqkv, wout, cos, sin, near_up, far_up)


def device_bits(bits):
    dp = lax.axis_index("dp")
    found = {bit: lax.rem(dp // (1 << bit), 2) for bit in range(bits)}
    found["seq"] = lax.axis_index("seq")
    return found


def block_place(axes, mine, upper, seq):
    place = 0
    for axis in axes:
        bit = seq if axis == "seq" else (upper >> (axis - 1)) & 1
        place = 2 * place + (1 - mine[axis] if bit else mine[axis])
    return place


def other_core():
    dp = lax.axis_index("dp")
    return (dp + 1 - 2 * lax.rem(dp, 2), lax.axis_index("seq"))


def meet(partners):
    barrier = pltpu.get_barrier_semaphore()
    for partner in partners:
        pl.semaphore_signal(barrier, inc=1, device_id=partner, device_id_type=MESH)
    pl.semaphore_wait(barrier, len(partners))


def remote(src, dst, send_sem, recv_sem, partner):
    return pltpu.make_async_remote_copy(
        src_ref=src,
        dst_ref=dst,
        send_sem=send_sem,
        recv_sem=recv_sem,
        device_id=partner,
        device_id_type=MESH,
    )


def split_blocks(value, keep, send, size, core, places):
    for index, there in enumerate(places):
        up, seq = index // 2, index % 2
        first = (4 * up + seq) * size
        second = first + 2 * size
        a = value[first : first + size, :].astype(BF16)
        b = value[second : second + size, :].astype(BF16)
        keep[there] = jnp.where(core == 0, a, b)
        send[there] = jnp.where(core == 0, b, a)


def add_into(keep, got):
    for index in range(keep.shape[0]):
        keep[index] = (keep[index].astype(F32) + got[index].astype(F32)).astype(BF16)


def wide_grad_kernel(bits, counts, orders, *refs):
    left, rights = refs[0], refs[1 : 1 + len(counts)]
    near_out, far_out, turned, keep, send, got, send_sem, recv_sem, out_sem = refs[1 + len(counts) :]
    steps = sum(counts)
    i = pl.program_id(0)
    mine = device_bits(bits)
    partner = other_core()
    blocks = keep.shape[1]
    size = keep.shape[2]
    tile = keep.shape[3]

    def crossing(step):
        return remote(send.at[step], got.at[step], send_sem.at[step], recv_sem.at[step], partner)

    def stores(step):
        columns = pl.ds(pl.multiple_of(step * tile, tile), tile)
        half = blocks // 2
        return (
            pltpu.make_async_copy(
                keep.at[step, pl.ds(0, half)], near_out.at[:, :, columns], out_sem.at[0, step]
            ),
            pltpu.make_async_copy(
                keep.at[step, pl.ds(half, half)], far_out.at[:, :, columns], out_sem.at[1, step]
            ),
        )

    @pl.when(i == 0)
    def _():
        meet([partner])
        turned[...] = left[...].T

    start = 0
    for right, count, axes in zip(rights, counts, orders):
        places = [block_place(axes, mine, up, seq) for up in range(blocks // 2) for seq in range(2)]
        @pl.when((i >= start) & (i < start + count))
        def _():
            value = dot_nn(turned[...], right[...])
            split_blocks(value, keep.at[i], send.at[i], size, mine[0], places)
            crossing(i).start()

        start += count

    def finish(step):
        crossing(step).wait()
        add_into(keep.at[step], got.at[step])
        for copy in stores(step):
            copy.start()

    @pl.when(i > 0)
    def _():
        finish(i - 1)

    @pl.when(i == steps - 1)
    def _():
        finish(i)
        for step in range(steps):
            for copy in stores(step):
                copy.wait()


def wide_grad(left, entries, tile, collective):
    tokens, d = left.shape
    bits = len(entries[0][3])
    blocks = 1 << bits
    size = d // (2 * blocks)
    counts = [entry[2] for entry in entries]
    orders = [entry[3] for entry in entries]
    steps = sum(counts)
    specs = []
    start = 0
    for entry in entries:

        def at(i, start=start, offset=entry[1], last=entry[2] - 1):
            return (1, 0, offset + jnp.clip(i - start, 0, last))

        specs.append(pl.BlockSpec((None, tokens, tile), at))
        start += entry[2]
    shape = jax.ShapeDtypeStruct((blocks // 2, size, steps * tile), BF16)
    anywhere = pl.BlockSpec(memory_space=pl.ANY)
    buffers = pltpu.VMEM((steps, blocks, size, tile), BF16)
    return pl.pallas_call(
        functools.partial(wide_grad_kernel, bits, counts, orders),
        grid=(steps,),
        in_specs=[whole((tokens, d))] + specs,
        out_specs=[anywhere, anywhere],
        out_shape=[shape, shape],
        scratch_shapes=[
            pltpu.VMEM((d, tokens), BF16),
            buffers,
            buffers,
            buffers,
            pltpu.SemaphoreType.DMA((steps,)),
            pltpu.SemaphoreType.DMA((steps,)),
            pltpu.SemaphoreType.DMA((2, steps)),
        ],
        compiler_params=params(collective_id=collective, has_side_effects=True),
        cost_estimate=cost(2 * tokens * d * steps * tile, 4 * tokens * (d + steps * tile)),
        name="wide_grad",
    )(left, *[entry[0] for entry in entries])


def partner_along(axis, mine):
    dp = lax.axis_index("dp")
    seq = lax.axis_index("seq")
    if axis == "seq":
        return (dp, 1 - seq)
    return (dp + (1 - 2 * mine[axis]) * (1 << axis), seq)


class Chunk:
    def __init__(self, axes, mine, near, far, columns, out, keep, got, near_sem, send_sem, recv_sem):
        self.axes, self.mine, self.near, self.far = axes, mine, near, far
        self.columns, self.out, self.keep, self.got = columns, out, keep, got
        self.near_sem, self.send_sem, self.recv_sem = near_sem, send_sem, recv_sem

    def load(self):
        return pltpu.make_async_copy(self.near.at[:, :, self.columns], self.keep, self.near_sem)

    def crossing(self, stage):
        count = (1 << len(self.axes)) >> (stage + 1)
        if stage == 0 and self.far is not None:
            source = self.far.at[:, :, self.columns]
        else:
            source = self.keep.at[pl.ds(count, count)]
        return remote(
            source,
            self.got[stage],
            self.send_sem.at[stage],
            self.recv_sem.at[stage],
            partner_along(self.axes[stage], self.mine),
        )

    def begin(self):
        if self.near is not None:
            self.load().start()
        self.crossing(0).start()

    def advance(self, stage):
        if stage == 1 and self.near is not None:
            self.load().wait()
        self.crossing(stage - 1).wait()
        count = (1 << len(self.axes)) >> stage

        def add(index, carry):
            self.keep[index] = (self.keep[index].astype(F32) + self.got[stage - 1][index].astype(F32)).astype(BF16)
            return carry

        lax.fori_loop(0, count, add, 0)
        self.crossing(stage).start()

    def finish(self):
        last = len(self.axes) - 1
        self.crossing(last).wait()
        self.out[:, self.columns] = self.keep[0].astype(F32) + self.got[last][0].astype(F32)

    def happen(self, stage):
        if stage == 0:
            self.begin()
        elif stage == len(self.axes):
            self.finish()
        else:
            self.advance(stage)


def chunk_scratch(axes, size, width, farther=False):
    half = 1 << (len(axes) - 1)
    return (
        [pltpu.VMEM((2 * half if farther else half, size, width), BF16)]
        + [pltpu.VMEM((half >> stage, size, width), BF16) for stage in range(len(axes))]
        + [
            pltpu.SemaphoreType.DMA,
            pltpu.SemaphoreType.DMA((len(axes),)),
            pltpu.SemaphoreType.DMA((len(axes),)),
        ]
    )


def chunks_from(refs, bits, mine, wanted):
    stages = bits
    found = []
    each = 1 + stages + 3
    for index, (axes, near, far, columns, out) in enumerate(wanted):
        part = refs[index * each : (index + 1) * each]
        found.append(
            Chunk(axes, mine, near, far, columns, out, part[0], part[1 : 1 + stages], *part[1 + stages :])
        )
    return found


def after(entry, *others):
    return lax.optimization_barrier((entry, *others))[0]


TAIL_TILE = 512
TAIL_STEP = 256


def tail_kernel(bits, orders, rows, marks, *refs):
    ids, norm_hbm, att_hbm, cot_hbm, dq_hbm, dk_hbm, dv_hbm, wqkv_hbm, wout_hbm = refs[:9]
    fam, ori, gain, bdn, bup_part, bdn_part, far_att = refs[9:16]
    both, wdn, wup, hid, cot = refs[16:21]
    layer_out, input_out, qkv_out, out_out, sums_out, all_out = refs[21:27]
    left, right, dq, dk, dv, wqkv, wout, turned, acc, ng_send, ng_own, ng_got = refs[27:39]
    gg, bg, rg, load_sem, ng_sem, held, got, vec, vgot, table, ssem, rsem, gsend, grecv = refs[39:53]
    in_start, in_end, out_start, out_end, last = marks
    i = pl.program_id(0)
    me = lax.axis_index("seq")
    dp = lax.axis_index("dp")
    mine = device_bits(bits)
    d = left.shape[1]
    seg = ng_own.shape[0]
    step = TAIL_STEP
    per_row = seg // step
    chunks = chunks_from(
        refs[53:],
        len(orders[0]),
        mine,
        [
            (orders[0], None, None, pl.ds(0, d), qkv_out),
            (orders[1], None, None, pl.ds(d, d), qkv_out),
            (orders[2], None, None, pl.ds(2 * d, d), qkv_out),
            (orders[3], None, None, pl.ds(0, d), out_out),
        ],
    )
    loads = {
        name: pltpu.make_async_copy(source, there, load_sem.at[index])
        for index, (name, source, there) in enumerate(
            (
                ("norm", norm_hbm, left),
                ("dq", dq_hbm, dq),
                ("dk", dk_hbm, dk),
                ("dv", dv_hbm, dv),
                ("wqkv", wqkv_hbm, wqkv),
                ("cot", cot_hbm, right),
                ("wout", wout_hbm, wout),
                ("att", att_hbm, left),
            )
        )
    }
    partners = [partner_along(axis, mine) for axis in ["seq"] + list(range(bits))]

    def gradient(index, operand):
        chunk = chunks[index]
        size = chunk.keep.shape[1]
        value = dot_nn(turned[...], operand[...])
        for block in range(chunk.keep.shape[0]):
            place = 0
            for axis in orders[index]:
                bit = block & 1 if axis == "seq" else (block >> (axis + 1)) & 1
                place = 2 * place + (1 - mine[axis] if bit else mine[axis])
            chunk.keep[place] = value[block * size : (block + 1) * size, :].astype(BF16)
        chunk.begin()

    def back_into(there, half):
        part = pl.ds(pl.multiple_of(half * seg, seg), seg)
        total = dot_nt(dq[part, :], wqkv[:, 0:d])
        total = total + dot_nt(dk[part, :], wqkv[:, d : 2 * d])
        total = total + dot_nt(dv[part, :], wqkv[:, 2 * d : 3 * d])
        there[...] = total.astype(BF16)

    ng_crossing = remote(ng_send, ng_got, ng_sem.at[0], ng_sem.at[1], partners[0])

    @pl.when(i == 0)
    def _():
        for name in ("norm", "dq", "dk", "dv", "wqkv", "cot", "wout"):
            loads[name].start()
        meet(partners)
        loads["norm"].wait()
        turned[...] = left[...].T
        loads["att"].start()
        loads["dq"].wait()
        gradient(0, dq)

    for when, what in LATE_EVENTS.items():
        if when < last:

            @pl.when(i == when)
            def _():
                for chunk, stage in what:
                    chunks[chunk].happen(stage)

    @pl.when(i == 1)
    def _():
        loads["dk"].wait()
        gradient(1, dk)

    @pl.when(i == 2)
    def _():
        loads["dv"].wait()
        gradient(2, dv)

    @pl.when(i == 3)
    def _():
        loads["wqkv"].wait()
        back_into(ng_send, 1 - me)
        ng_crossing.start()

    @pl.when(i == 4)
    def _():
        loads["att"].wait()
        loads["cot"].wait()
        turned[...] = left[...].T
        gradient(3, right)

    @pl.when(i == 5)
    def _():
        back_into(ng_own, me)

    @pl.when((i >= out_start) & (i < out_end))
    def _():
        value = dot_nn(both[0], wdn[...])

        @pl.when(i == out_start)
        def _():
            acc[...] = value

        @pl.when(i > out_start)
        def _():
            acc[...] += value

    @pl.when((i >= in_start) & (i < in_end))
    def _():
        value = dot_nt(both[0], wup[...])

        @pl.when(i == in_start)
        def _():
            acc[...] = value

        @pl.when(i > in_start)
        def _():
            acc[...] += value

    @pl.when(i == out_end)
    def _():
        loads["wout"].wait()

    def home_block(index, own, far, own_offset):
        row = index // per_row
        within = pl.multiple_of(lax.rem(index, per_row) * step, step)
        there = pl.ds(pl.multiple_of(own_offset + within, step), step)
        return row, jnp.where(row == me, own[there, :], far[pl.ds(within, step), :])

    @pl.when(i >= out_end)
    def _():
        index = i - out_end
        row, att = home_block(index, left, far_att, me * seg)
        flag = jnp.where(row == 0, ids[1], ids[2])
        emb = table_row(fam, ids[0]) + table_row(ori, flag)
        part = pl.ds(pl.multiple_of(index * step, step), step)
        total = hid[...].astype(F32) + emb + dot_nn(att, wout[...])
        layer_out[...] = (total + (acc[part, :] + bdn[...].astype(F32))).astype(BF16)

    @pl.when(i == in_end)
    def _():
        ng_crossing.wait()
        gg[...] = jnp.zeros_like(gg)
        bg[...] = jnp.zeros_like(bg)
        rg[...] = jnp.zeros_like(rg)

    @pl.when((i >= in_end) & (i < out_start))
    def _():
        index = i - in_end
        row, back = home_block(index, ng_own, ng_got, 0)
        flag = jnp.where(row == 0, ids[1], ids[2])
        emb = table_row(fam, ids[0]) + table_row(ori, flag)
        part = pl.ds(pl.multiple_of(index * step, step), step)
        hat, inv_std = normalise(hid[...].astype(F32) + emb)
        grad = acc[part, :] + back.astype(F32)
        gg[...] += jnp.sum(grad * hat, 0, keepdims=True)
        bg[...] += jnp.sum(grad, 0, keepdims=True)
        scaled = grad * gain[...].astype(F32)
        inner = (
            scaled
            - jnp.mean(scaled, -1, keepdims=True)
            - hat * jnp.mean(scaled * hat, -1, keepdims=True)
        )
        result = cot[...].astype(F32) + inv_std * inner
        input_out[...] = result
        sums = jnp.sum(result, 0, keepdims=True)
        which = lax.broadcasted_iota(jnp.int32, rg.shape, 0)
        rg[...] += jnp.where(which == flag, sums, 0.0)

    def sums_main(index):
        return remote(held.at[index], got.at[index], ssem.at[index], rsem.at[index], partners[index])

    def sums_side(index):
        if index == 0:
            return remote(vec, vgot, gsend.at[0], grecv.at[0], partners[0])
        size = 1 << (index - 1)
        now = pl.ds(dp - lax.rem(dp, size), size)
        return remote(table.at[now], table.at[now], gsend.at[index], grecv.at[index], partners[index])

    @pl.when(i == out_start)
    def _():
        at = 0
        for source in (bup_part[...], bdn_part[...], gg[...], bg[...], rg[0:1, :], rg[1:2, :]):
            for lane in range(0, source.shape[1], 128):
                held[0, at : at + 1, :] = source[:, lane : lane + 128]
                at += 1
        both_rows = rg[0:1, :] + rg[1:2, :]
        for lane in range(0, d, 128):
            vec[lane // 128 : lane // 128 + 1, :] = both_rows[:, lane : lane + 128]
        extra = d // 128
        vec[extra:, :] = jnp.full((vec.shape[0] - extra, 128), 0.5, F32) * ids[0].astype(F32)
        sums_main(0).start()
        sums_side(0).start()

    for index in range(len(partners)):

        @pl.when(i == out_start + 2 * (index + 1))
        def _():
            sums_main(index).wait()
            sums_side(index).wait()
            total = held[index] + got[index]
            if index == 0:
                table[dp] = vec[...] + vgot[...]
            if index + 1 < len(partners):
                held[index + 1] = total
                sums_main(index + 1).start()
                sums_side(index + 1).start()
            else:
                sums_out[...] = total
                all_out[...] = table[...]

    @pl.when(i == last - 1)
    def _():
        for chunk, stage in LATE_EVENTS[last]:
            chunks[chunk].happen(stage)


def tail(ids, norm, att, row_cot, dq, dk, dv, wqkv, wout, fam, ori, gain, bdn, bup_part, bdn_part, far_att, both, wdn, wup, hid, cot, orders, rows, collective):
    tokens, d = hid.shape
    ff = wup.shape[1]
    bits = len(orders[0]) - 1
    count = 1 << bits
    seg = far_att.shape[0]
    tile, step = TAIL_TILE, TAIL_STEP
    tiles, blocks = ff // tile, tokens // step
    in_start = 6
    in_end = in_start + tiles
    out_start = in_end + blocks
    out_end = out_start + tiles
    last = out_end + blocks
    marks = (in_start, in_end, out_start, out_end, last)
    size = d // (2 * count)
    rounds = bits + 1
    lines = (ff + 5 * d) // 128
    vec_shape = (d // 128 + 8, 128)
    anywhere = pl.BlockSpec(memory_space=pl.ANY)

    def plane(i):
        late = i >= out_start
        return (jnp.where(late, 0, 1), 0, jnp.clip(jnp.where(late, i - out_start, i - in_start), 0, tiles - 1))

    def home(i):
        return (jnp.clip(jnp.where(i >= out_start, i - out_end, i - in_end), 0, blocks - 1), 0)

    square = pltpu.VMEM((tokens, d), BF16)
    piece = pltpu.VMEM((seg, d), BF16)
    row = pltpu.VMEM((1, d), F32)
    return pl.pallas_call(
        functools.partial(tail_kernel, bits, orders, rows, marks),
        grid=(last,),
        in_specs=[pl.BlockSpec(memory_space=pltpu.SMEM)]
        + [anywhere] * 8
        + [
            whole(fam.shape),
            whole(ori.shape),
            whole((1, d)),
            whole((1, d)),
            whole((1, ff)),
            whole((1, d)),
            whole((seg, d)),
            pl.BlockSpec((1, tokens, tile), plane),
            pl.BlockSpec((tile, d), lambda i: (jnp.clip(i - out_start, 0, tiles - 1), 0)),
            pl.BlockSpec((d, tile), lambda i: (0, jnp.clip(i - in_start, 0, tiles - 1))),
            pl.BlockSpec((step, d), home),
            pl.BlockSpec((step, d), lambda i: (jnp.clip(i - in_end, 0, blocks - 1), 0)),
        ],
        out_specs=[
            pl.BlockSpec((step, d), lambda i: (jnp.clip(i - out_end, 0, blocks - 1), 0)),
            pl.BlockSpec((step, d), lambda i: (jnp.clip(i - in_end, 0, blocks - 1), 0)),
            whole((size, 3 * d)),
            whole((size, d)),
            whole((lines, 128)),
            whole((count,) + vec_shape),
        ],
        out_shape=[
            jax.ShapeDtypeStruct((tokens, d), BF16),
            jax.ShapeDtypeStruct((tokens, d), F32),
            jax.ShapeDtypeStruct((size, 3 * d), F32),
            jax.ShapeDtypeStruct((size, d), F32),
            jax.ShapeDtypeStruct((lines, 128), F32),
            jax.ShapeDtypeStruct((count,) + vec_shape, F32),
        ],
        scratch_shapes=[
            square,
            square,
            square,
            square,
            square,
            pltpu.VMEM((d, 3 * d), BF16),
            pltpu.VMEM((d, d), BF16),
            pltpu.VMEM((d, tokens), BF16),
            pltpu.VMEM((tokens, d), F32),
            piece,
            piece,
            piece,
            row,
            row,
            pltpu.VMEM((2, d), F32),
            pltpu.SemaphoreType.DMA((8,)),
            pltpu.SemaphoreType.DMA((2,)),
            pltpu.VMEM((rounds, lines, 128), F32),
            pltpu.VMEM((rounds, lines, 128), F32),
            pltpu.VMEM(vec_shape, F32),
            pltpu.VMEM(vec_shape, F32),
            pltpu.VMEM((count,) + vec_shape, F32),
            pltpu.SemaphoreType.DMA((rounds,)),
            pltpu.SemaphoreType.DMA((rounds,)),
            pltpu.SemaphoreType.DMA((rounds,)),
            pltpu.SemaphoreType.DMA((rounds,)),
        ]
        + [entry for axes in orders for entry in chunk_scratch(axes, size, d, True)],
        compiler_params=pltpu.CompilerParams(
            vmem_limit_bytes=67043328, collective_id=collective, has_side_effects=True
        ),
        cost_estimate=cost(16 * tokens * d * d + 4 * tokens * d * ff, 8 * d * ff + 40 * tokens * d),
        name="tail",
    )(ids, norm, att, row_cot, dq, dk, dv, wqkv, wout, fam, ori, gain, bdn, bup_part, bdn_part, far_att, both, wdn, wup, hid, cot)


def body_by_rows(
    hidden_in,
    family,
    orient,
    norm_gain,
    norm_bias,
    qkv_weight,
    out_weight,
    up_weight,
    up_bias,
    down_weight,
    down_bias,
    family_table,
    orient_table,
    cotangent,
):
    rows, seg, d = hidden_in.shape
    ff = up_weight.shape[1]
    tokens = rows * seg
    full = 2 * seg
    dp_count = lax.axis_size("dp")
    bits = int(math.log2(dp_count))
    upper = dp_count // 2
    dp = lax.axis_index("dp")
    seq = lax.axis_index("seq")
    ring = [(0, 1), (1, 0)]

    def mine(pair):
        return lax.dynamic_index_in_dim(pair, seq, 0, keepdims=False)

    def theirs(pair):
        return lax.dynamic_index_in_dim(pair, 1 - seq, 0, keepdims=False)

    far_hidden = lax.ppermute(theirs(hidden_in), "seq", ring)
    far_cot = lax.ppermute(theirs(cotangent), "seq", ring)

    gain = norm_gain.reshape(1, d)
    bias = norm_bias.reshape(1, d)
    hid = hidden_in.reshape(tokens, d)
    cot = cotangent.reshape(tokens, d)
    ids = jnp.concatenate([family, orient])
    row_ids = jnp.stack([family[0], mine(orient)])

    normed, both, up_bias_part, down_bias_part = ffn_forward(
        ids, hid, cot, family_table, orient_table, gain, bias, up_weight, up_bias.reshape(1, ff), down_weight, rows
    )
    parts = len(FFN_ORDERS) // 2
    ready = after(normed, far_hidden)
    up = wide_grad(ready, [(both, part, 1, FFN_ORDERS[part]) for part in range(parts)], ff // parts, 1)

    cosine, sine = rope_tables(jnp.arange(full).astype(F32), 128)
    row_normed, row_cot, att, dq, dk, dv, far_att, up_total, down_total, _, _ = middle(
        row_ids,
        mine(hidden_in),
        far_hidden,
        cot,
        far_cot,
        both,
        family_table,
        orient_table,
        gain,
        bias,
        qkv_weight,
        out_weight,
        cosine,
        sine,
        up,
        FFN_ORDERS,
        d // H,
        3,
    )
    layer_out, input_grad, qkv_total, out_total, sums, gathered = tail(
        ids,
        row_normed,
        att,
        row_cot,
        dq,
        dk,
        dv,
        qkv_weight,
        out_weight,
        family_table,
        orient_table,
        gain,
        down_bias.reshape(1, d),
        up_bias_part,
        down_bias_part,
        far_att,
        both,
        down_weight,
        up_weight,
        hid,
        cot,
        LATE_ORDERS,
        rows,
        4,
    )
    flat = sums.reshape(-1)
    up_bias_sum = flat[:ff]
    down_bias_sum, gain_sum, bias_sum = flat[ff : ff + 3 * d].reshape(3, d)
    orient_sum = flat[ff + 3 * d :].reshape(2, d)
    families = family_table.shape[0]
    hot = gathered[:, -1, 0].astype(jnp.int32)[None, :] == jnp.arange(families)[:, None]
    family_sum = jnp.dot(
        hot.astype(F32), gathered[:, :-8].reshape(dp_count, d), precision=lax.Precision.HIGHEST
    )
    return (
        layer_out.reshape(rows, seg, d),
        input_grad.reshape(rows, seg, d),
        gain_sum,
        bias_sum,
        qkv_total,
        out_total,
        up_total,
        up_bias_sum,
        down_total,
        down_bias_sum,
        family_sum,
        orient_sum,
    )


def body(*args):
    hidden_in = args[0]
    dp_count = lax.axis_size("dp")
    two_rows = lax.axis_size("seq") == 2 and hidden_in.shape[0] == 2
    if two_rows and dp_count == 16:
        return body_by_rows(*args)
    return body_by_heads(*args)


def solution(mesh):
    return jax.shard_map(
        body,
        mesh=mesh,
        in_specs=(
            P("dp", "seq", None),
            P("dp"),
            P("dp"),
            P(),
            P(),
            P(),
            P(),
            P(),
            P(),
            P(),
            P(),
            P(),
            P(),
            P("dp", "seq", None),
        ),
        out_specs=(
            P("dp", "seq", None),
            P("dp", "seq", None),
            P(),
            P(),
            P(("dp", "seq"), None),
            P(("dp", "seq"), None),
            P(("dp", "seq"), None),
            P(),
            P(("dp", "seq"), None),
            P(),
            P(),
            P(),
        ),
        check_vma=False,
    )
```

```python
import functools
import math

import jax
import jax.numpy as jnp
from jax import lax
from jax.experimental import pallas as pl
from jax.experimental.pallas import tpu as pltpu
from jax.sharding import PartitionSpec as P

H = 16
HD = 64
ROT = 32
MESH = pl.DeviceIdType.MESH
VMEM_LIMIT = 60 * 1024 * 1024
F32 = jnp.float32
BF16 = jnp.bfloat16


def for_sending(shard):

    def short(part):
        return part.astype(jnp.bfloat16) if part.dtype == jnp.float32 else part

    return jax.tree.map(short, shard)


def rope_tables(positions, features):
    column = jnp.arange(features, dtype=jnp.int32)
    within = column % HD
    frequency = jnp.exp(-(2.0 * (within // 2).astype(jnp.float32) / ROT) * math.log(10000.0))
    angles = positions[:, None] * frequency[None, :]
    rotary = within < ROT
    cosine = jnp.where(rotary[None, :], jnp.cos(angles), 1.0)
    sign_term = jnp.where(within % 2 == 0, -1.0, 1.0)
    sine_term = jnp.where(rotary[None, :], sign_term[None, :] * jnp.sin(angles), 0.0)
    return (cosine, sine_term)


def pair_swap(values):
    even_cols = jnp.arange(values.shape[-1]) % 2 == 0
    return jnp.where(even_cols, jnp.roll(values, -1, axis=-1), jnp.roll(values, 1, axis=-1))


def rotate(values, cosine, sine_term):
    return values * cosine + pair_swap(values) * sine_term


def rotate_back(values, cosine, sine_term):
    return values * cosine + pair_swap(values * sine_term)


def gelu_tanh(pre_values):
    return jax.nn.gelu(pre_values, approximate=True)


def body_by_heads(
    hidden_in,
    family,
    orient,
    norm_gain,
    norm_bias,
    qkv_weight,
    out_weight,
    up_weight,
    up_bias,
    down_weight,
    down_bias,
    family_table,
    orient_table,
    cotangent,
):
    seq_count = lax.axis_size("seq")
    row_count, seg_length, features = hidden_in.shape
    full_length = seg_length * seq_count
    local_heads = H // seq_count
    head_size = features // H
    slab_width = features // seq_count
    block_rows = min(512, full_length)
    block_count = full_length // block_rows
    score_scale = head_size ** (-0.5)
    token_count = row_count * seg_length
    family_rows = jnp.repeat(family, 2)
    family_hot = (family_rows[:, None] == jnp.arange(family_table.shape[0])[None, :]).astype(
        jnp.bfloat16
    )
    orient_hot = (orient[:, None] == jnp.arange(2)[None, :]).astype(jnp.bfloat16)
    embedding = jnp.dot(family_hot, family_table, preferred_element_type=jnp.float32) + jnp.dot(
        orient_hot, orient_table, preferred_element_type=jnp.float32
    )
    embedded = (hidden_in.astype(jnp.float32) + embedding[:, None, :]).reshape(
        token_count, features
    )
    row_mean = jnp.mean(embedded, -1, keepdims=True)
    centred = embedded - row_mean
    row_var = jnp.mean(centred * centred, -1, keepdims=True)
    inv_std = lax.rsqrt(row_var + 1e-05)
    normed_hat = centred * inv_std
    gain_f32 = norm_gain.astype(jnp.float32)
    normed_low = (normed_hat * gain_f32 + norm_bias.astype(jnp.float32)).astype(jnp.bfloat16)
    projected = jnp.dot(normed_low, qkv_weight, preferred_element_type=jnp.float32).reshape(
        row_count, seg_length, 3 * features
    )
    positions = (lax.axis_index("seq") * seg_length + jnp.arange(seg_length)).astype(jnp.float32)
    cosine, sine_term = rope_tables(positions, features)
    queries = rotate(projected[..., :features], cosine, sine_term).astype(jnp.bfloat16)
    keys_rot = rotate(projected[..., features : 2 * features], cosine, sine_term).astype(
        jnp.bfloat16
    )
    values = projected[..., 2 * features :].astype(jnp.bfloat16)
    query_heads, key_heads, value_heads = (
        lax.all_to_all(queries, "seq", split_axis=2, concat_axis=1, tiled=True),
        lax.all_to_all(keys_rot, "seq", split_axis=2, concat_axis=1, tiled=True),
        lax.all_to_all(values, "seq", split_axis=2, concat_axis=1, tiled=True),
    )

    def scores_for(query_block, key_rows, block_start):
        logits = (
            jnp.einsum("qhd,khd->hqk", query_block, key_rows, preferred_element_type=jnp.float32)
            * score_scale
        )
        causal = (block_start + jnp.arange(block_rows))[:, None] >= jnp.arange(full_length)[None, :]
        return jnp.where(causal[None], logits, -1e30)

    def attend(row_args):
        query_row, key_row, value_row = row_args
        key_rows = key_row.reshape(full_length, local_heads, head_size)
        value_rows = value_row.reshape(full_length, local_heads, head_size)
        pieces = []
        log_parts = []
        for block_index in range(block_count):
            block_start = block_index * block_rows
            query_block = query_row[block_start : block_start + block_rows].reshape(
                block_rows, local_heads, head_size
            )
            logits = scores_for(query_block, key_rows, block_start)
            row_peak = jnp.max(logits, -1, keepdims=True)
            weights = jnp.exp(logits - row_peak)
            row_total = jnp.sum(weights, -1, keepdims=True)
            prob_low = (weights / row_total).astype(jnp.bfloat16)
            output_block = jnp.einsum(
                "hqk,khd->qhd", prob_low, value_rows, preferred_element_type=jnp.float32
            )
            pieces.append(output_block.reshape(block_rows, slab_width).astype(jnp.bfloat16))
            log_parts.append((row_peak + jnp.log(row_total))[..., 0])
        return (jnp.concatenate(pieces, 0), jnp.concatenate(log_parts, 1))

    attended_heads, log_sums = lax.map(attend, (query_heads, key_heads, value_heads))
    attended = jax.tree.map(
        lambda part, own: part.astype(own.dtype),
        lax.all_to_all(for_sending(attended_heads), "seq", split_axis=1, concat_axis=2, tiled=True),
        attended_heads,
    )
    attended_flat = attended.reshape(token_count, features)
    branch_attn = jnp.dot(attended_flat, out_weight, preferred_element_type=jnp.float32)
    up_pre = jnp.dot(normed_low, up_weight, preferred_element_type=jnp.float32) + up_bias.astype(
        jnp.float32
    )
    up_act = gelu_tanh(up_pre).astype(jnp.bfloat16)
    branch_feed = jnp.dot(
        up_act, down_weight, preferred_element_type=jnp.float32
    ) + down_bias.astype(jnp.float32)
    layer_out = (
        (embedded + branch_attn + branch_feed)
        .astype(jnp.bfloat16)
        .reshape(row_count, seg_length, features)
    )
    grad_low = cotangent.reshape(token_count, features)
    grad_f32 = grad_low.astype(jnp.float32)
    down_grad = jnp.einsum("nf,nd->fd", up_act, grad_low, preferred_element_type=jnp.float32)
    down_bias_grad = jnp.sum(grad_f32, 0)
    act_grad = jnp.einsum("nd,fd->nf", grad_low, down_weight, preferred_element_type=jnp.float32)
    gelu_out, gelu_pull = jax.vjp(gelu_tanh, up_pre)
    pre_grad = gelu_pull(act_grad)[0].astype(jnp.bfloat16)
    up_bias_grad = jnp.sum(pre_grad.astype(jnp.float32), 0)
    up_grad = jnp.einsum("nd,nf->df", normed_low, pre_grad, preferred_element_type=jnp.float32)
    normed_grad = jnp.einsum("nf,df->nd", pre_grad, up_weight, preferred_element_type=jnp.float32)
    out_grad = jnp.einsum("nd,ne->de", attended_flat, grad_low, preferred_element_type=jnp.float32)
    attended_grad = jnp.einsum(
        "ne,de->nd", grad_low, out_weight, preferred_element_type=jnp.float32
    )
    attended_grad = attended_grad.astype(jnp.bfloat16).reshape(row_count, seg_length, features)
    grad_heads = lax.all_to_all(attended_grad, "seq", split_axis=2, concat_axis=1, tiled=True)

    def attend_back(row_args):
        query_row, key_row, value_row, grad_row, log_row = row_args
        key_rows = key_row.reshape(full_length, local_heads, head_size)
        value_rows = value_row.reshape(full_length, local_heads, head_size)
        keys_total = jnp.zeros((full_length, local_heads, head_size), jnp.float32)
        values_total = jnp.zeros((full_length, local_heads, head_size), jnp.float32)
        query_parts = []
        for block_index in range(block_count):
            block_start = block_index * block_rows
            query_block = query_row[block_start : block_start + block_rows].reshape(
                block_rows, local_heads, head_size
            )
            grad_block = grad_row[block_start : block_start + block_rows].reshape(
                block_rows, local_heads, head_size
            )
            logits = scores_for(query_block, key_rows, block_start)
            probs_full = jnp.exp(logits - log_row[:, block_start : block_start + block_rows, None])
            prob_low = probs_full.astype(jnp.bfloat16)
            probs_grad = jnp.einsum(
                "qhd,khd->hqk", grad_block, value_rows, preferred_element_type=jnp.float32
            )
            inner_sum = jnp.sum(probs_full * probs_grad, -1, keepdims=True)
            scores_grad = (probs_full * (probs_grad - inner_sum)).astype(jnp.bfloat16)
            values_total = values_total + jnp.einsum(
                "hqk,qhd->khd", prob_low, grad_block, preferred_element_type=jnp.float32
            )
            query_grad = (
                jnp.einsum(
                    "hqk,khd->qhd", scores_grad, key_rows, preferred_element_type=jnp.float32
                )
                * score_scale
            )
            query_parts.append(query_grad.reshape(block_rows, slab_width).astype(jnp.bfloat16))
            keys_total = (
                keys_total
                + jnp.einsum(
                    "hqk,qhd->khd", scores_grad, query_block, preferred_element_type=jnp.float32
                )
                * score_scale
            )
        return (
            jnp.concatenate(query_parts, 0),
            keys_total.reshape(full_length, slab_width).astype(jnp.bfloat16),
            values_total.reshape(full_length, slab_width).astype(jnp.bfloat16),
        )

    query_grad_heads, key_grad_heads, value_grad_heads = lax.map(
        attend_back, (query_heads, key_heads, value_heads, grad_heads, log_sums)
    )
    query_grad_pos, key_grad_pos, value_grad_pos = (
        lax.all_to_all(
            for_sending(query_grad_heads), "seq", split_axis=1, concat_axis=2, tiled=True
        ).astype(query_grad_heads.dtype),
        lax.all_to_all(
            for_sending(key_grad_heads), "seq", split_axis=1, concat_axis=2, tiled=True
        ).astype(key_grad_heads.dtype),
        lax.all_to_all(
            for_sending(value_grad_heads), "seq", split_axis=1, concat_axis=2, tiled=True
        ).astype(value_grad_heads.dtype),
    )
    projected_grad = jnp.concatenate(
        [
            rotate_back(query_grad_pos.astype(jnp.float32), cosine, sine_term),
            rotate_back(key_grad_pos.astype(jnp.float32), cosine, sine_term),
            value_grad_pos.astype(jnp.float32),
        ],
        -1,
    )
    projected_grad = projected_grad.astype(jnp.bfloat16).reshape(token_count, 3 * features)
    qkv_grad = jnp.einsum(
        "nd,ne->de", normed_low, projected_grad, preferred_element_type=jnp.float32
    )
    normed_grad = normed_grad + jnp.einsum(
        "ne,de->nd", projected_grad, qkv_weight, preferred_element_type=jnp.float32
    )
    gain_grad = jnp.sum(normed_grad * normed_hat, 0)
    bias_grad = jnp.sum(normed_grad, 0)
    scaled_grad = normed_grad * gain_f32
    hat_grad = (
        scaled_grad
        - jnp.mean(scaled_grad, -1, keepdims=True)
        - normed_hat * jnp.mean(scaled_grad * normed_hat, -1, keepdims=True)
    )
    input_grad = (grad_f32 + inv_std * hat_grad).reshape(row_count, seg_length, features)
    row_sums = jnp.sum(input_grad, 1)
    family_grad = jnp.einsum(
        "rf,rd->fd", family_hot.astype(jnp.float32), row_sums, precision=lax.Precision.HIGHEST
    )
    orient_grad = jnp.einsum(
        "rf,rd->fd", orient_hot.astype(jnp.float32), row_sums, precision=lax.Precision.HIGHEST
    )
    gain_sum, bias_sum, up_bias_sum, down_bias_sum, family_sum, orient_sum = lax.psum(
        (gain_grad, bias_grad, up_bias_grad, down_bias_grad, family_grad, orient_grad),
        ("dp", "seq"),
    )
    qkv_sum, out_sum, up_sum, down_sum = (
        lax.psum_scatter(qkv_grad, ("dp", "seq"), scatter_dimension=0, tiled=True),
        lax.psum_scatter(out_grad, ("dp", "seq"), scatter_dimension=0, tiled=True),
        lax.psum_scatter(up_grad, ("dp", "seq"), scatter_dimension=0, tiled=True),
        lax.psum_scatter(down_grad, ("dp", "seq"), scatter_dimension=0, tiled=True),
    )
    return (
        layer_out,
        input_grad,
        gain_sum,
        bias_sum,
        qkv_sum,
        out_sum,
        up_sum,
        up_bias_sum,
        down_sum,
        down_bias_sum,
        family_sum,
        orient_sum,
    )


def dot_nn(a, b):
    return lax.dot_general(a, b, (((1,), (0,)), ((), ())), preferred_element_type=F32)


def dot_nt(a, b):
    return lax.dot_general(a, b, (((1,), (1,)), ((), ())), preferred_element_type=F32)


def dot_tn(a, b):
    return lax.dot_general(a, b, (((0,), (0,)), ((), ())), preferred_element_type=F32)


def params(**more):
    return pltpu.CompilerParams(vmem_limit_bytes=VMEM_LIMIT, **more)


def cost(flops, moved, exps=0):
    return pl.CostEstimate(flops=flops, bytes_accessed=moved, transcendentals=exps)


def whole(shape):
    return pl.BlockSpec(shape, lambda *_: (0,) * len(shape), pipeline_mode=pl.Buffered(1))


def table_row(table, wanted):
    rows = lax.broadcasted_iota(jnp.int32, table.shape, 0)
    return jnp.sum(jnp.where(rows == wanted, table[...].astype(F32), 0.0), 0, keepdims=True)


def normalise(entries):
    centred = entries - jnp.mean(entries, -1, keepdims=True)
    inv_std = lax.rsqrt(jnp.mean(centred * centred, -1, keepdims=True) + 1e-05)
    return centred * inv_std, inv_std


GELU_C = math.sqrt(2.0 / math.pi)


def gelu_both(z):
    square = z * z
    half = 0.5 + 0.5 * jnp.tanh(z * (GELU_C + (GELU_C * 0.044715) * square))
    value = z * half
    slope = half + value * (1.0 - half) * (2 * GELU_C + (6 * GELU_C * 0.044715) * square)
    return value, slope


def ffn_kernel(rows, ids, hid, cot, fam, ori, gain, bias, wup, bup, wdn, turned, both, bupg, bdng, norm):
    tokens = hid.shape[0]
    seg = tokens // rows
    step = 256

    @pl.when(pl.program_id(0) == 0)
    def _():
        total = jnp.zeros((1, cot.shape[1]), F32)
        for row in range(rows):
            emb = table_row(fam, ids[0]) + table_row(ori, ids[1 + row])
            for start in range(row * seg, (row + 1) * seg, step):
                part = pl.ds(start, step)
                hat, _ = normalise(hid[part, :].astype(F32) + emb)
                norm[part, :] = (hat * gain[...].astype(F32) + bias[...].astype(F32)).astype(BF16)
                total = total + jnp.sum(cot[part, :].astype(F32), 0, keepdims=True)
        bdng[...] = total
        turned[...] = norm[...].T

    width = wup.shape[1]
    total = jnp.zeros((8, width), F32)
    lin = dot_nn(norm[...], wup[...])
    into = dot_nt(cot[...], wdn[...])
    step = 64
    for start in range(0, tokens, step):
        part = pl.ds(start, step)
        value, slope = gelu_both(lin[start : start + step] + bup[...].astype(F32))
        low = into[start : start + step] * slope
        both[0, part, :] = value.astype(BF16)
        both[1, part, :] = low.astype(BF16)
        total = total + jnp.sum(low.reshape(step // 8, 8, width), 0)
    bupg[...] = jnp.sum(total, 0, keepdims=True)


def ffn_forward(ids, hid, cot, fam, ori, gain, bias, wup, bup, wdn, rows):
    tokens, d = hid.shape
    ff = wup.shape[1]
    tile = 512
    return pl.pallas_call(
        functools.partial(ffn_kernel, rows),
        grid_spec=pltpu.PrefetchScalarGridSpec(
            num_scalar_prefetch=1,
            grid=(ff // tile,),
            in_specs=[
                whole((tokens, d)),
                whole((tokens, d)),
                whole(fam.shape),
                whole(ori.shape),
                whole((1, d)),
                whole((1, d)),
                pl.BlockSpec((d, tile), lambda i, s: (0, i)),
                pl.BlockSpec((1, tile), lambda i, s: (0, i)),
                pl.BlockSpec((tile, d), lambda i, s: (i, 0)),
            ],
            out_specs=[
                whole((d, tokens)),
                pl.BlockSpec((2, tokens, tile), lambda i, s: (0, 0, i)),
                pl.BlockSpec((1, tile), lambda i, s: (0, i)),
                whole((1, d)),
            ],
            scratch_shapes=[pltpu.VMEM((tokens, d), BF16)],
        ),
        out_shape=[
            jax.ShapeDtypeStruct((d, tokens), BF16),
            jax.ShapeDtypeStruct((2, tokens, ff), BF16),
            jax.ShapeDtypeStruct((1, ff), F32),
            jax.ShapeDtypeStruct((1, d), F32),
        ],
        compiler_params=params(),
        cost_estimate=cost(4 * tokens * d * ff, 4 * tokens * ff + 4 * d * ff, tokens * ff),
        name="ffn_forward",
    )(ids, hid, cot, fam, ori, gain, bias, wup, bup, wdn)


def turn(entries, cosine, sine):
    even = lax.broadcasted_iota(jnp.int32, entries.shape, 1) % 2 == 0
    other = jnp.where(even, pltpu.roll(entries, 127, 1), pltpu.roll(entries, 1, 1))
    return entries * cosine + other * sine


def turn_back(entries, cosine, sine):
    even = lax.broadcasted_iota(jnp.int32, entries.shape, 1) % 2 == 0
    side = entries * sine
    other = jnp.where(even, pltpu.roll(side, 127, 1), pltpu.roll(side, 1, 1))
    return entries * cosine + other


def attend(head_size, query_ref, k_ref, v_ref, g_ref, cos, sin, o_ref, dq_ref, dk_ref, dv_ref, dkt, dvt):
    full = query_ref.shape[0]
    block = 256
    scale = head_size ** (-0.5)
    first = lax.broadcasted_iota(jnp.int32, (block, 128), 1) < head_size
    below = lax.broadcasted_iota(jnp.int32, (block, block), 0) >= lax.broadcasted_iota(
        jnp.int32, (block, block), 1
    )
    dkt[...] = jnp.zeros_like(dkt)
    dvt[...] = jnp.zeros_like(dvt)

    def by_head(entries):
        none = jnp.zeros_like(entries)
        return jnp.concatenate([jnp.where(first, entries, none), jnp.where(first, none, entries)], 0)

    def front(start):
        part, end = pl.ds(start, block), start + block
        query = by_head((query_ref[part, :].astype(F32) * scale).astype(BF16))
        grad = by_head(g_ref[part, :])
        return query, grad, dot_nt(query, k_ref[0:end, :]), dot_nt(grad, v_ref[0:end, :])

    def back(start, query, grad, scores, into):
        part, end = pl.ds(start, block), start + block
        lows, slopes = [], []
        for head in range(2):
            rows = slice(head * block, (head + 1) * block)
            score = scores[rows]
            last = jnp.where(below, score[:, start:end], -1e30)
            score = last if start == 0 else jnp.concatenate([score[:, :start], last], 1)
            weights = jnp.exp(score - jnp.max(score, -1, keepdims=True))
            probs = weights * (1.0 / jnp.sum(weights, -1, keepdims=True))
            lows.append(probs.astype(BF16))
            inner = jnp.sum(probs * into[rows], -1, keepdims=True)
            slopes.append((probs * (into[rows] - inner)).astype(BF16))
        low = jnp.concatenate(lows, 0)
        slope = jnp.concatenate(slopes, 0)
        out = dot_nn(low, v_ref[0:end, :])
        dq = dot_nn(slope, k_ref[0:end, :])
        o_ref[part, :] = jnp.where(first, out[:block], out[block:]).astype(BF16)
        dq = jnp.where(first, dq[:block], dq[block:]) * scale
        dq_ref[part, :] = turn_back(dq, cos[part, :], sin[part, :]).astype(BF16)
        dkt[:, 0:end] += dot_tn(query, slope)
        dvt[:, 0:end] += dot_tn(grad, low)

    ready = front(0)
    for start in range(0, full, block):
        later = front(start + block) if start + block < full else None
        back(start, *ready)
        ready = later
    for start in range(0, full, block):
        part = pl.ds(start, block)
        dk = dkt[:, start : start + block].T
        dk_ref[part, :] = turn_back(dk, cos[part, :], sin[part, :]).astype(BF16)
        dv_ref[part, :] = dvt[:, start : start + block].T.astype(BF16)


FFN_ORDERS = [
    [2, "seq", 1, 3],
    [2, 1, "seq", 3],
    [1, "seq", 3, 2],
    [1, "seq", 2, 3],
    [1, "seq", 3, 2],
    [2, 1, "seq", 3],
    [2, 1, "seq", 3],
    ["seq", 2, 1, 3],
]
LATE_ORDERS = [
    [0, 2, 1, "seq", 3],
    [0, 1, 3, 2, "seq"],
    [0, 2, 1, "seq", 3],
    [0, 1, "seq", 3, 2],
]
FFN_EVENTS = {
    4: [(0, 0)],
    6: [(1, 0)],
    8: [(2, 0)],
    9: [(3, 0)],
    14: [(0, 1)],
    17: [(6, 0), (7, 0), (4, 0), (5, 0), (2, 1)],
    19: [(1, 1), (0, 2)],
    22: [(3, 1)],
    25: [(6, 1), (7, 1)],
    26: [(4, 1), (2, 2)],
    27: [(1, 2), (5, 1), (3, 2), (0, 3)],
    28: [(7, 2), (6, 2), (4, 2)],
    29: [(2, 3), (3, 3), (1, 3), (5, 2), (0, 4)],
    30: [(7, 3), (6, 3), (4, 3)],
    31: [(2, 4), (5, 3), (3, 4), (1, 4)],
    32: [(7, 4), (6, 4), (4, 4), (5, 4)],
}
LATE_EVENTS = {
    2: [(0, 1)],
    3: [(1, 1)],
    4: [(2, 1)],
    6: [(3, 1)],
    7: [(0, 2)],
    8: [(1, 2)],
    13: [(2, 2)],
    14: [(3, 2)],
    17: [(0, 3)],
    18: [(1, 3)],
    20: [(3, 3), (2, 3)],
    21: [(0, 4)],
    23: [(1, 4)],
    25: [(2, 4)],
    26: [(3, 4)],
    27: [(1, 5)],
    28: [(0, 5)],
    30: [(2, 5), (3, 5)],
}


def middle_kernel(tiles, pairs, head_size, bits, orders, *refs):
    ids, own, far, home_cot, turned, pre, act, fam, ori, gain, bias, wqkv, wout, cos, sin, cot_hbm = refs[:16]
    norm, cot, o_ref, dq_ref, dk_ref, dv_ref, far_att, up_out, down_out = refs[16:25]
    near_up, far_up, near_down, far_down = refs[25:29]
    heads, dkt, dvt, att_send, att_got, att_sems, cfar, cfar_sems = refs[29:37]
    keep, send, got, send_sem, recv_sem, out_sem = refs[37:43]
    up_keep, up_send, up_got, up_ssem, up_rsem, up_osem = refs[43:49]
    seg = own.shape[0]
    step = 256
    base = 1 << (bits - 1)
    now = pl.program_id(0)
    ups = up_out.shape[1] // up_keep.shape[3]
    late = now - ups
    i = late - base
    me = lax.axis_index("seq")
    mine = device_bits(bits)
    parts = len(orders) // 2
    up_part = up_out.shape[1] // parts
    down_part = down_out.shape[1] // parts
    chunks = chunks_from(
        refs[49:],
        bits,
        mine,
        [
            (orders[part], near_up, far_up, pl.ds(part * up_part, up_part), up_out)
            for part in range(parts)
        ]
        + [
            (orders[parts + part], near_down, far_down, pl.ds(part * down_part, down_part), down_out)
            for part in range(parts)
        ],
    )

    def happen(events):
        for chunk, stage in events:
            chunks[chunk].happen(stage)

    @pl.when(now == 0)
    def _():
        meet([partner_along(axis, mine) for axis in [0] + orders[0]])

    cot_crossing = remote(
        cot_hbm.at[pl.ds(pl.multiple_of((1 - me) * seg, seg), seg)],
        cfar,
        cfar_sems.at[0],
        cfar_sems.at[1],
        partner_along("seq", mine),
    )

    @pl.when(now == 0)
    def _():
        cot_crossing.start()

    last = ups + base + 4 * tiles + pairs
    def up_crossing(index):
        slot = lax.rem(index, 2)
        return remote(
            up_send.at[slot], up_got.at[slot], up_ssem.at[slot], up_rsem.at[slot], partner_along(0, mine)
        )

    def up_stores(index):
        slot = lax.rem(index, 2)
        width = up_keep.shape[3]
        columns = pl.ds(pl.multiple_of(index * width, width), width)
        return [
            pltpu.make_async_copy(
                up_keep.at[slot, pl.ds(half * base, base)], there.at[:, :, columns], up_osem.at[half, slot]
            )
            for half, there in enumerate((near_up, far_up))
        ]

    def up_finish(index):
        slot = lax.rem(index, 2)
        up_crossing(index).wait()
        add_into(up_keep.at[slot], up_got.at[slot])
        for copy in up_stores(index):
            copy.start()

    for when, what in FFN_EVENTS.items():
        if when < last:

            @pl.when(now == when)
            def _():
                happen(what)

    per_chunk = ups // parts
    for part in range(parts):
        places = [block_place(orders[part], mine, up, seq) for up in range(base) for seq in range(2)]

        @pl.when((now >= part * per_chunk) & (now < (part + 1) * per_chunk))
        def _():
            value = dot_nn(turned[...], pre[...])
            slot = lax.rem(now, 2)

            @pl.when(now > 0)
            def _():
                up_finish(now - 1)

            @pl.when(now > 1)
            def _():
                for copy in up_stores(now - 2):
                    copy.wait()

            split_blocks(value, up_keep.at[slot], up_send.at[slot], up_keep.shape[2], mine[0], places)
            up_crossing(now).start()

    @pl.when(now == ups)
    def _():
        up_finish(now - 1)
        for index in (now - 2, now - 1):
            for copy in up_stores(index):
                copy.wait()

    def crossing(index):
        slot = lax.rem(index, 2)
        return remote(
            send.at[slot], got.at[slot], send_sem.at[slot], recv_sem.at[slot], partner_along(0, mine)
        )

    def store(index, act_on):
        slot = lax.rem(index, 2)
        width = home_cot.shape[1] // parts
        for seq in range(2):
            for part in range(parts):
                place = 0
                for axis in orders[parts + part]:
                    if axis == "seq":
                        apart = lax.rem(mine["seq"] + seq, 2)
                    else:
                        apart = lax.rem(index // (1 << (axis - 1)) + mine[axis], 2)
                    place = 2 * place + apart
                columns = pl.ds(part * width, width)
                source = keep.at[slot, seq, :, columns]
                sem = out_sem.at[slot, seq, part]
                there = lax.rem(place, base)

                @pl.when(place < base)
                def _():
                    act_on(pltpu.make_async_copy(source, near_down.at[there, :, columns], sem))

                @pl.when(place >= base)
                def _():
                    act_on(pltpu.make_async_copy(source, far_down.at[there, :, columns], sem))

    def finish(index):
        slot = lax.rem(index, 2)
        crossing(index).wait()
        add_into(keep.at[slot], got.at[slot])
        store(index, lambda copy: copy.start())

    @pl.when((late >= 0) & (late < base))
    def _():
        value = dot_nn(act[...].T, home_cot[...])
        slot = lax.rem(late, 2)

        @pl.when(late > 0)
        def _():
            finish(late - 1)

        @pl.when(late > 1)
        def _():
            store(late - 2, lambda copy: copy.wait())

        split_blocks(value, keep.at[slot], send.at[slot], keep.shape[2], mine[0], [0, 1])
        crossing(late).start()

    @pl.when(late == base)
    def _():
        finish(late - 1)
        store(late - 2, lambda copy: copy.wait())
        store(late - 1, lambda copy: copy.wait())

    @pl.when(i == 0)
    def _():
        emb = table_row(fam, ids[0]) + table_row(ori, ids[1])
        for source, where in ((own, me), (far, 1 - me)):
            for start in range(0, seg, step):
                part = pl.ds(start, step)
                there = pl.ds(pl.multiple_of(where * seg + start, step), step)
                hat, _ = normalise(source[part, :].astype(F32) + emb)
                norm[there, :] = (hat * gain[...].astype(F32) + bias[...].astype(F32)).astype(BF16)
        held = pl.ds(pl.multiple_of(me * seg, seg), seg)
        cot[held, :] = home_cot[held, :]

    lanes = wqkv.shape[1] // 128

    def att_crossing(pair):
        return remote(
            att_send.at[pair],
            att_got.at[pair],
            att_sems.at[0, pair],
            att_sems.at[1, pair],
            partner_along("seq", mine),
        )

    @pl.when((i >= 0) & (i < 2 * tiles))
    def _():
        lin = dot_nn(norm[...], wqkv[...])
        for start in range(0, 2 * seg, step):
            part = pl.ds(start, step)
            for lane in range(lanes):
                piece = lin[start : start + step, lane * 128 : (lane + 1) * 128]
                heads[i * lanes + lane, part, :] = turn(piece, cos[part, :], sin[part, :]).astype(BF16)

    @pl.when((i >= 2 * tiles) & (i < 3 * tiles))
    def _():
        lin = dot_nn(norm[...], wqkv[...]).astype(BF16)
        for lane in range(lanes):
            heads[i * lanes + lane] = lin[:, lane * 128 : (lane + 1) * 128]

    @pl.when(i == 3 * tiles)
    def _():
        cot_crossing.wait()
        cot[pl.ds(pl.multiple_of((1 - me) * seg, seg), seg), :] = cfar[...]

    @pl.when((i >= 3 * tiles) & (i < 4 * tiles))
    def _():
        lin = dot_nt(cot[...], wout[...]).astype(BF16)
        for lane in range(lanes):
            heads[i * lanes + lane] = lin[:, lane * 128 : (lane + 1) * 128]

    @pl.when(i >= 4 * tiles)
    def _():
        pair = i - 4 * tiles
        attend(
            head_size,
            heads.at[pair],
            heads.at[pairs + pair],
            heads.at[2 * pairs + pair],
            heads.at[3 * pairs + pair],
            cos,
            sin,
            o_ref,
            dq_ref,
            dk_ref,
            dv_ref,
            dkt,
            dvt,
        )
        att_send[pair] = o_ref[pl.ds(pl.multiple_of((1 - me) * seg, seg), seg), :]
        att_crossing(pair).start()

    @pl.when(now == last - 1)
    def _():
        for pair in range(pairs):
            att_crossing(pair).wait()
            far_att[:, pair * 128 : (pair + 1) * 128] = att_got[pair]
        happen(FFN_EVENTS[last])


def middle(
    ids, own, far, home_cot, turned, both, fam, ori, gain, bias, wqkv, wout, cos, sin, orders, head_size, collective
):
    seg, d = own.shape
    full = 2 * seg
    tile = 512
    tiles = d // tile
    pairs = d // 128
    bits = len(orders[0])
    base = 1 << (bits - 1)
    parts = len(orders) // 2
    ff = both.shape[2]
    up_size = d // (4 * base)
    up_tile = 512
    ups = ff // up_tile
    down_tile = ff // base
    down_size = down_tile // 4
    smem = pl.BlockSpec(memory_space=pltpu.SMEM)
    anywhere = pl.BlockSpec(memory_space=pl.ANY)
    late = ups + base
    attend_at = late + 4 * tiles
    head_out = pl.BlockSpec((full, 128), lambda i: (0, jnp.maximum(i - attend_at, 0)))
    rows = jax.ShapeDtypeStruct((full, d), BF16)
    down = jax.ShapeDtypeStruct((base, down_size, d), BF16)
    up = jax.ShapeDtypeStruct((base, up_size, ff), BF16)
    slots = pltpu.VMEM((2, 2, down_size, d), BF16)
    up_slots = pltpu.VMEM((2, 2 * base, up_size, up_tile), BF16)
    return pl.pallas_call(
        functools.partial(middle_kernel, tiles, pairs, head_size, bits, orders),
        grid=(attend_at + pairs,),
        in_specs=[
            smem,
            whole((seg, d)),
            whole((seg, d)),
            whole((full, d)),
            whole((d, full)),
            pl.BlockSpec((None, full, up_tile), lambda i: (1, 0, jnp.minimum(i, ups - 1))),
            pl.BlockSpec((None, full, down_tile), lambda i: (0, 0, jnp.clip(i - ups, 0, base - 1))),
            whole(fam.shape),
            whole(ori.shape),
            whole((1, d)),
            whole((1, d)),
            pl.BlockSpec((d, tile), lambda i: (0, jnp.clip(i - late, 0, 3 * tiles - 1))),
            pl.BlockSpec((tile, d), lambda i: (jnp.clip(i - late - 3 * tiles, 0, tiles - 1), 0)),
            whole((full, 128)),
            whole((full, 128)),
        ]
        + [anywhere],
        out_specs=[
            whole((full, d)),
            whole((full, d)),
            head_out,
            head_out,
            head_out,
            head_out,
            whole((seg, d)),
            whole((up_size, ff)),
            whole((down_size, d)),
            anywhere,
            anywhere,
            anywhere,
            anywhere,
        ],
        out_shape=[
            rows,
            rows,
            rows,
            rows,
            rows,
            rows,
            jax.ShapeDtypeStruct((seg, d), BF16),
            jax.ShapeDtypeStruct((up_size, ff), F32),
            jax.ShapeDtypeStruct((down_size, d), F32),
            up,
            up,
            down,
            down,
        ],
        scratch_shapes=[
            pltpu.VMEM((4 * pairs, full, 128), BF16),
            pltpu.VMEM((128, full), F32),
            pltpu.VMEM((128, full), F32),
            pltpu.VMEM((pairs, seg, 128), BF16),
            pltpu.VMEM((pairs, seg, 128), BF16),
            pltpu.SemaphoreType.DMA((2, pairs)),
            pltpu.VMEM((seg, d), BF16),
            pltpu.SemaphoreType.DMA((2,)),
            slots,
            slots,
            slots,
            pltpu.SemaphoreType.DMA((2,)),
            pltpu.SemaphoreType.DMA((2,)),
            pltpu.SemaphoreType.DMA((2, 2, parts)),
            up_slots,
            up_slots,
            up_slots,
            pltpu.SemaphoreType.DMA((2,)),
            pltpu.SemaphoreType.DMA((2,)),
            pltpu.SemaphoreType.DMA((2, 2)),
        ]
        + [
            entry
            for index, axes in enumerate(orders)
            for entry in chunk_scratch(
                axes, *((up_size, ff // parts) if index < parts else (down_size, d // parts))
            )
        ],
        compiler_params=pltpu.CompilerParams(
            vmem_limit_bytes=67043328, collective_id=collective, has_side_effects=True
        ),
        cost_estimate=cost(16 * full * d * d + 12 * full * full * d, 8 * d * d + 18 * full * d, full * full * H),
        name="middle",
    )(ids, own, far, home_cot, turned, both, both, fam, ori, gain, bias, wqkv, wout, cos, sin, home_cot)


def device_bits(bits):
    dp = lax.axis_index("dp")
    found = {bit: lax.rem(dp // (1 << bit), 2) for bit in range(bits)}
    found["seq"] = lax.axis_index("seq")
    return found


def block_place(axes, mine, upper, seq):
    place = 0
    for axis in axes:
        bit = seq if axis == "seq" else (upper >> (axis - 1)) & 1
        place = 2 * place + (1 - mine[axis] if bit else mine[axis])
    return place


def other_core():
    dp = lax.axis_index("dp")
    return (dp + 1 - 2 * lax.rem(dp, 2), lax.axis_index("seq"))


def meet(partners):
    barrier = pltpu.get_barrier_semaphore()
    for partner in partners:
        pl.semaphore_signal(barrier, inc=1, device_id=partner, device_id_type=MESH)
    pl.semaphore_wait(barrier, len(partners))


def remote(src, dst, send_sem, recv_sem, partner):
    return pltpu.make_async_remote_copy(
        src_ref=src,
        dst_ref=dst,
        send_sem=send_sem,
        recv_sem=recv_sem,
        device_id=partner,
        device_id_type=MESH,
    )


def split_blocks(value, keep, send, size, core, places):
    for index, there in enumerate(places):
        up, seq = index // 2, index % 2
        first = (4 * up + seq) * size
        second = first + 2 * size
        a = value[first : first + size, :].astype(BF16)
        b = value[second : second + size, :].astype(BF16)
        keep[there] = jnp.where(core == 0, a, b)
        send[there] = jnp.where(core == 0, b, a)


def add_into(keep, got):
    def add(index, carry):
        keep[index] = (keep[index].astype(F32) + got[index].astype(F32)).astype(BF16)
        return carry

    lax.fori_loop(0, keep.shape[0], add, 0)


def partner_along(axis, mine):
    dp = lax.axis_index("dp")
    seq = lax.axis_index("seq")
    if axis == "seq":
        return (dp, 1 - seq)
    return (dp + (1 - 2 * mine[axis]) * (1 << axis), seq)


class Chunk:
    def __init__(self, axes, mine, near, far, columns, out, keep, got, near_sem, send_sem, recv_sem):
        self.axes, self.mine, self.near, self.far = axes, mine, near, far
        self.columns, self.out, self.keep, self.got = columns, out, keep, got
        self.near_sem, self.send_sem, self.recv_sem = near_sem, send_sem, recv_sem

    def load(self):
        return pltpu.make_async_copy(self.near.at[:, :, self.columns], self.keep, self.near_sem)

    def crossing(self, stage):
        count = (1 << len(self.axes)) >> (stage + 1)
        if stage == 0 and self.far is not None:
            source = self.far.at[:, :, self.columns]
        else:
            source = self.keep.at[pl.ds(count, count)]
        return remote(
            source,
            self.got[stage],
            self.send_sem.at[stage],
            self.recv_sem.at[stage],
            partner_along(self.axes[stage], self.mine),
        )

    def begin(self):
        if self.near is not None:
            self.load().start()
        self.crossing(0).start()

    def advance(self, stage):
        if stage == 1 and self.near is not None:
            self.load().wait()
        self.crossing(stage - 1).wait()
        count = (1 << len(self.axes)) >> stage

        def add(index, carry):
            self.keep[index] = (self.keep[index].astype(F32) + self.got[stage - 1][index].astype(F32)).astype(BF16)
            return carry

        lax.fori_loop(0, count, add, 0)
        self.crossing(stage).start()

    def finish(self):
        last = len(self.axes) - 1
        self.crossing(last).wait()
        self.out[:, self.columns] = self.keep[0].astype(F32) + self.got[last][0].astype(F32)

    def happen(self, stage):
        if stage == 0:
            self.begin()
        elif stage == len(self.axes):
            self.finish()
        else:
            self.advance(stage)


def chunk_scratch(axes, size, width, farther=False):
    half = 1 << (len(axes) - 1)
    return (
        [pltpu.VMEM((2 * half if farther else half, size, width), BF16)]
        + [pltpu.VMEM((half >> stage, size, width), BF16) for stage in range(len(axes))]
        + [
            pltpu.SemaphoreType.DMA,
            pltpu.SemaphoreType.DMA((len(axes),)),
            pltpu.SemaphoreType.DMA((len(axes),)),
        ]
    )


def chunks_from(refs, bits, mine, wanted):
    stages = bits
    found = []
    each = 1 + stages + 3
    for index, (axes, near, far, columns, out) in enumerate(wanted):
        part = refs[index * each : (index + 1) * each]
        found.append(
            Chunk(axes, mine, near, far, columns, out, part[0], part[1 : 1 + stages], *part[1 + stages :])
        )
    return found


def after(entry, *others):
    return lax.optimization_barrier((entry, *others))[0]


TAIL_TILE = 512
TAIL_STEP = 256


def tail_kernel(bits, orders, rows, marks, *refs):
    ids, norm_hbm, att_hbm, cot_hbm, dq_hbm, dk_hbm, dv_hbm, wqkv_hbm, wout_hbm = refs[:9]
    fam, ori, gain, bdn, bup_part, bdn_part, far_att = refs[9:16]
    both, wdn, wup, hid, cot = refs[16:21]
    layer_out, input_out, qkv_out, out_out, sums_out, all_out = refs[21:27]
    left, right, dq, dk, dv, wqkv, wout, turned, acc, ng_send, ng_own, ng_got = refs[27:39]
    gg, bg, rg, load_sem, ng_sem, held, got, vec, vgot, table, ssem, rsem, gsend, grecv = refs[39:53]
    in_start, in_end, out_start, out_end, last = marks
    i = pl.program_id(0)
    me = lax.axis_index("seq")
    dp = lax.axis_index("dp")
    mine = device_bits(bits)
    d = left.shape[1]
    seg = ng_own.shape[0]
    step = TAIL_STEP
    per_row = seg // step
    chunks = chunks_from(
        refs[53:],
        len(orders[0]),
        mine,
        [
            (orders[0], None, None, pl.ds(0, d), qkv_out),
            (orders[1], None, None, pl.ds(d, d), qkv_out),
            (orders[2], None, None, pl.ds(2 * d, d), qkv_out),
            (orders[3], None, None, pl.ds(0, d), out_out),
        ],
    )
    loads = {
        name: pltpu.make_async_copy(source, there, load_sem.at[index])
        for index, (name, source, there) in enumerate(
            (
                ("norm", norm_hbm, left),
                ("dq", dq_hbm, dq),
                ("dk", dk_hbm, dk),
                ("dv", dv_hbm, dv),
                ("wqkv", wqkv_hbm, wqkv),
                ("cot", cot_hbm, right),
                ("wout", wout_hbm, wout),
                ("att", att_hbm, left),
            )
        )
    }
    partners = [partner_along(axis, mine) for axis in ["seq"] + list(range(bits))]

    def gradient(index, operand):
        chunk = chunks[index]
        size = chunk.keep.shape[1]
        value = dot_nn(turned[...], operand[...])
        for block in range(chunk.keep.shape[0]):
            place = 0
            for axis in orders[index]:
                bit = block & 1 if axis == "seq" else (block >> (axis + 1)) & 1
                place = 2 * place + (1 - mine[axis] if bit else mine[axis])
            chunk.keep[place] = value[block * size : (block + 1) * size, :].astype(BF16)
        chunk.begin()

    def back_into(there, half):
        part = pl.ds(pl.multiple_of(half * seg, seg), seg)
        total = dot_nt(dq[part, :], wqkv[:, 0:d])
        total = total + dot_nt(dk[part, :], wqkv[:, d : 2 * d])
        total = total + dot_nt(dv[part, :], wqkv[:, 2 * d : 3 * d])
        there[...] = total.astype(BF16)

    ng_crossing = remote(ng_send, ng_got, ng_sem.at[0], ng_sem.at[1], partners[0])

    @pl.when(i == 0)
    def _():
        for name in ("norm", "dq", "dk", "dv", "wqkv", "cot", "wout"):
            loads[name].start()
        meet(partners)
        loads["norm"].wait()
        turned[...] = left[...].T
        loads["att"].start()
        loads["dq"].wait()
        gradient(0, dq)

    for when, what in LATE_EVENTS.items():
        if when < last:

            @pl.when(i == when)
            def _():
                for chunk, stage in what:
                    chunks[chunk].happen(stage)

    @pl.when(i == 1)
    def _():
        loads["dk"].wait()
        gradient(1, dk)

    @pl.when(i == 2)
    def _():
        loads["dv"].wait()
        gradient(2, dv)

    @pl.when(i == 3)
    def _():
        loads["wqkv"].wait()
        back_into(ng_send, 1 - me)
        ng_crossing.start()

    @pl.when(i == 4)
    def _():
        loads["att"].wait()
        loads["cot"].wait()
        turned[...] = left[...].T
        gradient(3, right)

    @pl.when(i == 5)
    def _():
        back_into(ng_own, me)

    @pl.when((i >= out_start) & (i < out_end))
    def _():
        value = dot_nn(both[0], wdn[...])

        @pl.when(i == out_start)
        def _():
            acc[...] = value

        @pl.when(i > out_start)
        def _():
            acc[...] += value

    @pl.when((i >= in_start) & (i < in_end))
    def _():
        value = dot_nt(both[0], wup[...])

        @pl.when(i == in_start)
        def _():
            acc[...] = value

        @pl.when(i > in_start)
        def _():
            acc[...] += value

    @pl.when(i == out_end)
    def _():
        loads["wout"].wait()

    def home_block(index, own, far, own_offset):
        row = index // per_row
        within = pl.multiple_of(lax.rem(index, per_row) * step, step)
        there = pl.ds(pl.multiple_of(own_offset + within, step), step)
        return row, jnp.where(row == me, own[there, :], far[pl.ds(within, step), :])

    @pl.when(i >= out_end)
    def _():
        index = i - out_end
        row, att = home_block(index, left, far_att, me * seg)
        flag = jnp.where(row == 0, ids[1], ids[2])
        emb = table_row(fam, ids[0]) + table_row(ori, flag)
        part = pl.ds(pl.multiple_of(index * step, step), step)
        total = hid[...].astype(F32) + emb + dot_nn(att, wout[...])
        layer_out[...] = (total + (acc[part, :] + bdn[...].astype(F32))).astype(BF16)

    @pl.when(i == in_end)
    def _():
        ng_crossing.wait()
        gg[...] = jnp.zeros_like(gg)
        bg[...] = jnp.zeros_like(bg)
        rg[...] = jnp.zeros_like(rg)

    @pl.when((i >= in_end) & (i < out_start))
    def _():
        index = i - in_end
        row, back = home_block(index, ng_own, ng_got, 0)
        flag = jnp.where(row == 0, ids[1], ids[2])
        emb = table_row(fam, ids[0]) + table_row(ori, flag)
        part = pl.ds(pl.multiple_of(index * step, step), step)
        hat, inv_std = normalise(hid[...].astype(F32) + emb)
        grad = acc[part, :] + back.astype(F32)
        gg[...] += jnp.sum(grad * hat, 0, keepdims=True)
        bg[...] += jnp.sum(grad, 0, keepdims=True)
        scaled = grad * gain[...].astype(F32)
        inner = (
            scaled
            - jnp.mean(scaled, -1, keepdims=True)
            - hat * jnp.mean(scaled * hat, -1, keepdims=True)
        )
        result = cot[...].astype(F32) + inv_std * inner
        input_out[...] = result
        sums = jnp.sum(result, 0, keepdims=True)
        which = lax.broadcasted_iota(jnp.int32, rg.shape, 0)
        rg[...] += jnp.where(which == flag, sums, 0.0)

    def sums_main(index):
        return remote(held.at[index], got.at[index], ssem.at[index], rsem.at[index], partners[index])

    def sums_side(index):
        if index == 0:
            return remote(vec, vgot, gsend.at[0], grecv.at[0], partners[0])
        size = 1 << (index - 1)
        now = pl.ds(dp - lax.rem(dp, size), size)
        return remote(table.at[now], table.at[now], gsend.at[index], grecv.at[index], partners[index])

    @pl.when(i == out_start)
    def _():
        at = 0
        for source in (bup_part[...], bdn_part[...], gg[...], bg[...], rg[0:1, :], rg[1:2, :]):
            for lane in range(0, source.shape[1], 128):
                held[0, at : at + 1, :] = source[:, lane : lane + 128]
                at += 1
        both_rows = rg[0:1, :] + rg[1:2, :]
        for lane in range(0, d, 128):
            vec[lane // 128 : lane // 128 + 1, :] = both_rows[:, lane : lane + 128]
        extra = d // 128
        vec[extra:, :] = jnp.full((vec.shape[0] - extra, 128), 0.5, F32) * ids[0].astype(F32)
        sums_main(0).start()
        sums_side(0).start()

    for index in range(len(partners)):

        @pl.when(i == out_start + 2 * (index + 1))
        def _():
            sums_main(index).wait()
            sums_side(index).wait()
            total = held[index] + got[index]
            if index == 0:
                table[dp] = vec[...] + vgot[...]
            if index + 1 < len(partners):
                held[index + 1] = total
                sums_main(index + 1).start()
                sums_side(index + 1).start()
            else:
                sums_out[...] = total
                all_out[...] = table[...]

    @pl.when(i == last - 1)
    def _():
        for chunk, stage in LATE_EVENTS[last]:
            chunks[chunk].happen(stage)


def tail(ids, norm, att, row_cot, dq, dk, dv, wqkv, wout, fam, ori, gain, bdn, bup_part, bdn_part, far_att, both, wdn, wup, hid, cot, orders, rows, collective):
    tokens, d = hid.shape
    ff = wup.shape[1]
    bits = len(orders[0]) - 1
    count = 1 << bits
    seg = far_att.shape[0]
    tile, step = TAIL_TILE, TAIL_STEP
    tiles, blocks = ff // tile, tokens // step
    in_start = 6
    in_end = in_start + tiles
    out_start = in_end + blocks
    out_end = out_start + tiles
    last = out_end + blocks
    marks = (in_start, in_end, out_start, out_end, last)
    size = d // (2 * count)
    rounds = bits + 1
    lines = (ff + 5 * d) // 128
    vec_shape = (d // 128 + 8, 128)
    anywhere = pl.BlockSpec(memory_space=pl.ANY)

    def plane(i):
        late = i >= out_start
        return (jnp.where(late, 0, 1), 0, jnp.clip(jnp.where(late, i - out_start, i - in_start), 0, tiles - 1))

    def home(i):
        return (jnp.clip(jnp.where(i >= out_start, i - out_end, i - in_end), 0, blocks - 1), 0)

    square = pltpu.VMEM((tokens, d), BF16)
    piece = pltpu.VMEM((seg, d), BF16)
    row = pltpu.VMEM((1, d), F32)
    return pl.pallas_call(
        functools.partial(tail_kernel, bits, orders, rows, marks),
        grid=(last,),
        in_specs=[pl.BlockSpec(memory_space=pltpu.SMEM)]
        + [anywhere] * 8
        + [
            whole(fam.shape),
            whole(ori.shape),
            whole((1, d)),
            whole((1, d)),
            whole((1, ff)),
            whole((1, d)),
            whole((seg, d)),
            pl.BlockSpec((1, tokens, tile), plane),
            pl.BlockSpec((tile, d), lambda i: (jnp.clip(i - out_start, 0, tiles - 1), 0)),
            pl.BlockSpec((d, tile), lambda i: (0, jnp.clip(i - in_start, 0, tiles - 1))),
            pl.BlockSpec((step, d), home),
            pl.BlockSpec((step, d), lambda i: (jnp.clip(i - in_end, 0, blocks - 1), 0)),
        ],
        out_specs=[
            pl.BlockSpec((step, d), lambda i: (jnp.clip(i - out_end, 0, blocks - 1), 0)),
            pl.BlockSpec((step, d), lambda i: (jnp.clip(i - in_end, 0, blocks - 1), 0)),
            whole((size, 3 * d)),
            whole((size, d)),
            whole((lines, 128)),
            whole((count,) + vec_shape),
        ],
        out_shape=[
            jax.ShapeDtypeStruct((tokens, d), BF16),
            jax.ShapeDtypeStruct((tokens, d), F32),
            jax.ShapeDtypeStruct((size, 3 * d), F32),
            jax.ShapeDtypeStruct((size, d), F32),
            jax.ShapeDtypeStruct((lines, 128), F32),
            jax.ShapeDtypeStruct((count,) + vec_shape, F32),
        ],
        scratch_shapes=[
            square,
            square,
            square,
            square,
            square,
            pltpu.VMEM((d, 3 * d), BF16),
            pltpu.VMEM((d, d), BF16),
            pltpu.VMEM((d, tokens), BF16),
            pltpu.VMEM((tokens, d), F32),
            piece,
            piece,
            piece,
            row,
            row,
            pltpu.VMEM((2, d), F32),
            pltpu.SemaphoreType.DMA((8,)),
            pltpu.SemaphoreType.DMA((2,)),
            pltpu.VMEM((rounds, lines, 128), F32),
            pltpu.VMEM((rounds, lines, 128), F32),
            pltpu.VMEM(vec_shape, F32),
            pltpu.VMEM(vec_shape, F32),
            pltpu.VMEM((count,) + vec_shape, F32),
            pltpu.SemaphoreType.DMA((rounds,)),
            pltpu.SemaphoreType.DMA((rounds,)),
            pltpu.SemaphoreType.DMA((rounds,)),
            pltpu.SemaphoreType.DMA((rounds,)),
        ]
        + [entry for axes in orders for entry in chunk_scratch(axes, size, d, True)],
        compiler_params=pltpu.CompilerParams(
            vmem_limit_bytes=67043328, collective_id=collective, has_side_effects=True
        ),
        cost_estimate=cost(16 * tokens * d * d + 4 * tokens * d * ff, 8 * d * ff + 40 * tokens * d),
        name="tail",
    )(ids, norm, att, row_cot, dq, dk, dv, wqkv, wout, fam, ori, gain, bdn, bup_part, bdn_part, far_att, both, wdn, wup, hid, cot)


def finish_kernel(ff, layer, inputs, qkv, out, up, down, sums, table, *outs):
    layer_out, input_out, qkv_out, out_out, up_out, down_out, bup, bdn, gain, bias, fam_out, ori_out = outs
    layer_out[...] = layer[...]
    input_out[...] = inputs[...]
    qkv_out[...] = qkv[...]
    out_out[...] = out[...]
    up_out[...] = up[...]
    down_out[...] = down[...]

    @pl.when(pl.program_id(0) == 0)
    def _():
        d = gain.shape[1]
        at = 0
        for there in (bup, bdn, gain, bias, ori_out.at[0:1], ori_out.at[1:2]):
            for lane in range(0, there.shape[1], 128):
                there[:, lane : lane + 128] = sums[at : at + 1, :]
                at += 1
        extra = d // 128
        rows = lax.broadcasted_iota(jnp.int32, (fam_out.shape[0], 128), 0).astype(F32)
        for lane in range(extra):
            total = jnp.zeros((fam_out.shape[0], 128), F32)
            for index in range(table.shape[0]):
                total = total + jnp.where(
                    rows == table[index, extra : extra + 1, :], table[index, lane : lane + 1, :], 0.0
                )
            fam_out[:, lane * 128 : (lane + 1) * 128] = total


def finish(layer, inputs, qkv, out, up, down, sums, table, families):
    tokens, d = layer.shape
    ff = up.shape[1]
    steps = 4

    def rows(entry):
        return pl.BlockSpec((entry.shape[0] // steps, entry.shape[1]), lambda i: (i, 0))

    big = [layer, inputs, qkv, out, up, down]
    small = [(1, ff), (1, d), (1, d), (1, d), (families, d), (2, d)]
    return pl.pallas_call(
        functools.partial(finish_kernel, ff),
        grid=(steps,),
        in_specs=[rows(entry) for entry in big] + [whole(sums.shape), whole(table.shape)],
        out_specs=[rows(entry) for entry in big] + [whole(shape) for shape in small],
        out_shape=[jax.ShapeDtypeStruct(entry.shape, entry.dtype) for entry in big]
        + [jax.ShapeDtypeStruct(shape, F32) for shape in small],
        compiler_params=params(),
        name="finish",
    )(*big, sums, table)


def body_by_rows(
    hidden_in,
    family,
    orient,
    norm_gain,
    norm_bias,
    qkv_weight,
    out_weight,
    up_weight,
    up_bias,
    down_weight,
    down_bias,
    family_table,
    orient_table,
    cotangent,
):
    rows, seg, d = hidden_in.shape
    ff = up_weight.shape[1]
    tokens = rows * seg
    full = 2 * seg
    dp_count = lax.axis_size("dp")
    bits = int(math.log2(dp_count))
    upper = dp_count // 2
    dp = lax.axis_index("dp")
    seq = lax.axis_index("seq")
    ring = [(0, 1), (1, 0)]

    def mine(pair):
        return lax.dynamic_index_in_dim(pair, seq, 0, keepdims=False)

    def theirs(pair):
        return lax.dynamic_index_in_dim(pair, 1 - seq, 0, keepdims=False)

    far_hidden = lax.ppermute(theirs(hidden_in), "seq", ring)

    gain = norm_gain.reshape(1, d)
    bias = norm_bias.reshape(1, d)
    hid = hidden_in.reshape(tokens, d)
    cot = cotangent.reshape(tokens, d)
    ids = jnp.concatenate([family, orient])
    row_ids = jnp.stack([family[0], mine(orient)])

    turned, both, up_bias_part, down_bias_part = ffn_forward(
        ids, hid, cot, family_table, orient_table, gain, bias, up_weight, up_bias.reshape(1, ff), down_weight, rows
    )
    cosine, sine = rope_tables(jnp.arange(full).astype(F32), 128)
    row_normed, row_cot, att, dq, dk, dv, far_att, up_total, down_total, *_ = middle(
        row_ids,
        mine(hidden_in),
        far_hidden,
        cot,
        turned,
        both,
        family_table,
        orient_table,
        gain,
        bias,
        qkv_weight,
        out_weight,
        cosine,
        sine,
        FFN_ORDERS,
        d // H,
        3,
    )
    layer_out, input_grad, qkv_total, out_total, sums, gathered = tail(
        ids,
        row_normed,
        att,
        row_cot,
        dq,
        dk,
        dv,
        qkv_weight,
        out_weight,
        family_table,
        orient_table,
        gain,
        down_bias.reshape(1, d),
        up_bias_part,
        down_bias_part,
        far_att,
        both,
        down_weight,
        up_weight,
        hid,
        cot,
        LATE_ORDERS,
        rows,
        4,
    )
    layer_out, input_grad, qkv_sum, out_sum, up_sum, down_sum, *small = finish(
        layer_out, input_grad, qkv_total, out_total, up_total, down_total, sums, gathered, family_table.shape[0]
    )
    up_bias_sum, down_bias_sum, gain_sum, bias_sum = (part.reshape(-1) for part in small[:4])
    return (
        layer_out.reshape(rows, seg, d),
        input_grad.reshape(rows, seg, d),
        gain_sum,
        bias_sum,
        qkv_sum,
        out_sum,
        up_sum,
        up_bias_sum,
        down_sum,
        down_bias_sum,
        small[4],
        small[5],
    )


def body(*args):
    hidden_in = args[0]
    dp_count = lax.axis_size("dp")
    two_rows = lax.axis_size("seq") == 2 and hidden_in.shape[0] == 2
    if two_rows and dp_count == 16:
        return body_by_rows(*args)
    return body_by_heads(*args)


def solution(mesh):
    return jax.shard_map(
        body,
        mesh=mesh,
        in_specs=(
            P("dp", "seq", None),
            P("dp"),
            P("dp"),
            P(),
            P(),
            P(),
            P(),
            P(),
            P(),
            P(),
            P(),
            P(),
            P(),
            P("dp", "seq", None),
        ),
        out_specs=(
            P("dp", "seq", None),
            P("dp", "seq", None),
            P(),
            P(),
            P(("dp", "seq"), None),
            P(("dp", "seq"), None),
            P(("dp", "seq"), None),
            P(),
            P(("dp", "seq"), None),
            P(),
            P(),
            P(),
        ),
        check_vma=False,
    )
```

```python
import functools
import math

import jax
import jax.numpy as jnp
from jax import lax
from jax.experimental import pallas as pl
from jax.experimental.pallas import tpu as pltpu
from jax.sharding import PartitionSpec as P

H = 16
HD = 64
ROT = 32
MESH = pl.DeviceIdType.MESH
VMEM_LIMIT = 60 * 1024 * 1024
F32 = jnp.float32
BF16 = jnp.bfloat16


def for_sending(shard):

    def short(part):
        return part.astype(jnp.bfloat16) if part.dtype == jnp.float32 else part

    return jax.tree.map(short, shard)


def rope_tables(positions, features):
    column = jnp.arange(features, dtype=jnp.int32)
    within = column % HD
    frequency = jnp.exp(-(2.0 * (within // 2).astype(jnp.float32) / ROT) * math.log(10000.0))
    angles = positions[:, None] * frequency[None, :]
    rotary = within < ROT
    cosine = jnp.where(rotary[None, :], jnp.cos(angles), 1.0)
    sign_term = jnp.where(within % 2 == 0, -1.0, 1.0)
    sine_term = jnp.where(rotary[None, :], sign_term[None, :] * jnp.sin(angles), 0.0)
    return (cosine, sine_term)


def pair_swap(values):
    even_cols = jnp.arange(values.shape[-1]) % 2 == 0
    return jnp.where(even_cols, jnp.roll(values, -1, axis=-1), jnp.roll(values, 1, axis=-1))


def rotate(values, cosine, sine_term):
    return values * cosine + pair_swap(values) * sine_term


def rotate_back(values, cosine, sine_term):
    return values * cosine + pair_swap(values * sine_term)


def gelu_tanh(pre_values):
    return jax.nn.gelu(pre_values, approximate=True)


def body_by_heads(
    hidden_in,
    family,
    orient,
    norm_gain,
    norm_bias,
    qkv_weight,
    out_weight,
    up_weight,
    up_bias,
    down_weight,
    down_bias,
    family_table,
    orient_table,
    cotangent,
):
    seq_count = lax.axis_size("seq")
    row_count, seg_length, features = hidden_in.shape
    full_length = seg_length * seq_count
    local_heads = H // seq_count
    head_size = features // H
    slab_width = features // seq_count
    block_rows = min(512, full_length)
    block_count = full_length // block_rows
    score_scale = head_size ** (-0.5)
    token_count = row_count * seg_length
    family_rows = jnp.repeat(family, 2)
    family_hot = (family_rows[:, None] == jnp.arange(family_table.shape[0])[None, :]).astype(
        jnp.bfloat16
    )
    orient_hot = (orient[:, None] == jnp.arange(2)[None, :]).astype(jnp.bfloat16)
    embedding = jnp.dot(family_hot, family_table, preferred_element_type=jnp.float32) + jnp.dot(
        orient_hot, orient_table, preferred_element_type=jnp.float32
    )
    embedded = (hidden_in.astype(jnp.float32) + embedding[:, None, :]).reshape(
        token_count, features
    )
    row_mean = jnp.mean(embedded, -1, keepdims=True)
    centred = embedded - row_mean
    row_var = jnp.mean(centred * centred, -1, keepdims=True)
    inv_std = lax.rsqrt(row_var + 1e-05)
    normed_hat = centred * inv_std
    gain_f32 = norm_gain.astype(jnp.float32)
    normed_low = (normed_hat * gain_f32 + norm_bias.astype(jnp.float32)).astype(jnp.bfloat16)
    projected = jnp.dot(normed_low, qkv_weight, preferred_element_type=jnp.float32).reshape(
        row_count, seg_length, 3 * features
    )
    positions = (lax.axis_index("seq") * seg_length + jnp.arange(seg_length)).astype(jnp.float32)
    cosine, sine_term = rope_tables(positions, features)
    queries = rotate(projected[..., :features], cosine, sine_term).astype(jnp.bfloat16)
    keys_rot = rotate(projected[..., features : 2 * features], cosine, sine_term).astype(
        jnp.bfloat16
    )
    values = projected[..., 2 * features :].astype(jnp.bfloat16)
    query_heads, key_heads, value_heads = (
        lax.all_to_all(queries, "seq", split_axis=2, concat_axis=1, tiled=True),
        lax.all_to_all(keys_rot, "seq", split_axis=2, concat_axis=1, tiled=True),
        lax.all_to_all(values, "seq", split_axis=2, concat_axis=1, tiled=True),
    )

    def scores_for(query_block, key_rows, block_start):
        logits = (
            jnp.einsum("qhd,khd->hqk", query_block, key_rows, preferred_element_type=jnp.float32)
            * score_scale
        )
        causal = (block_start + jnp.arange(block_rows))[:, None] >= jnp.arange(full_length)[None, :]
        return jnp.where(causal[None], logits, -1e30)

    def attend(row_args):
        query_row, key_row, value_row = row_args
        key_rows = key_row.reshape(full_length, local_heads, head_size)
        value_rows = value_row.reshape(full_length, local_heads, head_size)
        pieces = []
        log_parts = []
        for block_index in range(block_count):
            block_start = block_index * block_rows
            query_block = query_row[block_start : block_start + block_rows].reshape(
                block_rows, local_heads, head_size
            )
            logits = scores_for(query_block, key_rows, block_start)
            row_peak = jnp.max(logits, -1, keepdims=True)
            weights = jnp.exp(logits - row_peak)
            row_total = jnp.sum(weights, -1, keepdims=True)
            prob_low = (weights / row_total).astype(jnp.bfloat16)
            output_block = jnp.einsum(
                "hqk,khd->qhd", prob_low, value_rows, preferred_element_type=jnp.float32
            )
            pieces.append(output_block.reshape(block_rows, slab_width).astype(jnp.bfloat16))
            log_parts.append((row_peak + jnp.log(row_total))[..., 0])
        return (jnp.concatenate(pieces, 0), jnp.concatenate(log_parts, 1))

    attended_heads, log_sums = lax.map(attend, (query_heads, key_heads, value_heads))
    attended = jax.tree.map(
        lambda part, own: part.astype(own.dtype),
        lax.all_to_all(for_sending(attended_heads), "seq", split_axis=1, concat_axis=2, tiled=True),
        attended_heads,
    )
    attended_flat = attended.reshape(token_count, features)
    branch_attn = jnp.dot(attended_flat, out_weight, preferred_element_type=jnp.float32)
    up_pre = jnp.dot(normed_low, up_weight, preferred_element_type=jnp.float32) + up_bias.astype(
        jnp.float32
    )
    up_act = gelu_tanh(up_pre).astype(jnp.bfloat16)
    branch_feed = jnp.dot(
        up_act, down_weight, preferred_element_type=jnp.float32
    ) + down_bias.astype(jnp.float32)
    layer_out = (
        (embedded + branch_attn + branch_feed)
        .astype(jnp.bfloat16)
        .reshape(row_count, seg_length, features)
    )
    grad_low = cotangent.reshape(token_count, features)
    grad_f32 = grad_low.astype(jnp.float32)
    down_grad = jnp.einsum("nf,nd->fd", up_act, grad_low, preferred_element_type=jnp.float32)
    down_bias_grad = jnp.sum(grad_f32, 0)
    act_grad = jnp.einsum("nd,fd->nf", grad_low, down_weight, preferred_element_type=jnp.float32)
    gelu_out, gelu_pull = jax.vjp(gelu_tanh, up_pre)
    pre_grad = gelu_pull(act_grad)[0].astype(jnp.bfloat16)
    up_bias_grad = jnp.sum(pre_grad.astype(jnp.float32), 0)
    up_grad = jnp.einsum("nd,nf->df", normed_low, pre_grad, preferred_element_type=jnp.float32)
    normed_grad = jnp.einsum("nf,df->nd", pre_grad, up_weight, preferred_element_type=jnp.float32)
    out_grad = jnp.einsum("nd,ne->de", attended_flat, grad_low, preferred_element_type=jnp.float32)
    attended_grad = jnp.einsum(
        "ne,de->nd", grad_low, out_weight, preferred_element_type=jnp.float32
    )
    attended_grad = attended_grad.astype(jnp.bfloat16).reshape(row_count, seg_length, features)
    grad_heads = lax.all_to_all(attended_grad, "seq", split_axis=2, concat_axis=1, tiled=True)

    def attend_back(row_args):
        query_row, key_row, value_row, grad_row, log_row = row_args
        key_rows = key_row.reshape(full_length, local_heads, head_size)
        value_rows = value_row.reshape(full_length, local_heads, head_size)
        keys_total = jnp.zeros((full_length, local_heads, head_size), jnp.float32)
        values_total = jnp.zeros((full_length, local_heads, head_size), jnp.float32)
        query_parts = []
        for block_index in range(block_count):
            block_start = block_index * block_rows
            query_block = query_row[block_start : block_start + block_rows].reshape(
                block_rows, local_heads, head_size
            )
            grad_block = grad_row[block_start : block_start + block_rows].reshape(
                block_rows, local_heads, head_size
            )
            logits = scores_for(query_block, key_rows, block_start)
            probs_full = jnp.exp(logits - log_row[:, block_start : block_start + block_rows, None])
            prob_low = probs_full.astype(jnp.bfloat16)
            probs_grad = jnp.einsum(
                "qhd,khd->hqk", grad_block, value_rows, preferred_element_type=jnp.float32
            )
            inner_sum = jnp.sum(probs_full * probs_grad, -1, keepdims=True)
            scores_grad = (probs_full * (probs_grad - inner_sum)).astype(jnp.bfloat16)
            values_total = values_total + jnp.einsum(
                "hqk,qhd->khd", prob_low, grad_block, preferred_element_type=jnp.float32
            )
            query_grad = (
                jnp.einsum(
                    "hqk,khd->qhd", scores_grad, key_rows, preferred_element_type=jnp.float32
                )
                * score_scale
            )
            query_parts.append(query_grad.reshape(block_rows, slab_width).astype(jnp.bfloat16))
            keys_total = (
                keys_total
                + jnp.einsum(
                    "hqk,qhd->khd", scores_grad, query_block, preferred_element_type=jnp.float32
                )
                * score_scale
            )
        return (
            jnp.concatenate(query_parts, 0),
            keys_total.reshape(full_length, slab_width).astype(jnp.bfloat16),
            values_total.reshape(full_length, slab_width).astype(jnp.bfloat16),
        )

    query_grad_heads, key_grad_heads, value_grad_heads = lax.map(
        attend_back, (query_heads, key_heads, value_heads, grad_heads, log_sums)
    )
    query_grad_pos, key_grad_pos, value_grad_pos = (
        lax.all_to_all(
            for_sending(query_grad_heads), "seq", split_axis=1, concat_axis=2, tiled=True
        ).astype(query_grad_heads.dtype),
        lax.all_to_all(
            for_sending(key_grad_heads), "seq", split_axis=1, concat_axis=2, tiled=True
        ).astype(key_grad_heads.dtype),
        lax.all_to_all(
            for_sending(value_grad_heads), "seq", split_axis=1, concat_axis=2, tiled=True
        ).astype(value_grad_heads.dtype),
    )
    projected_grad = jnp.concatenate(
        [
            rotate_back(query_grad_pos.astype(jnp.float32), cosine, sine_term),
            rotate_back(key_grad_pos.astype(jnp.float32), cosine, sine_term),
            value_grad_pos.astype(jnp.float32),
        ],
        -1,
    )
    projected_grad = projected_grad.astype(jnp.bfloat16).reshape(token_count, 3 * features)
    qkv_grad = jnp.einsum(
        "nd,ne->de", normed_low, projected_grad, preferred_element_type=jnp.float32
    )
    normed_grad = normed_grad + jnp.einsum(
        "ne,de->nd", projected_grad, qkv_weight, preferred_element_type=jnp.float32
    )
    gain_grad = jnp.sum(normed_grad * normed_hat, 0)
    bias_grad = jnp.sum(normed_grad, 0)
    scaled_grad = normed_grad * gain_f32
    hat_grad = (
        scaled_grad
        - jnp.mean(scaled_grad, -1, keepdims=True)
        - normed_hat * jnp.mean(scaled_grad * normed_hat, -1, keepdims=True)
    )
    input_grad = (grad_f32 + inv_std * hat_grad).reshape(row_count, seg_length, features)
    row_sums = jnp.sum(input_grad, 1)
    family_grad = jnp.einsum(
        "rf,rd->fd", family_hot.astype(jnp.float32), row_sums, precision=lax.Precision.HIGHEST
    )
    orient_grad = jnp.einsum(
        "rf,rd->fd", orient_hot.astype(jnp.float32), row_sums, precision=lax.Precision.HIGHEST
    )
    gain_sum, bias_sum, up_bias_sum, down_bias_sum, family_sum, orient_sum = lax.psum(
        (gain_grad, bias_grad, up_bias_grad, down_bias_grad, family_grad, orient_grad),
        ("dp", "seq"),
    )
    qkv_sum, out_sum, up_sum, down_sum = (
        lax.psum_scatter(qkv_grad, ("dp", "seq"), scatter_dimension=0, tiled=True),
        lax.psum_scatter(out_grad, ("dp", "seq"), scatter_dimension=0, tiled=True),
        lax.psum_scatter(up_grad, ("dp", "seq"), scatter_dimension=0, tiled=True),
        lax.psum_scatter(down_grad, ("dp", "seq"), scatter_dimension=0, tiled=True),
    )
    return (
        layer_out,
        input_grad,
        gain_sum,
        bias_sum,
        qkv_sum,
        out_sum,
        up_sum,
        up_bias_sum,
        down_sum,
        down_bias_sum,
        family_sum,
        orient_sum,
    )


def dot_nn(a, b):
    return lax.dot_general(a, b, (((1,), (0,)), ((), ())), preferred_element_type=F32)


def dot_nt(a, b):
    return lax.dot_general(a, b, (((1,), (1,)), ((), ())), preferred_element_type=F32)


def dot_tn(a, b):
    return lax.dot_general(a, b, (((0,), (0,)), ((), ())), preferred_element_type=F32)


def params(**more):
    return pltpu.CompilerParams(vmem_limit_bytes=VMEM_LIMIT, **more)


def cost(flops, moved, exps=0):
    return pl.CostEstimate(flops=flops, bytes_accessed=moved, transcendentals=exps)


def whole(shape):
    return pl.BlockSpec(shape, lambda *_: (0,) * len(shape), pipeline_mode=pl.Buffered(1))


def table_row(table, wanted):
    rows = lax.broadcasted_iota(jnp.int32, table.shape, 0)
    return jnp.sum(jnp.where(rows == wanted, table[...].astype(F32), 0.0), 0, keepdims=True)


def line(vector):
    return vector[...].astype(F32).reshape(1, -1)


def normalise(entries):
    centred = entries - jnp.mean(entries, -1, keepdims=True)
    inv_std = lax.rsqrt(jnp.mean(centred * centred, -1, keepdims=True) + 1e-05)
    return centred * inv_std, inv_std


GELU_C = math.sqrt(2.0 / math.pi)


def gelu_both(z):
    square = z * z
    half = 0.5 + 0.5 * jnp.tanh(z * (GELU_C + (GELU_C * 0.044715) * square))
    value = z * half
    slope = half + value * (1.0 - half) * (2 * GELU_C + (6 * GELU_C * 0.044715) * square)
    return value, slope


def ffn_kernel(rows, fid, oid, hid, cot, fam, ori, gain, bias, wup, bup, wdn, turned, both, bupg, bdng, norm, shifts):
    tokens = hid.shape[0]
    seg = tokens // rows
    step = 256
    i = pl.program_id(0)
    @pl.when(i == 0)
    def _():
        total = jnp.zeros((1, cot.shape[1]), F32)
        for row in range(rows):
            emb = table_row(fam, fid[0]) + table_row(ori, oid[row])
            for start in range(row * seg, (row + 1) * seg, step):
                part = pl.ds(start, step)
                hat, _ = normalise(hid[part, :].astype(F32) + emb)
                norm[part, :] = (hat * line(gain) + line(bias)).astype(BF16)
                total = total + jnp.sum(cot[part, :].astype(F32), 0, keepdims=True)
        bdng[...] = total
        turned[...] = norm[...].T
        shifts[...] = line(bup)

    width = wup.shape[1]
    total = jnp.zeros((8, width), F32)
    lin = dot_nn(norm[...], wup[...])
    into = dot_nt(cot[...], wdn[...])
    shift = shifts[:, pl.ds(pl.multiple_of(i * width, width), width)]
    step = 64
    for start in range(0, tokens, step):
        part = pl.ds(start, step)
        value, slope = gelu_both(lin[start : start + step] + shift)
        low = into[start : start + step] * slope
        both[0, part, :] = value.astype(BF16)
        both[1, part, :] = low.astype(BF16)
        total = total + jnp.sum(low.reshape(step // 8, 8, width), 0)
    bupg[...] = jnp.sum(total, 0, keepdims=True)


def ffn_forward(fid, oid, hid, cot, fam, ori, gain, bias, wup, bup, wdn, rows):
    tokens, d = hid.shape
    ff = wup.shape[1]
    tile = 512
    smem = pl.BlockSpec(memory_space=pltpu.SMEM)
    return pl.pallas_call(
        functools.partial(ffn_kernel, rows),
        grid=(ff // tile,),
        in_specs=[
            smem,
            smem,
            whole((tokens, d)),
            whole((tokens, d)),
            whole(fam.shape),
            whole(ori.shape),
            whole(gain.shape),
            whole(bias.shape),
            pl.BlockSpec((d, tile), lambda i: (0, i)),
            whole(bup.shape),
            pl.BlockSpec((tile, d), lambda i: (i, 0)),
        ],
        out_specs=[
            whole((d, tokens)),
            pl.BlockSpec((2, tokens, tile), lambda i: (0, 0, i)),
            pl.BlockSpec((1, tile), lambda i: (0, i)),
            whole((1, d)),
        ],
        out_shape=[
            jax.ShapeDtypeStruct((d, tokens), BF16),
            jax.ShapeDtypeStruct((2, tokens, ff), BF16),
            jax.ShapeDtypeStruct((1, ff), F32),
            jax.ShapeDtypeStruct((1, d), F32),
        ],
        scratch_shapes=[
            pltpu.VMEM((tokens, d), BF16),
            pltpu.VMEM((1, ff), F32),
        ],
        compiler_params=params(),
        cost_estimate=cost(4 * tokens * d * ff, 4 * tokens * ff + 4 * d * ff, tokens * ff),
        name="ffn_forward",
    )(fid, oid, hid, cot, fam, ori, gain, bias, wup, bup, wdn)


def turn(entries, cosine, sine):
    even = lax.broadcasted_iota(jnp.int32, entries.shape, 1) % 2 == 0
    other = jnp.where(even, pltpu.roll(entries, 127, 1), pltpu.roll(entries, 1, 1))
    return entries * cosine + other * sine


def turn_back(entries, cosine, sine):
    even = lax.broadcasted_iota(jnp.int32, entries.shape, 1) % 2 == 0
    side = entries * sine
    other = jnp.where(even, pltpu.roll(side, 127, 1), pltpu.roll(side, 1, 1))
    return entries * cosine + other


def attend(head_size, query_ref, k_ref, v_ref, g_ref, cos, sin, o_ref, dq_ref, dk_ref, dv_ref, dkt, dvt):
    full = query_ref.shape[0]
    block = 256
    scale = head_size ** (-0.5)
    first = lax.broadcasted_iota(jnp.int32, (block, 128), 1) < head_size
    below = lax.broadcasted_iota(jnp.int32, (block, block), 0) >= lax.broadcasted_iota(
        jnp.int32, (block, block), 1
    )
    dkt[...] = jnp.zeros_like(dkt)
    dvt[...] = jnp.zeros_like(dvt)

    def by_head(entries):
        none = jnp.zeros_like(entries)
        return jnp.concatenate([jnp.where(first, entries, none), jnp.where(first, none, entries)], 0)

    def front(start):
        part, end = pl.ds(start, block), start + block
        query = by_head((query_ref[part, :].astype(F32) * scale).astype(BF16))
        grad = by_head(g_ref[part, :])
        return query, grad, dot_nt(query, k_ref[0:end, :]), dot_nt(grad, v_ref[0:end, :])

    def back(start, query, grad, scores, into):
        part, end = pl.ds(start, block), start + block
        lows, slopes = [], []
        for head in range(2):
            rows = slice(head * block, (head + 1) * block)
            score = scores[rows]
            last = jnp.where(below, score[:, start:end], -1e30)
            score = last if start == 0 else jnp.concatenate([score[:, :start], last], 1)
            weights = jnp.exp(score - jnp.max(score, -1, keepdims=True))
            probs = weights * (1.0 / jnp.sum(weights, -1, keepdims=True))
            lows.append(probs.astype(BF16))
            inner = jnp.sum(probs * into[rows], -1, keepdims=True)
            slopes.append((probs * (into[rows] - inner)).astype(BF16))
        low = jnp.concatenate(lows, 0)
        slope = jnp.concatenate(slopes, 0)
        out = dot_nn(low, v_ref[0:end, :])
        dq = dot_nn(slope, k_ref[0:end, :])
        o_ref[part, :] = jnp.where(first, out[:block], out[block:]).astype(BF16)
        dq = jnp.where(first, dq[:block], dq[block:]) * scale
        dq_ref[part, :] = turn_back(dq, cos[part, :], sin[part, :]).astype(BF16)
        dkt[:, 0:end] += dot_tn(query, slope)
        dvt[:, 0:end] += dot_tn(grad, low)

    ready = front(0)
    for start in range(0, full, block):
        later = front(start + block) if start + block < full else None
        back(start, *ready)
        ready = later
    for start in range(0, full, block):
        part = pl.ds(start, block)
        dk = dkt[:, start : start + block].T
        dk_ref[part, :] = turn_back(dk, cos[part, :], sin[part, :]).astype(BF16)
        dv_ref[part, :] = dvt[:, start : start + block].T.astype(BF16)


FFN_ORDERS = [
    [2, 1, "seq", 3],
    [1, 2, "seq", 3],
    [1, "seq", 3, 2],
    [2, 1, "seq", 3],
    [2, 1, "seq", 3],
    [2, 1, "seq", 3],
    [1, 2, "seq", 3],
    ["seq", 1, 3, 2],
]
LATE_ORDERS = [
    [0, 2, 1, "seq", 3],
    [0, 1, 3, 2, "seq"],
    [0, 2, 1, "seq", 3],
    [0, 1, "seq", 3, 2],
]
FFN_EVENTS = {
    4: [(0, 0)],
    6: [(1, 0)],
    8: [(2, 0)],
    9: [(3, 0)],
    14: [(0, 1)],
    15: [(1, 1)],
    17: [(7, 0), (4, 0), (5, 0), (6, 0)],
    18: [(3, 1)],
    20: [(2, 1)],
    21: [(1, 2)],
    23: [(0, 2)],
    25: [(4, 1)],
    26: [(6, 1), (7, 1)],
    27: [(3, 2), (2, 2), (5, 1), (1, 3)],
    28: [(4, 2), (0, 3), (6, 2), (7, 2)],
    29: [(3, 3), (2, 3), (5, 2)],
    30: [(1, 4), (4, 3), (0, 4), (6, 3)],
    31: [(7, 3), (5, 3), (3, 4)],
    32: [(2, 4), (4, 4), (6, 4), (7, 4), (5, 4)],
}
LATE_EVENTS = {
    2: [(0, 1)],
    3: [(1, 1)],
    4: [(2, 1)],
    6: [(3, 1)],
    7: [(0, 2)],
    8: [(1, 2)],
    13: [(2, 2)],
    14: [(3, 2)],
    17: [(0, 3)],
    18: [(1, 3)],
    20: [(3, 3), (2, 3)],
    21: [(0, 4)],
    23: [(1, 4)],
    25: [(2, 4)],
    26: [(3, 4)],
    27: [(1, 5)],
    28: [(0, 5)],
    30: [(2, 5), (3, 5)],
}


def middle_kernel(tiles, pairs, head_size, bits, orders, *refs):
    fid, oid, home_cot, turned, pre, act, fam, ori, gain, bias, wqkv, wout, angles, hid_hbm, cot_hbm = refs[:15]
    norm, cot, o_ref, dq_ref, dk_ref, dv_ref, far_att, up_out, down_out = refs[15:24]
    near_up, far_up, near_down, far_down = refs[24:28]
    heads, dkt, dvt, att_send, att_got, att_sems, cfar, cfar_sems = refs[28:36]
    keep, send, got, send_sem, recv_sem, out_sem = refs[36:42]
    up_keep, up_send, up_got, up_ssem, up_rsem, up_osem = refs[42:48]
    own, cos, sin, own_sem, far, far_sems = refs[48:54]
    seg = far.shape[0]
    step = 256
    base = 1 << (bits - 1)
    now = pl.program_id(0)
    ups = up_out.shape[1] // up_keep.shape[3]
    late = now - ups
    i = late - base
    me = lax.axis_index("seq")
    mine = device_bits(bits)
    parts = len(orders) // 2
    up_part = up_out.shape[1] // parts
    down_part = down_out.shape[1] // parts
    chunks = chunks_from(
        refs[54:],
        bits,
        mine,
        [
            (orders[part], near_up, far_up, pl.ds(part * up_part, up_part), up_out)
            for part in range(parts)
        ]
        + [
            (orders[parts + part], near_down, far_down, pl.ds(part * down_part, down_part), down_out)
            for part in range(parts)
        ],
    )

    def happen(events):
        for chunk, stage in events:
            chunks[chunk].happen(stage)

    @pl.when(now == 0)
    def _():
        meet([partner_along(axis, mine) for axis in [0] + orders[0]])

    cot_crossing = remote(
        cot_hbm.at[pl.ds(pl.multiple_of((1 - me) * seg, seg), seg)],
        cfar,
        cfar_sems.at[0],
        cfar_sems.at[1],
        partner_along("seq", mine),
    )

    far_crossing = remote(
        hid_hbm.at[pl.ds(pl.multiple_of((1 - me) * seg, seg), seg)],
        far,
        far_sems.at[0],
        far_sems.at[1],
        partner_along("seq", mine),
    )
    own_load = pltpu.make_async_copy(hid_hbm.at[pl.ds(pl.multiple_of(me * seg, seg), seg)], own, own_sem)

    @pl.when(now == 0)
    def _():
        far_crossing.start()
        cot_crossing.start()
        own_load.start()

    last = ups + base + 4 * tiles + pairs
    def up_crossing(index):
        slot = lax.rem(index, 2)
        return remote(
            up_send.at[slot], up_got.at[slot], up_ssem.at[slot], up_rsem.at[slot], partner_along(0, mine)
        )

    def up_stores(index):
        slot = lax.rem(index, 2)
        width = up_keep.shape[3]
        columns = pl.ds(pl.multiple_of(index * width, width), width)
        return [
            pltpu.make_async_copy(
                up_keep.at[slot, pl.ds(half * base, base)], there.at[:, :, columns], up_osem.at[half, slot]
            )
            for half, there in enumerate((near_up, far_up))
        ]

    def up_finish(index):
        slot = lax.rem(index, 2)
        up_crossing(index).wait()
        add_into(up_keep.at[slot], up_got.at[slot])
        for copy in up_stores(index):
            copy.start()

    for when, what in FFN_EVENTS.items():
        if when < last:

            @pl.when(now == when)
            def _():
                happen(what)

    per_chunk = ups // parts
    for part in range(parts):
        places = [block_place(orders[part], mine, up, seq) for up in range(base) for seq in range(2)]

        @pl.when((now >= part * per_chunk) & (now < (part + 1) * per_chunk))
        def _():
            value = dot_nn(turned[...], pre[...])
            slot = lax.rem(now, 2)

            @pl.when(now > 0)
            def _():
                up_finish(now - 1)

            @pl.when(now > 1)
            def _():
                for copy in up_stores(now - 2):
                    copy.wait()

            split_blocks(value, up_keep.at[slot], up_send.at[slot], up_keep.shape[2], mine[0], places)
            up_crossing(now).start()

    @pl.when(now == ups)
    def _():
        up_finish(now - 1)
        for index in (now - 2, now - 1):
            for copy in up_stores(index):
                copy.wait()

    def crossing(index):
        slot = lax.rem(index, 2)
        return remote(
            send.at[slot], got.at[slot], send_sem.at[slot], recv_sem.at[slot], partner_along(0, mine)
        )

    def store(index, act_on):
        slot = lax.rem(index, 2)
        width = home_cot.shape[1] // parts
        for seq in range(2):
            for part in range(parts):
                place = 0
                for axis in orders[parts + part]:
                    if axis == "seq":
                        apart = lax.rem(mine["seq"] + seq, 2)
                    else:
                        apart = lax.rem(index // (1 << (axis - 1)) + mine[axis], 2)
                    place = 2 * place + apart
                columns = pl.ds(part * width, width)
                source = keep.at[slot, seq, :, columns]
                sem = out_sem.at[slot, seq, part]
                there = lax.rem(place, base)

                @pl.when(place < base)
                def _():
                    act_on(pltpu.make_async_copy(source, near_down.at[there, :, columns], sem))

                @pl.when(place >= base)
                def _():
                    act_on(pltpu.make_async_copy(source, far_down.at[there, :, columns], sem))

    def finish(index):
        slot = lax.rem(index, 2)
        crossing(index).wait()
        add_into(keep.at[slot], got.at[slot])
        store(index, lambda copy: copy.start())

    @pl.when((late >= 0) & (late < base))
    def _():
        value = dot_nn(act[...].T, home_cot[...])
        slot = lax.rem(late, 2)

        @pl.when(late > 0)
        def _():
            finish(late - 1)

        @pl.when(late > 1)
        def _():
            store(late - 2, lambda copy: copy.wait())

        split_blocks(value, keep.at[slot], send.at[slot], keep.shape[2], mine[0], [0, 1])
        crossing(late).start()

    @pl.when(late == base)
    def _():
        finish(late - 1)
        store(late - 2, lambda copy: copy.wait())
        store(late - 1, lambda copy: copy.wait())

    @pl.when(i == 0)
    def _():
        own_load.wait()
        far_crossing.wait()
        fine = angles.shape[1]
        for coarse in range(2 * seg // fine):
            there = pl.ds(coarse * fine, fine)
            cos_a, sin_a = angles[0, coarse : coarse + 1, :], angles[1, coarse : coarse + 1, :]
            cos[there, :] = cos_a * angles[2] - sin_a * angles[3]
            sin[there, :] = sin_a * angles[2] + cos_a * angles[3]
        emb = table_row(fam, fid[0]) + table_row(ori, oid[me])
        for source, where in ((own, me), (far, 1 - me)):
            for start in range(0, seg, step):
                part = pl.ds(start, step)
                there = pl.ds(pl.multiple_of(where * seg + start, step), step)
                hat, _ = normalise(source[part, :].astype(F32) + emb)
                norm[there, :] = (hat * line(gain) + line(bias)).astype(BF16)
        held = pl.ds(pl.multiple_of(me * seg, seg), seg)
        cot[held, :] = home_cot[held, :]

    lanes = wqkv.shape[1] // 128

    def att_crossing(pair):
        return remote(
            att_send.at[pair],
            att_got.at[pair],
            att_sems.at[0, pair],
            att_sems.at[1, pair],
            partner_along("seq", mine),
        )

    @pl.when((i >= 0) & (i < 2 * tiles))
    def _():
        lin = dot_nn(norm[...], wqkv[...])
        for start in range(0, 2 * seg, step):
            part = pl.ds(start, step)
            for lane in range(lanes):
                piece = lin[start : start + step, lane * 128 : (lane + 1) * 128]
                heads[i * lanes + lane, part, :] = turn(piece, cos[part, :], sin[part, :]).astype(BF16)

    @pl.when((i >= 2 * tiles) & (i < 3 * tiles))
    def _():
        lin = dot_nn(norm[...], wqkv[...]).astype(BF16)
        for lane in range(lanes):
            heads[i * lanes + lane] = lin[:, lane * 128 : (lane + 1) * 128]

    @pl.when(i == 3 * tiles)
    def _():
        cot_crossing.wait()
        cot[pl.ds(pl.multiple_of((1 - me) * seg, seg), seg), :] = cfar[...]

    @pl.when((i >= 3 * tiles) & (i < 4 * tiles))
    def _():
        lin = dot_nt(cot[...], wout[...]).astype(BF16)
        for lane in range(lanes):
            heads[i * lanes + lane] = lin[:, lane * 128 : (lane + 1) * 128]

    @pl.when(i >= 4 * tiles)
    def _():
        pair = i - 4 * tiles
        attend(
            head_size,
            heads.at[pair],
            heads.at[pairs + pair],
            heads.at[2 * pairs + pair],
            heads.at[3 * pairs + pair],
            cos,
            sin,
            o_ref,
            dq_ref,
            dk_ref,
            dv_ref,
            dkt,
            dvt,
        )
        att_send[pair] = o_ref[pl.ds(pl.multiple_of((1 - me) * seg, seg), seg), :]
        att_crossing(pair).start()

    @pl.when(now == last - 1)
    def _():
        for pair in range(pairs):
            att_crossing(pair).wait()
            far_att[:, pair * 128 : (pair + 1) * 128] = att_got[pair]
        happen(FFN_EVENTS[last])


def middle(
    fid, oid, hid, home_cot, turned, both, fam, ori, gain, bias, wqkv, wout, angles, orders, head_size, collective
):
    full, d = hid.shape
    seg = full // 2
    tile = 512
    tiles = d // tile
    pairs = d // 128
    bits = len(orders[0])
    base = 1 << (bits - 1)
    parts = len(orders) // 2
    ff = both.shape[2]
    up_size = d // (4 * base)
    up_tile = 512
    ups = ff // up_tile
    down_tile = ff // base
    down_size = down_tile // 4
    smem = pl.BlockSpec(memory_space=pltpu.SMEM)
    anywhere = pl.BlockSpec(memory_space=pl.ANY)
    late = ups + base
    attend_at = late + 4 * tiles
    head_out = pl.BlockSpec((full, 128), lambda i: (0, jnp.maximum(i - attend_at, 0)))
    rows = jax.ShapeDtypeStruct((full, d), BF16)
    down = jax.ShapeDtypeStruct((base, down_size, d), BF16)
    up = jax.ShapeDtypeStruct((base, up_size, ff), BF16)
    slots = pltpu.VMEM((2, 2, down_size, d), BF16)
    up_slots = pltpu.VMEM((2, 2 * base, up_size, up_tile), BF16)
    return pl.pallas_call(
        functools.partial(middle_kernel, tiles, pairs, head_size, bits, orders),
        grid=(attend_at + pairs,),
        in_specs=[
            smem,
            smem,
            whole((full, d)),
            whole((d, full)),
            pl.BlockSpec((None, full, up_tile), lambda i: (1, 0, jnp.minimum(i, ups - 1))),
            pl.BlockSpec((None, full, down_tile), lambda i: (0, 0, jnp.clip(i - ups, 0, base - 1))),
            whole(fam.shape),
            whole(ori.shape),
            whole(gain.shape),
            whole(bias.shape),
            pl.BlockSpec((d, tile), lambda i: (0, jnp.clip(i - late, 0, 3 * tiles - 1))),
            pl.BlockSpec((tile, d), lambda i: (jnp.clip(i - late - 3 * tiles, 0, tiles - 1), 0)),
            whole(angles.shape),
        ]
        + [anywhere] * 2,
        out_specs=[
            whole((full, d)),
            whole((full, d)),
            head_out,
            head_out,
            head_out,
            head_out,
            whole((seg, d)),
            whole((up_size, ff)),
            whole((down_size, d)),
            anywhere,
            anywhere,
            anywhere,
            anywhere,
        ],
        out_shape=[
            rows,
            rows,
            rows,
            rows,
            rows,
            rows,
            jax.ShapeDtypeStruct((seg, d), BF16),
            jax.ShapeDtypeStruct((up_size, ff), F32),
            jax.ShapeDtypeStruct((down_size, d), F32),
            up,
            up,
            down,
            down,
        ],
        scratch_shapes=[
            pltpu.VMEM((4 * pairs, full, 128), BF16),
            pltpu.VMEM((128, full), F32),
            pltpu.VMEM((128, full), F32),
            pltpu.VMEM((pairs, seg, 128), BF16),
            pltpu.VMEM((pairs, seg, 128), BF16),
            pltpu.SemaphoreType.DMA((2, pairs)),
            pltpu.VMEM((seg, d), BF16),
            pltpu.SemaphoreType.DMA((2,)),
            slots,
            slots,
            slots,
            pltpu.SemaphoreType.DMA((2,)),
            pltpu.SemaphoreType.DMA((2,)),
            pltpu.SemaphoreType.DMA((2, 2, parts)),
            up_slots,
            up_slots,
            up_slots,
            pltpu.SemaphoreType.DMA((2,)),
            pltpu.SemaphoreType.DMA((2,)),
            pltpu.SemaphoreType.DMA((2, 2)),
            pltpu.VMEM((seg, d), BF16),
            pltpu.VMEM((full, 128), F32),
            pltpu.VMEM((full, 128), F32),
            pltpu.SemaphoreType.DMA,
            pltpu.VMEM((seg, d), BF16),
            pltpu.SemaphoreType.DMA((2,)),
        ]
        + [
            entry
            for index, axes in enumerate(orders)
            for entry in chunk_scratch(
                axes, *((up_size, ff // parts) if index < parts else (down_size, d // parts))
            )
        ],
        compiler_params=pltpu.CompilerParams(
            vmem_limit_bytes=67043328, collective_id=collective, has_side_effects=True
        ),
        cost_estimate=cost(16 * full * d * d + 12 * full * full * d, 8 * d * d + 18 * full * d, full * full * H),
        name="middle",
    )(fid, oid, home_cot, turned, both, both, fam, ori, gain, bias, wqkv, wout, angles, hid, home_cot)


def device_bits(bits):
    dp = lax.axis_index("dp")
    found = {bit: lax.rem(dp // (1 << bit), 2) for bit in range(bits)}
    found["seq"] = lax.axis_index("seq")
    return found


def block_place(axes, mine, upper, seq):
    place = 0
    for axis in axes:
        bit = seq if axis == "seq" else (upper >> (axis - 1)) & 1
        place = 2 * place + (1 - mine[axis] if bit else mine[axis])
    return place


def other_core():
    dp = lax.axis_index("dp")
    return (dp + 1 - 2 * lax.rem(dp, 2), lax.axis_index("seq"))


def meet(partners):
    barrier = pltpu.get_barrier_semaphore()
    for partner in partners:
        pl.semaphore_signal(barrier, inc=1, device_id=partner, device_id_type=MESH)
    pl.semaphore_wait(barrier, len(partners))


def remote(src, dst, send_sem, recv_sem, partner):
    return pltpu.make_async_remote_copy(
        src_ref=src,
        dst_ref=dst,
        send_sem=send_sem,
        recv_sem=recv_sem,
        device_id=partner,
        device_id_type=MESH,
    )


def split_blocks(value, keep, send, size, core, places):
    for index, there in enumerate(places):
        up, seq = index // 2, index % 2
        first = (4 * up + seq) * size
        second = first + 2 * size
        a = value[first : first + size, :].astype(BF16)
        b = value[second : second + size, :].astype(BF16)
        keep[there] = jnp.where(core == 0, a, b)
        send[there] = jnp.where(core == 0, b, a)


def add_into(keep, got):
    def add(index, carry):
        keep[index] = (keep[index].astype(F32) + got[index].astype(F32)).astype(BF16)
        return carry

    lax.fori_loop(0, got.shape[0], add, 0, unroll=2 if got.shape[0] > 1 else 1)


def partner_along(axis, mine):
    dp = lax.axis_index("dp")
    seq = lax.axis_index("seq")
    if axis == "seq":
        return (dp, 1 - seq)
    return (dp + (1 - 2 * mine[axis]) * (1 << axis), seq)


class Chunk:
    def __init__(self, axes, mine, near, far, columns, out, keep, got, near_sem, send_sem, recv_sem):
        self.axes, self.mine, self.near, self.far = axes, mine, near, far
        self.columns, self.out, self.keep, self.got = columns, out, keep, got
        self.near_sem, self.send_sem, self.recv_sem = near_sem, send_sem, recv_sem

    def load(self):
        return pltpu.make_async_copy(self.near.at[:, :, self.columns], self.keep, self.near_sem)

    def crossing(self, stage):
        count = (1 << len(self.axes)) >> (stage + 1)
        if stage == 0 and self.far is not None:
            source = self.far.at[:, :, self.columns]
        else:
            source = self.keep.at[pl.ds(count, count)]
        return remote(
            source,
            self.got[stage],
            self.send_sem.at[stage],
            self.recv_sem.at[stage],
            partner_along(self.axes[stage], self.mine),
        )

    def begin(self):
        if self.near is not None:
            self.load().start()
        self.crossing(0).start()

    def advance(self, stage):
        if stage == 1 and self.near is not None:
            self.load().wait()
        self.crossing(stage - 1).wait()
        add_into(self.keep, self.got[stage - 1])
        self.crossing(stage).start()

    def finish(self):
        last = len(self.axes) - 1
        self.crossing(last).wait()
        self.out[:, self.columns] = self.keep[0].astype(F32) + self.got[last][0].astype(F32)

    def happen(self, stage):
        if stage == 0:
            self.begin()
        elif stage == len(self.axes):
            self.finish()
        else:
            self.advance(stage)


def chunk_scratch(axes, size, width, farther=False):
    half = 1 << (len(axes) - 1)
    return (
        [pltpu.VMEM((2 * half if farther else half, size, width), BF16)]
        + [pltpu.VMEM((half >> stage, size, width), BF16) for stage in range(len(axes))]
        + [
            pltpu.SemaphoreType.DMA,
            pltpu.SemaphoreType.DMA((len(axes),)),
            pltpu.SemaphoreType.DMA((len(axes),)),
        ]
    )


def chunks_from(refs, bits, mine, wanted):
    stages = bits
    found = []
    each = 1 + stages + 3
    for index, (axes, near, far, columns, out) in enumerate(wanted):
        part = refs[index * each : (index + 1) * each]
        found.append(
            Chunk(axes, mine, near, far, columns, out, part[0], part[1 : 1 + stages], *part[1 + stages :])
        )
    return found


def after(entry, *others):
    return lax.optimization_barrier((entry, *others))[0]


TAIL_TILE = 512
TAIL_STEP = 256


def tail_kernel(bits, orders, rows, marks, *refs):
    fid, oid, norm_hbm, att_hbm, cot_hbm, dq_hbm, dk_hbm, dv_hbm, wqkv_hbm, wout_hbm = refs[:10]
    fam, ori, gain, bdn, bup_part, bdn_part, far_att = refs[10:17]
    both, wdn, wup, hid, cot = refs[17:22]
    layer_out, input_out, qkv_out, out_out, sums_out, all_out = refs[22:28]
    left, right, dq, dk, dv, wqkv, wout, turned, acc, ng_here, ng_got = refs[28:39]
    gg, bg, rg, load_sem, ng_sem, held, got, vec, vgot, table, ssem, rsem, gsend, grecv = refs[39:53]
    in_start, in_end, out_start, out_end, last = marks
    i = pl.program_id(0)
    me = lax.axis_index("seq")
    dp = lax.axis_index("dp")
    mine = device_bits(bits)
    d = left.shape[1]
    seg = ng_got.shape[0]
    step = TAIL_STEP
    per_row = seg // step
    chunks = chunks_from(
        refs[53:],
        len(orders[0]),
        mine,
        [
            (orders[0], None, None, pl.ds(0, d), qkv_out),
            (orders[1], None, None, pl.ds(d, d), qkv_out),
            (orders[2], None, None, pl.ds(2 * d, d), qkv_out),
            (orders[3], None, None, pl.ds(0, d), out_out),
        ],
    )
    loads = {
        name: pltpu.make_async_copy(source, there, load_sem.at[index])
        for index, (name, source, there) in enumerate(
            (
                ("norm", norm_hbm, left),
                ("dq", dq_hbm, dq),
                ("dk", dk_hbm, dk),
                ("dv", dv_hbm, dv),
                ("wqkv", wqkv_hbm, wqkv),
                ("cot", cot_hbm, right),
                ("wout", wout_hbm, wout),
                ("att", att_hbm, left),
            )
        )
    }
    partners = [partner_along(axis, mine) for axis in ["seq"] + list(range(bits))]

    def gradient(index, operand):
        chunk = chunks[index]
        size = chunk.keep.shape[1]
        value = dot_nn(turned[...], operand[...])
        for block in range(chunk.keep.shape[0]):
            place = 0
            for axis in orders[index]:
                bit = block & 1 if axis == "seq" else (block >> (axis + 1)) & 1
                place = 2 * place + (1 - mine[axis] if bit else mine[axis])
            chunk.keep[place] = value[block * size : (block + 1) * size, :].astype(BF16)
        chunk.begin()

    ng_crossing = remote(ng_here.at[0], ng_got, ng_sem.at[0], ng_sem.at[1], partners[0])

    @pl.when(i == 0)
    def _():
        loads["norm"].start()
        loads["dq"].start()
        meet(partners)
        loads["norm"].wait()
        turned[...] = left[...].T
        loads["dq"].wait()
        for name in ("dk", "dv", "wqkv", "att", "cot", "wout"):
            loads[name].start()
        gradient(0, dq)

    for when, what in LATE_EVENTS.items():
        if when < last:

            @pl.when(i == when)
            def _():
                for chunk, stage in what:
                    chunks[chunk].happen(stage)

    @pl.when(i == 1)
    def _():
        loads["dk"].wait()
        gradient(1, dk)

    @pl.when(i == 2)
    def _():
        loads["dv"].wait()
        gradient(2, dv)

    @pl.when(i == 3)
    def _():
        loads["wqkv"].wait()

    @pl.when((i == 3) | (i == 5))
    def _():
        first = (5 - i) // 2
        half = first * (1 - me) + (1 - first) * me
        part = pl.ds(pl.multiple_of(half * seg, seg), seg)
        total = dot_nt(dq[part, :], wqkv[:, 0:d])
        total = total + dot_nt(dk[part, :], wqkv[:, d : 2 * d])
        total = total + dot_nt(dv[part, :], wqkv[:, 2 * d : 3 * d])
        ng_here[1 - first] = total.astype(BF16)

    @pl.when(i == 3)
    def _():
        ng_crossing.start()

    @pl.when(i == 4)
    def _():
        loads["att"].wait()
        loads["cot"].wait()
        turned[...] = left[...].T
        gradient(3, right)

    @pl.when((i >= out_start) & (i < out_end))
    def _():
        value = dot_nn(both[0], wdn[...])

        @pl.when(i == out_start)
        def _():
            acc[...] = value

        @pl.when(i > out_start)
        def _():
            acc[...] += value

    @pl.when((i >= in_start) & (i < in_end))
    def _():
        value = dot_nt(both[0], wup[...])

        @pl.when(i == in_start)
        def _():
            acc[...] = value

        @pl.when(i > in_start)
        def _():
            acc[...] += value

    @pl.when(i == out_end)
    def _():
        loads["wout"].wait()

    def home_block(index, own, far, own_offset):
        row = index // per_row
        within = pl.multiple_of(lax.rem(index, per_row) * step, step)
        there = pl.ds(pl.multiple_of(own_offset + within, step), step)
        return row, jnp.where(row == me, own[there, :], far[pl.ds(within, step), :])

    @pl.when(i >= out_end)
    def _():
        index = i - out_end
        row, att = home_block(index, left, far_att, me * seg)
        flag = oid[row]
        emb = table_row(fam, fid[0]) + table_row(ori, flag)
        part = pl.ds(pl.multiple_of(index * step, step), step)
        total = hid[...].astype(F32) + emb + dot_nn(att, wout[...])
        layer_out[...] = (total + (acc[part, :] + line(bdn))).astype(BF16)

    @pl.when(i == in_end)
    def _():
        ng_crossing.wait()
        gg[...] = jnp.zeros_like(gg)
        bg[...] = jnp.zeros_like(bg)
        rg[...] = jnp.zeros_like(rg)

    @pl.when((i >= in_end) & (i < out_start))
    def _():
        index = i - in_end
        row, back = home_block(index, ng_here.at[1], ng_got, 0)
        flag = oid[row]
        emb = table_row(fam, fid[0]) + table_row(ori, flag)
        part = pl.ds(pl.multiple_of(index * step, step), step)
        hat, inv_std = normalise(hid[...].astype(F32) + emb)
        grad = acc[part, :] + back.astype(F32)
        gg[...] += jnp.sum(grad * hat, 0, keepdims=True)
        bg[...] += jnp.sum(grad, 0, keepdims=True)
        scaled = grad * line(gain)
        inner = (
            scaled
            - jnp.mean(scaled, -1, keepdims=True)
            - hat * jnp.mean(scaled * hat, -1, keepdims=True)
        )
        result = cot[...].astype(F32) + inv_std * inner
        input_out[...] = result
        sums = jnp.sum(result, 0, keepdims=True)
        which = lax.broadcasted_iota(jnp.int32, rg.shape, 0)
        rg[...] += jnp.where(which == flag, sums, 0.0)

    def sums_main(index):
        return remote(held.at[index], got.at[index], ssem.at[index], rsem.at[index], partners[index])

    def sums_side(index):
        if index == 0:
            return remote(vec, vgot, gsend.at[0], grecv.at[0], partners[0])
        size = 1 << (index - 1)
        now = pl.ds(dp - lax.rem(dp, size), size)
        return remote(table.at[now], table.at[now], gsend.at[index], grecv.at[index], partners[index])

    @pl.when(i == out_start)
    def _():
        at = 0
        for source in (bup_part[...], bdn_part[...], gg[...], bg[...], rg[0:1, :], rg[1:2, :]):
            for lane in range(0, source.shape[1], 128):
                held[0, at : at + 1, :] = source[:, lane : lane + 128]
                at += 1
        both_rows = rg[0:1, :] + rg[1:2, :]
        for lane in range(0, d, 128):
            vec[lane // 128 : lane // 128 + 1, :] = both_rows[:, lane : lane + 128]
        extra = d // 128
        vec[extra:, :] = jnp.full((vec.shape[0] - extra, 128), 0.5, F32) * fid[0].astype(F32)
        sums_main(0).start()
        sums_side(0).start()

    for index in range(len(partners)):

        @pl.when(i == out_start + 2 * (index + 1))
        def _():
            sums_main(index).wait()
            sums_side(index).wait()
            total = held[index] + got[index]
            if index == 0:
                table[dp] = vec[...] + vgot[...]
            if index + 1 < len(partners):
                held[index + 1] = total
                sums_main(index + 1).start()
                sums_side(index + 1).start()
            else:
                sums_out[...] = total
                all_out[...] = table[...]

    @pl.when(i == last - 1)
    def _():
        for chunk, stage in LATE_EVENTS[last]:
            chunks[chunk].happen(stage)


def tail(fid, oid, norm, att, row_cot, dq, dk, dv, wqkv, wout, fam, ori, gain, bdn, bup_part, bdn_part, far_att, both, wdn, wup, hid, cot, orders, rows, collective):
    tokens, d = hid.shape
    ff = wup.shape[1]
    bits = len(orders[0]) - 1
    count = 1 << bits
    seg = far_att.shape[0]
    tile, step = TAIL_TILE, TAIL_STEP
    tiles, blocks = ff // tile, tokens // step
    in_start = 6
    in_end = in_start + tiles
    out_start = in_end + blocks
    out_end = out_start + tiles
    last = out_end + blocks
    marks = (in_start, in_end, out_start, out_end, last)
    size = d // (2 * count)
    rounds = bits + 1
    lines = (ff + 5 * d) // 128
    vec_shape = (d // 128 + 8, 128)
    anywhere = pl.BlockSpec(memory_space=pl.ANY)

    def plane(i):
        late = i >= out_start
        return (jnp.where(late, 0, 1), 0, jnp.clip(jnp.where(late, i - out_start, i - in_start), 0, tiles - 1))

    def home(i):
        return (jnp.clip(jnp.where(i >= out_start, i - out_end, i - in_end), 0, blocks - 1), 0)

    square = pltpu.VMEM((tokens, d), BF16)
    piece = pltpu.VMEM((seg, d), BF16)
    row = pltpu.VMEM((1, d), F32)
    return pl.pallas_call(
        functools.partial(tail_kernel, bits, orders, rows, marks),
        grid=(last,),
        in_specs=[pl.BlockSpec(memory_space=pltpu.SMEM)] * 2
        + [anywhere] * 8
        + [
            whole(fam.shape),
            whole(ori.shape),
            whole(gain.shape),
            whole(bdn.shape),
            whole((1, ff)),
            whole((1, d)),
            whole((seg, d)),
            pl.BlockSpec((1, tokens, tile), plane),
            pl.BlockSpec((tile, d), lambda i: (jnp.clip(i - out_start, 0, tiles - 1), 0)),
            pl.BlockSpec((d, tile), lambda i: (0, jnp.clip(i - in_start, 0, tiles - 1))),
            pl.BlockSpec((step, d), home),
            pl.BlockSpec((step, d), lambda i: (jnp.clip(i - in_end, 0, blocks - 1), 0)),
        ],
        out_specs=[
            pl.BlockSpec((step, d), lambda i: (jnp.clip(i - out_end, 0, blocks - 1), 0)),
            pl.BlockSpec((step, d), lambda i: (jnp.clip(i - in_end, 0, blocks - 1), 0)),
            whole((size, 3 * d)),
            whole((size, d)),
            whole((lines, 128)),
            whole((count,) + vec_shape),
        ],
        out_shape=[
            jax.ShapeDtypeStruct((tokens, d), BF16),
            jax.ShapeDtypeStruct((tokens, d), F32),
            jax.ShapeDtypeStruct((size, 3 * d), F32),
            jax.ShapeDtypeStruct((size, d), F32),
            jax.ShapeDtypeStruct((lines, 128), F32),
            jax.ShapeDtypeStruct((count,) + vec_shape, F32),
        ],
        scratch_shapes=[
            square,
            square,
            square,
            square,
            square,
            pltpu.VMEM((d, 3 * d), BF16),
            pltpu.VMEM((d, d), BF16),
            pltpu.VMEM((d, tokens), BF16),
            pltpu.VMEM((tokens, d), F32),
            pltpu.VMEM((2, seg, d), BF16),
            piece,
            row,
            row,
            pltpu.VMEM((2, d), F32),
            pltpu.SemaphoreType.DMA((8,)),
            pltpu.SemaphoreType.DMA((2,)),
            pltpu.VMEM((rounds, lines, 128), F32),
            pltpu.VMEM((rounds, lines, 128), F32),
            pltpu.VMEM(vec_shape, F32),
            pltpu.VMEM(vec_shape, F32),
            pltpu.VMEM((count,) + vec_shape, F32),
            pltpu.SemaphoreType.DMA((rounds,)),
            pltpu.SemaphoreType.DMA((rounds,)),
            pltpu.SemaphoreType.DMA((rounds,)),
            pltpu.SemaphoreType.DMA((rounds,)),
        ]
        + [entry for axes in orders for entry in chunk_scratch(axes, size, d, True)],
        compiler_params=pltpu.CompilerParams(
            vmem_limit_bytes=67043328, collective_id=collective, has_side_effects=True
        ),
        cost_estimate=cost(16 * tokens * d * d + 4 * tokens * d * ff, 8 * d * ff + 40 * tokens * d),
        name="tail",
    )(fid, oid, norm, att, row_cot, dq, dk, dv, wqkv, wout, fam, ori, gain, bdn, bup_part, bdn_part, far_att, both, wdn, wup, hid, cot)


def finish_kernel(ff, layer, inputs, qkv, out, up, down, sums, table, *outs):
    layer_out, input_out, qkv_out, out_out, up_out, down_out, bup, bdn, gain, bias, fam_out, ori_out = outs
    layer_out[...] = layer[...]
    input_out[...] = inputs[...]
    qkv_out[...] = qkv[...]
    out_out[...] = out[...]
    up_out[...] = up[...]
    down_out[...] = down[...]

    @pl.when(pl.program_id(0) == 0)
    def _():
        d = gain.shape[1]
        at = 0
        for there in (bup, bdn, gain, bias, ori_out.at[0:1], ori_out.at[1:2]):
            for lane in range(0, there.shape[1], 128):
                there[:, lane : lane + 128] = sums[at : at + 1, :]
                at += 1
        extra = d // 128
        rows = lax.broadcasted_iota(jnp.int32, (fam_out.shape[0], 128), 0).astype(F32)
        for lane in range(extra):
            total = jnp.zeros((fam_out.shape[0], 128), F32)
            for index in range(table.shape[0]):
                total = total + jnp.where(
                    rows == table[index, extra : extra + 1, :], table[index, lane : lane + 1, :], 0.0
                )
            fam_out[:, lane * 128 : (lane + 1) * 128] = total


def finish(layer, inputs, qkv, out, up, down, sums, table, families):
    tokens, d = layer.shape
    ff = up.shape[1]
    steps = 4

    def rows(entry):
        return pl.BlockSpec((entry.shape[0] // steps, entry.shape[1]), lambda i: (i, 0))

    big = [layer, inputs, qkv, out, up, down]
    small = [(1, ff), (1, d), (1, d), (1, d), (families, d), (2, d)]
    return pl.pallas_call(
        functools.partial(finish_kernel, ff),
        grid=(steps,),
        in_specs=[rows(entry) for entry in big] + [whole(sums.shape), whole(table.shape)],
        out_specs=[rows(entry) for entry in big] + [whole(shape) for shape in small],
        out_shape=[jax.ShapeDtypeStruct(entry.shape, entry.dtype) for entry in big]
        + [jax.ShapeDtypeStruct(shape, F32) for shape in small],
        compiler_params=params(),
        name="finish",
    )(*big, sums, table)


def body_by_rows(
    hidden_in,
    family,
    orient,
    norm_gain,
    norm_bias,
    qkv_weight,
    out_weight,
    up_weight,
    up_bias,
    down_weight,
    down_bias,
    family_table,
    orient_table,
    cotangent,
):
    rows, seg, d = hidden_in.shape
    ff = up_weight.shape[1]
    tokens = rows * seg
    full = 2 * seg
    dp_count = lax.axis_size("dp")
    bits = int(math.log2(dp_count))
    upper = dp_count // 2
    dp = lax.axis_index("dp")
    seq = lax.axis_index("seq")
    hid = hidden_in.reshape(tokens, d)
    cot = cotangent.reshape(tokens, d)
    turned, both, up_bias_part, down_bias_part = ffn_forward(
        family, orient, hid, cot, family_table, orient_table, norm_gain, norm_bias, up_weight, up_bias, down_weight, rows
    )
    fine = 32
    positions = jnp.concatenate([fine * jnp.arange(full // fine), jnp.arange(fine)]).astype(F32)
    cosine, sine = rope_tables(positions, 128)
    coarse = full // fine
    angles = jnp.stack([cosine[:coarse], sine[:coarse], cosine[coarse:], sine[coarse:]])
    row_normed, row_cot, att, dq, dk, dv, far_att, up_total, down_total, *_ = middle(
        family,
        orient,
        hid,
        cot,
        turned,
        both,
        family_table,
        orient_table,
        norm_gain,
        norm_bias,
        qkv_weight,
        out_weight,
        angles,
        FFN_ORDERS,
        d // H,
        3,
    )
    layer_out, input_grad, qkv_total, out_total, sums, gathered = tail(
        family,
        orient,
        row_normed,
        att,
        row_cot,
        dq,
        dk,
        dv,
        qkv_weight,
        out_weight,
        family_table,
        orient_table,
        norm_gain,
        down_bias,
        up_bias_part,
        down_bias_part,
        far_att,
        both,
        down_weight,
        up_weight,
        hid,
        cot,
        LATE_ORDERS,
        rows,
        4,
    )
    layer_out, input_grad, qkv_sum, out_sum, up_sum, down_sum, *small = finish(
        layer_out, input_grad, qkv_total, out_total, up_total, down_total, sums, gathered, family_table.shape[0]
    )
    up_bias_sum, down_bias_sum, gain_sum, bias_sum = (part.reshape(-1) for part in small[:4])
    return (
        layer_out.reshape(rows, seg, d),
        input_grad.reshape(rows, seg, d),
        gain_sum,
        bias_sum,
        qkv_sum,
        out_sum,
        up_sum,
        up_bias_sum,
        down_sum,
        down_bias_sum,
        small[4],
        small[5],
    )


def body(*args):
    hidden_in = args[0]
    dp_count = lax.axis_size("dp")
    two_rows = lax.axis_size("seq") == 2 and hidden_in.shape[0] == 2
    if two_rows and dp_count == 16 and hidden_in.shape[1] == 512:
        return body_by_rows(*args)
    return body_by_heads(*args)


def solution(mesh):
    return jax.shard_map(
        body,
        mesh=mesh,
        in_specs=(
            P("dp", "seq", None),
            P("dp"),
            P("dp"),
            P(),
            P(),
            P(),
            P(),
            P(),
            P(),
            P(),
            P(),
            P(),
            P(),
            P("dp", "seq", None),
        ),
        out_specs=(
            P("dp", "seq", None),
            P("dp", "seq", None),
            P(),
            P(),
            P(("dp", "seq"), None),
            P(("dp", "seq"), None),
            P(("dp", "seq"), None),
            P(),
            P(("dp", "seq"), None),
            P(),
            P(),
            P(),
        ),
        check_vma=False,
    )
```

```python
import functools
import math

import jax
import jax.numpy as jnp
from jax import lax
from jax.experimental import pallas as pl
from jax.experimental.pallas import tpu as pltpu
from jax.sharding import PartitionSpec as P

H = 16
HD = 64
ROT = 32
MESH = pl.DeviceIdType.MESH
VMEM_LIMIT = 60 * 1024 * 1024
F32 = jnp.float32
BF16 = jnp.bfloat16


def for_sending(shard):

    def short(part):
        return part.astype(jnp.bfloat16) if part.dtype == jnp.float32 else part

    return jax.tree.map(short, shard)


def rope_tables(positions, features):
    column = jnp.arange(features, dtype=jnp.int32)
    within = column % HD
    frequency = jnp.exp(-(2.0 * (within // 2).astype(jnp.float32) / ROT) * math.log(10000.0))
    angles = positions[:, None] * frequency[None, :]
    rotary = within < ROT
    cosine = jnp.where(rotary[None, :], jnp.cos(angles), 1.0)
    sign_term = jnp.where(within % 2 == 0, -1.0, 1.0)
    sine_term = jnp.where(rotary[None, :], sign_term[None, :] * jnp.sin(angles), 0.0)
    return (cosine, sine_term)


def pair_swap(values):
    even_cols = jnp.arange(values.shape[-1]) % 2 == 0
    return jnp.where(even_cols, jnp.roll(values, -1, axis=-1), jnp.roll(values, 1, axis=-1))


def rotate(values, cosine, sine_term):
    return values * cosine + pair_swap(values) * sine_term


def rotate_back(values, cosine, sine_term):
    return values * cosine + pair_swap(values * sine_term)


def gelu_tanh(pre_values):
    return jax.nn.gelu(pre_values, approximate=True)


def body_by_heads(
    hidden_in,
    family,
    orient,
    norm_gain,
    norm_bias,
    qkv_weight,
    out_weight,
    up_weight,
    up_bias,
    down_weight,
    down_bias,
    family_table,
    orient_table,
    cotangent,
):
    seq_count = lax.axis_size("seq")
    row_count, seg_length, features = hidden_in.shape
    full_length = seg_length * seq_count
    local_heads = H // seq_count
    head_size = features // H
    slab_width = features // seq_count
    block_rows = min(512, full_length)
    block_count = full_length // block_rows
    score_scale = head_size ** (-0.5)
    token_count = row_count * seg_length
    family_rows = jnp.repeat(family, 2)
    family_hot = (family_rows[:, None] == jnp.arange(family_table.shape[0])[None, :]).astype(
        jnp.bfloat16
    )
    orient_hot = (orient[:, None] == jnp.arange(2)[None, :]).astype(jnp.bfloat16)
    embedding = jnp.dot(family_hot, family_table, preferred_element_type=jnp.float32) + jnp.dot(
        orient_hot, orient_table, preferred_element_type=jnp.float32
    )
    embedded = (hidden_in.astype(jnp.float32) + embedding[:, None, :]).reshape(
        token_count, features
    )
    row_mean = jnp.mean(embedded, -1, keepdims=True)
    centred = embedded - row_mean
    row_var = jnp.mean(centred * centred, -1, keepdims=True)
    inv_std = lax.rsqrt(row_var + 1e-05)
    normed_hat = centred * inv_std
    gain_f32 = norm_gain.astype(jnp.float32)
    normed_low = (normed_hat * gain_f32 + norm_bias.astype(jnp.float32)).astype(jnp.bfloat16)
    projected = jnp.dot(normed_low, qkv_weight, preferred_element_type=jnp.float32).reshape(
        row_count, seg_length, 3 * features
    )
    positions = (lax.axis_index("seq") * seg_length + jnp.arange(seg_length)).astype(jnp.float32)
    cosine, sine_term = rope_tables(positions, features)
    queries = rotate(projected[..., :features], cosine, sine_term).astype(jnp.bfloat16)
    keys_rot = rotate(projected[..., features : 2 * features], cosine, sine_term).astype(
        jnp.bfloat16
    )
    values = projected[..., 2 * features :].astype(jnp.bfloat16)
    query_heads, key_heads, value_heads = (
        lax.all_to_all(queries, "seq", split_axis=2, concat_axis=1, tiled=True),
        lax.all_to_all(keys_rot, "seq", split_axis=2, concat_axis=1, tiled=True),
        lax.all_to_all(values, "seq", split_axis=2, concat_axis=1, tiled=True),
    )

    def scores_for(query_block, key_rows, block_start):
        logits = (
            jnp.einsum("qhd,khd->hqk", query_block, key_rows, preferred_element_type=jnp.float32)
            * score_scale
        )
        causal = (block_start + jnp.arange(block_rows))[:, None] >= jnp.arange(full_length)[None, :]
        return jnp.where(causal[None], logits, -1e30)

    def attend(row_args):
        query_row, key_row, value_row = row_args
        key_rows = key_row.reshape(full_length, local_heads, head_size)
        value_rows = value_row.reshape(full_length, local_heads, head_size)
        pieces = []
        log_parts = []
        for block_index in range(block_count):
            block_start = block_index * block_rows
            query_block = query_row[block_start : block_start + block_rows].reshape(
                block_rows, local_heads, head_size
            )
            logits = scores_for(query_block, key_rows, block_start)
            row_peak = jnp.max(logits, -1, keepdims=True)
            weights = jnp.exp(logits - row_peak)
            row_total = jnp.sum(weights, -1, keepdims=True)
            prob_low = (weights / row_total).astype(jnp.bfloat16)
            output_block = jnp.einsum(
                "hqk,khd->qhd", prob_low, value_rows, preferred_element_type=jnp.float32
            )
            pieces.append(output_block.reshape(block_rows, slab_width).astype(jnp.bfloat16))
            log_parts.append((row_peak + jnp.log(row_total))[..., 0])
        return (jnp.concatenate(pieces, 0), jnp.concatenate(log_parts, 1))

    attended_heads, log_sums = lax.map(attend, (query_heads, key_heads, value_heads))
    attended = jax.tree.map(
        lambda part, own: part.astype(own.dtype),
        lax.all_to_all(for_sending(attended_heads), "seq", split_axis=1, concat_axis=2, tiled=True),
        attended_heads,
    )
    attended_flat = attended.reshape(token_count, features)
    branch_attn = jnp.dot(attended_flat, out_weight, preferred_element_type=jnp.float32)
    up_pre = jnp.dot(normed_low, up_weight, preferred_element_type=jnp.float32) + up_bias.astype(
        jnp.float32
    )
    up_act = gelu_tanh(up_pre).astype(jnp.bfloat16)
    branch_feed = jnp.dot(
        up_act, down_weight, preferred_element_type=jnp.float32
    ) + down_bias.astype(jnp.float32)
    layer_out = (
        (embedded + branch_attn + branch_feed)
        .astype(jnp.bfloat16)
        .reshape(row_count, seg_length, features)
    )
    grad_low = cotangent.reshape(token_count, features)
    grad_f32 = grad_low.astype(jnp.float32)
    down_grad = jnp.einsum("nf,nd->fd", up_act, grad_low, preferred_element_type=jnp.float32)
    down_bias_grad = jnp.sum(grad_f32, 0)
    act_grad = jnp.einsum("nd,fd->nf", grad_low, down_weight, preferred_element_type=jnp.float32)
    gelu_out, gelu_pull = jax.vjp(gelu_tanh, up_pre)
    pre_grad = gelu_pull(act_grad)[0].astype(jnp.bfloat16)
    up_bias_grad = jnp.sum(pre_grad.astype(jnp.float32), 0)
    up_grad = jnp.einsum("nd,nf->df", normed_low, pre_grad, preferred_element_type=jnp.float32)
    normed_grad = jnp.einsum("nf,df->nd", pre_grad, up_weight, preferred_element_type=jnp.float32)
    out_grad = jnp.einsum("nd,ne->de", attended_flat, grad_low, preferred_element_type=jnp.float32)
    attended_grad = jnp.einsum(
        "ne,de->nd", grad_low, out_weight, preferred_element_type=jnp.float32
    )
    attended_grad = attended_grad.astype(jnp.bfloat16).reshape(row_count, seg_length, features)
    grad_heads = lax.all_to_all(attended_grad, "seq", split_axis=2, concat_axis=1, tiled=True)

    def attend_back(row_args):
        query_row, key_row, value_row, grad_row, log_row = row_args
        key_rows = key_row.reshape(full_length, local_heads, head_size)
        value_rows = value_row.reshape(full_length, local_heads, head_size)
        keys_total = jnp.zeros((full_length, local_heads, head_size), jnp.float32)
        values_total = jnp.zeros((full_length, local_heads, head_size), jnp.float32)
        query_parts = []
        for block_index in range(block_count):
            block_start = block_index * block_rows
            query_block = query_row[block_start : block_start + block_rows].reshape(
                block_rows, local_heads, head_size
            )
            grad_block = grad_row[block_start : block_start + block_rows].reshape(
                block_rows, local_heads, head_size
            )
            logits = scores_for(query_block, key_rows, block_start)
            probs_full = jnp.exp(logits - log_row[:, block_start : block_start + block_rows, None])
            prob_low = probs_full.astype(jnp.bfloat16)
            probs_grad = jnp.einsum(
                "qhd,khd->hqk", grad_block, value_rows, preferred_element_type=jnp.float32
            )
            inner_sum = jnp.sum(probs_full * probs_grad, -1, keepdims=True)
            scores_grad = (probs_full * (probs_grad - inner_sum)).astype(jnp.bfloat16)
            values_total = values_total + jnp.einsum(
                "hqk,qhd->khd", prob_low, grad_block, preferred_element_type=jnp.float32
            )
            query_grad = (
                jnp.einsum(
                    "hqk,khd->qhd", scores_grad, key_rows, preferred_element_type=jnp.float32
                )
                * score_scale
            )
            query_parts.append(query_grad.reshape(block_rows, slab_width).astype(jnp.bfloat16))
            keys_total = (
                keys_total
                + jnp.einsum(
                    "hqk,qhd->khd", scores_grad, query_block, preferred_element_type=jnp.float32
                )
                * score_scale
            )
        return (
            jnp.concatenate(query_parts, 0),
            keys_total.reshape(full_length, slab_width).astype(jnp.bfloat16),
            values_total.reshape(full_length, slab_width).astype(jnp.bfloat16),
        )

    query_grad_heads, key_grad_heads, value_grad_heads = lax.map(
        attend_back, (query_heads, key_heads, value_heads, grad_heads, log_sums)
    )
    query_grad_pos, key_grad_pos, value_grad_pos = (
        lax.all_to_all(
            for_sending(query_grad_heads), "seq", split_axis=1, concat_axis=2, tiled=True
        ).astype(query_grad_heads.dtype),
        lax.all_to_all(
            for_sending(key_grad_heads), "seq", split_axis=1, concat_axis=2, tiled=True
        ).astype(key_grad_heads.dtype),
        lax.all_to_all(
            for_sending(value_grad_heads), "seq", split_axis=1, concat_axis=2, tiled=True
        ).astype(value_grad_heads.dtype),
    )
    projected_grad = jnp.concatenate(
        [
            rotate_back(query_grad_pos.astype(jnp.float32), cosine, sine_term),
            rotate_back(key_grad_pos.astype(jnp.float32), cosine, sine_term),
            value_grad_pos.astype(jnp.float32),
        ],
        -1,
    )
    projected_grad = projected_grad.astype(jnp.bfloat16).reshape(token_count, 3 * features)
    qkv_grad = jnp.einsum(
        "nd,ne->de", normed_low, projected_grad, preferred_element_type=jnp.float32
    )
    normed_grad = normed_grad + jnp.einsum(
        "ne,de->nd", projected_grad, qkv_weight, preferred_element_type=jnp.float32
    )
    gain_grad = jnp.sum(normed_grad * normed_hat, 0)
    bias_grad = jnp.sum(normed_grad, 0)
    scaled_grad = normed_grad * gain_f32
    hat_grad = (
        scaled_grad
        - jnp.mean(scaled_grad, -1, keepdims=True)
        - normed_hat * jnp.mean(scaled_grad * normed_hat, -1, keepdims=True)
    )
    input_grad = (grad_f32 + inv_std * hat_grad).reshape(row_count, seg_length, features)
    row_sums = jnp.sum(input_grad, 1)
    family_grad = jnp.einsum(
        "rf,rd->fd", family_hot.astype(jnp.float32), row_sums, precision=lax.Precision.HIGHEST
    )
    orient_grad = jnp.einsum(
        "rf,rd->fd", orient_hot.astype(jnp.float32), row_sums, precision=lax.Precision.HIGHEST
    )
    gain_sum, bias_sum, up_bias_sum, down_bias_sum, family_sum, orient_sum = lax.psum(
        (gain_grad, bias_grad, up_bias_grad, down_bias_grad, family_grad, orient_grad),
        ("dp", "seq"),
    )
    qkv_sum, out_sum, up_sum, down_sum = (
        lax.psum_scatter(qkv_grad, ("dp", "seq"), scatter_dimension=0, tiled=True),
        lax.psum_scatter(out_grad, ("dp", "seq"), scatter_dimension=0, tiled=True),
        lax.psum_scatter(up_grad, ("dp", "seq"), scatter_dimension=0, tiled=True),
        lax.psum_scatter(down_grad, ("dp", "seq"), scatter_dimension=0, tiled=True),
    )
    return (
        layer_out,
        input_grad,
        gain_sum,
        bias_sum,
        qkv_sum,
        out_sum,
        up_sum,
        up_bias_sum,
        down_sum,
        down_bias_sum,
        family_sum,
        orient_sum,
    )


def dot_nn(a, b):
    return lax.dot_general(a, b, (((1,), (0,)), ((), ())), preferred_element_type=F32)


def dot_nt(a, b):
    return lax.dot_general(a, b, (((1,), (1,)), ((), ())), preferred_element_type=F32)


def dot_tn(a, b):
    return lax.dot_general(a, b, (((0,), (0,)), ((), ())), preferred_element_type=F32)


def params(**more):
    return pltpu.CompilerParams(vmem_limit_bytes=VMEM_LIMIT, **more)


def cost(flops, moved, exps=0):
    return pl.CostEstimate(flops=flops, bytes_accessed=moved, transcendentals=exps)


def whole(shape):
    return pl.BlockSpec(shape, lambda *_: (0,) * len(shape), pipeline_mode=pl.Buffered(1))


def table_row(table, wanted):
    rows = lax.broadcasted_iota(jnp.int32, table.shape, 0)
    return jnp.sum(jnp.where(rows == wanted, table[...].astype(F32), 0.0), 0, keepdims=True)


def line(vector):
    return vector[...].astype(F32).reshape(1, -1)


def normalise(entries):
    centred = entries - jnp.mean(entries, -1, keepdims=True)
    inv_std = lax.rsqrt(jnp.mean(centred * centred, -1, keepdims=True) + 1e-05)
    return centred * inv_std, inv_std


GELU_C = math.sqrt(2.0 / math.pi)


def gelu_both(z):
    square = z * z
    half = 0.5 + 0.5 * jnp.tanh(z * (GELU_C + (GELU_C * 0.044715) * square))
    value = z * half
    slope = half + value * (1.0 - half) * (2 * GELU_C + (6 * GELU_C * 0.044715) * square)
    return value, slope


def ffn_kernel(rows, fid, oid, hid, cot, fam, ori, gain, bias, wup, bup, wdn, turned, both, bupg, bdng, norm, shifts):
    tokens = hid.shape[0]
    seg = tokens // rows
    step = 256
    i = pl.program_id(0)
    @pl.when(i == 0)
    def _():
        total = jnp.zeros((1, cot.shape[1]), F32)
        for row in range(rows):
            emb = table_row(fam, fid[0]) + table_row(ori, oid[row])
            for start in range(row * seg, (row + 1) * seg, step):
                part = pl.ds(start, step)
                hat, _ = normalise(hid[part, :].astype(F32) + emb)
                norm[part, :] = (hat * line(gain) + line(bias)).astype(BF16)
                total = total + jnp.sum(cot[part, :].astype(F32), 0, keepdims=True)
        bdng[...] = total
        turned[...] = norm[...].T
        shifts[...] = line(bup)

    width = wup.shape[1]
    total = jnp.zeros((8, width), F32)
    lin = dot_nn(norm[...], wup[...])
    into = dot_nt(cot[...], wdn[...])
    shift = shifts[:, pl.ds(pl.multiple_of(i * width, width), width)]
    step = 64
    for start in range(0, tokens, step):
        part = pl.ds(start, step)
        value, slope = gelu_both(lin[start : start + step] + shift)
        low = into[start : start + step] * slope
        both[0, part, :] = value.astype(BF16)
        both[1, part, :] = low.astype(BF16)
        total = total + jnp.sum(low.reshape(step // 8, 8, width), 0)
    bupg[...] = jnp.sum(total, 0, keepdims=True)


def ffn_forward(fid, oid, hid, cot, fam, ori, gain, bias, wup, bup, wdn, rows):
    tokens, d = hid.shape
    ff = wup.shape[1]
    tile = 512
    smem = pl.BlockSpec(memory_space=pltpu.SMEM)
    return pl.pallas_call(
        functools.partial(ffn_kernel, rows),
        grid=(ff // tile,),
        in_specs=[
            smem,
            smem,
            whole((tokens, d)),
            whole((tokens, d)),
            whole(fam.shape),
            whole(ori.shape),
            whole(gain.shape),
            whole(bias.shape),
            pl.BlockSpec((d, tile), lambda i: (0, i)),
            whole(bup.shape),
            pl.BlockSpec((tile, d), lambda i: (i, 0)),
        ],
        out_specs=[
            whole((d, tokens)),
            pl.BlockSpec((2, tokens, tile), lambda i: (0, 0, i)),
            pl.BlockSpec((1, tile), lambda i: (0, i)),
            whole((1, d)),
        ],
        out_shape=[
            jax.ShapeDtypeStruct((d, tokens), BF16),
            jax.ShapeDtypeStruct((2, tokens, ff), BF16),
            jax.ShapeDtypeStruct((1, ff), F32),
            jax.ShapeDtypeStruct((1, d), F32),
        ],
        scratch_shapes=[
            pltpu.VMEM((tokens, d), BF16),
            pltpu.VMEM((1, ff), F32),
        ],
        compiler_params=params(),
        cost_estimate=cost(4 * tokens * d * ff, 4 * tokens * ff + 4 * d * ff, tokens * ff),
        name="ffn_forward",
    )(fid, oid, hid, cot, fam, ori, gain, bias, wup, bup, wdn)


def turn(entries, cosine, sine):
    even = lax.broadcasted_iota(jnp.int32, entries.shape, 1) % 2 == 0
    other = jnp.where(even, pltpu.roll(entries, 127, 1), pltpu.roll(entries, 1, 1))
    return entries * cosine + other * sine


def turn_back(entries, cosine, sine):
    even = lax.broadcasted_iota(jnp.int32, entries.shape, 1) % 2 == 0
    side = entries * sine
    other = jnp.where(even, pltpu.roll(side, 127, 1), pltpu.roll(side, 1, 1))
    return entries * cosine + other


def attend(head_size, query_ref, k_ref, v_ref, g_ref, cos, sin, o_ref, dq_ref, dk_ref, dv_ref, dkt, dvt):
    full = query_ref.shape[0]
    block = 256
    scale = head_size ** (-0.5)
    first = lax.broadcasted_iota(jnp.int32, (block, 128), 1) < head_size
    below = lax.broadcasted_iota(jnp.int32, (block, block), 0) >= lax.broadcasted_iota(
        jnp.int32, (block, block), 1
    )
    dkt[...] = jnp.zeros_like(dkt)
    dvt[...] = jnp.zeros_like(dvt)

    def by_head(entries):
        none = jnp.zeros_like(entries)
        return jnp.concatenate([jnp.where(first, entries, none), jnp.where(first, none, entries)], 0)

    def front(start):
        part, end = pl.ds(start, block), start + block
        query = by_head((query_ref[part, :].astype(F32) * scale).astype(BF16))
        grad = by_head(g_ref[part, :])
        return query, grad, dot_nt(query, k_ref[0:end, :]), dot_nt(grad, v_ref[0:end, :])

    def back(start, query, grad, scores, into):
        part, end = pl.ds(start, block), start + block
        lows, slopes = [], []
        for head in range(2):
            rows = slice(head * block, (head + 1) * block)
            score = scores[rows]
            last = jnp.where(below, score[:, start:end], -1e30)
            score = last if start == 0 else jnp.concatenate([score[:, :start], last], 1)
            weights = jnp.exp(score - jnp.max(score, -1, keepdims=True))
            probs = weights * (1.0 / jnp.sum(weights, -1, keepdims=True))
            lows.append(probs.astype(BF16))
            inner = jnp.sum(probs * into[rows], -1, keepdims=True)
            slopes.append((probs * (into[rows] - inner)).astype(BF16))
        low = jnp.concatenate(lows, 0)
        slope = jnp.concatenate(slopes, 0)
        out = dot_nn(low, v_ref[0:end, :])
        dq = dot_nn(slope, k_ref[0:end, :])
        o_ref[part, :] = jnp.where(first, out[:block], out[block:]).astype(BF16)
        dq = jnp.where(first, dq[:block], dq[block:]) * scale
        dq_ref[part, :] = turn_back(dq, cos[part, :], sin[part, :]).astype(BF16)
        dkt[:, 0:end] += dot_tn(query, slope)
        dvt[:, 0:end] += dot_tn(grad, low)

    ready = front(0)
    for start in range(0, full, block):
        later = front(start + block) if start + block < full else None
        back(start, *ready)
        ready = later
    for start in range(0, full, block):
        part = pl.ds(start, block)
        dk = dkt[:, start : start + block].T
        dk_ref[part, :] = turn_back(dk, cos[part, :], sin[part, :]).astype(BF16)
        dv_ref[part, :] = dvt[:, start : start + block].T.astype(BF16)


FFN_ORDERS = [
    [2, 1, "seq", 3],
    [1, 2, 3, "seq"],
    [2, 1, "seq", 3],
    [1, "seq", 2, 3],
    [1, "seq", 2, 3],
    [2, 1, "seq", 3],
    [2, 1, "seq", 3],
    ["seq", 2, 1, 3],
]
LATE_ORDERS = [
    [0, 2, 1, 3, "seq"],
    [0, 1, 3, "seq", 2],
    [0, 2, "seq", 3, 1],
    [0, 1, 2, "seq", 3],
]
FFN_EVENTS = {
    4: [(0, 0)],
    6: [(1, 0)],
    8: [(2, 0)],
    9: [(3, 0)],
    14: [(0, 1)],
    15: [(1, 1)],
    17: [(7, 0), (4, 0), (5, 0), (6, 0), (2, 1)],
    20: [(3, 1)],
    21: [(1, 2)],
    23: [(0, 2)],
    26: [(5, 1), (7, 1), (4, 1)],
    27: [(3, 2), (2, 2), (0, 3), (6, 1)],
    28: [(1, 3), (5, 2), (4, 2)],
    29: [(7, 2), (2, 3), (3, 3), (6, 2)],
    30: [(0, 4), (1, 4), (4, 3), (5, 3)],
    31: [(7, 3), (2, 4), (6, 3), (3, 4)],
    32: [(4, 4), (5, 4), (7, 4), (6, 4)],
}
LATE_EVENTS = {
    2: [(0, 1)],
    3: [(1, 1)],
    4: [(2, 1)],
    6: [(0, 2)],
    7: [(3, 1), (1, 2)],
    10: [(0, 3), (2, 2)],
    13: [(3, 2), (1, 3)],
    15: [(2, 3), (0, 4)],
    16: [(1, 4)],
    17: [(3, 3), (0, 5)],
    18: [(2, 4)],
    19: [(1, 5)],
    20: [(3, 4)],
    21: [(2, 5)],
    22: [(3, 5)],
}


def middle_kernel(tiles, pairs, head_size, bits, orders, *refs):
    fid, oid, home_cot, turned, pre, act, fam, ori, gain, bias, wqkv, wout, angles, hid_hbm, cot_hbm = refs[:15]
    norm, cot, o_ref, dq_ref, dk_ref, dv_ref, far_att, up_out, down_out = refs[15:24]
    near_up, far_up, near_down, far_down = refs[24:28]
    heads, dkt, dvt, att_send, att_got, att_sems, cfar, cfar_sems = refs[28:36]
    keep, send, got, send_sem, recv_sem, out_sem = refs[36:42]
    up_keep, up_send, up_got, up_ssem, up_rsem, up_osem = refs[42:48]
    own, cos, sin, own_sem, far, far_sems = refs[48:54]
    seg = far.shape[0]
    step = 256
    base = 1 << (bits - 1)
    now = pl.program_id(0)
    ups = up_out.shape[1] // up_keep.shape[3]
    late = now - ups
    i = late - base
    me = lax.axis_index("seq")
    mine = device_bits(bits)
    parts = len(orders) // 2
    up_part = up_out.shape[1] // parts
    down_part = down_out.shape[1] // parts
    chunks = chunks_from(
        refs[54:],
        bits,
        mine,
        [
            (orders[part], near_up, far_up, pl.ds(part * up_part, up_part), up_out)
            for part in range(parts)
        ]
        + [
            (orders[parts + part], near_down, far_down, pl.ds(part * down_part, down_part), down_out)
            for part in range(parts)
        ],
    )

    def happen(events):
        for chunk, stage in events:
            chunks[chunk].happen(stage)

    @pl.when(now == 0)
    def _():
        meet([partner_along(axis, mine) for axis in [0] + orders[0]])

    cot_crossing = remote(
        cot_hbm.at[pl.ds(pl.multiple_of((1 - me) * seg, seg), seg)],
        cfar,
        cfar_sems.at[0],
        cfar_sems.at[1],
        partner_along("seq", mine),
    )

    far_crossing = remote(
        hid_hbm.at[pl.ds(pl.multiple_of((1 - me) * seg, seg), seg)],
        far,
        far_sems.at[0],
        far_sems.at[1],
        partner_along("seq", mine),
    )
    own_load = pltpu.make_async_copy(hid_hbm.at[pl.ds(pl.multiple_of(me * seg, seg), seg)], own, own_sem)

    @pl.when(now == 0)
    def _():
        far_crossing.start()
        cot_crossing.start()
        own_load.start()

    last = ups + base + 4 * tiles + pairs
    def up_crossing(index):
        slot = lax.rem(index, 2)
        return remote(
            up_send.at[slot], up_got.at[slot], up_ssem.at[slot], up_rsem.at[slot], partner_along(0, mine)
        )

    def up_stores(index):
        slot = lax.rem(index, 2)
        width = up_keep.shape[3]
        columns = pl.ds(pl.multiple_of(index * width, width), width)
        return [
            pltpu.make_async_copy(
                up_keep.at[slot, pl.ds(half * base, base)], there.at[:, :, columns], up_osem.at[half, slot]
            )
            for half, there in enumerate((near_up, far_up))
        ]

    def up_finish(index):
        slot = lax.rem(index, 2)
        up_crossing(index).wait()
        add_into(up_keep.at[slot], up_got.at[slot])
        for copy in up_stores(index):
            copy.start()

    for when, what in FFN_EVENTS.items():
        if when < last:

            @pl.when(now == when)
            def _():
                happen(what)

    per_chunk = ups // parts
    for part in range(parts):
        places = [block_place(orders[part], mine, up, seq) for up in range(base) for seq in range(2)]

        @pl.when((now >= part * per_chunk) & (now < (part + 1) * per_chunk))
        def _():
            value = dot_nn(turned[...], pre[...])
            slot = lax.rem(now, 2)

            @pl.when(now > 0)
            def _():
                up_finish(now - 1)

            @pl.when(now > 1)
            def _():
                for copy in up_stores(now - 2):
                    copy.wait()

            split_blocks(value, up_keep.at[slot], up_send.at[slot], up_keep.shape[2], mine[0], places)
            up_crossing(now).start()

    @pl.when(now == ups)
    def _():
        up_finish(now - 1)
        for index in (now - 2, now - 1):
            for copy in up_stores(index):
                copy.wait()

    def crossing(index):
        slot = lax.rem(index, 2)
        return remote(
            send.at[slot], got.at[slot], send_sem.at[slot], recv_sem.at[slot], partner_along(0, mine)
        )

    def store(index, act_on):
        slot = lax.rem(index, 2)
        width = home_cot.shape[1] // parts
        for seq in range(2):
            for part in range(parts):
                place = 0
                for axis in orders[parts + part]:
                    if axis == "seq":
                        apart = lax.rem(mine["seq"] + seq, 2)
                    else:
                        apart = lax.rem(index // (1 << (axis - 1)) + mine[axis], 2)
                    place = 2 * place + apart
                columns = pl.ds(part * width, width)
                source = keep.at[slot, seq, :, columns]
                sem = out_sem.at[slot, seq, part]
                there = lax.rem(place, base)

                @pl.when(place < base)
                def _():
                    act_on(pltpu.make_async_copy(source, near_down.at[there, :, columns], sem))

                @pl.when(place >= base)
                def _():
                    act_on(pltpu.make_async_copy(source, far_down.at[there, :, columns], sem))

    def finish(index):
        slot = lax.rem(index, 2)
        crossing(index).wait()
        add_into(keep.at[slot], got.at[slot])
        store(index, lambda copy: copy.start())

    @pl.when((late >= 0) & (late < base))
    def _():
        value = dot_nn(act[...].T, home_cot[...])
        slot = lax.rem(late, 2)

        @pl.when(late > 0)
        def _():
            finish(late - 1)

        @pl.when(late > 1)
        def _():
            store(late - 2, lambda copy: copy.wait())

        split_blocks(value, keep.at[slot], send.at[slot], keep.shape[2], mine[0], [0, 1])
        crossing(late).start()

    @pl.when(late == base)
    def _():
        finish(late - 1)
        store(late - 2, lambda copy: copy.wait())
        store(late - 1, lambda copy: copy.wait())

    @pl.when(i == 0)
    def _():
        own_load.wait()
        far_crossing.wait()
        fine = angles.shape[1]
        for coarse in range(2 * seg // fine):
            there = pl.ds(coarse * fine, fine)
            cos_a, sin_a = angles[0, coarse : coarse + 1, :], angles[1, coarse : coarse + 1, :]
            cos[there, :] = cos_a * angles[2] - sin_a * angles[3]
            sin[there, :] = sin_a * angles[2] + cos_a * angles[3]
        emb = table_row(fam, fid[0]) + table_row(ori, oid[me])
        for source, where in ((own, me), (far, 1 - me)):
            for start in range(0, seg, step):
                part = pl.ds(start, step)
                there = pl.ds(pl.multiple_of(where * seg + start, step), step)
                hat, _ = normalise(source[part, :].astype(F32) + emb)
                norm[there, :] = (hat * line(gain) + line(bias)).astype(BF16)
        held = pl.ds(pl.multiple_of(me * seg, seg), seg)
        cot[held, :] = home_cot[held, :]

    lanes = wqkv.shape[1] // 128

    def att_crossing(pair):
        return remote(
            att_send.at[pair],
            att_got.at[pair],
            att_sems.at[0, pair],
            att_sems.at[1, pair],
            partner_along("seq", mine),
        )

    @pl.when((i >= 0) & (i < 2 * tiles))
    def _():
        lin = dot_nn(norm[...], wqkv[...])
        for start in range(0, 2 * seg, step):
            part = pl.ds(start, step)
            for lane in range(lanes):
                piece = lin[start : start + step, lane * 128 : (lane + 1) * 128]
                heads[i * lanes + lane, part, :] = turn(piece, cos[part, :], sin[part, :]).astype(BF16)

    @pl.when((i >= 2 * tiles) & (i < 3 * tiles))
    def _():
        lin = dot_nn(norm[...], wqkv[...]).astype(BF16)
        for lane in range(lanes):
            heads[i * lanes + lane] = lin[:, lane * 128 : (lane + 1) * 128]

    @pl.when(i == 3 * tiles)
    def _():
        cot_crossing.wait()
        cot[pl.ds(pl.multiple_of((1 - me) * seg, seg), seg), :] = cfar[...]

    @pl.when((i >= 3 * tiles) & (i < 4 * tiles))
    def _():
        lin = dot_nt(cot[...], wout[...]).astype(BF16)
        for lane in range(lanes):
            heads[i * lanes + lane] = lin[:, lane * 128 : (lane + 1) * 128]

    @pl.when(i >= 4 * tiles)
    def _():
        pair = i - 4 * tiles
        attend(
            head_size,
            heads.at[pair],
            heads.at[pairs + pair],
            heads.at[2 * pairs + pair],
            heads.at[3 * pairs + pair],
            cos,
            sin,
            o_ref,
            dq_ref,
            dk_ref,
            dv_ref,
            dkt,
            dvt,
        )
        att_send[pair] = o_ref[pl.ds(pl.multiple_of((1 - me) * seg, seg), seg), :]
        att_crossing(pair).start()

    @pl.when(now == last - 1)
    def _():
        for pair in range(pairs):
            att_crossing(pair).wait()
            far_att[:, pair * 128 : (pair + 1) * 128] = att_got[pair]
        happen(FFN_EVENTS[last])


def middle(
    fid, oid, hid, home_cot, turned, both, fam, ori, gain, bias, wqkv, wout, angles, orders, head_size, collective
):
    full, d = hid.shape
    seg = full // 2
    tile = 512
    tiles = d // tile
    pairs = d // 128
    bits = len(orders[0])
    base = 1 << (bits - 1)
    parts = len(orders) // 2
    ff = both.shape[2]
    up_size = d // (4 * base)
    up_tile = 512
    ups = ff // up_tile
    down_tile = ff // base
    down_size = down_tile // 4
    smem = pl.BlockSpec(memory_space=pltpu.SMEM)
    anywhere = pl.BlockSpec(memory_space=pl.ANY)
    late = ups + base
    attend_at = late + 4 * tiles
    head_out = pl.BlockSpec((full, 128), lambda i: (0, jnp.maximum(i - attend_at, 0)))
    rows = jax.ShapeDtypeStruct((full, d), BF16)
    down = jax.ShapeDtypeStruct((base, down_size, d), BF16)
    up = jax.ShapeDtypeStruct((base, up_size, ff), BF16)
    slots = pltpu.VMEM((2, 2, down_size, d), BF16)
    up_slots = pltpu.VMEM((2, 2 * base, up_size, up_tile), BF16)
    return pl.pallas_call(
        functools.partial(middle_kernel, tiles, pairs, head_size, bits, orders),
        grid=(attend_at + pairs,),
        in_specs=[
            smem,
            smem,
            whole((full, d)),
            whole((d, full)),
            pl.BlockSpec((None, full, up_tile), lambda i: (1, 0, jnp.minimum(i, ups - 1))),
            pl.BlockSpec((None, full, down_tile), lambda i: (0, 0, jnp.clip(i - ups, 0, base - 1))),
            whole(fam.shape),
            whole(ori.shape),
            whole(gain.shape),
            whole(bias.shape),
            pl.BlockSpec((d, tile), lambda i: (0, jnp.clip(i - late, 0, 3 * tiles - 1))),
            pl.BlockSpec((tile, d), lambda i: (jnp.clip(i - late - 3 * tiles, 0, tiles - 1), 0)),
            whole(angles.shape),
        ]
        + [anywhere] * 2,
        out_specs=[
            whole((full, d)),
            whole((full, d)),
            head_out,
            head_out,
            head_out,
            head_out,
            whole((seg, d)),
            whole((up_size, ff)),
            whole((down_size, d)),
            anywhere,
            anywhere,
            anywhere,
            anywhere,
        ],
        out_shape=[
            rows,
            rows,
            rows,
            rows,
            rows,
            rows,
            jax.ShapeDtypeStruct((seg, d), BF16),
            jax.ShapeDtypeStruct((up_size, ff), F32),
            jax.ShapeDtypeStruct((down_size, d), F32),
            up,
            up,
            down,
            down,
        ],
        scratch_shapes=[
            pltpu.VMEM((4 * pairs, full, 128), BF16),
            pltpu.VMEM((128, full), F32),
            pltpu.VMEM((128, full), F32),
            pltpu.VMEM((pairs, seg, 128), BF16),
            pltpu.VMEM((pairs, seg, 128), BF16),
            pltpu.SemaphoreType.DMA((2, pairs)),
            pltpu.VMEM((seg, d), BF16),
            pltpu.SemaphoreType.DMA((2,)),
            slots,
            slots,
            slots,
            pltpu.SemaphoreType.DMA((2,)),
            pltpu.SemaphoreType.DMA((2,)),
            pltpu.SemaphoreType.DMA((2, 2, parts)),
            up_slots,
            up_slots,
            up_slots,
            pltpu.SemaphoreType.DMA((2,)),
            pltpu.SemaphoreType.DMA((2,)),
            pltpu.SemaphoreType.DMA((2, 2)),
            pltpu.VMEM((seg, d), BF16),
            pltpu.VMEM((full, 128), F32),
            pltpu.VMEM((full, 128), F32),
            pltpu.SemaphoreType.DMA,
            pltpu.VMEM((seg, d), BF16),
            pltpu.SemaphoreType.DMA((2,)),
        ]
        + [
            entry
            for index, axes in enumerate(orders)
            for entry in chunk_scratch(
                axes, *((up_size, ff // parts) if index < parts else (down_size, d // parts))
            )
        ],
        compiler_params=pltpu.CompilerParams(
            vmem_limit_bytes=67043328, collective_id=collective, has_side_effects=True
        ),
        cost_estimate=cost(16 * full * d * d + 12 * full * full * d, 8 * d * d + 18 * full * d, full * full * H),
        name="middle",
    )(fid, oid, home_cot, turned, both, both, fam, ori, gain, bias, wqkv, wout, angles, hid, home_cot)


def device_bits(bits):
    dp = lax.axis_index("dp")
    found = {bit: lax.rem(dp // (1 << bit), 2) for bit in range(bits)}
    found["seq"] = lax.axis_index("seq")
    return found


def block_place(axes, mine, upper, seq):
    place = 0
    for axis in axes:
        bit = seq if axis == "seq" else (upper >> (axis - 1)) & 1
        place = 2 * place + (1 - mine[axis] if bit else mine[axis])
    return place


def other_core():
    dp = lax.axis_index("dp")
    return (dp + 1 - 2 * lax.rem(dp, 2), lax.axis_index("seq"))


def meet(partners):
    barrier = pltpu.get_barrier_semaphore()
    for partner in partners:
        pl.semaphore_signal(barrier, inc=1, device_id=partner, device_id_type=MESH)
    pl.semaphore_wait(barrier, len(partners))


def remote(src, dst, send_sem, recv_sem, partner):
    return pltpu.make_async_remote_copy(
        src_ref=src,
        dst_ref=dst,
        send_sem=send_sem,
        recv_sem=recv_sem,
        device_id=partner,
        device_id_type=MESH,
    )


def split_blocks(value, keep, send, size, core, places):
    for index, there in enumerate(places):
        up, seq = index // 2, index % 2
        first = (4 * up + seq) * size
        second = first + 2 * size
        a = value[first : first + size, :].astype(BF16)
        b = value[second : second + size, :].astype(BF16)
        keep[there] = jnp.where(core == 0, a, b)
        send[there] = jnp.where(core == 0, b, a)


def add_into(keep, got):
    def add(index, carry):
        keep[index] = (keep[index].astype(F32) + got[index].astype(F32)).astype(BF16)
        return carry

    lax.fori_loop(0, got.shape[0], add, 0, unroll=2 if got.shape[0] > 1 else 1)


def partner_along(axis, mine):
    dp = lax.axis_index("dp")
    seq = lax.axis_index("seq")
    if axis == "seq":
        return (dp, 1 - seq)
    return (dp + (1 - 2 * mine[axis]) * (1 << axis), seq)


class Chunk:
    def __init__(self, axes, mine, near, far, columns, out, keep, got, near_sem, send_sem, recv_sem):
        self.axes, self.mine, self.near, self.far = axes, mine, near, far
        self.columns, self.out, self.keep, self.got = columns, out, keep, got
        self.near_sem, self.send_sem, self.recv_sem = near_sem, send_sem, recv_sem

    def load(self):
        return pltpu.make_async_copy(self.near.at[:, :, self.columns], self.keep, self.near_sem)

    def crossing(self, stage):
        count = (1 << len(self.axes)) >> (stage + 1)
        if stage == 0 and self.far is not None:
            source = self.far.at[:, :, self.columns]
        else:
            source = self.keep.at[pl.ds(count, count)]
        return remote(
            source,
            self.got[stage],
            self.send_sem.at[stage],
            self.recv_sem.at[stage],
            partner_along(self.axes[stage], self.mine),
        )

    def begin(self):
        if self.near is not None:
            self.load().start()
        self.crossing(0).start()

    def advance(self, stage):
        if stage == 1 and self.near is not None:
            self.load().wait()
        self.crossing(stage - 1).wait()
        add_into(self.keep, self.got[stage - 1])
        self.crossing(stage).start()

    def finish(self):
        last = len(self.axes) - 1
        self.crossing(last).wait()
        self.out[:, self.columns] = self.keep[0].astype(F32) + self.got[last][0].astype(F32)

    def happen(self, stage):
        if stage == 0:
            self.begin()
        elif stage == len(self.axes):
            self.finish()
        else:
            self.advance(stage)


def chunk_scratch(axes, size, width, farther=False):
    half = 1 << (len(axes) - 1)
    return (
        [pltpu.VMEM((2 * half if farther else half, size, width), BF16)]
        + [pltpu.VMEM((half >> stage, size, width), BF16) for stage in range(len(axes))]
        + [
            pltpu.SemaphoreType.DMA,
            pltpu.SemaphoreType.DMA((len(axes),)),
            pltpu.SemaphoreType.DMA((len(axes),)),
        ]
    )


def chunks_from(refs, bits, mine, wanted):
    stages = bits
    found = []
    each = 1 + stages + 3
    for index, (axes, near, far, columns, out) in enumerate(wanted):
        part = refs[index * each : (index + 1) * each]
        found.append(
            Chunk(axes, mine, near, far, columns, out, part[0], part[1 : 1 + stages], *part[1 + stages :])
        )
    return found


def after(entry, *others):
    return lax.optimization_barrier((entry, *others))[0]


TAIL_TILE = 1024
TAIL_STEP = 256


def tail_kernel(bits, orders, rows, marks, *refs):
    fid, oid, norm_hbm, att_hbm, cot_hbm, dq_hbm, dk_hbm, dv_hbm, wqkv_hbm, wout_hbm = refs[:10]
    fam, ori, gain, bdn, bup_part, bdn_part, far_att = refs[10:17]
    both, wdn, wup, hid, cot = refs[17:22]
    layer_out, input_out, qkv_out, out_out, sums_out, all_out = refs[22:28]
    left, dq, dk, dv, wqkv, wout, turned, acc, ng_here, ng_got = refs[28:38]
    gg, bg, rg, load_sem, ng_sem, held, got, vec, vgot, table, ssem, rsem, gsend, grecv = refs[38:52]
    in_start, in_end, out_start, out_end, last = marks
    i = pl.program_id(0)
    me = lax.axis_index("seq")
    dp = lax.axis_index("dp")
    mine = device_bits(bits)
    d = left.shape[1]
    seg = ng_got.shape[0]
    step = TAIL_STEP
    per_row = seg // step
    chunks = chunks_from(
        refs[52:],
        len(orders[0]),
        mine,
        [
            (orders[0], None, None, pl.ds(0, d), qkv_out),
            (orders[1], None, None, pl.ds(d, d), qkv_out),
            (orders[2], None, None, pl.ds(2 * d, d), qkv_out),
            (orders[3], None, None, pl.ds(0, d), out_out),
        ],
    )
    loads = {
        name: pltpu.make_async_copy(source, there, load_sem.at[index])
        for index, (name, source, there) in enumerate(
            (
                ("norm", norm_hbm, left),
                ("dq", dq_hbm, dq),
                ("dk", dk_hbm, dk),
                ("dv", dv_hbm, dv),
                ("wqkv", wqkv_hbm, wqkv),
                ("cot", cot_hbm, dq),
                ("wout", wout_hbm, wout),
                ("att", att_hbm, left),
            )
        )
    }
    partners = [partner_along(axis, mine) for axis in ["seq"] + list(range(bits))]

    def gradient(index, operand):
        chunk = chunks[index]
        size = chunk.keep.shape[1]
        value = dot_nn(turned[...], operand[...])
        for block in range(chunk.keep.shape[0]):
            place = 0
            for axis in orders[index]:
                bit = block & 1 if axis == "seq" else (block >> (axis + 1)) & 1
                place = 2 * place + (1 - mine[axis] if bit else mine[axis])
            chunk.keep[place] = value[block * size : (block + 1) * size, :].astype(BF16)
        chunk.begin()

    ng_crossing = remote(ng_here.at[0], ng_got, ng_sem.at[0], ng_sem.at[1], partners[0])

    @pl.when(i == 0)
    def _():
        loads["norm"].start()
        loads["dq"].start()
        meet(partners)
        loads["norm"].wait()
        turned[...] = left[...].T
        loads["dq"].wait()
        for name in ("dk", "dv", "wqkv", "att", "wout"):
            loads[name].start()
        gradient(0, dq)

    def sums_main(index):
        return remote(held.at[index], got.at[index], ssem.at[index], rsem.at[index], partners[index])

    def sums_side(index):
        if index == 0:
            return remote(vec, vgot, gsend.at[0], grecv.at[0], partners[0])
        size = 1 << (index - 1)
        now = pl.ds(dp - lax.rem(dp, size), size)
        return remote(table.at[now], table.at[now], gsend.at[index], grecv.at[index], partners[index])

    @pl.when(i == out_start)
    def _():
        at = 0
        for source in (bup_part[...], bdn_part[...], gg[...], bg[...], rg[0:1, :], rg[1:2, :]):
            for lane in range(0, source.shape[1], 128):
                held[0, at : at + 1, :] = source[:, lane : lane + 128]
                at += 1
        both_rows = rg[0:1, :] + rg[1:2, :]
        for lane in range(0, d, 128):
            vec[lane // 128 : lane // 128 + 1, :] = both_rows[:, lane : lane + 128]
        extra = d // 128
        vec[extra:, :] = jnp.full((vec.shape[0] - extra, 128), 0.5, F32) * fid[0].astype(F32)
        sums_main(0).start()
        sums_side(0).start()

    for index in range(len(partners)):

        @pl.when(i == out_start + (index + 1 if index < len(partners) - 1 else last - 1 - out_start))
        def _():
            sums_main(index).wait()
            sums_side(index).wait()
            total = held[index] + got[index]
            if index == 0:
                table[dp] = vec[...] + vgot[...]
            if index + 1 < len(partners):
                held[index + 1] = total
                sums_main(index + 1).start()
                sums_side(index + 1).start()
            else:
                sums_out[...] = total
                all_out[...] = table[...]

    for when, what in LATE_EVENTS.items():
        if when < last:

            @pl.when(i == when)
            def _():
                for chunk, stage in what:
                    chunks[chunk].happen(stage)

    @pl.when(i == 1)
    def _():
        loads["dk"].wait()
        gradient(1, dk)

    @pl.when(i == 2)
    def _():
        loads["dv"].wait()
        gradient(2, dv)

    @pl.when(i == 3)
    def _():
        loads["wqkv"].wait()

    @pl.when((i == 3) | (i == 4))
    def _():
        first = 4 - i
        half = first * (1 - me) + (1 - first) * me
        part = pl.ds(pl.multiple_of(half * seg, seg), seg)
        total = dot_nt(dq[part, :], wqkv[:, 0:d])
        total = total + dot_nt(dk[part, :], wqkv[:, d : 2 * d])
        total = total + dot_nt(dv[part, :], wqkv[:, 2 * d : 3 * d])
        ng_here[1 - first] = total.astype(BF16)

    @pl.when(i == 3)
    def _():
        ng_crossing.start()

    @pl.when(i == 5)
    def _():
        loads["cot"].start()
        loads["att"].wait()
        turned[...] = left[...].T
        loads["cot"].wait()
        gradient(3, dq)

    @pl.when((i >= out_start) & (i < out_end))
    def _():
        value = dot_nn(both[0], wdn[...])

        @pl.when(i == out_start)
        def _():
            acc[...] = value

        @pl.when(i > out_start)
        def _():
            acc[...] += value

    @pl.when((i >= in_start) & (i < in_end))
    def _():
        value = dot_nt(both[0], wup[...])

        @pl.when(i == in_start)
        def _():
            acc[...] = value

        @pl.when(i > in_start)
        def _():
            acc[...] += value

    @pl.when(i == out_end)
    def _():
        loads["wout"].wait()

    def home_block(index, own, far, own_offset):
        row = index // per_row
        within = pl.multiple_of(lax.rem(index, per_row) * step, step)
        there = pl.ds(pl.multiple_of(own_offset + within, step), step)
        return row, jnp.where(row == me, own[there, :], far[pl.ds(within, step), :])

    @pl.when(i >= out_end)
    def _():
        index = i - out_end
        row, att = home_block(index, left, far_att, me * seg)
        flag = oid[row]
        emb = table_row(fam, fid[0]) + table_row(ori, flag)
        part = pl.ds(pl.multiple_of(index * step, step), step)
        total = hid[...].astype(F32) + emb + dot_nn(att, wout[...])
        layer_out[...] = (total + (acc[part, :] + line(bdn))).astype(BF16)

    @pl.when(i == in_end)
    def _():
        ng_crossing.wait()
        gg[...] = jnp.zeros_like(gg)
        bg[...] = jnp.zeros_like(bg)
        rg[...] = jnp.zeros_like(rg)

    @pl.when((i >= in_end) & (i < out_start))
    def _():
        index = i - in_end
        row, back = home_block(index, ng_here.at[1], ng_got, 0)
        flag = oid[row]
        emb = table_row(fam, fid[0]) + table_row(ori, flag)
        part = pl.ds(pl.multiple_of(index * step, step), step)
        hat, inv_std = normalise(hid[...].astype(F32) + emb)
        grad = acc[part, :] + back.astype(F32)
        gg[...] += jnp.sum(grad * hat, 0, keepdims=True)
        bg[...] += jnp.sum(grad, 0, keepdims=True)
        scaled = grad * line(gain)
        inner = (
            scaled
            - jnp.mean(scaled, -1, keepdims=True)
            - hat * jnp.mean(scaled * hat, -1, keepdims=True)
        )
        result = cot[...].astype(F32) + inv_std * inner
        input_out[...] = result
        sums = jnp.sum(result, 0, keepdims=True)
        which = lax.broadcasted_iota(jnp.int32, rg.shape, 0)
        rg[...] += jnp.where(which == flag, sums, 0.0)

    @pl.when(i == last - 1)
    def _():
        for chunk, stage in LATE_EVENTS[last]:
            chunks[chunk].happen(stage)


def tail(fid, oid, norm, att, row_cot, dq, dk, dv, wqkv, wout, fam, ori, gain, bdn, bup_part, bdn_part, far_att, both, wdn, wup, hid, cot, orders, rows, collective):
    tokens, d = hid.shape
    ff = wup.shape[1]
    bits = len(orders[0]) - 1
    count = 1 << bits
    seg = far_att.shape[0]
    tile, step = TAIL_TILE, TAIL_STEP
    tiles, blocks = ff // tile, tokens // step
    in_start = 6
    in_end = in_start + tiles
    out_start = in_end + blocks
    out_end = out_start + tiles
    last = out_end + blocks
    marks = (in_start, in_end, out_start, out_end, last)
    size = d // (2 * count)
    rounds = bits + 1
    lines = (ff + 5 * d) // 128
    vec_shape = (d // 128 + 8, 128)
    anywhere = pl.BlockSpec(memory_space=pl.ANY)

    def plane(i):
        late = i >= out_start
        return (jnp.where(late, 0, 1), 0, jnp.clip(jnp.where(late, i - out_start, i - in_start), 0, tiles - 1))

    def home(i):
        return (jnp.clip(jnp.where(i >= out_start, i - out_end, i - in_end), 0, blocks - 1), 0)

    square = pltpu.VMEM((tokens, d), BF16)
    piece = pltpu.VMEM((seg, d), BF16)
    row = pltpu.VMEM((1, d), F32)
    return pl.pallas_call(
        functools.partial(tail_kernel, bits, orders, rows, marks),
        grid=(last,),
        in_specs=[pl.BlockSpec(memory_space=pltpu.SMEM)] * 2
        + [anywhere] * 8
        + [
            whole(fam.shape),
            whole(ori.shape),
            whole(gain.shape),
            whole(bdn.shape),
            whole((1, ff)),
            whole((1, d)),
            whole((seg, d)),
            pl.BlockSpec((1, tokens, tile), plane),
            pl.BlockSpec((tile, d), lambda i: (jnp.clip(i - out_start, 0, tiles - 1), 0)),
            pl.BlockSpec((d, tile), lambda i: (0, jnp.clip(i - in_start, 0, tiles - 1))),
            pl.BlockSpec((step, d), home),
            pl.BlockSpec((step, d), lambda i: (jnp.clip(i - in_end, 0, blocks - 1), 0)),
        ],
        out_specs=[
            pl.BlockSpec((step, d), lambda i: (jnp.clip(i - out_end, 0, blocks - 1), 0)),
            pl.BlockSpec((step, d), lambda i: (jnp.clip(i - in_end, 0, blocks - 1), 0)),
            whole((size, 3 * d)),
            whole((size, d)),
            whole((lines, 128)),
            whole((count,) + vec_shape),
        ],
        out_shape=[
            jax.ShapeDtypeStruct((tokens, d), BF16),
            jax.ShapeDtypeStruct((tokens, d), F32),
            jax.ShapeDtypeStruct((size, 3 * d), F32),
            jax.ShapeDtypeStruct((size, d), F32),
            jax.ShapeDtypeStruct((lines, 128), F32),
            jax.ShapeDtypeStruct((count,) + vec_shape, F32),
        ],
        scratch_shapes=[
            square,
            square,
            square,
            square,
            pltpu.VMEM((d, 3 * d), BF16),
            pltpu.VMEM((d, d), BF16),
            pltpu.VMEM((d, tokens), BF16),
            pltpu.VMEM((tokens, d), F32),
            pltpu.VMEM((2, seg, d), BF16),
            piece,
            row,
            row,
            pltpu.VMEM((2, d), F32),
            pltpu.SemaphoreType.DMA((8,)),
            pltpu.SemaphoreType.DMA((2,)),
            pltpu.VMEM((rounds, lines, 128), F32),
            pltpu.VMEM((rounds, lines, 128), F32),
            pltpu.VMEM(vec_shape, F32),
            pltpu.VMEM(vec_shape, F32),
            pltpu.VMEM((count,) + vec_shape, F32),
            pltpu.SemaphoreType.DMA((rounds,)),
            pltpu.SemaphoreType.DMA((rounds,)),
            pltpu.SemaphoreType.DMA((rounds,)),
            pltpu.SemaphoreType.DMA((rounds,)),
        ]
        + [entry for axes in orders for entry in chunk_scratch(axes, size, d, True)],
        compiler_params=pltpu.CompilerParams(
            vmem_limit_bytes=67043328, collective_id=collective, has_side_effects=True
        ),
        cost_estimate=cost(16 * tokens * d * d + 4 * tokens * d * ff, 8 * d * ff + 40 * tokens * d),
        name="tail",
    )(fid, oid, norm, att, row_cot, dq, dk, dv, wqkv, wout, fam, ori, gain, bdn, bup_part, bdn_part, far_att, both, wdn, wup, hid, cot)


def finish_kernel(ff, layer, inputs, qkv, out, up, down, sums, table, *outs):
    layer_out, input_out, qkv_out, out_out, up_out, down_out, bup, bdn, gain, bias, fam_out, ori_out = outs
    layer_out[...] = layer[...]
    input_out[...] = inputs[...]
    qkv_out[...] = qkv[...]
    out_out[...] = out[...]
    up_out[...] = up[...]
    down_out[...] = down[...]

    @pl.when(pl.program_id(0) == 0)
    def _():
        d = gain.shape[1]
        at = 0
        for there in (bup, bdn, gain, bias, ori_out.at[0:1], ori_out.at[1:2]):
            for lane in range(0, there.shape[1], 128):
                there[:, lane : lane + 128] = sums[at : at + 1, :]
                at += 1
        extra = d // 128
        rows = lax.broadcasted_iota(jnp.int32, (fam_out.shape[0], 128), 0).astype(F32)
        for lane in range(extra):
            total = jnp.zeros((fam_out.shape[0], 128), F32)
            for index in range(table.shape[0]):
                total = total + jnp.where(
                    rows == table[index, extra : extra + 1, :], table[index, lane : lane + 1, :], 0.0
                )
            fam_out[:, lane * 128 : (lane + 1) * 128] = total


def finish(layer, inputs, qkv, out, up, down, sums, table, families):
    tokens, d = layer.shape
    ff = up.shape[1]
    steps = 4

    def rows(entry):
        count = max(entry.shape[0] // steps, 8)
        each = steps * count // entry.shape[0]
        return pl.BlockSpec((count, entry.shape[1]), lambda i: (i // each, 0))

    big = [layer, inputs, qkv, out, up, down]
    small = [(1, ff), (1, d), (1, d), (1, d), (families, d), (2, d)]
    return pl.pallas_call(
        functools.partial(finish_kernel, ff),
        grid=(steps,),
        in_specs=[rows(entry) for entry in big] + [whole(sums.shape), whole(table.shape)],
        out_specs=[rows(entry) for entry in big] + [whole(shape) for shape in small],
        out_shape=[jax.ShapeDtypeStruct(entry.shape, entry.dtype) for entry in big]
        + [jax.ShapeDtypeStruct(shape, F32) for shape in small],
        compiler_params=params(),
        name="finish",
    )(*big, sums, table)


def body_by_rows(
    hidden_in,
    family,
    orient,
    norm_gain,
    norm_bias,
    qkv_weight,
    out_weight,
    up_weight,
    up_bias,
    down_weight,
    down_bias,
    family_table,
    orient_table,
    cotangent,
):
    rows, seg, d = hidden_in.shape
    ff = up_weight.shape[1]
    tokens = rows * seg
    full = 2 * seg
    dp_count = lax.axis_size("dp")
    bits = int(math.log2(dp_count))
    upper = dp_count // 2
    dp = lax.axis_index("dp")
    seq = lax.axis_index("seq")
    hid = hidden_in.reshape(tokens, d)
    cot = cotangent.reshape(tokens, d)
    turned, both, up_bias_part, down_bias_part = ffn_forward(
        family, orient, hid, cot, family_table, orient_table, norm_gain, norm_bias, up_weight, up_bias, down_weight, rows
    )
    fine = 32
    positions = jnp.concatenate([fine * jnp.arange(full // fine), jnp.arange(fine)]).astype(F32)
    cosine, sine = rope_tables(positions, 128)
    coarse = full // fine
    angles = jnp.stack([cosine[:coarse], sine[:coarse], cosine[coarse:], sine[coarse:]])
    row_normed, row_cot, att, dq, dk, dv, far_att, up_total, down_total, *_ = middle(
        family,
        orient,
        hid,
        cot,
        turned,
        both,
        family_table,
        orient_table,
        norm_gain,
        norm_bias,
        qkv_weight,
        out_weight,
        angles,
        FFN_ORDERS,
        d // H,
        3,
    )
    layer_out, input_grad, qkv_total, out_total, sums, gathered = tail(
        family,
        orient,
        row_normed,
        att,
        row_cot,
        dq,
        dk,
        dv,
        qkv_weight,
        out_weight,
        family_table,
        orient_table,
        norm_gain,
        down_bias,
        up_bias_part,
        down_bias_part,
        far_att,
        both,
        down_weight,
        up_weight,
        hid,
        cot,
        LATE_ORDERS,
        rows,
        4,
    )
    layer_out, input_grad, qkv_sum, out_sum, up_sum, down_sum, *small = finish(
        layer_out, input_grad, qkv_total, out_total, up_total, down_total, sums, gathered, family_table.shape[0]
    )
    up_bias_sum, down_bias_sum, gain_sum, bias_sum = (part.reshape(-1) for part in small[:4])
    return (
        layer_out.reshape(rows, seg, d),
        input_grad.reshape(rows, seg, d),
        gain_sum,
        bias_sum,
        qkv_sum,
        out_sum,
        up_sum,
        up_bias_sum,
        down_sum,
        down_bias_sum,
        small[4],
        small[5],
    )


def body(*args):
    hidden_in = args[0]
    dp_count = lax.axis_size("dp")
    two_rows = lax.axis_size("seq") == 2 and hidden_in.shape[0] == 2
    if two_rows and dp_count == 16 and hidden_in.shape[1] == 512:
        return body_by_rows(*args)
    return body_by_heads(*args)


def solution(mesh):
    return jax.shard_map(
        body,
        mesh=mesh,
        in_specs=(
            P("dp", "seq", None),
            P("dp"),
            P("dp"),
            P(),
            P(),
            P(),
            P(),
            P(),
            P(),
            P(),
            P(),
            P(),
            P(),
            P("dp", "seq", None),
        ),
        out_specs=(
            P("dp", "seq", None),
            P("dp", "seq", None),
            P(),
            P(),
            P(("dp", "seq"), None),
            P(("dp", "seq"), None),
            P(("dp", "seq"), None),
            P(),
            P(("dp", "seq"), None),
            P(),
            P(),
            P(),
        ),
        check_vma=False,
    )
```

```python
import functools
import math

import jax
import jax.numpy as jnp
from jax import lax
from jax.experimental import pallas as pl
from jax.experimental.pallas import tpu as pltpu
from jax.sharding import PartitionSpec as P

H = 16
HD = 64
ROT = 32
MESH = pl.DeviceIdType.MESH
VMEM_LIMIT = 60 * 1024 * 1024
F32 = jnp.float32
BF16 = jnp.bfloat16


def for_sending(shard):

    def short(part):
        return part.astype(jnp.bfloat16) if part.dtype == jnp.float32 else part

    return jax.tree.map(short, shard)


def rope_tables(positions, features):
    column = jnp.arange(features, dtype=jnp.int32)
    within = column % HD
    frequency = jnp.exp(-(2.0 * (within // 2).astype(jnp.float32) / ROT) * math.log(10000.0))
    angles = positions[:, None] * frequency[None, :]
    rotary = within < ROT
    cosine = jnp.where(rotary[None, :], jnp.cos(angles), 1.0)
    sign_term = jnp.where(within % 2 == 0, -1.0, 1.0)
    sine_term = jnp.where(rotary[None, :], sign_term[None, :] * jnp.sin(angles), 0.0)
    return (cosine, sine_term)


def pair_swap(values):
    even_cols = jnp.arange(values.shape[-1]) % 2 == 0
    return jnp.where(even_cols, jnp.roll(values, -1, axis=-1), jnp.roll(values, 1, axis=-1))


def rotate(values, cosine, sine_term):
    return values * cosine + pair_swap(values) * sine_term


def rotate_back(values, cosine, sine_term):
    return values * cosine + pair_swap(values * sine_term)


def gelu_tanh(pre_values):
    return jax.nn.gelu(pre_values, approximate=True)


def body_by_heads(
    hidden_in,
    family,
    orient,
    norm_gain,
    norm_bias,
    qkv_weight,
    out_weight,
    up_weight,
    up_bias,
    down_weight,
    down_bias,
    family_table,
    orient_table,
    cotangent,
):
    seq_count = lax.axis_size("seq")
    row_count, seg_length, features = hidden_in.shape
    full_length = seg_length * seq_count
    local_heads = H // seq_count
    head_size = features // H
    slab_width = features // seq_count
    block_rows = min(512, full_length)
    block_count = full_length // block_rows
    score_scale = head_size ** (-0.5)
    token_count = row_count * seg_length
    family_rows = jnp.repeat(family, 2)
    family_hot = (family_rows[:, None] == jnp.arange(family_table.shape[0])[None, :]).astype(
        jnp.bfloat16
    )
    orient_hot = (orient[:, None] == jnp.arange(2)[None, :]).astype(jnp.bfloat16)
    embedding = jnp.dot(family_hot, family_table, preferred_element_type=jnp.float32) + jnp.dot(
        orient_hot, orient_table, preferred_element_type=jnp.float32
    )
    embedded = (hidden_in.astype(jnp.float32) + embedding[:, None, :]).reshape(
        token_count, features
    )
    row_mean = jnp.mean(embedded, -1, keepdims=True)
    centred = embedded - row_mean
    row_var = jnp.mean(centred * centred, -1, keepdims=True)
    inv_std = lax.rsqrt(row_var + 1e-05)
    normed_hat = centred * inv_std
    gain_f32 = norm_gain.astype(jnp.float32)
    normed_low = (normed_hat * gain_f32 + norm_bias.astype(jnp.float32)).astype(jnp.bfloat16)
    projected = jnp.dot(normed_low, qkv_weight, preferred_element_type=jnp.float32).reshape(
        row_count, seg_length, 3 * features
    )
    positions = (lax.axis_index("seq") * seg_length + jnp.arange(seg_length)).astype(jnp.float32)
    cosine, sine_term = rope_tables(positions, features)
    queries = rotate(projected[..., :features], cosine, sine_term).astype(jnp.bfloat16)
    keys_rot = rotate(projected[..., features : 2 * features], cosine, sine_term).astype(
        jnp.bfloat16
    )
    values = projected[..., 2 * features :].astype(jnp.bfloat16)
    query_heads, key_heads, value_heads = (
        lax.all_to_all(queries, "seq", split_axis=2, concat_axis=1, tiled=True),
        lax.all_to_all(keys_rot, "seq", split_axis=2, concat_axis=1, tiled=True),
        lax.all_to_all(values, "seq", split_axis=2, concat_axis=1, tiled=True),
    )

    def scores_for(query_block, key_rows, block_start):
        logits = (
            jnp.einsum("qhd,khd->hqk", query_block, key_rows, preferred_element_type=jnp.float32)
            * score_scale
        )
        causal = (block_start + jnp.arange(block_rows))[:, None] >= jnp.arange(full_length)[None, :]
        return jnp.where(causal[None], logits, -1e30)

    def attend(row_args):
        query_row, key_row, value_row = row_args
        key_rows = key_row.reshape(full_length, local_heads, head_size)
        value_rows = value_row.reshape(full_length, local_heads, head_size)
        pieces = []
        log_parts = []
        for block_index in range(block_count):
            block_start = block_index * block_rows
            query_block = query_row[block_start : block_start + block_rows].reshape(
                block_rows, local_heads, head_size
            )
            logits = scores_for(query_block, key_rows, block_start)
            row_peak = jnp.max(logits, -1, keepdims=True)
            weights = jnp.exp(logits - row_peak)
            row_total = jnp.sum(weights, -1, keepdims=True)
            prob_low = (weights / row_total).astype(jnp.bfloat16)
            output_block = jnp.einsum(
                "hqk,khd->qhd", prob_low, value_rows, preferred_element_type=jnp.float32
            )
            pieces.append(output_block.reshape(block_rows, slab_width).astype(jnp.bfloat16))
            log_parts.append((row_peak + jnp.log(row_total))[..., 0])
        return (jnp.concatenate(pieces, 0), jnp.concatenate(log_parts, 1))

    attended_heads, log_sums = lax.map(attend, (query_heads, key_heads, value_heads))
    attended = jax.tree.map(
        lambda part, own: part.astype(own.dtype),
        lax.all_to_all(for_sending(attended_heads), "seq", split_axis=1, concat_axis=2, tiled=True),
        attended_heads,
    )
    attended_flat = attended.reshape(token_count, features)
    branch_attn = jnp.dot(attended_flat, out_weight, preferred_element_type=jnp.float32)
    up_pre = jnp.dot(normed_low, up_weight, preferred_element_type=jnp.float32) + up_bias.astype(
        jnp.float32
    )
    up_act = gelu_tanh(up_pre).astype(jnp.bfloat16)
    branch_feed = jnp.dot(
        up_act, down_weight, preferred_element_type=jnp.float32
    ) + down_bias.astype(jnp.float32)
    layer_out = (
        (embedded + branch_attn + branch_feed)
        .astype(jnp.bfloat16)
        .reshape(row_count, seg_length, features)
    )
    grad_low = cotangent.reshape(token_count, features)
    grad_f32 = grad_low.astype(jnp.float32)
    down_grad = jnp.einsum("nf,nd->fd", up_act, grad_low, preferred_element_type=jnp.float32)
    down_bias_grad = jnp.sum(grad_f32, 0)
    act_grad = jnp.einsum("nd,fd->nf", grad_low, down_weight, preferred_element_type=jnp.float32)
    gelu_out, gelu_pull = jax.vjp(gelu_tanh, up_pre)
    pre_grad = gelu_pull(act_grad)[0].astype(jnp.bfloat16)
    up_bias_grad = jnp.sum(pre_grad.astype(jnp.float32), 0)
    up_grad = jnp.einsum("nd,nf->df", normed_low, pre_grad, preferred_element_type=jnp.float32)
    normed_grad = jnp.einsum("nf,df->nd", pre_grad, up_weight, preferred_element_type=jnp.float32)
    out_grad = jnp.einsum("nd,ne->de", attended_flat, grad_low, preferred_element_type=jnp.float32)
    attended_grad = jnp.einsum(
        "ne,de->nd", grad_low, out_weight, preferred_element_type=jnp.float32
    )
    attended_grad = attended_grad.astype(jnp.bfloat16).reshape(row_count, seg_length, features)
    grad_heads = lax.all_to_all(attended_grad, "seq", split_axis=2, concat_axis=1, tiled=True)

    def attend_back(row_args):
        query_row, key_row, value_row, grad_row, log_row = row_args
        key_rows = key_row.reshape(full_length, local_heads, head_size)
        value_rows = value_row.reshape(full_length, local_heads, head_size)
        keys_total = jnp.zeros((full_length, local_heads, head_size), jnp.float32)
        values_total = jnp.zeros((full_length, local_heads, head_size), jnp.float32)
        query_parts = []
        for block_index in range(block_count):
            block_start = block_index * block_rows
            query_block = query_row[block_start : block_start + block_rows].reshape(
                block_rows, local_heads, head_size
            )
            grad_block = grad_row[block_start : block_start + block_rows].reshape(
                block_rows, local_heads, head_size
            )
            logits = scores_for(query_block, key_rows, block_start)
            probs_full = jnp.exp(logits - log_row[:, block_start : block_start + block_rows, None])
            prob_low = probs_full.astype(jnp.bfloat16)
            probs_grad = jnp.einsum(
                "qhd,khd->hqk", grad_block, value_rows, preferred_element_type=jnp.float32
            )
            inner_sum = jnp.sum(probs_full * probs_grad, -1, keepdims=True)
            scores_grad = (probs_full * (probs_grad - inner_sum)).astype(jnp.bfloat16)
            values_total = values_total + jnp.einsum(
                "hqk,qhd->khd", prob_low, grad_block, preferred_element_type=jnp.float32
            )
            query_grad = (
                jnp.einsum(
                    "hqk,khd->qhd", scores_grad, key_rows, preferred_element_type=jnp.float32
                )
                * score_scale
            )
            query_parts.append(query_grad.reshape(block_rows, slab_width).astype(jnp.bfloat16))
            keys_total = (
                keys_total
                + jnp.einsum(
                    "hqk,qhd->khd", scores_grad, query_block, preferred_element_type=jnp.float32
                )
                * score_scale
            )
        return (
            jnp.concatenate(query_parts, 0),
            keys_total.reshape(full_length, slab_width).astype(jnp.bfloat16),
            values_total.reshape(full_length, slab_width).astype(jnp.bfloat16),
        )

    query_grad_heads, key_grad_heads, value_grad_heads = lax.map(
        attend_back, (query_heads, key_heads, value_heads, grad_heads, log_sums)
    )
    query_grad_pos, key_grad_pos, value_grad_pos = (
        lax.all_to_all(
            for_sending(query_grad_heads), "seq", split_axis=1, concat_axis=2, tiled=True
        ).astype(query_grad_heads.dtype),
        lax.all_to_all(
            for_sending(key_grad_heads), "seq", split_axis=1, concat_axis=2, tiled=True
        ).astype(key_grad_heads.dtype),
        lax.all_to_all(
            for_sending(value_grad_heads), "seq", split_axis=1, concat_axis=2, tiled=True
        ).astype(value_grad_heads.dtype),
    )
    projected_grad = jnp.concatenate(
        [
            rotate_back(query_grad_pos.astype(jnp.float32), cosine, sine_term),
            rotate_back(key_grad_pos.astype(jnp.float32), cosine, sine_term),
            value_grad_pos.astype(jnp.float32),
        ],
        -1,
    )
    projected_grad = projected_grad.astype(jnp.bfloat16).reshape(token_count, 3 * features)
    qkv_grad = jnp.einsum(
        "nd,ne->de", normed_low, projected_grad, preferred_element_type=jnp.float32
    )
    normed_grad = normed_grad + jnp.einsum(
        "ne,de->nd", projected_grad, qkv_weight, preferred_element_type=jnp.float32
    )
    gain_grad = jnp.sum(normed_grad * normed_hat, 0)
    bias_grad = jnp.sum(normed_grad, 0)
    scaled_grad = normed_grad * gain_f32
    hat_grad = (
        scaled_grad
        - jnp.mean(scaled_grad, -1, keepdims=True)
        - normed_hat * jnp.mean(scaled_grad * normed_hat, -1, keepdims=True)
    )
    input_grad = (grad_f32 + inv_std * hat_grad).reshape(row_count, seg_length, features)
    row_sums = jnp.sum(input_grad, 1)
    family_grad = jnp.einsum(
        "rf,rd->fd", family_hot.astype(jnp.float32), row_sums, precision=lax.Precision.HIGHEST
    )
    orient_grad = jnp.einsum(
        "rf,rd->fd", orient_hot.astype(jnp.float32), row_sums, precision=lax.Precision.HIGHEST
    )
    gain_sum, bias_sum, up_bias_sum, down_bias_sum, family_sum, orient_sum = lax.psum(
        (gain_grad, bias_grad, up_bias_grad, down_bias_grad, family_grad, orient_grad),
        ("dp", "seq"),
    )
    qkv_sum, out_sum, up_sum, down_sum = (
        lax.psum_scatter(qkv_grad, ("dp", "seq"), scatter_dimension=0, tiled=True),
        lax.psum_scatter(out_grad, ("dp", "seq"), scatter_dimension=0, tiled=True),
        lax.psum_scatter(up_grad, ("dp", "seq"), scatter_dimension=0, tiled=True),
        lax.psum_scatter(down_grad, ("dp", "seq"), scatter_dimension=0, tiled=True),
    )
    return (
        layer_out,
        input_grad,
        gain_sum,
        bias_sum,
        qkv_sum,
        out_sum,
        up_sum,
        up_bias_sum,
        down_sum,
        down_bias_sum,
        family_sum,
        orient_sum,
    )


def dot_nn(a, b):
    return lax.dot_general(a, b, (((1,), (0,)), ((), ())), preferred_element_type=F32)


def dot_nt(a, b):
    return lax.dot_general(a, b, (((1,), (1,)), ((), ())), preferred_element_type=F32)


def dot_tn(a, b):
    return lax.dot_general(a, b, (((0,), (0,)), ((), ())), preferred_element_type=F32)


def params(**more):
    return pltpu.CompilerParams(vmem_limit_bytes=VMEM_LIMIT, **more)


def cost(flops, moved, exps=0):
    return pl.CostEstimate(flops=flops, bytes_accessed=moved, transcendentals=exps)


def whole(shape):
    return pl.BlockSpec(shape, lambda *_: (0,) * len(shape), pipeline_mode=pl.Buffered(1))


def table_row(table, wanted):
    rows = lax.broadcasted_iota(jnp.int32, table.shape, 0)
    return jnp.sum(jnp.where(rows == wanted, table[...].astype(F32), 0.0), 0, keepdims=True)


def line(vector):
    return vector[...].astype(F32).reshape(1, -1)


def normalise(entries):
    centred = entries - jnp.mean(entries, -1, keepdims=True)
    inv_std = lax.rsqrt(jnp.mean(centred * centred, -1, keepdims=True) + 1e-05)
    return centred * inv_std, inv_std


GELU_C = math.sqrt(2.0 / math.pi)


def gelu_both(z):
    square = z * z
    half = 0.5 + 0.5 * jnp.tanh(z * (GELU_C + (GELU_C * 0.044715) * square))
    value = z * half
    slope = half + value * (1.0 - half) * (2 * GELU_C + (6 * GELU_C * 0.044715) * square)
    return value, slope


def ffn_kernel(rows, fid, oid, hid, cot, fam, ori, gain, bias, wup, bup, wdn, turned, both, bupg, bdng, norm, shifts):
    tokens = hid.shape[0]
    seg = tokens // rows
    step = 256
    i = pl.program_id(0)
    @pl.when(i == 0)
    def _():
        total = jnp.zeros((1, cot.shape[1]), F32)
        for row in range(rows):
            emb = table_row(fam, fid[0]) + table_row(ori, oid[row])
            for start in range(row * seg, (row + 1) * seg, step):
                part = pl.ds(start, step)
                hat, _ = normalise(hid[part, :].astype(F32) + emb)
                norm[part, :] = (hat * line(gain) + line(bias)).astype(BF16)
                total = total + jnp.sum(cot[part, :].astype(F32), 0, keepdims=True)
        bdng[...] = total
        turned[...] = norm[...].T
        shifts[...] = line(bup)

    width = wup.shape[1]
    total = jnp.zeros((8, width), F32)
    lin = dot_nn(norm[...], wup[...])
    into = dot_nt(cot[...], wdn[...])
    shift = shifts[:, pl.ds(pl.multiple_of(i * width, width), width)]
    step = 64
    for start in range(0, tokens, step):
        part = pl.ds(start, step)
        value, slope = gelu_both(lin[start : start + step] + shift)
        low = into[start : start + step] * slope
        both[0, part, :] = value.astype(BF16)
        both[1, part, :] = low.astype(BF16)
        total = total + jnp.sum(low.reshape(step // 8, 8, width), 0)
    bupg[...] = jnp.sum(total, 0, keepdims=True)


def ffn_forward(fid, oid, hid, cot, fam, ori, gain, bias, wup, bup, wdn, rows):
    tokens, d = hid.shape
    ff = wup.shape[1]
    tile = 512
    smem = pl.BlockSpec(memory_space=pltpu.SMEM)
    return pl.pallas_call(
        functools.partial(ffn_kernel, rows),
        grid=(ff // tile,),
        in_specs=[
            smem,
            smem,
            whole((tokens, d)),
            whole((tokens, d)),
            whole(fam.shape),
            whole(ori.shape),
            whole(gain.shape),
            whole(bias.shape),
            pl.BlockSpec((d, tile), lambda i: (0, i)),
            whole(bup.shape),
            pl.BlockSpec((tile, d), lambda i: (i, 0)),
        ],
        out_specs=[
            whole((d, tokens)),
            pl.BlockSpec((2, tokens, tile), lambda i: (0, 0, i)),
            pl.BlockSpec((1, tile), lambda i: (0, i)),
            whole((1, d)),
        ],
        out_shape=[
            jax.ShapeDtypeStruct((d, tokens), BF16),
            jax.ShapeDtypeStruct((2, tokens, ff), BF16),
            jax.ShapeDtypeStruct((1, ff), F32),
            jax.ShapeDtypeStruct((1, d), F32),
        ],
        scratch_shapes=[
            pltpu.VMEM((tokens, d), BF16),
            pltpu.VMEM((1, ff), F32),
        ],
        compiler_params=params(),
        cost_estimate=cost(4 * tokens * d * ff, 4 * tokens * ff + 4 * d * ff, tokens * ff),
        name="ffn_forward",
    )(fid, oid, hid, cot, fam, ori, gain, bias, wup, bup, wdn)


def turn(entries, cosine, sine):
    even = lax.broadcasted_iota(jnp.int32, entries.shape, 1) % 2 == 0
    other = jnp.where(even, pltpu.roll(entries, 127, 1), pltpu.roll(entries, 1, 1))
    return entries * cosine + other * sine


def turn_back(entries, cosine, sine):
    even = lax.broadcasted_iota(jnp.int32, entries.shape, 1) % 2 == 0
    side = entries * sine
    other = jnp.where(even, pltpu.roll(side, 127, 1), pltpu.roll(side, 1, 1))
    return entries * cosine + other


def attend(head_size, query_ref, k_ref, v_ref, g_ref, cos, sin, o_ref, dq_ref, dk_ref, dv_ref, dkt, dvt):
    full = query_ref.shape[0]
    block = 256
    scale = head_size ** (-0.5)
    first = lax.broadcasted_iota(jnp.int32, (block, 128), 1) < head_size
    below = lax.broadcasted_iota(jnp.int32, (block, block), 0) >= lax.broadcasted_iota(
        jnp.int32, (block, block), 1
    )
    dkt[...] = jnp.zeros_like(dkt)
    dvt[...] = jnp.zeros_like(dvt)

    def by_head(entries):
        none = jnp.zeros_like(entries)
        return jnp.concatenate([jnp.where(first, entries, none), jnp.where(first, none, entries)], 0)

    def front(start):
        part, end = pl.ds(start, block), start + block
        query = by_head((query_ref[part, :].astype(F32) * scale).astype(BF16))
        grad = by_head(g_ref[part, :])
        return query, grad, dot_nt(query, k_ref[0:end, :]), dot_nt(grad, v_ref[0:end, :])

    def back(start, query, grad, scores, into):
        part, end = pl.ds(start, block), start + block
        lows, slopes = [], []
        for head in range(2):
            rows = slice(head * block, (head + 1) * block)
            score = scores[rows]
            last = jnp.where(below, score[:, start:end], -1e30)
            score = last if start == 0 else jnp.concatenate([score[:, :start], last], 1)
            weights = jnp.exp(score - jnp.max(score, -1, keepdims=True))
            probs = weights * (1.0 / jnp.sum(weights, -1, keepdims=True))
            lows.append(probs.astype(BF16))
            inner = jnp.sum(probs * into[rows], -1, keepdims=True)
            slopes.append((probs * (into[rows] - inner)).astype(BF16))
        low = jnp.concatenate(lows, 0)
        slope = jnp.concatenate(slopes, 0)
        out = dot_nn(low, v_ref[0:end, :])
        dq = dot_nn(slope, k_ref[0:end, :])
        o_ref[part, :] = jnp.where(first, out[:block], out[block:]).astype(BF16)
        dq = jnp.where(first, dq[:block], dq[block:]) * scale
        dq_ref[part, :] = turn_back(dq, cos[part, :], sin[part, :]).astype(BF16)
        dkt[:, 0:end] += dot_tn(query, slope)
        dvt[:, 0:end] += dot_tn(grad, low)

    ready = front(0)
    for start in range(0, full, block):
        later = front(start + block) if start + block < full else None
        back(start, *ready)
        ready = later
    for start in range(0, full, block):
        part = pl.ds(start, block)
        dk = dkt[:, start : start + block].T
        dk_ref[part, :] = turn_back(dk, cos[part, :], sin[part, :]).astype(BF16)
        dv_ref[part, :] = dvt[:, start : start + block].T.astype(BF16)


FFN_ORDERS = [
    [2, 1, "seq", 3],
    [1, 2, 3, "seq"],
    [2, 1, "seq", 3],
    [1, "seq", 2, 3],
    [1, "seq", 2, 3],
    [2, 1, "seq", 3],
    [2, 1, "seq", 3],
    ["seq", 2, 1, 3],
]
LATE_ORDERS = [
    [0, 2, 1, 3, "seq"],
    [0, 1, 2, 3, "seq"],
    [0, 2, "seq", 1, 3],
    [0, 1, 2, "seq", 3],
]
FFN_EVENTS = {
    4: [(0, 0)],
    6: [(1, 0)],
    8: [(2, 0)],
    9: [(3, 0)],
    14: [(0, 1)],
    15: [(1, 1)],
    17: [(7, 0), (4, 0), (5, 0), (6, 0), (2, 1)],
    20: [(3, 1)],
    21: [(1, 2)],
    23: [(0, 2)],
    26: [(5, 1), (7, 1), (4, 1)],
    27: [(3, 2), (2, 2), (0, 3), (6, 1)],
    28: [(1, 3), (5, 2), (4, 2)],
    29: [(7, 2), (2, 3), (3, 3), (6, 2)],
    30: [(0, 4), (1, 4), (4, 3), (5, 3)],
    31: [(7, 3), (2, 4), (6, 3), (3, 4)],
    32: [(4, 4), (5, 4), (7, 4), (6, 4)],
}
LATE_EVENTS = {
    2: [(0, 1)],
    3: [(1, 1)],
    4: [(2, 1)],
    6: [(0, 2)],
    7: [(3, 1), (1, 2)],
    9: [(0, 3), (2, 2)],
    10: [(1, 3)],
    13: [(3, 2), (0, 4)],
    14: [(2, 3)],
    15: [(0, 5), (1, 4)],
    16: [(2, 4)],
    17: [(1, 5), (3, 3)],
    18: [(2, 5)],
    20: [(3, 4)],
    22: [(3, 5)],
}


def middle_kernel(tiles, pairs, head_size, bits, orders, *refs):
    fid, oid, home_cot, turned, pre, act, fam, ori, gain, bias, wqkv, wout, angles, hid_hbm, cot_hbm = refs[:15]
    norm, cot, o_ref, dq_ref, dk_ref, dv_ref, far_att, up_out, down_out = refs[15:24]
    near_up, far_up, near_down, far_down = refs[24:28]
    heads, dkt, dvt, att_send, att_got, att_sems, cfar, cfar_sems = refs[28:36]
    keep, send, got, send_sem, recv_sem, out_sem = refs[36:42]
    up_keep, up_send, up_got, up_ssem, up_rsem, up_osem = refs[42:48]
    own, cos, sin, own_sem, far, far_sems = refs[48:54]
    seg = far.shape[0]
    step = 256
    base = 1 << (bits - 1)
    now = pl.program_id(0)
    ups = up_out.shape[1] // up_keep.shape[3]
    late = now - ups
    i = late - base
    me = lax.axis_index("seq")
    mine = device_bits(bits)
    parts = len(orders) // 2
    up_part = up_out.shape[1] // parts
    down_part = down_out.shape[1] // parts
    chunks = chunks_from(
        refs[54:],
        bits,
        mine,
        [
            (orders[part], near_up, far_up, pl.ds(part * up_part, up_part), up_out)
            for part in range(parts)
        ]
        + [
            (orders[parts + part], near_down, far_down, pl.ds(part * down_part, down_part), down_out)
            for part in range(parts)
        ],
    )

    def happen(events):
        for chunk, stage in events:
            chunks[chunk].happen(stage)

    @pl.when(now == 0)
    def _():
        meet([partner_along(axis, mine) for axis in [0] + orders[0]])

    cot_crossing = remote(
        cot_hbm.at[pl.ds(pl.multiple_of((1 - me) * seg, seg), seg)],
        cfar,
        cfar_sems.at[0],
        cfar_sems.at[1],
        partner_along("seq", mine),
    )

    far_crossing = remote(
        hid_hbm.at[pl.ds(pl.multiple_of((1 - me) * seg, seg), seg)],
        far,
        far_sems.at[0],
        far_sems.at[1],
        partner_along("seq", mine),
    )
    own_load = pltpu.make_async_copy(hid_hbm.at[pl.ds(pl.multiple_of(me * seg, seg), seg)], own, own_sem)

    @pl.when(now == 0)
    def _():
        far_crossing.start()
        cot_crossing.start()
        own_load.start()

    last = ups + base + 4 * tiles + pairs
    def up_crossing(index):
        slot = lax.rem(index, 2)
        return remote(
            up_send.at[slot], up_got.at[slot], up_ssem.at[slot], up_rsem.at[slot], partner_along(0, mine)
        )

    def up_stores(index):
        slot = lax.rem(index, 2)
        width = up_keep.shape[3]
        columns = pl.ds(pl.multiple_of(index * width, width), width)
        return [
            pltpu.make_async_copy(
                up_keep.at[slot, pl.ds(half * base, base)], there.at[:, :, columns], up_osem.at[half, slot]
            )
            for half, there in enumerate((near_up, far_up))
        ]

    def up_finish(index):
        slot = lax.rem(index, 2)
        up_crossing(index).wait()
        add_into(up_keep.at[slot], up_got.at[slot])
        for copy in up_stores(index):
            copy.start()

    for when, what in FFN_EVENTS.items():
        if when < last:

            @pl.when(now == when)
            def _():
                happen(what)

    per_chunk = ups // parts
    for part in range(parts):
        places = [block_place(orders[part], mine, up, seq) for up in range(base) for seq in range(2)]

        @pl.when((now >= part * per_chunk) & (now < (part + 1) * per_chunk))
        def _():
            value = dot_nn(turned[...], pre[...])
            slot = lax.rem(now, 2)

            @pl.when(now > 0)
            def _():
                up_finish(now - 1)

            @pl.when(now > 1)
            def _():
                for copy in up_stores(now - 2):
                    copy.wait()

            split_blocks(value, up_keep.at[slot], up_send.at[slot], up_keep.shape[2], mine[0], places)
            up_crossing(now).start()

    @pl.when(now == ups)
    def _():
        up_finish(now - 1)
        for index in (now - 2, now - 1):
            for copy in up_stores(index):
                copy.wait()

    def crossing(index):
        slot = lax.rem(index, 2)
        return remote(
            send.at[slot], got.at[slot], send_sem.at[slot], recv_sem.at[slot], partner_along(0, mine)
        )

    def store(index, act_on):
        slot = lax.rem(index, 2)
        width = home_cot.shape[1] // parts
        for seq in range(2):
            for part in range(parts):
                place = 0
                for axis in orders[parts + part]:
                    if axis == "seq":
                        apart = lax.rem(mine["seq"] + seq, 2)
                    else:
                        apart = lax.rem(index // (1 << (axis - 1)) + mine[axis], 2)
                    place = 2 * place + apart
                columns = pl.ds(part * width, width)
                source = keep.at[slot, seq, :, columns]
                sem = out_sem.at[slot, seq, part]
                there = lax.rem(place, base)

                @pl.when(place < base)
                def _():
                    act_on(pltpu.make_async_copy(source, near_down.at[there, :, columns], sem))

                @pl.when(place >= base)
                def _():
                    act_on(pltpu.make_async_copy(source, far_down.at[there, :, columns], sem))

    def finish(index):
        slot = lax.rem(index, 2)
        crossing(index).wait()
        add_into(keep.at[slot], got.at[slot])
        store(index, lambda copy: copy.start())

    @pl.when((late >= 0) & (late < base))
    def _():
        value = dot_nn(act[...].T, home_cot[...])
        slot = lax.rem(late, 2)

        @pl.when(late > 0)
        def _():
            finish(late - 1)

        @pl.when(late > 1)
        def _():
            store(late - 2, lambda copy: copy.wait())

        split_blocks(value, keep.at[slot], send.at[slot], keep.shape[2], mine[0], [0, 1])
        crossing(late).start()

    @pl.when(late == base)
    def _():
        finish(late - 1)
        store(late - 2, lambda copy: copy.wait())
        store(late - 1, lambda copy: copy.wait())

    @pl.when(i == 0)
    def _():
        own_load.wait()
        far_crossing.wait()
        fine = angles.shape[1]
        for coarse in range(2 * seg // fine):
            there = pl.ds(coarse * fine, fine)
            cos_a, sin_a = angles[0, coarse : coarse + 1, :], angles[1, coarse : coarse + 1, :]
            cos[there, :] = cos_a * angles[2] - sin_a * angles[3]
            sin[there, :] = sin_a * angles[2] + cos_a * angles[3]
        emb = table_row(fam, fid[0]) + table_row(ori, oid[me])
        for source, where in ((own, me), (far, 1 - me)):
            for start in range(0, seg, step):
                part = pl.ds(start, step)
                there = pl.ds(pl.multiple_of(where * seg + start, step), step)
                hat, _ = normalise(source[part, :].astype(F32) + emb)
                norm[there, :] = (hat * line(gain) + line(bias)).astype(BF16)
        held = pl.ds(pl.multiple_of(me * seg, seg), seg)
        cot[held, :] = home_cot[held, :]

    lanes = wqkv.shape[1] // 128

    def att_crossing(pair):
        return remote(
            att_send.at[pair],
            att_got.at[pair],
            att_sems.at[0, pair],
            att_sems.at[1, pair],
            partner_along("seq", mine),
        )

    @pl.when((i >= 0) & (i < 2 * tiles))
    def _():
        lin = dot_nn(norm[...], wqkv[...])
        for start in range(0, 2 * seg, step):
            part = pl.ds(start, step)
            for lane in range(lanes):
                piece = lin[start : start + step, lane * 128 : (lane + 1) * 128]
                heads[i * lanes + lane, part, :] = turn(piece, cos[part, :], sin[part, :]).astype(BF16)

    @pl.when((i >= 2 * tiles) & (i < 3 * tiles))
    def _():
        lin = dot_nn(norm[...], wqkv[...]).astype(BF16)
        for lane in range(lanes):
            heads[i * lanes + lane] = lin[:, lane * 128 : (lane + 1) * 128]

    @pl.when(i == 3 * tiles)
    def _():
        cot_crossing.wait()
        cot[pl.ds(pl.multiple_of((1 - me) * seg, seg), seg), :] = cfar[...]

    @pl.when((i >= 3 * tiles) & (i < 4 * tiles))
    def _():
        lin = dot_nt(cot[...], wout[...]).astype(BF16)
        for lane in range(lanes):
            heads[i * lanes + lane] = lin[:, lane * 128 : (lane + 1) * 128]

    @pl.when(i >= 4 * tiles)
    def _():
        pair = i - 4 * tiles
        attend(
            head_size,
            heads.at[pair],
            heads.at[pairs + pair],
            heads.at[2 * pairs + pair],
            heads.at[3 * pairs + pair],
            cos,
            sin,
            o_ref,
            dq_ref,
            dk_ref,
            dv_ref,
            dkt,
            dvt,
        )
        att_send[pair] = o_ref[pl.ds(pl.multiple_of((1 - me) * seg, seg), seg), :]
        att_crossing(pair).start()

    @pl.when(now == last - 1)
    def _():
        for pair in range(pairs):
            att_crossing(pair).wait()
            far_att[:, pair * 128 : (pair + 1) * 128] = att_got[pair]
        happen(FFN_EVENTS[last])


def middle(
    fid, oid, hid, home_cot, turned, both, fam, ori, gain, bias, wqkv, wout, angles, orders, head_size, collective
):
    full, d = hid.shape
    seg = full // 2
    tile = 512
    tiles = d // tile
    pairs = d // 128
    bits = len(orders[0])
    base = 1 << (bits - 1)
    parts = len(orders) // 2
    ff = both.shape[2]
    up_size = d // (4 * base)
    up_tile = 512
    ups = ff // up_tile
    down_tile = ff // base
    down_size = down_tile // 4
    smem = pl.BlockSpec(memory_space=pltpu.SMEM)
    anywhere = pl.BlockSpec(memory_space=pl.ANY)
    late = ups + base
    attend_at = late + 4 * tiles
    head_out = pl.BlockSpec((full, 128), lambda i: (0, jnp.maximum(i - attend_at, 0)))
    rows = jax.ShapeDtypeStruct((full, d), BF16)
    down = jax.ShapeDtypeStruct((base, down_size, d), BF16)
    up = jax.ShapeDtypeStruct((base, up_size, ff), BF16)
    slots = pltpu.VMEM((2, 2, down_size, d), BF16)
    up_slots = pltpu.VMEM((2, 2 * base, up_size, up_tile), BF16)
    return pl.pallas_call(
        functools.partial(middle_kernel, tiles, pairs, head_size, bits, orders),
        grid=(attend_at + pairs,),
        in_specs=[
            smem,
            smem,
            whole((full, d)),
            whole((d, full)),
            pl.BlockSpec((None, full, up_tile), lambda i: (1, 0, jnp.minimum(i, ups - 1))),
            pl.BlockSpec((None, full, down_tile), lambda i: (0, 0, jnp.clip(i - ups, 0, base - 1))),
            whole(fam.shape),
            whole(ori.shape),
            whole(gain.shape),
            whole(bias.shape),
            pl.BlockSpec((d, tile), lambda i: (0, jnp.clip(i - late, 0, 3 * tiles - 1))),
            pl.BlockSpec((tile, d), lambda i: (jnp.clip(i - late - 3 * tiles, 0, tiles - 1), 0)),
            whole(angles.shape),
        ]
        + [anywhere] * 2,
        out_specs=[
            whole((full, d)),
            whole((full, d)),
            head_out,
            head_out,
            head_out,
            head_out,
            whole((seg, d)),
            whole((up_size, ff)),
            whole((down_size, d)),
            anywhere,
            anywhere,
            anywhere,
            anywhere,
        ],
        out_shape=[
            rows,
            rows,
            rows,
            rows,
            rows,
            rows,
            jax.ShapeDtypeStruct((seg, d), BF16),
            jax.ShapeDtypeStruct((up_size, ff), F32),
            jax.ShapeDtypeStruct((down_size, d), F32),
            up,
            up,
            down,
            down,
        ],
        scratch_shapes=[
            pltpu.VMEM((4 * pairs, full, 128), BF16),
            pltpu.VMEM((128, full), F32),
            pltpu.VMEM((128, full), F32),
            pltpu.VMEM((pairs, seg, 128), BF16),
            pltpu.VMEM((pairs, seg, 128), BF16),
            pltpu.SemaphoreType.DMA((2, pairs)),
            pltpu.VMEM((seg, d), BF16),
            pltpu.SemaphoreType.DMA((2,)),
            slots,
            slots,
            slots,
            pltpu.SemaphoreType.DMA((2,)),
            pltpu.SemaphoreType.DMA((2,)),
            pltpu.SemaphoreType.DMA((2, 2, parts)),
            up_slots,
            up_slots,
            up_slots,
            pltpu.SemaphoreType.DMA((2,)),
            pltpu.SemaphoreType.DMA((2,)),
            pltpu.SemaphoreType.DMA((2, 2)),
            pltpu.VMEM((seg, d), BF16),
            pltpu.VMEM((full, 128), F32),
            pltpu.VMEM((full, 128), F32),
            pltpu.SemaphoreType.DMA,
            pltpu.VMEM((seg, d), BF16),
            pltpu.SemaphoreType.DMA((2,)),
        ]
        + [
            entry
            for index, axes in enumerate(orders)
            for entry in chunk_scratch(
                axes, *((up_size, ff // parts) if index < parts else (down_size, d // parts))
            )
        ],
        compiler_params=pltpu.CompilerParams(
            vmem_limit_bytes=67043328, collective_id=collective, has_side_effects=True
        ),
        cost_estimate=cost(16 * full * d * d + 12 * full * full * d, 8 * d * d + 18 * full * d, full * full * H),
        name="middle",
    )(fid, oid, home_cot, turned, both, both, fam, ori, gain, bias, wqkv, wout, angles, hid, home_cot)


def device_bits(bits):
    dp = lax.axis_index("dp")
    found = {bit: lax.rem(dp // (1 << bit), 2) for bit in range(bits)}
    found["seq"] = lax.axis_index("seq")
    return found


def block_place(axes, mine, upper, seq):
    place = 0
    for axis in axes:
        bit = seq if axis == "seq" else (upper >> (axis - 1)) & 1
        place = 2 * place + (1 - mine[axis] if bit else mine[axis])
    return place


def other_core():
    dp = lax.axis_index("dp")
    return (dp + 1 - 2 * lax.rem(dp, 2), lax.axis_index("seq"))


def meet(partners):
    barrier = pltpu.get_barrier_semaphore()
    for partner in partners:
        pl.semaphore_signal(barrier, inc=1, device_id=partner, device_id_type=MESH)
    pl.semaphore_wait(barrier, len(partners))


def remote(src, dst, send_sem, recv_sem, partner):
    return pltpu.make_async_remote_copy(
        src_ref=src,
        dst_ref=dst,
        send_sem=send_sem,
        recv_sem=recv_sem,
        device_id=partner,
        device_id_type=MESH,
    )


def split_blocks(value, keep, send, size, core, places):
    for index, there in enumerate(places):
        up, seq = index // 2, index % 2
        first = (4 * up + seq) * size
        second = first + 2 * size
        a = value[first : first + size, :].astype(BF16)
        b = value[second : second + size, :].astype(BF16)
        keep[there] = jnp.where(core == 0, a, b)
        send[there] = jnp.where(core == 0, b, a)


def add_into(keep, got):
    def add(index, carry):
        keep[index] = (keep[index].astype(F32) + got[index].astype(F32)).astype(BF16)
        return carry

    lax.fori_loop(0, got.shape[0], add, 0, unroll=2 if got.shape[0] > 1 else 1)


def partner_along(axis, mine):
    dp = lax.axis_index("dp")
    seq = lax.axis_index("seq")
    if axis == "seq":
        return (dp, 1 - seq)
    return (dp + (1 - 2 * mine[axis]) * (1 << axis), seq)


class Chunk:
    def __init__(self, axes, mine, near, far, columns, out, keep, got, near_sem, send_sem, recv_sem):
        self.axes, self.mine, self.near, self.far = axes, mine, near, far
        self.columns, self.out, self.keep, self.got = columns, out, keep, got
        self.near_sem, self.send_sem, self.recv_sem = near_sem, send_sem, recv_sem

    def load(self):
        return pltpu.make_async_copy(self.near.at[:, :, self.columns], self.keep, self.near_sem)

    def crossing(self, stage):
        count = (1 << len(self.axes)) >> (stage + 1)
        if stage == 0 and self.far is not None:
            source = self.far.at[:, :, self.columns]
        else:
            source = self.keep.at[pl.ds(count, count)]
        return remote(
            source,
            self.got[stage],
            self.send_sem.at[stage],
            self.recv_sem.at[stage],
            partner_along(self.axes[stage], self.mine),
        )

    def begin(self):
        if self.near is not None:
            self.load().start()
        self.crossing(0).start()

    def advance(self, stage):
        if stage == 1 and self.near is not None:
            self.load().wait()
        self.crossing(stage - 1).wait()
        add_into(self.keep, self.got[stage - 1])
        self.crossing(stage).start()

    def finish(self):
        last = len(self.axes) - 1
        self.crossing(last).wait()
        self.out[:, self.columns] = self.keep[0].astype(F32) + self.got[last][0].astype(F32)

    def happen(self, stage):
        if stage == 0:
            self.begin()
        elif stage == len(self.axes):
            self.finish()
        else:
            self.advance(stage)


def chunk_scratch(axes, size, width, farther=False):
    half = 1 << (len(axes) - 1)
    return (
        [pltpu.VMEM((2 * half if farther else half, size, width), BF16)]
        + [pltpu.VMEM((half >> stage, size, width), BF16) for stage in range(len(axes))]
        + [
            pltpu.SemaphoreType.DMA,
            pltpu.SemaphoreType.DMA((len(axes),)),
            pltpu.SemaphoreType.DMA((len(axes),)),
        ]
    )


def chunks_from(refs, bits, mine, wanted):
    stages = bits
    found = []
    each = 1 + stages + 3
    for index, (axes, near, far, columns, out) in enumerate(wanted):
        part = refs[index * each : (index + 1) * each]
        found.append(
            Chunk(axes, mine, near, far, columns, out, part[0], part[1 : 1 + stages], *part[1 + stages :])
        )
    return found


def after(entry, *others):
    return lax.optimization_barrier((entry, *others))[0]


TAIL_TILE = 1024
TAIL_STEP = 256


def tail_kernel(bits, orders, rows, marks, *refs):
    fid, oid, norm_hbm, att_hbm, cot_hbm, dq_hbm, dk_hbm, dv_hbm, wqkv_hbm, wout_hbm = refs[:10]
    fam, ori, gain, bdn, bup_part, bdn_part, far_att = refs[10:17]
    both, wdn, wup, hid, cot = refs[17:22]
    layer_out, input_out, qkv_out, out_out, sums_out, all_out = refs[22:28]
    left, dq, dk, dv, wqkv, wout, turned, acc, ng_here, ng_got = refs[28:38]
    gg, bg, rg, load_sem, ng_sem, held, got, vec, vgot, table, ssem, rsem, gsend, grecv = refs[38:52]
    in_start, in_end, out_start, out_end, last = marks
    i = pl.program_id(0)
    me = lax.axis_index("seq")
    dp = lax.axis_index("dp")
    mine = device_bits(bits)
    d = left.shape[1]
    seg = ng_got.shape[0]
    step = TAIL_STEP
    per_row = seg // step
    chunks = chunks_from(
        refs[52:],
        len(orders[0]),
        mine,
        [
            (orders[0], None, None, pl.ds(0, d), qkv_out),
            (orders[1], None, None, pl.ds(d, d), qkv_out),
            (orders[2], None, None, pl.ds(2 * d, d), qkv_out),
            (orders[3], None, None, pl.ds(0, d), out_out),
        ],
    )
    loads = {
        name: pltpu.make_async_copy(source, there, load_sem.at[index])
        for index, (name, source, there) in enumerate(
            (
                ("norm", norm_hbm, left),
                ("dq", dq_hbm, dq),
                ("dk", dk_hbm, dk),
                ("dv", dv_hbm, dv),
                ("wqkv", wqkv_hbm, wqkv),
                ("cot", cot_hbm, dq),
                ("wout", wout_hbm, wout),
                ("att", att_hbm, left),
            )
        )
    }
    partners = [partner_along(axis, mine) for axis in ["seq"] + list(range(bits))]

    def gradient(index, operand):
        chunk = chunks[index]
        size = chunk.keep.shape[1]
        value = dot_nn(turned[...], operand[...])
        for block in range(chunk.keep.shape[0]):
            place = 0
            for axis in orders[index]:
                bit = block & 1 if axis == "seq" else (block >> (axis + 1)) & 1
                place = 2 * place + (1 - mine[axis] if bit else mine[axis])
            chunk.keep[place] = value[block * size : (block + 1) * size, :].astype(BF16)
        chunk.begin()

    ng_crossing = remote(ng_here.at[0], ng_got, ng_sem.at[0], ng_sem.at[1], partners[0])

    @pl.when(i == 0)
    def _():
        loads["norm"].start()
        loads["dq"].start()
        meet(partners)
        loads["norm"].wait()
        turned[...] = left[...].T
        loads["dq"].wait()
        for name in ("dk", "dv", "wqkv", "att", "wout"):
            loads[name].start()
        gradient(0, dq)

    def sums_main(index):
        return remote(held.at[index], got.at[index], ssem.at[index], rsem.at[index], partners[index])

    def sums_side(index):
        if index == 0:
            return remote(vec, vgot, gsend.at[0], grecv.at[0], partners[0])
        size = 1 << (index - 1)
        now = pl.ds(dp - lax.rem(dp, size), size)
        return remote(table.at[now], table.at[now], gsend.at[index], grecv.at[index], partners[index])

    @pl.when(i == out_start)
    def _():
        at = 0
        for source in (bup_part[...], bdn_part[...], gg[...], bg[...], rg[0:1, :], rg[1:2, :]):
            for lane in range(0, source.shape[1], 128):
                held[0, at : at + 1, :] = source[:, lane : lane + 128]
                at += 1
        both_rows = rg[0:1, :] + rg[1:2, :]
        for lane in range(0, d, 128):
            vec[lane // 128 : lane // 128 + 1, :] = both_rows[:, lane : lane + 128]
        extra = d // 128
        vec[extra:, :] = jnp.full((vec.shape[0] - extra, 128), 0.5, F32) * fid[0].astype(F32)
        sums_main(0).start()
        sums_side(0).start()

    for index in range(len(partners)):

        @pl.when(i == out_start + (index + 1 if index < len(partners) - 1 else last - 1 - out_start))
        def _():
            sums_main(index).wait()
            sums_side(index).wait()
            total = held[index] + got[index]
            if index == 0:
                table[dp] = vec[...] + vgot[...]
            if index + 1 < len(partners):
                held[index + 1] = total
                sums_main(index + 1).start()
                sums_side(index + 1).start()
            else:
                sums_out[...] = total
                all_out[...] = table[...]

    for when, what in LATE_EVENTS.items():
        if when < last:

            @pl.when(i == when)
            def _():
                for chunk, stage in what:
                    chunks[chunk].happen(stage)

    @pl.when(i == 1)
    def _():
        loads["dk"].wait()
        gradient(1, dk)

    @pl.when(i == 2)
    def _():
        loads["dv"].wait()
        gradient(2, dv)

    @pl.when(i == 3)
    def _():
        loads["wqkv"].wait()

    @pl.when((i == 3) | (i == 4))
    def _():
        first = 4 - i
        half = first * (1 - me) + (1 - first) * me
        part = pl.ds(pl.multiple_of(half * seg, seg), seg)
        total = dot_nt(dq[part, :], wqkv[:, 0:d])
        total = total + dot_nt(dk[part, :], wqkv[:, d : 2 * d])
        total = total + dot_nt(dv[part, :], wqkv[:, 2 * d : 3 * d])
        ng_here[1 - first] = total.astype(BF16)

    @pl.when(i == 3)
    def _():
        ng_crossing.start()

    @pl.when(i == 5)
    def _():
        loads["cot"].start()
        loads["att"].wait()
        turned[...] = left[...].T
        loads["cot"].wait()
        gradient(3, dq)

    @pl.when((i >= out_start) & (i < out_end))
    def _():
        value = dot_nn(both[0], wdn[...])

        @pl.when(i == out_start)
        def _():
            acc[...] = value

        @pl.when(i > out_start)
        def _():
            acc[...] += value

    @pl.when((i >= in_start) & (i < in_end))
    def _():
        value = dot_nt(both[0], wup[...])

        @pl.when(i == in_start)
        def _():
            acc[...] = value

        @pl.when(i > in_start)
        def _():
            acc[...] += value

    @pl.when(i == out_end)
    def _():
        loads["wout"].wait()

    def home_block(index, own, far, own_offset):
        row = index // per_row
        within = pl.multiple_of(lax.rem(index, per_row) * step, step)
        there = pl.ds(pl.multiple_of(own_offset + within, step), step)
        return row, jnp.where(row == me, own[there, :], far[pl.ds(within, step), :])

    @pl.when(i >= out_end)
    def _():
        index = i - out_end
        row, att = home_block(index, left, far_att, me * seg)
        flag = oid[row]
        emb = table_row(fam, fid[0]) + table_row(ori, flag)
        part = pl.ds(pl.multiple_of(index * step, step), step)
        total = hid[...].astype(F32) + emb + dot_nn(att, wout[...])
        layer_out[...] = (total + (acc[part, :] + line(bdn))).astype(BF16)

    @pl.when(i == in_end)
    def _():
        ng_crossing.wait()
        gg[...] = jnp.zeros_like(gg)
        bg[...] = jnp.zeros_like(bg)
        rg[...] = jnp.zeros_like(rg)

    @pl.when((i >= in_end) & (i < out_start))
    def _():
        index = i - in_end
        row, back = home_block(index, ng_here.at[1], ng_got, 0)
        flag = oid[row]
        emb = table_row(fam, fid[0]) + table_row(ori, flag)
        part = pl.ds(pl.multiple_of(index * step, step), step)
        hat, inv_std = normalise(hid[...].astype(F32) + emb)
        grad = acc[part, :] + back.astype(F32)
        gg[...] += jnp.sum(grad * hat, 0, keepdims=True)
        bg[...] += jnp.sum(grad, 0, keepdims=True)
        scaled = grad * line(gain)
        inner = (
            scaled
            - jnp.mean(scaled, -1, keepdims=True)
            - hat * jnp.mean(scaled * hat, -1, keepdims=True)
        )
        result = cot[...].astype(F32) + inv_std * inner
        input_out[...] = result
        sums = jnp.sum(result, 0, keepdims=True)
        which = lax.broadcasted_iota(jnp.int32, rg.shape, 0)
        rg[...] += jnp.where(which == flag, sums, 0.0)

    @pl.when(i == last - 1)
    def _():
        for chunk, stage in LATE_EVENTS[last]:
            chunks[chunk].happen(stage)


def tail(fid, oid, norm, att, row_cot, dq, dk, dv, wqkv, wout, fam, ori, gain, bdn, bup_part, bdn_part, far_att, both, wdn, wup, hid, cot, orders, rows, collective):
    tokens, d = hid.shape
    ff = wup.shape[1]
    bits = len(orders[0]) - 1
    count = 1 << bits
    seg = far_att.shape[0]
    tile, step = TAIL_TILE, TAIL_STEP
    tiles, blocks = ff // tile, tokens // step
    in_start = 6
    in_end = in_start + tiles
    out_start = in_end + blocks
    out_end = out_start + tiles
    last = out_end + blocks
    marks = (in_start, in_end, out_start, out_end, last)
    size = d // (2 * count)
    rounds = bits + 1
    lines = (ff + 5 * d) // 128
    vec_shape = (d // 128 + 8, 128)
    anywhere = pl.BlockSpec(memory_space=pl.ANY)

    def plane(i):
        late = i >= out_start
        return (jnp.where(late, 0, 1), 0, jnp.clip(jnp.where(late, i - out_start, i - in_start), 0, tiles - 1))

    def home(i):
        return (jnp.clip(jnp.where(i >= out_start, i - out_end, i - in_end), 0, blocks - 1), 0)

    square = pltpu.VMEM((tokens, d), BF16)
    piece = pltpu.VMEM((seg, d), BF16)
    row = pltpu.VMEM((1, d), F32)
    return pl.pallas_call(
        functools.partial(tail_kernel, bits, orders, rows, marks),
        grid=(last,),
        in_specs=[pl.BlockSpec(memory_space=pltpu.SMEM)] * 2
        + [anywhere] * 8
        + [
            whole(fam.shape),
            whole(ori.shape),
            whole(gain.shape),
            whole(bdn.shape),
            whole((1, ff)),
            whole((1, d)),
            whole((seg, d)),
            pl.BlockSpec((1, tokens, tile), plane),
            pl.BlockSpec((tile, d), lambda i: (jnp.clip(i - out_start, 0, tiles - 1), 0)),
            pl.BlockSpec((d, tile), lambda i: (0, jnp.clip(i - in_start, 0, tiles - 1))),
            pl.BlockSpec((step, d), home),
            pl.BlockSpec((step, d), lambda i: (jnp.clip(i - in_end, 0, blocks - 1), 0)),
        ],
        out_specs=[
            pl.BlockSpec((step, d), lambda i: (jnp.clip(i - out_end, 0, blocks - 1), 0)),
            pl.BlockSpec((step, d), lambda i: (jnp.clip(i - in_end, 0, blocks - 1), 0)),
            whole((size, 3 * d)),
            whole((size, d)),
            whole((lines, 128)),
            whole((count,) + vec_shape),
        ],
        out_shape=[
            jax.ShapeDtypeStruct((tokens, d), BF16),
            jax.ShapeDtypeStruct((tokens, d), F32),
            jax.ShapeDtypeStruct((size, 3 * d), F32),
            jax.ShapeDtypeStruct((size, d), F32),
            jax.ShapeDtypeStruct((lines, 128), F32),
            jax.ShapeDtypeStruct((count,) + vec_shape, F32),
        ],
        scratch_shapes=[
            square,
            square,
            square,
            square,
            pltpu.VMEM((d, 3 * d), BF16),
            pltpu.VMEM((d, d), BF16),
            pltpu.VMEM((d, tokens), BF16),
            pltpu.VMEM((tokens, d), F32),
            pltpu.VMEM((2, seg, d), BF16),
            piece,
            row,
            row,
            pltpu.VMEM((2, d), F32),
            pltpu.SemaphoreType.DMA((8,)),
            pltpu.SemaphoreType.DMA((2,)),
            pltpu.VMEM((rounds, lines, 128), F32),
            pltpu.VMEM((rounds, lines, 128), F32),
            pltpu.VMEM(vec_shape, F32),
            pltpu.VMEM(vec_shape, F32),
            pltpu.VMEM((count,) + vec_shape, F32),
            pltpu.SemaphoreType.DMA((rounds,)),
            pltpu.SemaphoreType.DMA((rounds,)),
            pltpu.SemaphoreType.DMA((rounds,)),
            pltpu.SemaphoreType.DMA((rounds,)),
        ]
        + [entry for axes in orders for entry in chunk_scratch(axes, size, d, True)],
        compiler_params=pltpu.CompilerParams(
            vmem_limit_bytes=67043328, collective_id=collective, has_side_effects=True
        ),
        cost_estimate=cost(16 * tokens * d * d + 4 * tokens * d * ff, 8 * d * ff + 40 * tokens * d),
        name="tail",
    )(fid, oid, norm, att, row_cot, dq, dk, dv, wqkv, wout, fam, ori, gain, bdn, bup_part, bdn_part, far_att, both, wdn, wup, hid, cot)


def finish_kernel(ff, layer, inputs, qkv, out, up, down, sums, table, *outs):
    layer_out, input_out, qkv_out, out_out, up_out, down_out, bup, bdn, gain, bias, fam_out, ori_out = outs
    layer_out[...] = layer[...]
    input_out[...] = inputs[...]
    qkv_out[...] = qkv[...]
    out_out[...] = out[...]
    up_out[...] = up[...]
    down_out[...] = down[...]

    @pl.when(pl.program_id(0) == 0)
    def _():
        d = gain.shape[1]
        at = 0
        for there in (bup, bdn, gain, bias, ori_out.at[0:1], ori_out.at[1:2]):
            for lane in range(0, there.shape[1], 128):
                there[:, lane : lane + 128] = sums[at : at + 1, :]
                at += 1
        extra = d // 128
        rows = lax.broadcasted_iota(jnp.int32, (fam_out.shape[0], 128), 0).astype(F32)
        for lane in range(extra):
            total = jnp.zeros((fam_out.shape[0], 128), F32)
            for index in range(table.shape[0]):
                total = total + jnp.where(
                    rows == table[index, extra : extra + 1, :], table[index, lane : lane + 1, :], 0.0
                )
            fam_out[:, lane * 128 : (lane + 1) * 128] = total


def finish(layer, inputs, qkv, out, up, down, sums, table, families):
    tokens, d = layer.shape
    ff = up.shape[1]
    steps = 4

    def rows(entry):
        count = max(entry.shape[0] // steps, 8)
        each = steps * count // entry.shape[0]
        return pl.BlockSpec((count, entry.shape[1]), lambda i: (i // each, 0))

    big = [layer, inputs, qkv, out, up, down]
    small = [(1, ff), (1, d), (1, d), (1, d), (families, d), (2, d)]
    return pl.pallas_call(
        functools.partial(finish_kernel, ff),
        grid=(steps,),
        in_specs=[rows(entry) for entry in big] + [whole(sums.shape), whole(table.shape)],
        out_specs=[rows(entry) for entry in big] + [whole(shape) for shape in small],
        out_shape=[jax.ShapeDtypeStruct(entry.shape, entry.dtype) for entry in big]
        + [jax.ShapeDtypeStruct(shape, F32) for shape in small],
        compiler_params=params(),
        name="finish",
    )(*big, sums, table)


def body_by_rows(
    hidden_in,
    family,
    orient,
    norm_gain,
    norm_bias,
    qkv_weight,
    out_weight,
    up_weight,
    up_bias,
    down_weight,
    down_bias,
    family_table,
    orient_table,
    cotangent,
):
    rows, seg, d = hidden_in.shape
    ff = up_weight.shape[1]
    tokens = rows * seg
    full = 2 * seg
    dp_count = lax.axis_size("dp")
    bits = int(math.log2(dp_count))
    upper = dp_count // 2
    dp = lax.axis_index("dp")
    seq = lax.axis_index("seq")
    hid = hidden_in.reshape(tokens, d)
    cot = cotangent.reshape(tokens, d)
    turned, both, up_bias_part, down_bias_part = ffn_forward(
        family, orient, hid, cot, family_table, orient_table, norm_gain, norm_bias, up_weight, up_bias, down_weight, rows
    )
    fine = 32
    positions = jnp.concatenate([fine * jnp.arange(full // fine), jnp.arange(fine)]).astype(F32)
    cosine, sine = rope_tables(positions, 128)
    coarse = full // fine
    angles = jnp.stack([cosine[:coarse], sine[:coarse], cosine[coarse:], sine[coarse:]])
    row_normed, row_cot, att, dq, dk, dv, far_att, up_total, down_total, *_ = middle(
        family,
        orient,
        hid,
        cot,
        turned,
        both,
        family_table,
        orient_table,
        norm_gain,
        norm_bias,
        qkv_weight,
        out_weight,
        angles,
        FFN_ORDERS,
        d // H,
        3,
    )
    layer_out, input_grad, qkv_total, out_total, sums, gathered = tail(
        family,
        orient,
        row_normed,
        att,
        row_cot,
        dq,
        dk,
        dv,
        qkv_weight,
        out_weight,
        family_table,
        orient_table,
        norm_gain,
        down_bias,
        up_bias_part,
        down_bias_part,
        far_att,
        both,
        down_weight,
        up_weight,
        hid,
        cot,
        LATE_ORDERS,
        rows,
        4,
    )
    layer_out, input_grad, qkv_sum, out_sum, up_sum, down_sum, *small = finish(
        layer_out, input_grad, qkv_total, out_total, up_total, down_total, sums, gathered, family_table.shape[0]
    )
    up_bias_sum, down_bias_sum, gain_sum, bias_sum = (part.reshape(-1) for part in small[:4])
    return (
        layer_out.reshape(rows, seg, d),
        input_grad.reshape(rows, seg, d),
        gain_sum,
        bias_sum,
        qkv_sum,
        out_sum,
        up_sum,
        up_bias_sum,
        down_sum,
        down_bias_sum,
        small[4],
        small[5],
    )


def body(*args):
    hidden_in = args[0]
    dp_count = lax.axis_size("dp")
    two_rows = lax.axis_size("seq") == 2 and hidden_in.shape[0] == 2
    if two_rows and dp_count == 16 and hidden_in.shape[1] == 512:
        return body_by_rows(*args)
    return body_by_heads(*args)


def solution(mesh):
    return jax.shard_map(
        body,
        mesh=mesh,
        in_specs=(
            P("dp", "seq", None),
            P("dp"),
            P("dp"),
            P(),
            P(),
            P(),
            P(),
            P(),
            P(),
            P(),
            P(),
            P(),
            P(),
            P("dp", "seq", None),
        ),
        out_specs=(
            P("dp", "seq", None),
            P("dp", "seq", None),
            P(),
            P(),
            P(("dp", "seq"), None),
            P(("dp", "seq"), None),
            P(("dp", "seq"), None),
            P(),
            P(("dp", "seq"), None),
            P(),
            P(),
            P(),
        ),
        check_vma=False,
    )
```
